32 devices in a mesh: dp: 8 (over z, x), shard: 4 (over y, core).
Axes of the slice: x: 2, y: 2, z: 4, core: 2. Of those that a mesh axis runs over, the one named last changes fastest.
Arguments:
- images: bfloat16 [8, 591, 768], P('dp'), may hold values from -6 to 6
- out_grad: bfloat16 [8, 591, 768], P('dp'), may hold values from -6 to 6
- slot_kind: int32 [8], P('dp'), may hold values from 0 to 1
- small_index: int32 [197, 197], replicated, may hold values from 0 to 731, as said below
- large_index: int32 [577, 577], replicated, may hold values from 0 to 2211, as said below
- qkv_weight: bfloat16 [768, 3, 768], P('dp', None, 'shard'), may hold values from -0.21875 to 0.21875
- out_weight: bfloat16 [768, 768], P('shard', 'dp'), may hold values from -1.75 to 1.75
- fc1_weight: bfloat16 [768, 3072], P('dp', 'shard'), may hold values from -0.21875 to 0.21875
- fc2_weight: bfloat16 [3072, 768], P('shard', 'dp'), may hold values from -0.109375 to 0.109375
- norm1_gain: bfloat16 [768], P('dp'), may hold values from 0.099609375 to 1.8984375
- norm1_shift: bfloat16 [768], P('dp'), may hold values from -1.796875 to 1.796875
- query_bias: bfloat16 [768], P('shard'), may hold values from -1.796875 to 1.796875
- value_bias: bfloat16 [768], P('shard'), may hold values from -1.796875 to 1.796875
- out_bias: bfloat16 [768], P('dp'), may hold values from -1.796875 to 1.796875
- gamma_attn: bfloat16 [768], P('dp'), may hold values from 0.099609375 to 1.8984375
- norm2_gain: bfloat16 [768], P('dp'), may hold values from 0.099609375 to 1.8984375
- norm2_shift: bfloat16 [768], P('dp'), may hold values from -1.796875 to 1.796875
- fc1_bias: bfloat16 [3072], P('shard'), may hold values from -1.796875 to 1.796875
- fc2_bias: bfloat16 [768], P('dp'), may hold values from -1.796875 to 1.796875
- gamma_mlp: bfloat16 [768], P('dp'), may hold values from 0.099609375 to 1.8984375
- small_table: bfloat16 [732, 12], P(None, 'shard'), may hold values from -4 to 4
- large_table: bfloat16 [2212, 12], P(None, 'shard'), may hold values from -4 to 4
Outputs:
- layer_out: bfloat16 [8, 591, 768], P('dp')
- input_grad: bfloat16 [8, 591, 768], P('dp')
- qkv_weight_grad: float32 [768, 3, 768], P('dp', None, 'shard')
- out_weight_grad: float32 [768, 768], P('shard', 'dp')
- fc1_weight_grad: float32 [768, 3072], P('dp', 'shard')
- fc2_weight_grad: float32 [3072, 768], P('shard', 'dp')
- norm1_gain_grad: float32 [768], P('dp')
- norm1_shift_grad: float32 [768], P('dp')
- query_bias_grad: float32 [768], P('shard')
- value_bias_grad: float32 [768], P('shard')
- out_bias_grad: float32 [768], P('dp')
- gamma_attn_grad: float32 [768], P('dp')
- norm2_gain_grad: float32 [768], P('dp')
- norm2_shift_grad: float32 [768], P('dp')
- fc1_bias_grad: float32 [3072], P('shard')
- fc2_bias_grad: float32 [768], P('dp')
- gamma_mlp_grad: float32 [768], P('dp')
- small_table_grad: float32 [732, 12], P(None, 'shard')
- large_table_grad: float32 [2212, 12], P(None, 'shard')
The draws below stay inside these ranges and needn't reach their ends.
Inputs may be any that keep to these rules, and one draw needn't show every extreme that they name: `slot_kind`: 0: three images of 197 rows; 1: one image of 577 rows. `small_index`: every entry of the table is named by some pair. `large_index`: every entry of the table is named by some pair.
All inputs are finite; a program needn't handle non-finite values.
Results may differ from the reference program's by a relative error of at most 0.012.
The reference program's roundings to bfloat16 on the way count: a program that leaves them out, or rounds other values in their place, can miss the bound.
Values may be sent and summed in bfloat16 or wider, within the bound.
A program may use at most 384 MiB of HBM per device.

```python
import jax
import jax.numpy as jnp
from jax import lax

D = 768
HEADS = 12
HEAD_DIM = 64
FF = 3072
SMALL_GRID = 14
LARGE_GRID = 24
SMALL_LEN = 197
LARGE_LEN = 577
SLOT_ROWS = 591
SMALL_TAB = 732
LARGE_TAB = 2212
SLOTS = 8


def relative_map(grid_side):
    cell_count = grid_side * grid_side
    places = jnp.arange(cell_count, dtype=jnp.int32)
    row_index = places // grid_side
    column_index = places % grid_side
    row_step = row_index[:, None] - row_index[None, :] + grid_side - 1
    column_step = column_index[:, None] - column_index[None, :] + grid_side - 1
    inside = row_step * (2 * grid_side - 1) + column_step
    corner = (2 * grid_side - 1) ** 2
    result = jnp.full((cell_count + 1, cell_count + 1), corner + 2, jnp.int32)
    result = result.at[1:, 1:].set(inside.astype(jnp.int32))
    result = result.at[0, 1:].set(corner)
    result = result.at[1:, 0].set(corner + 1)
    return result


def mixed_map(key, grid_side, table_size):
    base = relative_map(grid_side)
    side = base.shape[0]
    flat = base.reshape(-1).astype(jnp.int32)
    order = jax.random.permutation(jax.random.fold_in(key, 7), side * side).astype(jnp.int32)
    scattered = flat[order].reshape(side, side).astype(jnp.int32)
    shuffled = jax.random.permutation(jax.random.fold_in(key, 5), table_size).astype(jnp.int32)
    return shuffled[scattered].astype(jnp.int32)


def draw_small_index(key, part):
    return mixed_map(jax.random.fold_in(key, 11), SMALL_GRID, SMALL_TAB)


def draw_large_index(key, part):
    return mixed_map(jax.random.fold_in(key, 13), LARGE_GRID, LARGE_TAB)


def set_ends(entries, own_key, low, high):
    longest = entries.shape.index(max(entries.shape))
    spots = []
    for shift in (0, 1):
        where = [jax.random.randint(jax.random.fold_in(own_key, axis), (), 0, length) for axis, length in enumerate(entries.shape)]
        where[longest] = (where[longest] + shift) % entries.shape[longest]
        spots.append(tuple(where))
    return entries.at[spots[0]].set(low).at[spots[1]].set(high)


def raised(values, own_key, source, target, blocks, factor):
    def block_of(axis_at):
        return (jnp.arange(values.shape[axis_at]) // (values.shape[axis_at] // blocks)).reshape((-1,) + (1,) * (values.ndim - 1 - axis_at))

    near = jax.random.permutation(own_key, blocks)[block_of(target)]
    far = (block_of(target) + blocks // 2) % blocks
    return jnp.where((block_of(source) == near) | (block_of(source) == far), factor * values, values)


def block_levels(own_key, extent, cuts, low, top_value):
    loudness = 1.0
    for position, blocks in cuts:
        steps = jax.random.uniform(jax.random.fold_in(jax.random.fold_in(own_key, 6), position), (blocks,), jnp.float32, low / len(cuts), top_value / len(cuts))
        loudness = loudness * jnp.repeat(jnp.exp(steps), extent[position] // blocks).reshape((-1,) + (1,) * (len(extent) - 1 - position))
    return loudness


def bell_draw(key, extent, scale, reach, cuts=(), kind=jnp.bfloat16):
    entries = jax.random.normal(key, extent, jnp.float32) * scale
    if len(cuts) > 0:
        entries = block_levels(key, extent, cuts, -0.22, 0.18) * entries
    return jnp.clip(entries, min=-reach, max=reach).astype(kind)


def bell_draw_with(rng, dims, deviation, most, shards, heavy, kind=jnp.bfloat16):
    entries = deviation * jax.random.normal(rng, dims, jnp.float32)
    if shards:
        entries = entries * block_levels(rng, dims, shards, -0.22, 0.18)
    return jnp.clip(raised(entries, jax.random.fold_in(rng, 3), *heavy), -most, most).astype(kind)


def setup_inputs(seed: int = 0) -> dict:
    seeds = jax.random.split(jax.random.key(seed), 23)
    return {
        "images": bell_draw(seeds[0], (SLOTS, SLOT_ROWS, D), 1.0, 6.0, ((0, 8),)),
        "out_grad": bell_draw_with(seeds[1], (SLOTS, SLOT_ROWS, D), 1.0, 6.0, ((0, 8),), (0, 2, 8, 2.0)),
        "slot_kind": set_ends(jax.random.randint(seeds[2], (SLOTS,), 0, 2), jax.random.fold_in(seeds[2], 1), 0, 1).astype(jnp.int32),
        "small_index": draw_small_index(jax.random.fold_in(seeds[22], 71), 0),
        "large_index": draw_large_index(jax.random.fold_in(seeds[22], 71), 0),
        "qkv_weight": bell_draw(seeds[5], (D, 3, D), D ** -0.5, 0.21875, ((0, 8), (2, 4))),
        "out_weight": bell_draw(seeds[6], (D, D), (D // 64) ** -0.5, 1.75, ((0, 4), (1, 8))),
        "fc1_weight": bell_draw(seeds[7], (D, FF), D ** -0.5, 0.21875, ((0, 8), (1, 4))),
        "fc2_weight": bell_draw(seeds[8], (FF, D), FF ** -0.5, 0.109375, ((0, 4), (1, 8))),
        "norm1_gain": jnp.clip(1.0 + 0.18 * jax.random.normal(seeds[9], (D,), jnp.float32), 0.099609375, 1.8984375).astype(jnp.bfloat16),
        "norm1_shift": bell_draw(seeds[10], (D,), 0.3, 1.796875, ((0, 8),)),
        "query_bias": bell_draw(seeds[11], (D,), 0.3, 1.796875, ((0, 4),)),
        "value_bias": bell_draw(seeds[12], (D,), 0.3, 1.796875, ((0, 4),)),
        "out_bias": bell_draw(seeds[13], (D,), 0.3, 1.796875, ((0, 8),)),
        "gamma_attn": jnp.clip(1.0 + 0.18 * jax.random.normal(seeds[14], (D,), jnp.float32), 0.099609375, 1.8984375).astype(jnp.bfloat16),
        "norm2_gain": jnp.clip(1.0 + 0.18 * jax.random.normal(seeds[15], (D,), jnp.float32), 0.099609375, 1.8984375).astype(jnp.bfloat16),
        "norm2_shift": bell_draw(seeds[16], (D,), 0.3, 1.796875, ((0, 8),)),
        "fc1_bias": bell_draw(seeds[17], (FF,), 0.3, 1.796875, ((0, 4),)),
        "fc2_bias": bell_draw(seeds[18], (D,), 0.3, 1.796875, ((0, 8),)),
        "gamma_mlp": jnp.clip(1.0 + 0.18 * jax.random.normal(seeds[19], (D,), jnp.float32), 0.099609375, 1.8984375).astype(jnp.bfloat16),
        "small_table": bell_draw(seeds[20], (SMALL_TAB, HEADS), 1.0, 4.0, ((1, 4),)),
        "large_table": bell_draw(seeds[21], (LARGE_TAB, HEADS), 1.0, 4.0, ((1, 4),)),
    }


@jax.custom_vjp
def low(v):
    return lax.optimization_barrier(v.astype(jnp.bfloat16)).astype(jnp.float32)

@jax.custom_vjp
def low_back(v):
    return v

def low_keep(v):
    return (low(v), None)

def low_pass(kept, grad):
    return (grad,)

def back_keep(v):
    return (v, None)

def back_low(kept, grad):
    return (low(grad),)
low.defvjp(low_keep, low_pass)
low_back.defvjp(back_keep, back_low)
HIGHEST = lax.Precision.HIGHEST
EPS = 1e-06

def layer_norm(activations, norm_gain, norm_shift):
    center = activations - lax.optimization_barrier(jnp.mean(activations, -1, keepdims=True))
    return center * lax.rsqrt(lax.optimization_barrier(jnp.mean(center * center, -1, keepdims=True)) + EPS) * norm_gain + norm_shift

def matmul(left_side, right_side):
    return jnp.einsum('gre,ef->grf', left_side, right_side, precision=HIGHEST)

def layer_group(activations, slot_kinds, parameters, small_index, large_index):
    qkv_weight, out_weight, fc1_weight, fc2_weight, norm1_gain, norm1_shift, query_bias, value_bias, out_bias, gamma_attn, norm2_gain, norm2_shift, fc1_bias, fc2_bias, gamma_mlp, small_table, large_table = parameters
    groups, slot_rows, model_width = activations.shape
    qkv_matrix = qkv_weight.reshape(model_width, 3 * model_width)
    normed_one = low(layer_norm(activations, norm1_gain, norm1_shift))
    projected = matmul(normed_one, qkv_matrix)
    query_rows = low_back(low(projected[..., :model_width] + query_bias))
    key_rows = low_back(low(projected[..., model_width:2 * model_width]))
    value_rows = low_back(low(projected[..., 2 * model_width:] + value_bias))
    positions = jnp.arange(slot_rows).astype(jnp.int32)
    is_large = (slot_kinds == 1)[:, None]
    large_segment = jnp.where(positions < LARGE_LEN, 0, slot_rows + positions)
    segment = jnp.where(is_large, large_segment[None, :], (positions // SMALL_LEN)[None, :])
    allowed = segment[:, :, None] == segment[:, None, :]
    small_place = (positions % SMALL_LEN).astype(jnp.int32)
    small_map = small_index[small_place[:, None], small_place[None, :]]
    extra_rows = slot_rows - LARGE_LEN
    large_map = jnp.pad(large_index, ((0, extra_rows), (0, extra_rows)))
    small_bias = jnp.transpose(small_table[small_map], (2, 0, 1))
    large_bias = jnp.transpose(large_table[large_map], (2, 0, 1))
    pair_bias = jnp.where(is_large[:, :, None, None], large_bias[None], small_bias[None])
    head_shape = (groups, slot_rows, HEADS, HEAD_DIM)
    scores = jnp.einsum('grhd,gchd->ghrc', query_rows.reshape(head_shape), key_rows.reshape(head_shape), precision=HIGHEST)
    scores = scores * HEAD_DIM ** (-0.5) + pair_bias
    scores = low_back(jnp.where(allowed[:, None], scores, -1e+30))
    softmax_weights = low(jax.nn.softmax(scores, axis=-1))
    attended = jnp.einsum('ghrc,gchd->grhd', softmax_weights, value_rows.reshape(head_shape), precision=HIGHEST)
    attended = low_back(low(attended.reshape(groups, slot_rows, model_width)))
    branch = low_back(matmul(attended, out_weight) + out_bias)
    middle = activations + gamma_attn * branch
    normed_two = low(layer_norm(middle, norm2_gain, norm2_shift))
    hidden = low_back(matmul(normed_two, fc1_weight) + fc1_bias)
    active = low(jax.nn.gelu(hidden, approximate=False))
    result = low_back(matmul(active, fc2_weight) + fc2_bias)
    live_rows = jnp.where(is_large, positions[None, :] < LARGE_LEN, True).astype(jnp.float32)
    return (middle + gamma_mlp * result) * live_rows[:, :, None]

def reference(images, out_grad, slot_kind, small_index, large_index, qkv_weight, out_weight, fc1_weight, fc2_weight, norm1_gain, norm1_shift, query_bias, value_bias, out_bias, gamma_attn, norm2_gain, norm2_shift, fc1_bias, fc2_bias, gamma_mlp, small_table, large_table):
    parameters = tuple((member.astype(jnp.float32) for member in (qkv_weight, out_weight, fc1_weight, fc2_weight, norm1_gain, norm1_shift, query_bias, value_bias, out_bias, gamma_attn, norm2_gain, norm2_shift, fc1_bias, fc2_bias, gamma_mlp, small_table, large_table)))
    groups = SLOTS // 4
    slot_kinds = slot_kind.reshape(groups, 4)
    layer_step = jax.checkpoint(layer_group)

    def forward(inputs, weights):

        def advance(members):
            return layer_step(members[0], members[1], weights, small_index, large_index)
        outputs = lax.map(advance, (inputs.reshape(groups, 4, SLOT_ROWS, D), slot_kinds))
        return outputs.reshape(SLOTS, SLOT_ROWS, D)
    layer_out, pullback = jax.vjp(forward, images.astype(jnp.float32), parameters)
    input_grad, gradients = pullback(out_grad.astype(jnp.float32))
    return (layer_out.astype(jnp.bfloat16), input_grad.astype(jnp.bfloat16), gradients[0], gradients[1], gradients[2], gradients[3], gradients[4], gradients[5], gradients[6], gradients[7], gradients[8], gradients[9], gradients[10], gradients[11], gradients[12], gradients[13], gradients[14], gradients[15], gradients[16])
```

```python
import functools

import jax
import jax.numpy as jnp
from jax import lax
from jax.experimental import pallas as pl
from jax.experimental.pallas import tpu as pltpu
from jax.sharding import PartitionSpec as P

HEAD_DIM = 64
SMALL_LEN = 197
LARGE_LEN = 577
EPS = 1e-06
NEG = -1e30
LANES = 128
SPLIT = 64
VMEM_LIMIT = 56 << 20

f32 = jnp.float32
bf16 = jnp.bfloat16


def up_to(value, unit):
    return -(-value // unit) * unit


def in_vmem(count):
    return [pl.BlockSpec(memory_space=pltpu.VMEM)] * count


def params(**more):
    return pltpu.CompilerParams(vmem_limit_bytes=VMEM_LIMIT, **more)


def dot(a, b, da, db):
    return lax.dot_general(a, b, (((da,), (db,)), ((), ())), preferred_element_type=f32)


def bias_body(heads, groups, index_ref, table_ref, out_ref):
    rows, columns = index_ref.shape

    def step(r, carry):
        here = pl.ds(pl.multiple_of(r * 16, 16), 16)
        for c in range(columns // LANES):
            there = pl.ds(c * LANES, LANES)
            index = index_ref[here, there]
            high = lax.shift_right_arithmetic(index, 7)
            low = lax.bitwise_and(index, LANES - 1)
            found = [jnp.full((16, LANES), NEG, f32) for _ in range(heads)]
            for k in range(groups):
                match = high == k
                for h in range(heads):
                    line = table_ref[h * groups + k : h * groups + k + 1, :]
                    values = jnp.take_along_axis(
                        jnp.broadcast_to(line, (16, LANES)), low, axis=1
                    )
                    found[h] = jnp.where(match, values, found[h])
            for h in range(heads):
                out_ref[h, here, there] = found[h].astype(bf16)
        return carry

    lax.fori_loop(0, rows // 16, step, 0)


def gather_bias(pair_index, table):
    heads, entries = table.shape
    groups = entries // LANES
    return pl.pallas_call(
        functools.partial(bias_body, heads, groups),
        out_shape=jax.ShapeDtypeStruct((heads,) + pair_index.shape, bf16),
        in_specs=in_vmem(2),
        out_specs=in_vmem(1)[0],
        compiler_params=params(),
        cost_estimate=pl.CostEstimate(flops=10**9, bytes_accessed=4 * 10**7, transcendentals=0),
        name="bias",
    )(pair_index, table.reshape(heads * groups, LANES))


def table_body(heads, groups, index_ref, grad_ref, out_ref):
    rows, columns = index_ref.shape
    shift = SPLIT.bit_length() - 1
    out_ref[...] = jnp.zeros_like(out_ref)

    def step(r, carry):
        here = pl.ds(pl.multiple_of(r * 16, 16), 16)
        index = index_ref[here, :]
        high = lax.shift_right_arithmetic(index, shift).astype(jnp.int16)
        low = lax.bitwise_and(index, SPLIT - 1).astype(jnp.int16)
        grads = [grad_ref[h, here, :] for h in range(heads)]
        places_low = lax.broadcasted_iota(jnp.int16, (SPLIT, columns), 0)
        places_high = lax.broadcasted_iota(jnp.int16, (groups, columns), 0)
        total = jnp.zeros(out_ref.shape, f32)
        for i in range(16):
            hot_low = jnp.where(
                places_low == jnp.broadcast_to(low[i : i + 1], (SPLIT, columns)),
                jnp.ones((), bf16),
                jnp.zeros((), bf16),
            )
            match = places_high == jnp.broadcast_to(high[i : i + 1], (groups, columns))
            spread = jnp.concatenate(
                [
                    jnp.where(
                        match,
                        jnp.broadcast_to(grads[h][i : i + 1], (groups, columns)),
                        jnp.zeros((), bf16),
                    )
                    for h in range(heads)
                ],
                0,
            )
            total = total + dot(spread, hot_low, 1, 1)
        out_ref[...] += total
        return carry

    lax.fori_loop(0, rows // 16, step, 0)


def table_sums(pair_index, grad_scores, entries):
    heads = grad_scores.shape[0]
    groups = up_to(-(-entries // SPLIT), 8)
    sums = pl.pallas_call(
        functools.partial(table_body, heads, groups),
        out_shape=jax.ShapeDtypeStruct((heads * groups, SPLIT), f32),
        in_specs=in_vmem(2),
        out_specs=in_vmem(1)[0],
        compiler_params=params(),
        cost_estimate=pl.CostEstimate(flops=2 * 10**9, bytes_accessed=6 * 10**7, transcendentals=0),
        name="table_sums",
    )(pair_index, grad_scores)
    return sums.reshape(heads, groups * SPLIT)


def forward_body(heads, q_ref, k_ref, v_ref, bias_ref, out_ref):
    rows = q_ref.shape[0]
    for h in range(heads):
        part = slice(h * HEAD_DIM, (h + 1) * HEAD_DIM)
        scores = dot(q_ref[:, part], k_ref[:, part], 1, 1) * HEAD_DIM ** (-0.5)
        scores = scores + bias_ref[h, :, :rows].astype(f32)
        weights = jnp.exp(scores - jnp.max(scores, -1, keepdims=True))
        weights = weights / jnp.sum(weights, -1, keepdims=True)
        out_ref[:, part] = dot(weights.astype(bf16), v_ref[:, part], 1, 0).astype(bf16)


def backward_body(
    heads, q_ref, k_ref, v_ref, bias_ref, grad_ref, dq_ref, dk_ref, dv_ref, ds_ref
):
    rows = q_ref.shape[0]
    factor = HEAD_DIM ** (-0.5)
    for h in range(heads):
        part = slice(h * HEAD_DIM, (h + 1) * HEAD_DIM)
        scores = dot(q_ref[:, part], k_ref[:, part], 1, 1) * factor
        scores = scores + bias_ref[h, :, :rows].astype(f32)
        weights = jnp.exp(scores - jnp.max(scores, -1, keepdims=True))
        weights = weights / jnp.sum(weights, -1, keepdims=True)
        dv_ref[:, part] = dot(weights.astype(bf16), grad_ref[:, part], 0, 0).astype(bf16)
        grad = dot(grad_ref[:, part], v_ref[:, part], 1, 1)
        mean = jnp.sum(weights * grad, -1, keepdims=True)
        grad = (weights * (grad - mean)).astype(bf16)
        ds_ref[h, :, :rows] = grad
        dq_ref[:, part] = (dot(grad, k_ref[:, part], 1, 0) * factor).astype(bf16)
        dk_ref[:, part] = (dot(grad, q_ref[:, part], 0, 0) * factor).astype(bf16)


def attend_forward(queries, keys, values, bias):
    heads = bias.shape[0]
    return pl.pallas_call(
        functools.partial(forward_body, heads),
        out_shape=jax.ShapeDtypeStruct(queries.shape, bf16),
        in_specs=in_vmem(4),
        out_specs=in_vmem(1)[0],
        compiler_params=params(),
        cost_estimate=pl.CostEstimate(flops=10**9, bytes_accessed=10**7, transcendentals=10**6),
        name="attend_forward",
    )(queries, keys, values, bias)


def attend_backward(queries, keys, values, bias, grad):
    heads = bias.shape[0]
    rows = jax.ShapeDtypeStruct(queries.shape, bf16)
    return pl.pallas_call(
        functools.partial(backward_body, heads),
        out_shape=(rows, rows, rows, jax.ShapeDtypeStruct(bias.shape, bf16)),
        in_specs=in_vmem(5),
        out_specs=tuple(in_vmem(4)),
        compiler_params=params(),
        cost_estimate=pl.CostEstimate(flops=2 * 10**9, bytes_accessed=2 * 10**7, transcendentals=10**6),
        name="attend_backward",
    )(queries, keys, values, bias, grad)


def layer_norm(activations, norm_gain, norm_shift):
    center = activations - jnp.mean(activations, -1, keepdims=True)
    inverse = lax.rsqrt(jnp.mean(center * center, -1, keepdims=True) + EPS)
    normal = center * inverse
    return (normal * norm_gain + norm_shift, normal, inverse)


def norm_back(grad_normed, normal, inverse, norm_gain):
    scaled = grad_normed * norm_gain
    return inverse * (
        scaled
        - jnp.mean(scaled, -1, keepdims=True)
        - normal * jnp.mean(scaled * normal, -1, keepdims=True)
    )


def gelu_slope(hidden):
    cumulative = 0.5 * (1.0 + jax.scipy.special.erf(hidden * 0.7071067811865476))
    return cumulative + hidden * jnp.exp(-0.5 * hidden * hidden) * 0.3989422804014327


def pair_map(kind, small_index, large_index, rows, columns):
    length = small_index.shape[0]
    images = rows // length
    tiled = jnp.tile(small_index, (images, images))
    tiled = jnp.pad(
        tiled,
        ((0, rows - images * length), (0, columns - images * length)),
        constant_values=-1,
    )
    image_row = jnp.arange(rows) // length
    image_column = jnp.arange(columns) // length
    tiled = jnp.where(image_row[:, None] == image_column[None, :], tiled, -1)
    side = large_index.shape[0]
    large = jnp.pad(
        large_index, ((0, rows - side), (0, columns - side)), constant_values=-1
    )
    return jnp.where(kind == 1, large, tiled)


def on_device(
    images,
    out_grad,
    slot_kind,
    small_index,
    large_index,
    qkv_weight,
    out_weight,
    fc1_weight,
    fc2_weight,
    norm1_gain,
    norm1_shift,
    query_bias,
    value_bias,
    out_bias,
    gamma_attn,
    norm2_gain,
    norm2_shift,
    fc1_bias,
    fc2_bias,
    gamma_mlp,
    small_table,
    large_table,
):
    depth = qkv_weight.shape[0]
    width = query_bias.shape[0]
    hidden_width = fc1_bias.shape[0]
    heads = width // HEAD_DIM
    _, slot_rows, model_width = images.shape
    rows = up_to(slot_rows, 16)
    columns = up_to(rows, LANES)
    kind = slot_kind[0]

    block = jnp.concatenate(
        (
            qkv_weight.reshape(depth, 3 * width),
            fc1_weight,
            out_weight.T,
            fc2_weight.T,
        ),
        1,
    )
    whole = lax.all_gather(block, "dp", axis=0, tiled=True)
    cuts = (3 * width, 3 * width + hidden_width, 4 * width + hidden_width)
    qkv_matrix = whole[:, : cuts[0]]
    fc1_matrix = whole[:, cuts[0] : cuts[1]]
    out_turned = whole[:, cuts[1] : cuts[2]]
    fc2_turned = whole[:, cuts[2] :]
    small_vectors = jnp.stack(
        (norm1_gain, norm1_shift, out_bias, gamma_attn, norm2_gain, norm2_shift, fc2_bias, gamma_mlp)
    )
    vectors = lax.all_gather(small_vectors, "dp", axis=0)
    vectors = jnp.moveaxis(vectors, 0, 1).reshape(8, model_width).astype(f32)

    query_shift = query_bias.astype(f32)
    value_shift = value_bias.astype(f32)
    hidden_shift = fc1_bias.astype(f32)
    small_entries, large_entries = small_table.shape[0], large_table.shape[0]
    entries = up_to(max(small_entries, large_entries), LANES)
    table = jnp.where(
        kind == 1,
        jnp.pad(large_table, ((0, entries - large_entries), (0, 0))),
        jnp.pad(small_table, ((0, entries - small_entries), (0, 0))),
    )
    table = table.T.astype(f32)
    pair_index = pair_map(kind, small_index, large_index, rows, columns)
    bias = gather_bias(pair_index, table)

    positions = jnp.arange(rows)
    live_count = jnp.where(kind == 1, LARGE_LEN, slot_rows)
    live_rows = (positions < live_count).astype(f32).reshape(-1, 1)
    inputs = jnp.pad(images[0], ((0, rows - slot_rows), (0, 0))).astype(f32)
    normed_one, normal_one, inverse_one = layer_norm(inputs, vectors[0], vectors[1])
    normed_one = normed_one.astype(bf16)
    projected = dot(normed_one, qkv_matrix, 1, 0)
    queries = (projected[:, :width] + query_shift).astype(bf16)
    keys = projected[:, width : 2 * width].astype(bf16)
    values = (projected[:, 2 * width :] + value_shift).astype(bf16)
    pieces = attend_forward(queries, keys, values, bias)
    branch_part = dot(pieces, out_turned, 1, 1)
    branch = lax.psum(branch_part, "shard") + vectors[2]
    middle = inputs + vectors[3] * branch
    normed_two, normal_two, inverse_two = layer_norm(middle, vectors[4], vectors[5])
    normed_two = normed_two.astype(bf16)
    hidden = dot(normed_two, fc1_matrix, 1, 0) + hidden_shift
    active = jax.nn.gelu(hidden, approximate=False).astype(bf16)
    result_part = dot(active, fc2_turned, 1, 1)
    result = lax.psum(result_part.astype(bf16), "shard").astype(f32) + vectors[6]
    layer_out = ((middle + vectors[7] * result) * live_rows).astype(bf16)[:slot_rows][None]

    grad_out = jnp.pad(out_grad[0], ((0, rows - slot_rows), (0, 0))).astype(f32) * live_rows
    grad_gamma_mlp = jnp.sum(grad_out * result, 0)
    grad_result = (grad_out * vectors[7]).astype(bf16)
    grad_fc2_bias = jnp.sum(grad_result.astype(f32), 0)
    grad_fc2_turned = dot(grad_result, active, 0, 0)
    grad_active = dot(grad_result, fc2_turned, 1, 0)
    grad_hidden = (grad_active * gelu_slope(hidden)).astype(bf16)
    grad_fc1_bias = jnp.sum(grad_hidden.astype(f32), 0)
    grad_fc1 = dot(normed_two, grad_hidden, 0, 0)
    grad_normed_two = lax.psum(dot(grad_hidden, fc1_matrix, 1, 1), "shard")
    grad_norm2_gain = jnp.sum(grad_normed_two * normal_two, 0)
    grad_norm2_shift = jnp.sum(grad_normed_two, 0)
    grad_middle = grad_out + norm_back(grad_normed_two, normal_two, inverse_two, vectors[4])
    grad_gamma_attn = jnp.sum(grad_middle * branch, 0)
    grad_branch = (grad_middle * vectors[3]).astype(bf16)
    grad_out_bias = jnp.sum(grad_branch.astype(f32), 0)
    grad_out_turned = dot(grad_branch, pieces, 0, 0)
    grad_attended = dot(grad_branch, out_turned, 1, 0).astype(bf16)
    grad_queries, grad_keys, grad_values, grad_scores = attend_backward(
        queries, keys, values, bias, grad_attended
    )
    sums = table_sums(pair_index, grad_scores, entries)
    grad_projected = jnp.concatenate((grad_queries, grad_keys, grad_values), 1)
    grad_qkv = dot(normed_one, grad_projected, 0, 0)
    grad_query_bias = jnp.sum(grad_queries.astype(f32), 0)
    grad_value_bias = jnp.sum(grad_values.astype(f32), 0)
    grad_normed_one = lax.psum(dot(grad_projected, qkv_matrix, 1, 1), "shard")
    grad_norm1_gain = jnp.sum(grad_normed_one * normal_one, 0)
    grad_norm1_shift = jnp.sum(grad_normed_one, 0)
    input_grad = grad_middle + norm_back(grad_normed_one, normal_one, inverse_one, vectors[0])
    input_grad = input_grad.astype(bf16)[:slot_rows][None]

    small_sums = jnp.where(kind == 1, 0.0, sums[:, :small_entries])
    large_sums = jnp.where(kind == 1, sums[:, :large_entries], 0.0)
    local_sums = lax.psum(
        (small_sums, large_sums, grad_query_bias, grad_value_bias, grad_fc1_bias), "dp"
    )
    peers = lax.axis_size("dp")

    def sent_and_summed(value):
        parts = value.astype(bf16).reshape(peers, value.shape[0] // peers, -1)
        arrived = lax.all_to_all(parts, "dp", split_axis=0, concat_axis=0, tiled=True)
        return arrived.astype(f32).sum(axis=0)

    grad_block = sent_and_summed(
        jnp.concatenate((grad_qkv, grad_fc1, grad_out_turned, grad_fc2_turned), 1)
    )
    vector_grads = sent_and_summed(
        jnp.stack(
            (
                grad_norm1_gain,
                grad_norm1_shift,
                grad_out_bias,
                grad_gamma_attn,
                grad_norm2_gain,
                grad_norm2_shift,
                grad_fc2_bias,
                grad_gamma_mlp,
            ),
            1,
        )
    )
    return (
        layer_out,
        input_grad,
        grad_block[:, : cuts[0]].reshape(depth, 3, width),
        grad_block[:, cuts[1] : cuts[2]].T,
        grad_block[:, cuts[0] : cuts[1]],
        grad_block[:, cuts[2] :].T,
        vector_grads[:, 0],
        vector_grads[:, 1],
        local_sums[2],
        local_sums[3],
        vector_grads[:, 2],
        vector_grads[:, 3],
        vector_grads[:, 4],
        vector_grads[:, 5],
        local_sums[4],
        vector_grads[:, 6],
        vector_grads[:, 7],
        local_sums[0].T,
        local_sums[1].T,
    )


def solution(mesh):
    return jax.shard_map(
        on_device,
        mesh=mesh,
        in_specs=(
            P("dp", None, None),
            P("dp", None, None),
            P("dp"),
            P(),
            P(),
            P("dp", None, "shard"),
            P("shard", "dp"),
            P("dp", "shard"),
            P("shard", "dp"),
            P("dp"),
            P("dp"),
            P("shard"),
            P("shard"),
            P("dp"),
            P("dp"),
            P("dp"),
            P("dp"),
            P("shard"),
            P("dp"),
            P("dp"),
            P(None, "shard"),
            P(None, "shard"),
        ),
        out_specs=(
            P("dp", None, None),
            P("dp", None, None),
            P("dp", None, "shard"),
            P("shard", "dp"),
            P("dp", "shard"),
            P("shard", "dp"),
            P("dp"),
            P("dp"),
            P("shard"),
            P("shard"),
            P("dp"),
            P("dp"),
            P("dp"),
            P("dp"),
            P("shard"),
            P("dp"),
            P("dp"),
            P(None, "shard"),
            P(None, "shard"),
        ),
        check_vma=False,
    )
```

```python
import functools

import jax
import jax.numpy as jnp
from jax import lax
from jax.experimental import pallas as pl
from jax.experimental.pallas import tpu as pltpu
from jax.sharding import PartitionSpec as P

HEAD_DIM = 64
SMALL_LEN = 197
LARGE_LEN = 577
EPS = 1e-06
NEG = -1e30
LANES = 128
SPLIT = 64
VMEM_LIMIT = 56 << 20

MESH = pl.DeviceIdType.MESH

f32 = jnp.float32
bf16 = jnp.bfloat16


def up_to(value, unit):
    return -(-value // unit) * unit


def in_vmem(count):
    return [pl.BlockSpec(memory_space=pltpu.VMEM)] * count


def params(**more):
    return pltpu.CompilerParams(vmem_limit_bytes=VMEM_LIMIT, **more)


def dot(a, b, da, db):
    return lax.dot_general(a, b, (((da,), (db,)), ((), ())), preferred_element_type=f32)


def bias_body(heads, groups, index_ref, table_ref, out_ref):
    rows, columns = index_ref.shape

    def step(r, carry):
        here = pl.ds(pl.multiple_of(r * 16, 16), 16)
        for c in range(columns // LANES):
            there = pl.ds(c * LANES, LANES)
            index = index_ref[here, there]
            high = lax.shift_right_arithmetic(index, 7)
            low = lax.bitwise_and(index, LANES - 1)
            found = [jnp.full((16, LANES), NEG, f32) for _ in range(heads)]
            for k in range(groups):
                match = high == k
                for h in range(heads):
                    line = table_ref[h * groups + k : h * groups + k + 1, :]
                    values = jnp.take_along_axis(
                        jnp.broadcast_to(line, (16, LANES)), low, axis=1
                    )
                    found[h] = jnp.where(match, values, found[h])
            for h in range(heads):
                out_ref[h, here, there] = found[h].astype(bf16)
        return carry

    lax.fori_loop(0, rows // 16, step, 0)


def gather_bias(pair_index, table):
    heads, entries = table.shape
    groups = entries // LANES
    return pl.pallas_call(
        functools.partial(bias_body, heads, groups),
        out_shape=jax.ShapeDtypeStruct((heads,) + pair_index.shape, bf16),
        in_specs=in_vmem(2),
        out_specs=in_vmem(1)[0],
        compiler_params=params(),
        cost_estimate=pl.CostEstimate(flops=10**9, bytes_accessed=4 * 10**7, transcendentals=0),
        name="bias",
    )(pair_index, table.reshape(heads * groups, LANES))


def table_body(heads, groups, index_ref, grad_ref, out_ref):
    rows, columns = index_ref.shape
    shift = SPLIT.bit_length() - 1
    out_ref[...] = jnp.zeros_like(out_ref)

    def step(r, carry):
        here = pl.ds(pl.multiple_of(r * 16, 16), 16)
        index = index_ref[here, :]
        high = lax.shift_right_arithmetic(index, shift).astype(jnp.int16)
        low = lax.bitwise_and(index, SPLIT - 1).astype(jnp.int16)
        grads = [grad_ref[h, here, :] for h in range(heads)]
        places_low = lax.broadcasted_iota(jnp.int16, (SPLIT, columns), 0)
        places_high = lax.broadcasted_iota(jnp.int16, (groups, columns), 0)
        total = jnp.zeros(out_ref.shape, f32)
        for i in range(16):
            hot_low = jnp.where(
                places_low == jnp.broadcast_to(low[i : i + 1], (SPLIT, columns)),
                jnp.ones((), bf16),
                jnp.zeros((), bf16),
            )
            match = places_high == jnp.broadcast_to(high[i : i + 1], (groups, columns))
            spread = jnp.concatenate(
                [
                    jnp.where(
                        match,
                        jnp.broadcast_to(grads[h][i : i + 1], (groups, columns)),
                        jnp.zeros((), bf16),
                    )
                    for h in range(heads)
                ],
                0,
            )
            total = total + dot(spread, hot_low, 1, 1)
        out_ref[...] += total
        return carry

    lax.fori_loop(0, rows // 16, step, 0)


def table_sums(pair_index, grad_scores, entries):
    heads = grad_scores.shape[0]
    groups = up_to(-(-entries // SPLIT), 8)
    sums = pl.pallas_call(
        functools.partial(table_body, heads, groups),
        out_shape=jax.ShapeDtypeStruct((heads * groups, SPLIT), f32),
        in_specs=in_vmem(2),
        out_specs=in_vmem(1)[0],
        compiler_params=params(),
        cost_estimate=pl.CostEstimate(flops=2 * 10**9, bytes_accessed=6 * 10**7, transcendentals=0),
        name="table_sums",
    )(pair_index, grad_scores)
    return sums.reshape(heads, groups * SPLIT)


def forward_body(heads, q_ref, k_ref, v_ref, bias_ref, out_ref):
    rows = q_ref.shape[0]
    for h in range(heads):
        part = slice(h * HEAD_DIM, (h + 1) * HEAD_DIM)
        scores = dot(q_ref[:, part], k_ref[:, part], 1, 1) * HEAD_DIM ** (-0.5)
        scores = scores + bias_ref[h, :, :rows].astype(f32)
        weights = jnp.exp(scores - jnp.max(scores, -1, keepdims=True))
        weights = weights / jnp.sum(weights, -1, keepdims=True)
        out_ref[:, part] = dot(weights.astype(bf16), v_ref[:, part], 1, 0).astype(bf16)


def backward_body(
    heads, q_ref, k_ref, v_ref, bias_ref, grad_ref, dq_ref, dk_ref, dv_ref, ds_ref
):
    rows = q_ref.shape[0]
    factor = HEAD_DIM ** (-0.5)
    for h in range(heads):
        part = slice(h * HEAD_DIM, (h + 1) * HEAD_DIM)
        scores = dot(q_ref[:, part], k_ref[:, part], 1, 1) * factor
        scores = scores + bias_ref[h, :, :rows].astype(f32)
        weights = jnp.exp(scores - jnp.max(scores, -1, keepdims=True))
        weights = weights / jnp.sum(weights, -1, keepdims=True)
        dv_ref[:, part] = dot(weights.astype(bf16), grad_ref[:, part], 0, 0).astype(bf16)
        grad = dot(grad_ref[:, part], v_ref[:, part], 1, 1)
        mean = jnp.sum(weights * grad, -1, keepdims=True)
        grad = (weights * (grad - mean)).astype(bf16)
        ds_ref[h, :, :rows] = grad
        dq_ref[:, part] = (dot(grad, k_ref[:, part], 1, 0) * factor).astype(bf16)
        dk_ref[:, part] = (dot(grad, q_ref[:, part], 0, 0) * factor).astype(bf16)


def attend_forward(queries, keys, values, bias):
    heads = bias.shape[0]
    return pl.pallas_call(
        functools.partial(forward_body, heads),
        out_shape=jax.ShapeDtypeStruct(queries.shape, bf16),
        in_specs=in_vmem(4),
        out_specs=in_vmem(1)[0],
        compiler_params=params(),
        cost_estimate=pl.CostEstimate(flops=10**9, bytes_accessed=10**7, transcendentals=10**6),
        name="attend_forward",
    )(queries, keys, values, bias)


def attend_backward(queries, keys, values, bias, grad):
    heads = bias.shape[0]
    rows = jax.ShapeDtypeStruct(queries.shape, bf16)
    return pl.pallas_call(
        functools.partial(backward_body, heads),
        out_shape=(rows, rows, rows, jax.ShapeDtypeStruct(bias.shape, bf16)),
        in_specs=in_vmem(5),
        out_specs=tuple(in_vmem(4)),
        compiler_params=params(),
        cost_estimate=pl.CostEstimate(flops=2 * 10**9, bytes_accessed=2 * 10**7, transcendentals=10**6),
        name="attend_backward",
    )(queries, keys, values, bias, grad)


def cuts_of(total, pieces, unit=16):
    n=total//unit; base,extra=divmod(n,pieces)
    out=[];at=0
    for i in range(pieces):
        size=(base+(i<extra))*unit
        if size: out.append((at,size))
        at+=size
    return out

def shard_sum_body(chunks, part_ref, out_ref, near, sent, far, send_sem, recv_sem):
    me=lax.axis_index("shard")
    outer=me//2; inner=lax.rem(me,2)
    near_peer=outer*2+(1-inner); far_peer=(1-outer)*2+inner
    barrier=pltpu.get_barrier_semaphore()
    for peer in (near_peer,far_peer):
        pl.semaphore_signal(barrier,inc=1,device_id={"shard":peer},device_id_type=MESH)
    pl.semaphore_wait(barrier,2)
    half=near.shape[0]
    def rows(which,at,size):
        return pl.ds(pl.multiple_of(which*half+at,16),size)
    def copy(stage,j,src,dst,peer):
        return pltpu.make_async_remote_copy(src_ref=src,dst_ref=dst,send_sem=send_sem.at[stage,j],recv_sem=recv_sem.at[stage,j],device_id={"shard":peer},device_id_type=MESH)
    first=[];second=[];third=[]
    for j,(at,size) in enumerate(chunks):
        c=copy(0,j,part_ref.at[rows(1-inner,at,size)],near.at[pl.ds(at,size)],near_peer); c.start(); first.append(c)
    for j,(at,size) in enumerate(chunks):
        first[j].wait_recv()
        here=pl.ds(at,size)
        sent[here]=(part_ref[rows(inner,at,size)]+near[here]).astype(bf16)
        c=copy(1,j,sent.at[here],far.at[here],far_peer); c.start(); second.append(c)
    for j,(at,size) in enumerate(chunks):
        second[j].wait_recv()
        here=pl.ds(at,size)
        mine=rows(inner,at,size)
        out_ref[mine]=sent[here].astype(f32)+far[here].astype(f32)
        c=copy(2,j,out_ref.at[mine],out_ref.at[mine],near_peer); c.start(); third.append(c)
    for j in range(len(chunks)):
        first[j].wait_send(); second[j].wait_send(); third[j].wait()

def shard_sum(part, pieces=4, cid=0):
    rows,width=part.shape
    half=rows//2
    chunks=cuts_of(half,pieces)
    return pl.pallas_call(functools.partial(shard_sum_body,chunks),
        out_shape=jax.ShapeDtypeStruct(part.shape,f32),
        in_specs=[pl.BlockSpec(memory_space=pltpu.VMEM)],out_specs=pl.BlockSpec(memory_space=pltpu.VMEM),
        scratch_shapes=[pltpu.VMEM((half,width),f32),pltpu.VMEM((half,width),bf16),pltpu.VMEM((half,width),bf16),
            pltpu.SemaphoreType.DMA((3,len(chunks))),pltpu.SemaphoreType.DMA((3,len(chunks)))],
        compiler_params=pltpu.CompilerParams(collective_id=cid,has_side_effects=True,vmem_limit_bytes=VMEM_LIMIT),name="shard_sum%d"%pieces)(part)

def gather_body(blocks, *refs):
    n=blocks
    ins=refs[:n]; outs=refs[n:2*n]; loc,up_s,up_r,dn_s,dn_r,x_s,x_r=refs[2*n:]
    X=2
    dp=outs[0].shape[0]; Z=dp//X
    me=lax.axis_index("dp"); z=me//X; x=lax.rem(me,X)
    barrier=pltpu.get_barrier_semaphore()
    up=me+X; dn=me-X; xp=z*X+(1-x)
    has_up=z<Z-1; has_dn=z>0
    def sig(p): pl.semaphore_signal(barrier,inc=1,device_id={"dp":p},device_id_type=MESH)
    sig(xp)
    @pl.when(has_up)
    def _(): sig(up)
    @pl.when(has_dn)
    def _(): sig(dn)
    pl.semaphore_wait(barrier,1+has_up.astype(jnp.int32)+has_dn.astype(jnp.int32))
    def rc(src,dst,s,r,p):
        return pltpu.make_async_remote_copy(src_ref=src,dst_ref=dst,send_sem=s,recv_sem=r,device_id={"dp":p},device_id_type=MESH)
    def blk(j,zz): return outs[j].at[jnp.clip(zz,0,Z-1)*X+x]
    locs=[]
    for j in range(n):
        c=pltpu.make_async_copy(ins[j],outs[j].at[me],loc.at[j]); c.start(); locs.append(c)
    def send_up(j,s):
        src = ins[j] if s==0 else blk(j,z-s)
        return rc(src, outs[j].at[(jnp.maximum(z-s,0))*X+x], up_s.at[j,s], up_r.at[j,s], up)
    def send_dn(j,s):
        src = ins[j] if s==0 else blk(j,z+s)
        return rc(src, outs[j].at[(jnp.minimum(z+s,Z-1))*X+x], dn_s.at[j,s], dn_r.at[j,s], dn)
    def send_x(j,k,src,zz):
        return rc(src, outs[j].at[zz*X+x], x_s.at[j,zz], x_r.at[j,zz], xp)
    for s in range(Z):
        for j in range(n):
            if s>0:
                @pl.when(z-s>=0)
                def _():
                    b=blk(j,z-s)
                    pltpu.make_async_remote_copy(src_ref=b,dst_ref=b,send_sem=up_s.at[j,s-1],recv_sem=up_r.at[j,s-1],device_id={"dp":dn},device_id_type=MESH).wait_recv()
                @pl.when(jnp.logical_and(z-s>=0,has_up))
                def _(): send_up(j,s).start()
                @pl.when(z-s>=0)
                def _():
                    zz=jnp.maximum(z-s,0); send_x(j,s,blk(j,z-s),zz).start()
                @pl.when(z+s<Z)
                def _():
                    b=blk(j,z+s)
                    pltpu.make_async_remote_copy(src_ref=b,dst_ref=b,send_sem=dn_s.at[j,s-1],recv_sem=dn_r.at[j,s-1],device_id={"dp":up},device_id_type=MESH).wait_recv()
                @pl.when(jnp.logical_and(z+s<Z,has_dn))
                def _(): send_dn(j,s).start()
                @pl.when(z+s<Z)
                def _():
                    zz=jnp.minimum(z+s,Z-1); send_x(j,s,blk(j,z+s),zz).start()
            else:
                @pl.when(has_up)
                def _(): send_up(j,0).start()
                @pl.when(has_dn)
                def _(): send_dn(j,0).start()
                send_x(j,0,ins[j],z).start()
    for j in range(n):
        locs[j].wait()
        for zz in range(Z):
            b=outs[j].at[zz*X+(1-x)]
            c=pltpu.make_async_remote_copy(src_ref=b,dst_ref=b,send_sem=x_s.at[j,zz],recv_sem=x_r.at[j,zz],device_id={"dp":xp},device_id_type=MESH)
            c.wait_recv(); c.wait_send()
        for s in range(Z-1):
            @pl.when(jnp.logical_and(z-s>=0,has_up))
            def _(): send_up(j,s).wait_send()
            @pl.when(jnp.logical_and(z+s<Z,has_dn))
            def _(): send_dn(j,s).wait_send()

def gather(parts, dp, cid=1):
    n=len(parts); Z=dp//2
    sems=[pltpu.SemaphoreType.DMA((n,)),]+[pltpu.SemaphoreType.DMA((n,max(Z-1,1)))]*4+[pltpu.SemaphoreType.DMA((n,Z))]*2
    return list(pl.pallas_call(functools.partial(gather_body,n),
        out_shape=[jax.ShapeDtypeStruct((dp,)+p.shape,p.dtype) for p in parts],
        in_specs=[pl.BlockSpec(memory_space=pltpu.VMEM)]*n,out_specs=[pl.BlockSpec(memory_space=pltpu.VMEM)]*n,
        scratch_shapes=sems,
        compiler_params=pltpu.CompilerParams(collective_id=cid,has_side_effects=True,vmem_limit_bytes=VMEM_LIMIT),name="gather%d"%n)(*parts))


def layer_norm(activations, norm_gain, norm_shift):
    center = activations - jnp.mean(activations, -1, keepdims=True)
    inverse = lax.rsqrt(jnp.mean(center * center, -1, keepdims=True) + EPS)
    normal = center * inverse
    return (normal * norm_gain + norm_shift, normal, inverse)


def norm_back(grad_normed, normal, inverse, norm_gain):
    scaled = grad_normed * norm_gain
    return inverse * (
        scaled
        - jnp.mean(scaled, -1, keepdims=True)
        - normal * jnp.mean(scaled * normal, -1, keepdims=True)
    )


def gelu_slope(hidden):
    cumulative = 0.5 * (1.0 + jax.scipy.special.erf(hidden * 0.7071067811865476))
    return cumulative + hidden * jnp.exp(-0.5 * hidden * hidden) * 0.3989422804014327


def pair_map(kind, small_index, large_index, rows, columns):
    length = small_index.shape[0]
    images = rows // length
    tiled = jnp.tile(small_index, (images, images))
    tiled = jnp.pad(
        tiled,
        ((0, rows - images * length), (0, columns - images * length)),
        constant_values=-1,
    )
    image_row = jnp.arange(rows) // length
    image_column = jnp.arange(columns) // length
    tiled = jnp.where(image_row[:, None] == image_column[None, :], tiled, -1)
    side = large_index.shape[0]
    large = jnp.pad(
        large_index, ((0, rows - side), (0, columns - side)), constant_values=-1
    )
    return jnp.where(kind == 1, large, tiled)


def on_device(
    images,
    out_grad,
    slot_kind,
    small_index,
    large_index,
    qkv_weight,
    out_weight,
    fc1_weight,
    fc2_weight,
    norm1_gain,
    norm1_shift,
    query_bias,
    value_bias,
    out_bias,
    gamma_attn,
    norm2_gain,
    norm2_shift,
    fc1_bias,
    fc2_bias,
    gamma_mlp,
    small_table,
    large_table,
):
    depth = qkv_weight.shape[0]
    width = query_bias.shape[0]
    hidden_width = fc1_bias.shape[0]
    heads = width // HEAD_DIM
    _, slot_rows, model_width = images.shape
    rows = up_to(slot_rows, 32)
    columns = up_to(rows, LANES)
    kind = slot_kind[0]

    small_vectors = jnp.stack(
        (norm1_gain, norm1_shift, out_bias, gamma_attn, norm2_gain, norm2_shift, fc2_bias, gamma_mlp),
        1,
    )
    first = jnp.concatenate(
        (
            qkv_weight.reshape(depth, 3 * width),
            out_weight.T,
            jnp.pad(small_vectors, ((0, 0), (0, LANES - 8))),
        ),
        1,
    )
    first, fc1_matrix, fc2_turned = (
        part.reshape(model_width, -1)
        for part in gather((first, fc1_weight, fc2_weight.T), lax.axis_size("dp"))
    )
    cuts = (3 * width, 3 * width + hidden_width, 4 * width + hidden_width)
    qkv_matrix = first[:, : 3 * width]
    out_turned = first[:, 3 * width : 4 * width]
    vectors = first[:, 4 * width : 4 * width + 8].T.astype(f32)

    query_shift = query_bias.astype(f32)
    value_shift = value_bias.astype(f32)
    hidden_shift = fc1_bias.astype(f32)
    small_entries, large_entries = small_table.shape[0], large_table.shape[0]
    entries = up_to(max(small_entries, large_entries), LANES)
    table = jnp.where(
        kind == 1,
        jnp.pad(large_table, ((0, entries - large_entries), (0, 0))),
        jnp.pad(small_table, ((0, entries - small_entries), (0, 0))),
    )
    table = table.T.astype(f32)
    pair_index = pair_map(kind, small_index, large_index, rows, columns)
    bias = gather_bias(pair_index, table)

    positions = jnp.arange(rows)
    live_count = jnp.where(kind == 1, LARGE_LEN, slot_rows)
    live_rows = (positions < live_count).astype(f32).reshape(-1, 1)
    inputs = jnp.pad(images[0], ((0, rows - slot_rows), (0, 0))).astype(f32)
    normed_one, normal_one, inverse_one = layer_norm(inputs, vectors[0], vectors[1])
    normed_one = normed_one.astype(bf16)
    projected = dot(normed_one, qkv_matrix, 1, 0)
    queries = (projected[:, :width] + query_shift).astype(bf16)
    keys = projected[:, width : 2 * width].astype(bf16)
    values = (projected[:, 2 * width :] + value_shift).astype(bf16)
    pieces = attend_forward(queries, keys, values, bias)
    branch_part = dot(pieces, out_turned, 1, 1)
    branch = shard_sum(branch_part) + vectors[2]
    middle = inputs + vectors[3] * branch
    normed_two, normal_two, inverse_two = layer_norm(middle, vectors[4], vectors[5])
    normed_two = normed_two.astype(bf16)
    hidden = dot(normed_two, fc1_matrix, 1, 0) + hidden_shift
    active = jax.nn.gelu(hidden, approximate=False).astype(bf16)
    result_part = dot(active, fc2_turned, 1, 1)
    result = shard_sum(result_part) + vectors[6]
    layer_out = ((middle + vectors[7] * result) * live_rows).astype(bf16)[:slot_rows][None]

    grad_out = jnp.pad(out_grad[0], ((0, rows - slot_rows), (0, 0))).astype(f32) * live_rows
    grad_gamma_mlp = jnp.sum(grad_out * result, 0)
    grad_result = (grad_out * vectors[7]).astype(bf16)
    grad_fc2_bias = jnp.sum(grad_result.astype(f32), 0)
    grad_fc2_turned = dot(grad_result, active, 0, 0)
    grad_active = dot(grad_result, fc2_turned, 1, 0)
    grad_hidden = (grad_active * gelu_slope(hidden)).astype(bf16)
    grad_fc1_bias = jnp.sum(grad_hidden.astype(f32), 0)
    grad_fc1 = dot(normed_two, grad_hidden, 0, 0)
    grad_normed_two = shard_sum(dot(grad_hidden, fc1_matrix, 1, 1))
    grad_norm2_gain = jnp.sum(grad_normed_two * normal_two, 0)
    grad_norm2_shift = jnp.sum(grad_normed_two, 0)
    grad_middle = grad_out + norm_back(grad_normed_two, normal_two, inverse_two, vectors[4])
    grad_gamma_attn = jnp.sum(grad_middle * branch, 0)
    grad_branch = (grad_middle * vectors[3]).astype(bf16)
    grad_out_bias = jnp.sum(grad_branch.astype(f32), 0)
    grad_out_turned = dot(grad_branch, pieces, 0, 0)
    grad_attended = dot(grad_branch, out_turned, 1, 0).astype(bf16)
    grad_queries, grad_keys, grad_values, grad_scores = attend_backward(
        queries, keys, values, bias, grad_attended
    )
    sums = table_sums(pair_index, grad_scores, entries)
    grad_projected = jnp.concatenate((grad_queries, grad_keys, grad_values), 1)
    grad_qkv = dot(normed_one, grad_projected, 0, 0)
    grad_query_bias = jnp.sum(grad_queries.astype(f32), 0)
    grad_value_bias = jnp.sum(grad_values.astype(f32), 0)
    grad_normed_one = shard_sum(dot(grad_projected, qkv_matrix, 1, 1))
    grad_norm1_gain = jnp.sum(grad_normed_one * normal_one, 0)
    grad_norm1_shift = jnp.sum(grad_normed_one, 0)
    input_grad = grad_middle + norm_back(grad_normed_one, normal_one, inverse_one, vectors[0])
    input_grad = input_grad.astype(bf16)[:slot_rows][None]

    small_sums = jnp.where(kind == 1, 0.0, sums[:, :small_entries])
    large_sums = jnp.where(kind == 1, sums[:, :large_entries], 0.0)
    local_sums = lax.psum(
        (small_sums, large_sums, grad_query_bias, grad_value_bias, grad_fc1_bias), "dp"
    )
    peers = lax.axis_size("dp")

    def sent_and_summed(value):
        parts = value.astype(bf16).reshape(peers, value.shape[0] // peers, -1)
        arrived = lax.all_to_all(parts, "dp", split_axis=0, concat_axis=0, tiled=True)
        return arrived.astype(f32).sum(axis=0)

    grad_block = sent_and_summed(
        jnp.concatenate((grad_qkv, grad_fc1, grad_out_turned, grad_fc2_turned), 1)
    )
    vector_grads = sent_and_summed(
        jnp.stack(
            (
                grad_norm1_gain,
                grad_norm1_shift,
                grad_out_bias,
                grad_gamma_attn,
                grad_norm2_gain,
                grad_norm2_shift,
                grad_fc2_bias,
                grad_gamma_mlp,
            ),
            1,
        )
    )
    return (
        layer_out,
        input_grad,
        grad_block[:, : cuts[0]].reshape(depth, 3, width),
        grad_block[:, cuts[1] : cuts[2]].T,
        grad_block[:, cuts[0] : cuts[1]],
        grad_block[:, cuts[2] :].T,
        vector_grads[:, 0],
        vector_grads[:, 1],
        local_sums[2],
        local_sums[3],
        vector_grads[:, 2],
        vector_grads[:, 3],
        vector_grads[:, 4],
        vector_grads[:, 5],
        local_sums[4],
        vector_grads[:, 6],
        vector_grads[:, 7],
        local_sums[0].T,
        local_sums[1].T,
    )


def solution(mesh):
    return jax.shard_map(
        on_device,
        mesh=mesh,
        in_specs=(
            P("dp", None, None),
            P("dp", None, None),
            P("dp"),
            P(),
            P(),
            P("dp", None, "shard"),
            P("shard", "dp"),
            P("dp", "shard"),
            P("shard", "dp"),
            P("dp"),
            P("dp"),
            P("shard"),
            P("shard"),
            P("dp"),
            P("dp"),
            P("dp"),
            P("dp"),
            P("shard"),
            P("dp"),
            P("dp"),
            P(None, "shard"),
            P(None, "shard"),
        ),
        out_specs=(
            P("dp", None, None),
            P("dp", None, None),
            P("dp", None, "shard"),
            P("shard", "dp"),
            P("dp", "shard"),
            P("shard", "dp"),
            P("dp"),
            P("dp"),
            P("shard"),
            P("shard"),
            P("dp"),
            P("dp"),
            P("dp"),
            P("dp"),
            P("shard"),
            P("dp"),
            P("dp"),
            P(None, "shard"),
            P(None, "shard"),
        ),
        check_vma=False,
    )
```

```python
import functools
import types

import jax
import jax.numpy as jnp
from jax import lax
from jax.experimental import pallas as pl
from jax.experimental.pallas import tpu as pltpu
from jax.sharding import PartitionSpec as P

HEAD_DIM = 64
SMALL_LEN = 197
LARGE_LEN = 577
SLOT_ROWS = 591
EPS = 1e-06
NEG = -1e30
LANES = 128
SPLIT = 80
VMEM_LIMIT = 56 << 20

MESH = pl.DeviceIdType.MESH

f32 = jnp.float32
bf16 = jnp.bfloat16


def up_to(value, unit):
    return -(-value // unit) * unit


def in_vmem(count):
    return [pl.BlockSpec(memory_space=pltpu.VMEM)] * count


def params(**more):
    return pltpu.CompilerParams(vmem_limit_bytes=VMEM_LIMIT, **more)


def dot(a, b, da, db):
    return lax.dot_general(a, b, (((da,), (db,)), ((), ())), preferred_element_type=f32)


def bias_rows(heads, groups, index_ref, table_ref, out_ref, first, last):
    columns = index_ref.shape[1]

    def step(r, carry):
        here = pl.ds(pl.multiple_of(r * 16, 16), 16)
        for c in range(columns // LANES):
            there = pl.ds(c * LANES, LANES)
            index = index_ref[here, there]
            high = lax.shift_right_arithmetic(index, 7)
            low = lax.bitwise_and(index, LANES - 1)
            found = [jnp.full((16, LANES), NEG, f32) for _ in range(heads)]
            for k in range(groups):
                match = high == k
                for h in range(heads):
                    line = table_ref[h * groups + k : h * groups + k + 1, :]
                    values = jnp.take_along_axis(
                        jnp.broadcast_to(line, (16, LANES)), low, axis=1
                    )
                    found[h] = jnp.where(match, values, found[h])
            for h in range(heads):
                out_ref[h, here, there] = found[h].astype(bf16)
        return carry

    lax.fori_loop(first, last, step, 0)


def table_rows(heads, groups, index_ref, grad_ref, out_ref, first, last):
    columns = index_ref.shape[1]
    inverse = -(-(1 << 22) // SPLIT)

    def step(r, carry):
        here = pl.ds(pl.multiple_of(r * 16, 16), 16)
        index = index_ref[here, :]
        high = lax.shift_right_arithmetic(index * inverse, 22)
        low = (index - high * SPLIT).astype(jnp.int16)
        high = high.astype(jnp.int16)
        grads = [grad_ref[h, here, :] for h in range(heads)]
        places_low = lax.broadcasted_iota(jnp.int16, (SPLIT, columns), 0)
        places_high = lax.broadcasted_iota(jnp.int16, (groups, columns), 0)
        one, zero = jnp.ones((), bf16), jnp.zeros((), bf16)
        total = jnp.zeros((heads * groups, SPLIT), f32)
        for pair in range(0, 16, 2):
            lows, highs = [], []
            for i in (pair, pair + 1):
                lows.append(
                    jnp.where(
                        places_low == jnp.broadcast_to(low[i : i + 1], (SPLIT, columns)), one, zero
                    )
                )
                match = places_high == jnp.broadcast_to(high[i : i + 1], (groups, columns))
                highs.append(
                    jnp.concatenate(
                        [
                            jnp.where(
                                match,
                                jnp.broadcast_to(grads[h][i : i + 1], (groups, columns)),
                                zero,
                            )
                            for h in range(heads)
                        ],
                        0,
                    )
                )
            total = total + dot(jnp.concatenate(highs, 1), jnp.concatenate(lows, 1), 1, 1)
        out_ref[: heads * groups, :SPLIT] += total
        return carry

    lax.fori_loop(first, last, step, 0)


def forward_body(heads, q_ref, k_ref, v_ref, bias_ref, out_ref):
    rows = q_ref.shape[0]
    for h in range(heads):
        part = slice(h * HEAD_DIM, (h + 1) * HEAD_DIM)
        scores = dot(q_ref[:, part], k_ref[:, part], 1, 1) * HEAD_DIM ** (-0.5)
        scores = scores + bias_ref[h, :, :rows].astype(f32)
        weights = jnp.exp(scores - jnp.max(scores, -1, keepdims=True))
        weights = weights / jnp.sum(weights, -1, keepdims=True)
        out_ref[:, part] = dot(weights.astype(bf16), v_ref[:, part], 1, 0).astype(bf16)


def backward_body(
    heads, q_ref, k_ref, v_ref, bias_ref, grad_ref, dq_ref, dk_ref, dv_ref, ds_ref
):
    rows = q_ref.shape[0]
    factor = HEAD_DIM ** (-0.5)
    for h in range(heads):
        part = slice(h * HEAD_DIM, (h + 1) * HEAD_DIM)
        scores = dot(q_ref[:, part], k_ref[:, part], 1, 1) * factor
        scores = scores + bias_ref[h, :, :rows].astype(f32)
        weights = jnp.exp(scores - jnp.max(scores, -1, keepdims=True))
        weights = weights / jnp.sum(weights, -1, keepdims=True)
        dv_ref[:, part] = dot(weights.astype(bf16), grad_ref[:, part], 0, 0).astype(bf16)
        grad = dot(grad_ref[:, part], v_ref[:, part], 1, 1)
        mean = jnp.sum(weights * grad, -1, keepdims=True)
        grad = (weights * (grad - mean)).astype(bf16)
        ds_ref[h, :, :rows] = grad
        dq_ref[:, part] = (dot(grad, k_ref[:, part], 1, 0) * factor).astype(bf16)
        dk_ref[:, part] = (dot(grad, q_ref[:, part], 0, 0) * factor).astype(bf16)


def attend_forward(queries, keys, values, bias):
    heads = bias.shape[0]
    return pl.pallas_call(
        functools.partial(forward_body, heads),
        out_shape=jax.ShapeDtypeStruct(queries.shape, bf16),
        in_specs=in_vmem(4),
        out_specs=in_vmem(1)[0],
        compiler_params=params(),
        cost_estimate=pl.CostEstimate(flops=10**9, bytes_accessed=10**7, transcendentals=10**6),
        name="attend_forward",
    )(queries, keys, values, bias)


def attend_backward(queries, keys, values, bias, grad):
    heads = bias.shape[0]
    rows = jax.ShapeDtypeStruct(queries.shape, bf16)
    return pl.pallas_call(
        functools.partial(backward_body, heads),
        out_shape=(rows, rows, rows, jax.ShapeDtypeStruct(bias.shape, bf16)),
        in_specs=in_vmem(5),
        out_specs=tuple(in_vmem(4)),
        compiler_params=params(),
        cost_estimate=pl.CostEstimate(flops=2 * 10**9, bytes_accessed=2 * 10**7, transcendentals=10**6),
        name="attend_backward",
    )(queries, keys, values, bias, grad)


def bias_body(heads, groups, index_ref, table_ref, out_ref):
    bias_rows(heads, groups, index_ref, table_ref, out_ref, 0, index_ref.shape[0] // 16)


def gather_bias(pair_index, table):
    heads, entries = table.shape
    groups = entries // LANES
    return pl.pallas_call(
        functools.partial(bias_body, heads, groups),
        out_shape=jax.ShapeDtypeStruct((heads,) + pair_index.shape, bf16),
        in_specs=in_vmem(2),
        out_specs=in_vmem(1)[0],
        compiler_params=params(),
        cost_estimate=pl.CostEstimate(flops=10**9, bytes_accessed=4 * 10**7, transcendentals=0),
        name="bias",
    )(pair_index, table.reshape(heads * groups, LANES))


def table_body(heads, groups, index_ref, grad_ref, out_ref):
    out_ref[...] = jnp.zeros_like(out_ref)
    table_rows(heads, groups, index_ref, grad_ref, out_ref, 0, index_ref.shape[0] // 16)


def table_sums(pair_index, grad_scores, entries):
    heads = grad_scores.shape[0]
    groups = up_to(-(-entries // SPLIT), 16)
    sums = pl.pallas_call(
        functools.partial(table_body, heads, groups),
        out_shape=jax.ShapeDtypeStruct((heads * groups, SPLIT), f32),
        in_specs=in_vmem(2),
        out_specs=in_vmem(1)[0],
        compiler_params=params(),
        cost_estimate=pl.CostEstimate(flops=2 * 10**9, bytes_accessed=6 * 10**7, transcendentals=0),
        name="table_sums",
    )(pair_index, grad_scores)
    return sums.reshape(heads, groups * SPLIT)


def cuts_of(total, pieces, unit=16):
    count, extra = divmod(total // unit, pieces)
    cuts, at = [], 0
    for i in range(pieces):
        size = (count + (i < extra)) * unit
        if size:
            cuts.append((at, size))
        at += size
    return cuts


def remote(src, dst, send_sem, recv_sem, axis, peer):
    return pltpu.make_async_remote_copy(
        src_ref=src,
        dst_ref=dst,
        send_sem=send_sem,
        recv_sem=recv_sem,
        device_id={axis: peer},
        device_id_type=MESH,
    )


def greet(barrier, axis, peer):
    pl.semaphore_signal(barrier, inc=1, device_id={axis: peer}, device_id_type=MESH)


class ShardSum:
    def __init__(self, chunks, part_ref, out_ref, near, sent, far, send_sem, recv_sem):
        me = lax.axis_index("shard")
        outer, self.inner = me // 2, lax.rem(me, 2)
        self.near_peer = outer * 2 + (1 - self.inner)
        self.far_peer = (1 - outer) * 2 + self.inner
        self.chunks, self.part, self.out = chunks, part_ref, out_ref
        self.near, self.sent, self.far = near, sent, far
        self.sems = (send_sem, recv_sem)
        self.half = near.shape[0]

    def greet(self, barrier):
        greet(barrier, "shard", self.near_peer)
        greet(barrier, "shard", self.far_peer)
        return 2

    def rows(self, which, at, size):
        return pl.ds(pl.multiple_of(which * self.half + at, 16), size)

    def copy(self, stage, j, src, dst, peer):
        send_sem, recv_sem = self.sems
        return remote(src, dst, send_sem.at[stage, j], recv_sem.at[stage, j], "shard", peer)

    def first(self, j):
        at, size = self.chunks[j]
        return self.copy(
            0, j, self.part.at[self.rows(1 - self.inner, at, size)], self.near.at[pl.ds(at, size)], self.near_peer
        )

    def second(self, j):
        here = pl.ds(*self.chunks[j])
        return self.copy(1, j, self.sent.at[here], self.far.at[here], self.far_peer)

    def third(self, j):
        mine = self.out.at[self.rows(self.inner, *self.chunks[j])]
        return self.copy(2, j, mine, mine, self.near_peer)

    def start(self):
        for j in range(len(self.chunks)):
            self.first(j).start()

    def cross_one(self, j):
        at, size = self.chunks[j]
        self.first(j).wait_recv()
        here = pl.ds(at, size)
        mine = self.rows(self.inner, at, size)
        self.sent[here] = (self.part[mine] + self.near[here]).astype(bf16)
        self.second(j).start()

    def cross(self):
        for j in range(len(self.chunks)):
            self.cross_one(j)

    def close_one(self, j):
        at, size = self.chunks[j]
        self.second(j).wait_recv()
        here = pl.ds(at, size)
        mine = self.rows(self.inner, at, size)
        self.out[mine] = self.sent[here].astype(f32) + self.far[here].astype(f32)
        self.third(j).start()

    def close(self):
        for j in range(len(self.chunks)):
            self.close_one(j)

    def arrive(self):
        for j in range(len(self.chunks)):
            self.third(j).wait_recv()

    def drain(self):
        for j in range(len(self.chunks)):
            self.first(j).wait_send()
            self.second(j).wait_send()
            self.third(j).wait_send()


class Grid:
    def __init__(self, peers):
        self.length = peers // 2
        self.me = lax.axis_index("dp")
        self.at, self.side = self.me // 2, lax.rem(self.me, 2)
        self.up, self.down = self.me + 2, self.me - 2
        self.across = self.at * 2 + 1 - self.side
        self.has_up, self.has_down = self.at < self.length - 1, self.at > 0

    def greet(self, barrier):
        greet(barrier, "dp", self.across)

        @pl.when(self.has_up)
        def _():
            greet(barrier, "dp", self.up)

        @pl.when(self.has_down)
        def _():
            greet(barrier, "dp", self.down)

        return 1 + self.has_up.astype(jnp.int32) + self.has_down.astype(jnp.int32)

    def clip(self, place):
        return jnp.clip(place, 0, self.length - 1)


class Flood:
    def __init__(self, grid, own, out, up_send, up_recv, down_send, down_recv, side_send, side_recv):
        self.grid, self.own, self.out = grid, own, out
        self.up_sems, self.down_sems = (up_send, up_recv), (down_send, down_recv)
        self.side_sems = (side_send, side_recv)

    def at(self, device):
        depth = self.own.shape[0]
        return self.out.at[pl.ds(pl.multiple_of(device * depth, 8), depth)]

    def block(self, place):
        return self.at(self.grid.clip(place) * 2 + self.grid.side)

    def up(self, s):
        grid, (send, recv) = self.grid, self.up_sems
        block = self.block(grid.at - s)
        return remote(self.own if s == 0 else block, block, send.at[s], recv.at[s], "dp", grid.up)

    def down(self, s):
        grid, (send, recv) = self.grid, self.down_sems
        block = self.block(grid.at + s)
        return remote(self.own if s == 0 else block, block, send.at[s], recv.at[s], "dp", grid.down)

    def across(self, place, own=False):
        grid, (send, recv) = self.grid, self.side_sems
        place = grid.clip(place)
        block = self.block(place)
        return remote(
            self.own if own else block, block, send.at[place], recv.at[place], "dp", grid.across
        )

    def step(self, s):
        grid = self.grid
        if s == 0:

            @pl.when(grid.has_up)
            def _():
                self.up(0).start()

            @pl.when(grid.has_down)
            def _():
                self.down(0).start()

            self.across(grid.at, own=True).start()
            return

        @pl.when(grid.at - s >= 0)
        def _():
            block = self.block(grid.at - s)
            send, recv = self.up_sems
            remote(block, block, send.at[s - 1], recv.at[s - 1], "dp", grid.down).wait_recv()

            @pl.when(grid.has_up)
            def _():
                self.up(s).start()

            self.across(grid.at - s).start()

        @pl.when(grid.at + s < grid.length)
        def _():
            block = self.block(grid.at + s)
            send, recv = self.down_sems
            remote(block, block, send.at[s - 1], recv.at[s - 1], "dp", grid.up).wait_recv()

            @pl.when(grid.has_down)
            def _():
                self.down(s).start()

            self.across(grid.at + s).start()

    def arrive(self):
        grid, (send, recv) = self.grid, self.side_sems
        for place in range(grid.length):
            block = self.at(place * 2 + 1 - grid.side)
            remote(block, block, send.at[place], recv.at[place], "dp", grid.across).wait_recv()

    def drain(self):
        grid = self.grid
        for place in range(grid.length):
            self.across(place).wait_send()
        for s in range(grid.length - 1):

            @pl.when(jnp.logical_and(grid.at - s >= 0, grid.has_up))
            def _():
                self.up(s).wait_send()

            @pl.when(jnp.logical_and(grid.at + s < grid.length, grid.has_down))
            def _():
                self.down(s).wait_send()


SIDE, UP, DOWN = range(3)


class ReduceScatter:
    def __init__(self, grid, grads, out, side, up, down, sems):
        self.grid, self.grads, self.out = grid, grads, out
        self.buffers = (side, up, down)
        self.sems = (sems[:2], sems[2:4], sems[4:6])

    def at(self, device):
        depth = self.out.shape[0]
        return pl.ds(pl.multiple_of(device * depth, 16), depth)

    def prepare(self):
        grid = self.grid

        @pl.when(jnp.logical_not(grid.has_down))
        def _():
            self.buffers[UP][...] = jnp.zeros_like(self.buffers[UP])

        @pl.when(jnp.logical_not(grid.has_up))
        def _():
            self.buffers[DOWN][...] = jnp.zeros_like(self.buffers[DOWN])

    def copy(self, way, place, peer, src=None):
        send, recv = self.sems[way]
        place = self.grid.clip(place)
        dst = self.buffers[way].at[place]
        return remote(dst if src is None else src, dst, send.at[place], recv.at[place], "dp", peer)

    def cross(self, place):
        grid = self.grid
        src = self.grads.at[self.at(grid.clip(place) * 2 + 1 - grid.side)]
        return self.copy(SIDE, place, grid.across, src)

    def start(self, s):
        grid = self.grid

        @pl.when(grid.at + s < grid.length)
        def _():
            self.cross(grid.at + s).start()

        if s:

            @pl.when(grid.at - s >= 0)
            def _():
                self.cross(grid.at - s).start()

    def step(self, s):
        grid = self.grid
        side, up, down = self.buffers
        if s == 0:
            place = grid.at
            self.copy(SIDE, place, grid.across).wait_recv()

            @pl.when(grid.has_down)
            def _():
                self.copy(UP, place, grid.down).wait_recv()

            @pl.when(grid.has_up)
            def _():
                self.copy(DOWN, place, grid.up).wait_recv()

            total = self.grads[self.at(grid.me)].astype(f32) + side[place].astype(f32)
            self.out[...] = total + (up[place].astype(f32) + down[place].astype(f32))
            return

        @pl.when(grid.at + s < grid.length)
        def _():
            place = grid.clip(grid.at + s)
            self.copy(SIDE, place, grid.across).wait_recv()

            @pl.when(grid.has_down)
            def _():
                self.copy(UP, place, grid.down).wait_recv()

            total = self.grads[self.at(place * 2 + grid.side)].astype(f32) + side[place].astype(f32)
            side[place] = (total + up[place].astype(f32)).astype(bf16)
            self.copy(UP, place, grid.up, side.at[place]).start()

        @pl.when(grid.at - s >= 0)
        def _():
            place = grid.clip(grid.at - s)
            self.copy(SIDE, place, grid.across).wait_recv()

            @pl.when(grid.has_up)
            def _():
                self.copy(DOWN, place, grid.up).wait_recv()

            total = self.grads[self.at(place * 2 + grid.side)].astype(f32) + side[place].astype(f32)
            side[place] = (total + down[place].astype(f32)).astype(bf16)
            self.copy(DOWN, place, grid.down, side.at[place]).start()

    def drain(self):
        grid = self.grid
        for place in range(grid.length):
            self.cross(place).wait_send()
        for s in range(1, grid.length):

            @pl.when(grid.at + s < grid.length)
            def _():
                self.copy(UP, grid.at + s, grid.up).wait_send()

            @pl.when(grid.at - s >= 0)
            def _():
                self.copy(DOWN, grid.at - s, grid.down).wait_send()


ROW_STEP = 16
CHUNKS = 5
VECTORS = 8


def layer_body(plan, *refs):
    tree, heads, groups, slot_rows, peers = plan
    named = {}
    for part in jax.tree.unflatten(tree, refs):
        named.update(part)
    r = types.SimpleNamespace(**named)
    rows = r.kept.shape[0]
    model = r.inputs.shape[1]
    inner = heads * HEAD_DIM
    half = rows // 2
    chunks = cuts_of(half, CHUNKS)
    count = len(chunks)
    out_at = 3 * inner + HEAD_DIM
    factor = HEAD_DIM ** (-0.5)

    grid = Grid(peers)
    sums = [
        ShardSum(chunks, *buffers)
        for buffers in zip(r.part, r.total, r.near, r.sent, r.far, r.sum_send, r.sum_recv)
    ]
    floods = [
        Flood(grid, own, out, *sems) for own, out, sems in zip(r.own, r.whole, r.flood_sems)
    ]
    scatters = [
        ReduceScatter(grid, *buffers)
        for buffers in zip(r.grad, r.summed, r.side, r.up, r.down, r.scatter_sems)
    ]

    barrier = pltpu.get_barrier_semaphore()
    pl.semaphore_wait(barrier, sums[0].greet(barrier) + grid.greet(barrier))
    floods[0].step(0)
    copies = [
        pltpu.make_async_copy(flood.own, flood.at(grid.me), r.local_sem.at[j])
        for j, flood in enumerate(floods)
    ]
    for copy in copies:
        copy.start()
    for scatter in scatters:
        scatter.prepare()

    body_rows = slot_rows // 32 * 32
    tail = slot_rows - body_rows
    r.kept[:body_rows] = r.inputs[:body_rows]
    r.kept[body_rows:] = jnp.concatenate(
        (
            r.inputs[body_rows:slot_rows].astype(f32),
            jnp.zeros((rows - slot_rows, model), f32),
        ),
        0,
    ).astype(bf16)
    blocks = r.index.shape[0] // ROW_STEP

    def bias_part(first, last):
        bias_rows(heads, r.table.shape[0] // heads, r.index, r.table, r.bias, first, last)

    length = grid.length
    order = [(0, s) for s in range(1, length - 1)] + [(1, 0), (0, length - 1), (2, 0)]
    later = [(j, s) for s in range(1, length) for j in (1, 2)]
    order += later[: len(later) // 2]
    later = later[len(later) // 2 :]
    for k, (j, s) in enumerate(order):
        bias_part(k * blocks // len(order), (k + 1) * blocks // len(order))
        floods[j].step(s)
    for copy in copies:
        copy.wait()
    floods[0].arrive()

    places = lax.broadcasted_iota(jnp.int32, (VECTORS, LANES), 0) + HEAD_DIM
    lanes = lax.broadcasted_iota(jnp.int32, (VECTORS, LANES), 1)
    pick = jnp.where(places == lanes, jnp.ones((), f32), jnp.zeros((), f32)).astype(bf16)
    r.vectors[...] = dot(pick, r.whole[0][:, out_at - LANES : out_at], 1, 1)

    def vector(i):
        return r.vectors[i : i + 1, :]

    def moments(value):
        mean = jnp.mean(value, -1, keepdims=True)
        center = value - mean
        inverse = lax.rsqrt(jnp.mean(center * center, -1, keepdims=True) + EPS)
        return center * inverse, mean, inverse

    def both(ref, c):
        at, size = chunks[c]
        return jnp.concatenate((ref[at : at + size], ref[half + at : half + at + size]), 0)

    def put(ref, c, value):
        at, size = chunks[c]
        ref[at : at + size] = value[:size]
        ref[half + at : half + at + size] = value[size:]

    def add(i, value):
        r.running[i] += value.reshape(value.shape[0] // 8, 8, value.shape[1]).sum(0)

    r.running[...] = jnp.zeros_like(r.running)
    for c in range(count):
        normal, mean, inverse = moments(both(r.kept, c).astype(f32))
        put(r.mean[0], c, mean)
        put(r.inverse[0], c, inverse)
        normed = (normal * vector(0) + vector(1)).astype(bf16)
        put(r.normed[0], c, normed)
        projected = dot(normed, r.whole[0][:, : 3 * inner], 1, 0) + r.qkv_shift[...]
        put(r.qkv, c, projected.astype(bf16))

    def serve(items):
        for j, s in items:
            floods[j].step(s)

    def weights_of(h):
        part = slice(h * HEAD_DIM, (h + 1) * HEAD_DIM)
        keys = slice(inner + h * HEAD_DIM, inner + (h + 1) * HEAD_DIM)
        scores = dot(r.qkv[:, part], r.qkv[:, keys], 1, 1) * factor
        scores = scores + r.bias[h, :, :rows].astype(f32)
        weights = jnp.exp(scores - jnp.max(scores, -1, keepdims=True))
        return weights * (1.0 / jnp.sum(weights, -1, keepdims=True))

    for h in range(heads):
        serve(later[h * len(later) // heads : (h + 1) * len(later) // heads])
        part = slice(h * HEAD_DIM, (h + 1) * HEAD_DIM)
        values = slice(2 * inner + h * HEAD_DIM, 2 * inner + (h + 1) * HEAD_DIM)
        r.attended[:, part] = dot(weights_of(h).astype(bf16), r.qkv[:, values], 1, 0).astype(bf16)

    def out_turned():
        return r.whole[0][:, out_at : out_at + inner]

    def live_rows(c):
        at, size = chunks[c]
        first = lax.broadcasted_iota(jnp.int32, (size, 1), 0) + at
        places = jnp.concatenate((first, first + half), 0).astype(f32)
        return jnp.where(places < r.slot[1:2, 0:1], 1.0, 0.0)

    def padded(ref, c):
        at, size = chunks[c]
        last = min(half + at + size, slot_rows)
        low = ref[half + at : last]
        missing = half + at + size - last
        if missing:
            low = jnp.concatenate(
                (low.astype(f32), jnp.zeros((missing, low.shape[1]), f32)), 0
            )
        return jnp.concatenate((ref[at : at + size].astype(f32), low.astype(f32)), 0)

    def keep(ref, c, value):
        at, size = chunks[c]
        last = min(half + at + size, slot_rows)
        ref[at : at + size] = value[:size]
        ref[half + at : last] = value[size : size + last - half - at]

    def project(c):
        put(r.part[0], c, dot(both(r.attended, c), out_turned(), 1, 1))
        sums[0].first(c).start()

    def forward(c):
        if c == 0:
            floods[1].arrive()
            floods[2].arrive()
        sums[0].third(c).wait_recv()
        middle = both(r.kept, c).astype(f32) + vector(3) * (both(r.total[0], c) + vector(2))
        put(r.middle, c, middle)
        normal, mean, inverse = moments(middle)
        put(r.mean[1], c, mean)
        put(r.inverse[1], c, inverse)
        normed = (normal * vector(4) + vector(5)).astype(bf16)
        put(r.normed[1], c, normed)
        hidden = dot(normed, r.whole[1][...], 1, 0) + r.hidden_shift[...]
        cumulative = 0.5 * (1.0 + lax.erf(hidden * 0.7071067811865476))
        put(
            r.slope,
            c,
            cumulative + hidden * jnp.exp(-0.5 * hidden * hidden) * 0.3989422804014327,
        )
        active = (hidden * cumulative).astype(bf16)
        put(r.active, c, active)
        put(r.part[1], c, dot(active, r.whole[2][...], 1, 1))
        sums[1].first(c).start()

    def turn(c):
        sums[1].third(c).wait_recv()
        result = both(r.total[1], c) + vector(6)
        live = live_rows(c)
        keep(r.layer_out, c, (live * (both(r.middle, c) + vector(7) * result)).astype(bf16))
        grad = padded(r.out_grad, c) * live
        add(6, grad * result)
        grad_result = (grad * vector(7)).astype(bf16)
        put(r.grad_result, c, grad_result)
        add(5, grad_result.astype(f32))
        grad_hidden = (dot(grad_result, r.whole[2][...], 1, 0) * both(r.slope, c)).astype(bf16)
        put(r.grad_hidden, c, grad_hidden)
        add(0, grad_hidden.astype(f32))
        put(r.part[2], c, dot(grad_hidden, r.whole[1][...], 1, 1))
        sums[2].first(c).start()

    def back_norm(grad, normal, inverse, gain):
        scaled = grad * gain
        along = jnp.mean(scaled * normal, -1, keepdims=True)
        return inverse * (scaled - jnp.mean(scaled, -1, keepdims=True) - normal * along)

    def backward(c):
        sums[2].third(c).wait_recv()
        grad = both(r.total[2], c)
        inverse = both(r.inverse[1], c)
        normal = (both(r.middle, c) - both(r.mean[1], c)) * inverse
        add(3, grad * normal)
        add(4, grad)
        grad_middle = padded(r.out_grad, c) * live_rows(c)
        grad_middle = grad_middle + back_norm(grad, normal, inverse, vector(4))
        put(r.middle, c, grad_middle)
        add(2, grad_middle * (both(r.total[0], c) + vector(2)))
        grad_branch = (grad_middle * vector(3)).astype(bf16)
        put(r.grad_branch, c, grad_branch)
        add(1, grad_branch.astype(f32))
        put(r.grad_attended, c, dot(grad_branch, out_turned(), 1, 0).astype(bf16))

    def close(work):
        return lambda c: work.close_one(c)

    def cross(work):
        return lambda c: work.cross_one(c)

    stages = [project, cross(sums[0]), close(sums[0]), forward, cross(sums[1]), close(sums[1])]
    stages += [turn, cross(sums[2]), close(sums[2]), backward]

    def weight_grad(j, left, right, at=0):
        value = dot(left[...], right[...], 0, 0).astype(bf16)
        r.grad[j][:, at : at + value.shape[1]] = value

    def send_grads(j):
        for s in range(length - 1, -1, -1):
            scatters[j].start(s)

    for t in range(count + len(stages) - 1):
        for k in range(len(stages) - 1, -1, -1):
            if 0 <= t - k < count:
                stages[k](t - k)
        if t == count + 6:
            weight_grad(2, r.grad_result, r.active)
            send_grads(2)
        if t == count + 7:
            weight_grad(1, r.normed[1], r.grad_hidden)
            send_grads(1)

    r.grad[0][:, 3 * inner : out_at] = jnp.zeros((model, HEAD_DIM), bf16)
    weight_grad(0, r.grad_branch, r.attended, out_at)
    steps = list(range(length - 1, -1, -1))
    for h in range(heads):
        part = slice(h * HEAD_DIM, (h + 1) * HEAD_DIM)
        keys = slice(inner + h * HEAD_DIM, inner + (h + 1) * HEAD_DIM)
        values = slice(2 * inner + h * HEAD_DIM, 2 * inner + (h + 1) * HEAD_DIM)
        weights = weights_of(h)
        grad_part = r.grad_attended[:, part]
        r.grad_qkv[:, values] = dot(weights.astype(bf16), grad_part, 0, 0).astype(bf16)
        grad = dot(grad_part, r.qkv[:, values], 1, 1)
        mean = jnp.sum(weights * grad, -1, keepdims=True)
        grad = (weights * (grad - mean)).astype(bf16)
        r.bias[h, :, :rows] = grad
        r.grad_qkv[:, part] = (dot(grad, r.qkv[:, keys], 1, 0) * factor).astype(bf16)
        r.grad_qkv[:, keys] = (dot(grad, r.qkv[:, part], 0, 0) * factor).astype(bf16)
        if h + 1 < length:
            scatters[2].step(steps[h])

    sums[0].drain()
    last = sums[0]
    for c in range(count):
        put(r.part[0], c, dot(both(r.grad_qkv, c), r.whole[0][:, : 3 * inner], 1, 1))
        last.first(c).start()
    weight_grad(0, r.normed[0], r.grad_qkv)
    send_grads(0)

    height = heads * groups
    r.own_small[...] = jnp.zeros_like(r.own_small)

    def line_to(at, line):
        for c in range(line.shape[1] // LANES):
            r.own_small[at + c : at + c + 1] = line[:, c * LANES : (c + 1) * LANES]

    wide = model // LANES
    hidden_lines = r.running.shape[2] // LANES
    inner_lines = up_to(inner, LANES) // LANES
    at = height
    r.own_small[at : at + 1] = r.slot[0:1, :]
    at += 1
    line_to(at, jnp.sum(r.running[0], 0, keepdims=True))
    at += hidden_lines
    for first in (0, 2 * inner):
        value = jnp.sum(r.grad_qkv[:, first : first + inner].astype(f32), 0, keepdims=True)
        value = jnp.concatenate(
            (value, jnp.zeros((1, inner_lines * LANES - inner), f32)), 1
        )
        line_to(at, value)
        at += inner_lines
    for i in range(1, 7):
        line_to(at, jnp.sum(r.running[i], 0, keepdims=True))
        at += wide
    late = at

    def tables(first, last):
        table_rows(heads, groups, r.index, r.bias, r.own_small, first, last)

    def norm_step(here, out_rows):
        grad = r.total[0][here]
        normal = (r.kept[here].astype(f32) - r.mean[0][here]) * r.inverse[0][here]
        back = back_norm(grad, normal, r.inverse[0][here], vector(0))
        value = (r.middle[here] + back).astype(bf16)
        if out_rows is None:
            r.input_grad[here] = value
        else:
            r.input_grad[out_rows] = value[:tail]
        product = (grad * normal).reshape(4, 8, model).sum(0)
        return product, grad.reshape(4, 8, model).sum(0)

    def norm_rows():
        def step(i, totals):
            gain, shift = norm_step(pl.ds(pl.multiple_of(i * 32, 32), 32), None)
            return totals[0] + gain, totals[1] + shift

        zero = jnp.zeros((8, model), f32)
        gain, shift = lax.fori_loop(0, body_rows // 32, step, (zero, zero))
        if tail:
            more = norm_step(slice(body_rows, rows), slice(body_rows, slot_rows))
            gain, shift = gain + more[0], shift + more[1]
        line_to(late, jnp.sum(gain, 0, keepdims=True))
        line_to(late + wide, jnp.sum(shift, 0, keepdims=True))

    events = [last.cross, last.close]
    events += [functools.partial(scatters[2].step, s) for s in steps[min(heads, length - 1) :]]
    events += [functools.partial(scatters[1].step, s) for s in steps]
    events.insert(4, lambda: (last.arrive(), norm_rows()))
    for k, event in enumerate(events):
        tables(k * blocks // len(events), (k + 1) * blocks // len(events))
        event()
    flood = Flood(grid, r.own_small, r.all_small, *r.flood_sems[3])
    for s in range(length):
        flood.step(s)
        scatters[0].step(steps[s])
    own_lines = r.own_small.shape[0]
    r.all_small[pl.ds(pl.multiple_of(grid.me * own_lines, 8), own_lines)] = r.own_small[...]
    flood.arrive()
    small = jnp.zeros((height, LANES), f32)
    large = jnp.zeros((height, LANES), f32)
    total = jnp.zeros(r.vector_sums.shape, f32)
    for d in range(peers):
        at = d * own_lines
        kind = r.all_small[at + height : at + height + 1] > 0.5
        table = r.all_small[at : at + height]
        small += jnp.where(kind, 0.0, table)
        large += jnp.where(kind, table, 0.0)
        total += r.all_small[at + height : at + own_lines]
    r.small_sums[...] = small
    r.large_sums[...] = large
    r.vector_sums[...] = total
    for work in sums:
        work.drain()
    for work in floods + [flood] + scatters:
        work.drain()


def layer(arguments, peers, entries, slot_rows):
    model = arguments["inputs"].shape[1]
    rows, columns = arguments["index"].shape
    widths = [w.shape[1] for w in arguments["own"]]
    depth = model // peers
    hidden = arguments["hidden_shift"].shape[1]
    inner = arguments["qkv_shift"].shape[1] // 3
    heads = inner // HEAD_DIM
    groups = up_to(-(-entries // SPLIT), 16)
    height = heads * groups
    lines = 1 + hidden // LANES + 2 * (up_to(inner, LANES) // LANES) + VECTORS * (model // LANES)
    lines = up_to(lines, 8)
    count = len(cuts_of(rows // 2, CHUNKS))
    length = peers // 2
    array = jax.ShapeDtypeStruct

    def sems(*shape):
        return pltpu.SemaphoreType.DMA(shape)

    def each(kind, shape, times):
        return [pltpu.VMEM(shape, kind) for _ in range(times)]

    outs = dict(
        layer_out=array((slot_rows, model), bf16),
        input_grad=array((slot_rows, model), bf16),
        small_sums=array((height, LANES), f32),
        large_sums=array((height, LANES), f32),
        vector_sums=array((lines, LANES), f32),
        summed=[array((depth, w), f32) for w in widths],
    )
    blocks = [pltpu.VMEM((length, depth, w), bf16) for w in widths]
    scratch = dict(
        whole=[pltpu.VMEM((model, w), bf16) for w in widths],
        grad=[pltpu.VMEM((model, w), bf16) for w in widths],
        side=blocks,
        up=blocks,
        down=blocks,
        scatter_sems=[[sems(length)] * 6] * 3,
        flood_sems=[[sems(length)] * 6] * 4,
        part=each(f32, (rows, model), 3),
        total=each(f32, (rows, model), 3),
        near=each(f32, (rows // 2, model), 3),
        sent=each(bf16, (rows // 2, model), 3),
        far=each(bf16, (rows // 2, model), 3),
        sum_send=[sems(3, count)] * 3,
        sum_recv=[sems(3, count)] * 3,
        local_sem=sems(3),
        bias=pltpu.VMEM((heads, rows, columns), bf16),
        vectors=pltpu.VMEM((VECTORS, model), f32),
        running=pltpu.VMEM((7, 8, max(model, hidden)), f32),
        mean=each(f32, (rows, 1), 2),
        inverse=each(f32, (rows, 1), 2),
        normed=each(bf16, (rows, model), 2),
        kept=pltpu.VMEM((rows, model), bf16),
        grad_result=pltpu.VMEM((rows, model), bf16),
        grad_branch=pltpu.VMEM((rows, model), bf16),
        active=pltpu.VMEM((rows, hidden), bf16),
        grad_hidden=pltpu.VMEM((rows, hidden), bf16),
        qkv=pltpu.VMEM((rows, 3 * inner), bf16),
        grad_qkv=pltpu.VMEM((rows, 3 * inner), bf16),
        attended=pltpu.VMEM((rows, inner), bf16),
        grad_attended=pltpu.VMEM((rows, inner), bf16),
        middle=pltpu.VMEM((rows, model), f32),
        slope=pltpu.VMEM((rows, hidden), f32),
        own_small=pltpu.VMEM((height + lines, LANES), f32),
        all_small=pltpu.VMEM((peers * (height + lines), LANES), f32),
    )
    flat = jax.tree.leaves(arguments)
    shapes, out_tree = jax.tree.flatten(outs)
    tree = jax.tree.structure((arguments, outs, scratch))
    results = pl.pallas_call(
        functools.partial(layer_body, (tree, heads, groups, slot_rows, peers)),
        out_shape=shapes,
        in_specs=in_vmem(len(flat)),
        out_specs=in_vmem(len(shapes)),
        scratch_shapes=jax.tree.leaves(scratch),
        compiler_params=params(collective_id=0, has_side_effects=True),
        name="layer",
    )(*flat)
    found = types.SimpleNamespace(**jax.tree.unflatten(out_tree, results))
    found.tables = [
        table[:, :SPLIT].reshape(heads, groups * SPLIT)
        for table in (found.small_sums, found.large_sums)
    ]
    return found


def layer_norm(activations, norm_gain, norm_shift):
    center = activations - jnp.mean(activations, -1, keepdims=True)
    inverse = lax.rsqrt(jnp.mean(center * center, -1, keepdims=True) + EPS)
    normal = center * inverse
    return (normal * norm_gain + norm_shift, normal, inverse)


def norm_back(grad_normed, normal, inverse, norm_gain):
    scaled = grad_normed * norm_gain
    return inverse * (
        scaled
        - jnp.mean(scaled, -1, keepdims=True)
        - normal * jnp.mean(scaled * normal, -1, keepdims=True)
    )


def gelu_slope(hidden):
    cumulative = 0.5 * (1.0 + jax.scipy.special.erf(hidden * 0.7071067811865476))
    return cumulative + hidden * jnp.exp(-0.5 * hidden * hidden) * 0.3989422804014327


def pair_map(kind, small_index, large_index, rows, columns):
    def placed(index, at):
        side = index.shape[0]
        return jnp.pad(
            index, ((at, rows - at - side), (at, columns - at - side)), constant_values=-1
        )

    length = small_index.shape[0]
    small = placed(small_index, 0)
    for image in range(1, SLOT_ROWS // length):
        small = jnp.maximum(small, placed(small_index, image * length))
    return jnp.where(kind == 1, placed(large_index, 0), small)


def plain_device(
    images,
    out_grad,
    slot_kind,
    small_index,
    large_index,
    qkv_weight,
    out_weight,
    fc1_weight,
    fc2_weight,
    norm1_gain,
    norm1_shift,
    query_bias,
    value_bias,
    out_bias,
    gamma_attn,
    norm2_gain,
    norm2_shift,
    fc1_bias,
    fc2_bias,
    gamma_mlp,
    small_table,
    large_table,
):
    depth = qkv_weight.shape[0]
    width = query_bias.shape[0]
    hidden_width = fc1_bias.shape[0]
    heads = width // HEAD_DIM
    _, slot_rows, model_width = images.shape
    rows = up_to(slot_rows, 32)
    columns = up_to(rows, LANES)
    kind = slot_kind[0]

    block = jnp.concatenate(
        (
            qkv_weight.reshape(depth, 3 * width),
            fc1_weight,
            out_weight.T,
            fc2_weight.T,
        ),
        1,
    )
    whole = lax.all_gather(block, "dp", axis=0, tiled=True)
    cuts = (3 * width, 3 * width + hidden_width, 4 * width + hidden_width)
    qkv_matrix = whole[:, : cuts[0]]
    fc1_matrix = whole[:, cuts[0] : cuts[1]]
    out_turned = whole[:, cuts[1] : cuts[2]]
    fc2_turned = whole[:, cuts[2] :]
    small_vectors = jnp.stack(
        (norm1_gain, norm1_shift, out_bias, gamma_attn, norm2_gain, norm2_shift, fc2_bias, gamma_mlp)
    )
    vectors = lax.all_gather(small_vectors, "dp", axis=0)
    vectors = jnp.moveaxis(vectors, 0, 1).reshape(8, model_width).astype(f32)

    query_shift = query_bias.astype(f32)
    value_shift = value_bias.astype(f32)
    hidden_shift = fc1_bias.astype(f32)
    small_entries, large_entries = small_table.shape[0], large_table.shape[0]
    entries = up_to(max(small_entries, large_entries), LANES)
    table = jnp.where(
        kind == 1,
        jnp.pad(large_table, ((0, entries - large_entries), (0, 0))),
        jnp.pad(small_table, ((0, entries - small_entries), (0, 0))),
    )
    table = table.T.astype(f32)
    pair_index = pair_map(kind, small_index, large_index, rows, columns)
    bias = gather_bias(pair_index, table)

    positions = jnp.arange(rows)
    live_count = jnp.where(kind == 1, LARGE_LEN, slot_rows)
    live_rows = (positions < live_count).astype(f32).reshape(-1, 1)
    inputs = jnp.pad(images[0], ((0, rows - slot_rows), (0, 0))).astype(f32)
    normed_one, normal_one, inverse_one = layer_norm(inputs, vectors[0], vectors[1])
    normed_one = normed_one.astype(bf16)
    projected = dot(normed_one, qkv_matrix, 1, 0)
    queries = (projected[:, :width] + query_shift).astype(bf16)
    keys = projected[:, width : 2 * width].astype(bf16)
    values = (projected[:, 2 * width :] + value_shift).astype(bf16)
    pieces = attend_forward(queries, keys, values, bias)
    branch_part = dot(pieces, out_turned, 1, 1)
    branch = lax.psum(branch_part, "shard") + vectors[2]
    middle = inputs + vectors[3] * branch
    normed_two, normal_two, inverse_two = layer_norm(middle, vectors[4], vectors[5])
    normed_two = normed_two.astype(bf16)
    hidden = dot(normed_two, fc1_matrix, 1, 0) + hidden_shift
    active = jax.nn.gelu(hidden, approximate=False).astype(bf16)
    result_part = dot(active, fc2_turned, 1, 1)
    result = lax.psum(result_part.astype(bf16), "shard").astype(f32) + vectors[6]
    layer_out = ((middle + vectors[7] * result) * live_rows).astype(bf16)[:slot_rows][None]

    grad_out = jnp.pad(out_grad[0], ((0, rows - slot_rows), (0, 0))).astype(f32) * live_rows
    grad_gamma_mlp = jnp.sum(grad_out * result, 0)
    grad_result = (grad_out * vectors[7]).astype(bf16)
    grad_fc2_bias = jnp.sum(grad_result.astype(f32), 0)
    grad_fc2_turned = dot(grad_result, active, 0, 0)
    grad_active = dot(grad_result, fc2_turned, 1, 0)
    grad_hidden = (grad_active * gelu_slope(hidden)).astype(bf16)
    grad_fc1_bias = jnp.sum(grad_hidden.astype(f32), 0)
    grad_fc1 = dot(normed_two, grad_hidden, 0, 0)
    grad_normed_two = lax.psum(dot(grad_hidden, fc1_matrix, 1, 1), "shard")
    grad_norm2_gain = jnp.sum(grad_normed_two * normal_two, 0)
    grad_norm2_shift = jnp.sum(grad_normed_two, 0)
    grad_middle = grad_out + norm_back(grad_normed_two, normal_two, inverse_two, vectors[4])
    grad_gamma_attn = jnp.sum(grad_middle * branch, 0)
    grad_branch = (grad_middle * vectors[3]).astype(bf16)
    grad_out_bias = jnp.sum(grad_branch.astype(f32), 0)
    grad_out_turned = dot(grad_branch, pieces, 0, 0)
    grad_attended = dot(grad_branch, out_turned, 1, 0).astype(bf16)
    grad_queries, grad_keys, grad_values, grad_scores = attend_backward(
        queries, keys, values, bias, grad_attended
    )
    sums = table_sums(pair_index, grad_scores, entries)
    grad_projected = jnp.concatenate((grad_queries, grad_keys, grad_values), 1)
    grad_qkv = dot(normed_one, grad_projected, 0, 0)
    grad_query_bias = jnp.sum(grad_queries.astype(f32), 0)
    grad_value_bias = jnp.sum(grad_values.astype(f32), 0)
    grad_normed_one = lax.psum(dot(grad_projected, qkv_matrix, 1, 1), "shard")
    grad_norm1_gain = jnp.sum(grad_normed_one * normal_one, 0)
    grad_norm1_shift = jnp.sum(grad_normed_one, 0)
    input_grad = grad_middle + norm_back(grad_normed_one, normal_one, inverse_one, vectors[0])
    input_grad = input_grad.astype(bf16)[:slot_rows][None]

    small_sums = jnp.where(kind == 1, 0.0, sums[:, :small_entries])
    large_sums = jnp.where(kind == 1, sums[:, :large_entries], 0.0)
    local_sums = lax.psum(
        (small_sums, large_sums, grad_query_bias, grad_value_bias, grad_fc1_bias), "dp"
    )
    peers = lax.axis_size("dp")

    def sent_and_summed(value):
        parts = value.astype(bf16).reshape(peers, value.shape[0] // peers, -1)
        arrived = lax.all_to_all(parts, "dp", split_axis=0, concat_axis=0, tiled=True)
        return arrived.astype(f32).sum(axis=0)

    grad_block = sent_and_summed(
        jnp.concatenate((grad_qkv, grad_fc1, grad_out_turned, grad_fc2_turned), 1)
    )
    vector_grads = sent_and_summed(
        jnp.stack(
            (
                grad_norm1_gain,
                grad_norm1_shift,
                grad_out_bias,
                grad_gamma_attn,
                grad_norm2_gain,
                grad_norm2_shift,
                grad_fc2_bias,
                grad_gamma_mlp,
            ),
            1,
        )
    )
    return (
        layer_out,
        input_grad,
        grad_block[:, : cuts[0]].reshape(depth, 3, width),
        grad_block[:, cuts[1] : cuts[2]].T,
        grad_block[:, cuts[0] : cuts[1]],
        grad_block[:, cuts[2] :].T,
        vector_grads[:, 0],
        vector_grads[:, 1],
        local_sums[2],
        local_sums[3],
        vector_grads[:, 2],
        vector_grads[:, 3],
        vector_grads[:, 4],
        vector_grads[:, 5],
        local_sums[4],
        vector_grads[:, 6],
        vector_grads[:, 7],
        local_sums[0].T,
        local_sums[1].T,
    )


def on_device(*arguments):
    depth = arguments[5].shape[0]
    if depth % 16 or lax.axis_size("shard") != 4:
        return plain_device(*arguments)
    return whole_device(*arguments)


def whole_device(
    images,
    out_grad,
    slot_kind,
    small_index,
    large_index,
    qkv_weight,
    out_weight,
    fc1_weight,
    fc2_weight,
    norm1_gain,
    norm1_shift,
    query_bias,
    value_bias,
    out_bias,
    gamma_attn,
    norm2_gain,
    norm2_shift,
    fc1_bias,
    fc2_bias,
    gamma_mlp,
    small_table,
    large_table,
):
    depth = qkv_weight.shape[0]
    width = query_bias.shape[0]
    hidden_width = fc1_bias.shape[0]
    heads = width // HEAD_DIM
    _, slot_rows, model_width = images.shape
    rows = up_to(slot_rows, 32)
    columns = up_to(rows, LANES)
    kind = slot_kind[0]
    peers = lax.axis_size("dp")

    small_vectors = jnp.stack(
        (norm1_gain, norm1_shift, out_bias, gamma_attn, norm2_gain, norm2_shift, fc2_bias, gamma_mlp),
        1,
    )
    first = jnp.concatenate(
        (
            qkv_weight.reshape(depth, 3 * width),
            jnp.pad(small_vectors, ((0, 0), (0, HEAD_DIM - VECTORS))),
            out_weight.T,
        ),
        1,
    )
    small_entries, large_entries = small_table.shape[0], large_table.shape[0]
    entries = up_to(max(small_entries, large_entries), LANES)
    table = jnp.where(
        kind == 1,
        jnp.pad(large_table, ((0, entries - large_entries), (0, 0))),
        jnp.pad(small_table, ((0, entries - small_entries), (0, 0))),
    )
    live_count = jnp.where(kind == 1, LARGE_LEN, slot_rows)
    slot = jnp.stack((kind, live_count)).astype(f32)
    found = layer(
        dict(
            inputs=images[0],
            out_grad=out_grad[0],
            index=pair_map(kind, small_index, large_index, rows, columns),
            table=table.T.astype(f32).reshape(-1, LANES),
            own=[first, fc1_weight, fc2_weight.T],
            qkv_shift=jnp.concatenate(
                (query_bias, jnp.zeros((width,), bf16), value_bias)
            ).astype(f32)[None],
            hidden_shift=fc1_bias.astype(f32)[None],
            slot=jnp.broadcast_to(slot[:, None], (2, LANES)),
        ),
        peers,
        entries,
        slot_rows,
    )
    here = lax.axis_index("dp") * depth
    vector_sums = found.vector_sums
    wide = model_width // LANES
    hidden_lines = hidden_width // LANES
    narrow = up_to(width, LANES) // LANES
    at = 1 + hidden_lines + 2 * narrow
    vector_grads = lax.dynamic_slice_in_dim(
        vector_sums[at : at + VECTORS * wide].reshape(VECTORS, model_width), here, depth, 1
    )

    def taken(first, count, size):
        return vector_sums[first : first + count].reshape(-1)[:size]

    summed = found.summed
    return (
        found.layer_out[None],
        found.input_grad[None],
        summed[0][:, : 3 * width].reshape(depth, 3, width),
        summed[0][:, 3 * width + HEAD_DIM :].T,
        summed[1],
        summed[2].T,
        vector_grads[6],
        vector_grads[7],
        taken(1 + hidden_lines, narrow, width),
        taken(1 + hidden_lines + narrow, narrow, width),
        vector_grads[0],
        vector_grads[1],
        vector_grads[2],
        vector_grads[3],
        taken(1, hidden_lines, hidden_width),
        vector_grads[4],
        vector_grads[5],
        found.tables[0][:, :small_entries].T,
        found.tables[1][:, :large_entries].T,
    )


def solution(mesh):
    return jax.shard_map(
        on_device,
        mesh=mesh,
        in_specs=(
            P("dp", None, None),
            P("dp", None, None),
            P("dp"),
            P(),
            P(),
            P("dp", None, "shard"),
            P("shard", "dp"),
            P("dp", "shard"),
            P("shard", "dp"),
            P("dp"),
            P("dp"),
            P("shard"),
            P("shard"),
            P("dp"),
            P("dp"),
            P("dp"),
            P("dp"),
            P("shard"),
            P("dp"),
            P("dp"),
            P(None, "shard"),
            P(None, "shard"),
        ),
        out_specs=(
            P("dp", None, None),
            P("dp", None, None),
            P("dp", None, "shard"),
            P("shard", "dp"),
            P("dp", "shard"),
            P("shard", "dp"),
            P("dp"),
            P("dp"),
            P("shard"),
            P("shard"),
            P("dp"),
            P("dp"),
            P("dp"),
            P("dp"),
            P("shard"),
            P("dp"),
            P("dp"),
            P(None, "shard"),
            P(None, "shard"),
        ),
        check_vma=False,
    )
```

```python
import functools
import types

import jax
import jax.numpy as jnp
from jax import lax
from jax.experimental import pallas as pl
from jax.experimental.pallas import tpu as pltpu
from jax.sharding import PartitionSpec as P

HEAD_DIM = 64
SMALL_LEN = 197
LARGE_LEN = 577
SLOT_ROWS = 591
EPS = 1e-06
NEG = -1e30
LANES = 128
SPLIT = 80
VMEM_LIMIT = 56 << 20

MESH = pl.DeviceIdType.MESH

f32 = jnp.float32
bf16 = jnp.bfloat16


def up_to(value, unit):
    return -(-value // unit) * unit


def in_vmem(count):
    return [pl.BlockSpec(memory_space=pltpu.VMEM)] * count


def params(**more):
    return pltpu.CompilerParams(vmem_limit_bytes=VMEM_LIMIT, **more)


def dot(a, b, da, db):
    return lax.dot_general(a, b, (((da,), (db,)), ((), ())), preferred_element_type=f32)


def bias_block_of(heads, index_ref, table_ref, out_ref, here):
    columns, entries = index_ref.shape[1], table_ref.shape[1]
    for c in range(columns // LANES):
        there = pl.ds(c * LANES, LANES)
        index = index_ref[here, there]
        high = lax.shift_right_arithmetic(index, 7)
        low = lax.bitwise_and(index, LANES - 1)
        found = [jnp.full(index.shape, NEG, f32) for _ in range(heads)]
        for k in range(entries // LANES):
            match = high == k
            for h in range(heads):
                line = table_ref[h : h + 1, k * LANES : (k + 1) * LANES]
                values = jnp.take_along_axis(jnp.broadcast_to(line, index.shape), low, axis=1)
                found[h] = jnp.where(match, values, found[h])
        for h in range(heads):
            out_ref[h, here, there] = found[h].astype(bf16)


def table_block(heads, groups, index_ref, grad_ref, out_ref, here):
    columns = index_ref.shape[1]
    inverse = -(-(1 << 22) // SPLIT)
    index = index_ref[here, :]
    high = lax.shift_right_arithmetic(index * inverse, 22)
    low = (index - high * SPLIT).astype(jnp.int16)
    high = high.astype(jnp.int16)
    grads = [grad_ref[h, here, :] for h in range(heads)]
    places_low = lax.broadcasted_iota(jnp.int16, (SPLIT, columns), 0)
    places_high = lax.broadcasted_iota(jnp.int16, (groups, columns), 0)
    one, zero = jnp.ones((), bf16), jnp.zeros((), bf16)
    total = jnp.zeros((heads * groups, SPLIT), f32)
    for pair in range(0, 16, 2):
        lows, highs = [], []
        for i in (pair, pair + 1):
            lows.append(
                jnp.where(
                    places_low == jnp.broadcast_to(low[i : i + 1], (SPLIT, columns)), one, zero
                )
            )
            match = places_high == jnp.broadcast_to(high[i : i + 1], (groups, columns))
            highs.append(
                jnp.concatenate(
                    [
                        jnp.where(
                            match,
                            jnp.broadcast_to(grads[h][i : i + 1], (groups, columns)),
                            zero,
                        )
                        for h in range(heads)
                    ],
                    0,
                )
            )
        total = total + dot(jnp.concatenate(highs, 1), jnp.concatenate(lows, 1), 1, 1)
    out_ref[: heads * groups, :SPLIT] += total


def forward_body(heads, q_ref, k_ref, v_ref, bias_ref, out_ref):
    rows = q_ref.shape[0]
    for h in range(heads):
        part = slice(h * HEAD_DIM, (h + 1) * HEAD_DIM)
        scores = dot(q_ref[:, part], k_ref[:, part], 1, 1) * HEAD_DIM ** (-0.5)
        scores = scores + bias_ref[h, :, :rows].astype(f32)
        weights = jnp.exp(scores - jnp.max(scores, -1, keepdims=True))
        weights = weights / jnp.sum(weights, -1, keepdims=True)
        out_ref[:, part] = dot(weights.astype(bf16), v_ref[:, part], 1, 0).astype(bf16)


def backward_body(
    heads, q_ref, k_ref, v_ref, bias_ref, grad_ref, dq_ref, dk_ref, dv_ref, ds_ref
):
    rows = q_ref.shape[0]
    factor = HEAD_DIM ** (-0.5)
    for h in range(heads):
        part = slice(h * HEAD_DIM, (h + 1) * HEAD_DIM)
        scores = dot(q_ref[:, part], k_ref[:, part], 1, 1) * factor
        scores = scores + bias_ref[h, :, :rows].astype(f32)
        weights = jnp.exp(scores - jnp.max(scores, -1, keepdims=True))
        weights = weights / jnp.sum(weights, -1, keepdims=True)
        dv_ref[:, part] = dot(weights.astype(bf16), grad_ref[:, part], 0, 0).astype(bf16)
        grad = dot(grad_ref[:, part], v_ref[:, part], 1, 1)
        mean = jnp.sum(weights * grad, -1, keepdims=True)
        grad = (weights * (grad - mean)).astype(bf16)
        ds_ref[h, :, :rows] = grad
        dq_ref[:, part] = (dot(grad, k_ref[:, part], 1, 0) * factor).astype(bf16)
        dk_ref[:, part] = (dot(grad, q_ref[:, part], 0, 0) * factor).astype(bf16)


def attend_forward(queries, keys, values, bias):
    heads = bias.shape[0]
    return pl.pallas_call(
        functools.partial(forward_body, heads),
        out_shape=jax.ShapeDtypeStruct(queries.shape, bf16),
        in_specs=in_vmem(4),
        out_specs=in_vmem(1)[0],
        compiler_params=params(),
        cost_estimate=pl.CostEstimate(flops=10**9, bytes_accessed=10**7, transcendentals=10**6),
        name="attend_forward",
    )(queries, keys, values, bias)


def attend_backward(queries, keys, values, bias, grad):
    heads = bias.shape[0]
    rows = jax.ShapeDtypeStruct(queries.shape, bf16)
    return pl.pallas_call(
        functools.partial(backward_body, heads),
        out_shape=(rows, rows, rows, jax.ShapeDtypeStruct(bias.shape, bf16)),
        in_specs=in_vmem(5),
        out_specs=tuple(in_vmem(4)),
        compiler_params=params(),
        cost_estimate=pl.CostEstimate(flops=2 * 10**9, bytes_accessed=2 * 10**7, transcendentals=10**6),
        name="attend_backward",
    )(queries, keys, values, bias, grad)


def bias_body(heads, index_ref, table_ref, out_ref):
    def work(block):
        here = pl.ds(pl.multiple_of(block * ROW_STEP, ROW_STEP), ROW_STEP)
        bias_block_of(heads, index_ref, table_ref, out_ref, here)

    with_events(index_ref.shape[0] // ROW_STEP, [], work)


def gather_bias(pair_index, table):
    heads, entries = table.shape
    return pl.pallas_call(
        functools.partial(bias_body, heads),
        out_shape=jax.ShapeDtypeStruct((heads,) + pair_index.shape, bf16),
        in_specs=in_vmem(2),
        out_specs=in_vmem(1)[0],
        compiler_params=params(),
        cost_estimate=pl.CostEstimate(flops=10**9, bytes_accessed=4 * 10**7, transcendentals=0),
        name="bias",
    )(pair_index, table)


def table_body(heads, groups, index_ref, grad_ref, out_ref):
    out_ref[...] = jnp.zeros_like(out_ref)

    def work(block):
        here = pl.ds(pl.multiple_of(block * ROW_STEP, ROW_STEP), ROW_STEP)
        table_block(heads, groups, index_ref, grad_ref, out_ref, here)

    with_events(index_ref.shape[0] // ROW_STEP, [], work)


def table_sums(pair_index, grad_scores, entries):
    heads = grad_scores.shape[0]
    groups = up_to(-(-entries // SPLIT), 16)
    sums = pl.pallas_call(
        functools.partial(table_body, heads, groups),
        out_shape=jax.ShapeDtypeStruct((heads * groups, SPLIT), f32),
        in_specs=in_vmem(2),
        out_specs=in_vmem(1)[0],
        compiler_params=params(),
        cost_estimate=pl.CostEstimate(flops=2 * 10**9, bytes_accessed=6 * 10**7, transcendentals=0),
        name="table_sums",
    )(pair_index, grad_scores)
    return sums.reshape(heads, groups * SPLIT)


def cuts_of(total, pieces, unit=16):
    count, extra = divmod(total // unit, pieces)
    cuts, at = [], 0
    for i in range(pieces):
        size = (count + (i < extra)) * unit
        if size:
            cuts.append((at, size))
        at += size
    return cuts


def remote(src, dst, send_sem, recv_sem, axis, peer):
    return pltpu.make_async_remote_copy(
        src_ref=src,
        dst_ref=dst,
        send_sem=send_sem,
        recv_sem=recv_sem,
        device_id={axis: peer},
        device_id_type=MESH,
    )


def greet(barrier, axis, peer):
    pl.semaphore_signal(barrier, inc=1, device_id={axis: peer}, device_id_type=MESH)


class ShardSum:
    def __init__(self, chunks, part_ref, out_ref, near, sent, far, send_sem, recv_sem):
        me = lax.axis_index("shard")
        outer, self.inner = me // 2, lax.rem(me, 2)
        self.near_peer = outer * 2 + (1 - self.inner)
        self.far_peer = (1 - outer) * 2 + self.inner
        self.chunks, self.part, self.out = chunks, part_ref, out_ref
        self.near, self.sent, self.far = near, sent, far
        self.sems = (send_sem, recv_sem)
        self.half = near.shape[0]

    def greet(self, barrier):
        greet(barrier, "shard", self.near_peer)
        greet(barrier, "shard", self.far_peer)
        return 2

    def rows(self, which, at, size):
        return pl.ds(pl.multiple_of(which * self.half + at, 16), size)

    def copy(self, stage, j, src, dst, peer):
        send_sem, recv_sem = self.sems
        return remote(src, dst, send_sem.at[stage, j], recv_sem.at[stage, j], "shard", peer)

    def first(self, j):
        at, size = self.chunks[j]
        return self.copy(
            0, j, self.part.at[self.rows(1 - self.inner, at, size)], self.near.at[pl.ds(at, size)], self.near_peer
        )

    def second(self, j):
        here = pl.ds(*self.chunks[j])
        return self.copy(1, j, self.sent.at[here], self.far.at[here], self.far_peer)

    def third(self, j):
        mine = self.out.at[self.rows(self.inner, *self.chunks[j])]
        return self.copy(2, j, mine, mine, self.near_peer)

    def start(self):
        for j in range(len(self.chunks)):
            self.first(j).start()

    def cross_one(self, j):
        at, size = self.chunks[j]
        self.first(j).wait_recv()
        here = pl.ds(at, size)
        mine = self.rows(self.inner, at, size)
        self.sent[here] = (self.part[mine] + self.near[here]).astype(bf16)
        self.second(j).start()

    def cross(self):
        for j in range(len(self.chunks)):
            self.cross_one(j)

    def close_one(self, j):
        at, size = self.chunks[j]
        self.second(j).wait_recv()
        here = pl.ds(at, size)
        mine = self.rows(self.inner, at, size)
        self.out[mine] = self.sent[here].astype(f32) + self.far[here].astype(f32)
        self.third(j).start()

    def close(self):
        for j in range(len(self.chunks)):
            self.close_one(j)

    def arrive(self):
        for j in range(len(self.chunks)):
            self.third(j).wait_recv()

    def drain(self):
        for j in range(len(self.chunks)):
            self.first(j).wait_send()
            self.second(j).wait_send()
            self.third(j).wait_send()


class Grid:
    def __init__(self, peers):
        self.length = peers // 2
        self.me = lax.axis_index("dp")
        self.at, self.side = self.me // 2, lax.rem(self.me, 2)
        self.up, self.down = self.me + 2, self.me - 2
        self.across = self.at * 2 + 1 - self.side
        self.has_up, self.has_down = self.at < self.length - 1, self.at > 0

    def greet(self, barrier):
        greet(barrier, "dp", self.across)

        @pl.when(self.has_up)
        def _():
            greet(barrier, "dp", self.up)

        @pl.when(self.has_down)
        def _():
            greet(barrier, "dp", self.down)

        return 1 + self.has_up.astype(jnp.int32) + self.has_down.astype(jnp.int32)

    def clip(self, place):
        return jnp.clip(place, 0, self.length - 1)


class Flood:
    def __init__(self, grid, own, out, up_send, up_recv, down_send, down_recv, side_send, side_recv):
        self.grid, self.own, self.out = grid, own, out
        self.up_sems, self.down_sems = (up_send, up_recv), (down_send, down_recv)
        self.side_sems = (side_send, side_recv)

    def at(self, device):
        depth = self.own.shape[0]
        return self.out.at[pl.ds(pl.multiple_of(device * depth, 8), depth)]

    def block(self, place):
        return self.at(self.grid.clip(place) * 2 + self.grid.side)

    def up(self, s):
        grid, (send, recv) = self.grid, self.up_sems
        block = self.block(grid.at - s)
        return remote(self.own if s == 0 else block, block, send.at[s], recv.at[s], "dp", grid.up)

    def down(self, s):
        grid, (send, recv) = self.grid, self.down_sems
        block = self.block(grid.at + s)
        return remote(self.own if s == 0 else block, block, send.at[s], recv.at[s], "dp", grid.down)

    def across(self, place, own=False):
        grid, (send, recv) = self.grid, self.side_sems
        place = grid.clip(place)
        block = self.block(place)
        return remote(
            self.own if own else block, block, send.at[place], recv.at[place], "dp", grid.across
        )

    def step(self, s):
        grid = self.grid
        if s == 0:

            @pl.when(grid.has_up)
            def _():
                self.up(0).start()

            @pl.when(grid.has_down)
            def _():
                self.down(0).start()

            self.across(grid.at, own=True).start()
            return

        @pl.when(grid.at - s >= 0)
        def _():
            block = self.block(grid.at - s)
            send, recv = self.up_sems
            remote(block, block, send.at[s - 1], recv.at[s - 1], "dp", grid.down).wait_recv()

            @pl.when(grid.has_up)
            def _():
                self.up(s).start()

            self.across(grid.at - s).start()

        @pl.when(grid.at + s < grid.length)
        def _():
            block = self.block(grid.at + s)
            send, recv = self.down_sems
            remote(block, block, send.at[s - 1], recv.at[s - 1], "dp", grid.up).wait_recv()

            @pl.when(grid.has_down)
            def _():
                self.down(s).start()

            self.across(grid.at + s).start()

    def arrive(self):
        grid, (send, recv) = self.grid, self.side_sems
        for place in range(grid.length):
            block = self.at(place * 2 + 1 - grid.side)
            remote(block, block, send.at[place], recv.at[place], "dp", grid.across).wait_recv()

    def drain(self):
        grid = self.grid
        for place in range(grid.length):
            self.across(place).wait_send()
        for s in range(grid.length - 1):

            @pl.when(jnp.logical_and(grid.at - s >= 0, grid.has_up))
            def _():
                self.up(s).wait_send()

            @pl.when(jnp.logical_and(grid.at + s < grid.length, grid.has_down))
            def _():
                self.down(s).wait_send()


SIDE, UP, DOWN = range(3)


class ReduceScatter:
    def __init__(self, grid, grads, out, side, up, down, sems):
        self.grid, self.grads, self.out = grid, grads, out
        self.buffers = (side, up, down)
        self.sems = (sems[:2], sems[2:4], sems[4:6])

    def at(self, device):
        depth = self.out.shape[0]
        return pl.ds(pl.multiple_of(device * depth, 16), depth)

    def prepare(self):
        grid = self.grid

        @pl.when(jnp.logical_not(grid.has_down))
        def _():
            self.buffers[UP][...] = jnp.zeros_like(self.buffers[UP])

        @pl.when(jnp.logical_not(grid.has_up))
        def _():
            self.buffers[DOWN][...] = jnp.zeros_like(self.buffers[DOWN])

    def copy(self, way, place, peer, src=None):
        send, recv = self.sems[way]
        place = self.grid.clip(place)
        dst = self.buffers[way].at[place]
        return remote(dst if src is None else src, dst, send.at[place], recv.at[place], "dp", peer)

    def cross(self, place):
        grid = self.grid
        src = self.grads.at[self.at(grid.clip(place) * 2 + 1 - grid.side)]
        return self.copy(SIDE, place, grid.across, src)

    def start(self, s):
        grid = self.grid

        @pl.when(grid.at + s < grid.length)
        def _():
            self.cross(grid.at + s).start()

        if s:

            @pl.when(grid.at - s >= 0)
            def _():
                self.cross(grid.at - s).start()

    def step(self, s):
        grid = self.grid
        side, up, down = self.buffers
        if s == 0:
            place = grid.at
            self.copy(SIDE, place, grid.across).wait_recv()

            @pl.when(grid.has_down)
            def _():
                self.copy(UP, place, grid.down).wait_recv()

            @pl.when(grid.has_up)
            def _():
                self.copy(DOWN, place, grid.up).wait_recv()

            total = self.grads[self.at(grid.me)].astype(f32) + side[place].astype(f32)
            self.out[...] = total + (up[place].astype(f32) + down[place].astype(f32))
            return

        @pl.when(grid.at + s < grid.length)
        def _():
            place = grid.clip(grid.at + s)
            self.copy(SIDE, place, grid.across).wait_recv()

            @pl.when(grid.has_down)
            def _():
                self.copy(UP, place, grid.down).wait_recv()

            total = self.grads[self.at(place * 2 + grid.side)].astype(f32) + side[place].astype(f32)
            side[place] = (total + up[place].astype(f32)).astype(bf16)
            self.copy(UP, place, grid.up, side.at[place]).start()

        @pl.when(grid.at - s >= 0)
        def _():
            place = grid.clip(grid.at - s)
            self.copy(SIDE, place, grid.across).wait_recv()

            @pl.when(grid.has_up)
            def _():
                self.copy(DOWN, place, grid.up).wait_recv()

            total = self.grads[self.at(place * 2 + grid.side)].astype(f32) + side[place].astype(f32)
            side[place] = (total + down[place].astype(f32)).astype(bf16)
            self.copy(DOWN, place, grid.down, side.at[place]).start()

    def drain(self):
        grid = self.grid
        for place in range(grid.length):
            self.cross(place).wait_send()
        for s in range(1, grid.length):

            @pl.when(grid.at + s < grid.length)
            def _():
                self.copy(UP, grid.at + s, grid.up).wait_send()

            @pl.when(grid.at - s >= 0)
            def _():
                self.copy(DOWN, grid.at - s, grid.down).wait_send()


ROW_STEP = 16
CHUNKS = 5
VECTORS = 8
EARLY_LINES = 16
LAG = 0
BIAS_PLACES = [5, 11, 17, 11, 19, 25, 32, 20, 28, 36, 99]
TABLE_PLACES = [1, 3, 10, 15, 20, 24, 30, 36, 99]
CLOSE_PLACE = 17
NORM_PLACE = 22


def with_events(blocks, events, work):
    def step(block, carry):
        for at, event in events:
            pl.when(block == at)(event)

        @pl.when(block < blocks)
        def _():
            work(block)

        return carry

    lax.fori_loop(0, max([blocks] + [at + 1 for at, _ in events]), step, 0)


class Spread:
    def __init__(self, peers, out, send_sem, recv_sem):
        self.peers, self.out, self.sems = peers, out, (send_sem, recv_sem)
        self.me = lax.axis_index("dp")

    def peer(self, i):
        return lax.rem(self.me + i, self.peers)

    def copy(self, src, slot, peer):
        send_sem, recv_sem = self.sems
        return remote(
            src, self.out.at[slot], send_sem.at[peer], recv_sem.at[slot], "dp", peer
        )

    def start(self, src_for):
        for i in range(1, self.peers):
            self.copy(src_for(self.peer(i)), self.me, self.peer(i)).start()

    def arrive(self):
        for i in range(1, self.peers):
            peer = self.peer(i)
            self.copy(self.out.at[peer], peer, peer).wait_recv()

    def drain(self):
        for i in range(1, self.peers):
            peer = self.peer(i)
            self.copy(self.out.at[peer], peer, peer).wait_send()


def layer_body(plan, *refs):
    tree, heads, groups, slot_rows, peers = plan
    named = {}
    for part in jax.tree.unflatten(tree, refs):
        named.update(part)
    r = types.SimpleNamespace(**named)
    rows, columns = r.index.shape
    model = r.inputs.shape[1]
    depth = model // peers
    inner = heads * HEAD_DIM
    half = rows // 2
    chunks = cuts_of(half, CHUNKS)
    count = len(chunks)
    factor = HEAD_DIM ** (-0.5)
    height = heads * groups

    grid = Grid(peers)
    sums = [
        ShardSum(chunks, *buffers)
        for buffers in zip(r.part, r.total, r.near, r.sent, r.far, r.sum_send, r.sum_recv)
    ]
    lines = Flood(grid, r.own_lines, r.all_lines, *r.flood_sems[3])
    floods = [
        Flood(grid, own, out, *sems) for own, out, sems in zip((r.own_first, r.fc1_weight, r.fc2_weight), r.whole, r.flood_sems)
    ]
    scatters = [
        ReduceScatter(grid, *buffers)
        for buffers in zip(r.grad, r.summed, r.side, r.up, r.down, r.scatter_sems)
    ]
    spreads = [
        Spread(peers, out, *sems)
        for out, sems in zip((r.all_early, r.all_late, r.all_table), r.spread_sems)
    ]

    loads = [
        pltpu.make_async_copy(src, dst, r.load_sem.at[j])
        for j, (src, dst) in enumerate(
            ((r.large_index, r.wide_from), (r.inputs, r.inputs_here), (r.out_grad, r.grad_here))
        )
    ]
    for load in loads:
        load.start()
    for i, member in enumerate(r.small_vectors):
        r.own_lines[i : i + 1, :depth] = member[...].astype(f32).reshape(1, depth)
    for j in range(3):
        r.own_first[:, j * inner : (j + 1) * inner] = r.qkv_weight[j]
    r.own_first[:, 3 * inner :] = r.out_weight[...].T
    barrier = pltpu.get_barrier_semaphore()
    met = sums[0].greet(barrier)
    for i in range(1, peers):
        greet(barrier, "dp", lax.rem(grid.me + i, peers))
    pl.semaphore_wait(barrier, met + peers - 1)
    lines.step(0)
    floods[0].step(0)
    copies = [
        pltpu.make_async_copy(flood.own, flood.at(grid.me), r.local_sem.at[j])
        for j, flood in enumerate(floods + [lines])
    ]
    for copy in copies:
        copy.start()
    for scatter in scatters:
        scatter.prepare()

    kind = r.slot_kind[0]
    r.slot[0:1] = jnp.full((1, LANES), kind.astype(f32))
    r.slot[1:2] = jnp.full((1, LANES), (slot_rows - kind * (slot_rows - LARGE_LEN)).astype(f32))
    is_large = jnp.broadcast_to(r.slot[0:1, :], (8, LANES)) > 0.5
    small_side, large_side = r.small_index.shape[0], r.large_index.shape[0]
    r.index[...] = jnp.full((rows, columns), -1, jnp.int32)
    for image in range(slot_rows // small_side):
        at = image * small_side
        r.index[at : at + small_side, at : at + small_side] = r.small_index[...]
    r.wide_index[...] = jnp.full((rows, columns), -1, jnp.int32)
    for load in loads:
        load.wait()
    r.wide_index[:large_side, :large_side] = r.wide_from[...]
    r.table[...] = jnp.zeros_like(r.table)
    entries_small, entries_large = r.small_table.shape[1], r.large_table.shape[1]
    r.table[:heads, :entries_small] = r.small_table[...].astype(f32)
    r.wide_table[...] = jnp.zeros_like(r.wide_table)
    r.wide_table[:heads, :entries_large] = r.large_table[...].astype(f32)
    tall = jnp.broadcast_to(is_large[:, 0:1], r.table.shape)
    r.table[...] = jnp.where(tall, r.wide_table[...], r.table[...])
    large_block = jnp.broadcast_to(r.slot[0:1, 0:1], (ROW_STEP, columns)) > 0.5

    body_rows = slot_rows // 32 * 32
    tail = slot_rows - body_rows
    r.kept[:body_rows] = r.inputs_here[:body_rows]
    r.kept[body_rows:] = jnp.concatenate(
        (
            r.inputs_here[body_rows:slot_rows].astype(f32),
            jnp.zeros((rows - slot_rows, model), f32),
        ),
        0,
    ).astype(bf16)
    blocks = up_to(slot_rows, ROW_STEP) // ROW_STEP

    def bias_block(block):
        here = pl.ds(pl.multiple_of(block * ROW_STEP, ROW_STEP), ROW_STEP)
        r.index[here] = jnp.where(large_block, r.wide_index[here], r.index[here])
        bias_block_of(heads, r.index, r.table, r.bias, here)

    r.index[blocks * ROW_STEP :] = jnp.full((rows - blocks * ROW_STEP, columns), -1, jnp.int32)
    r.bias[:, blocks * ROW_STEP :] = jnp.full(
        (heads, rows - blocks * ROW_STEP, columns), NEG, bf16
    )
    length = grid.length

    def flood_event(j, s):
        return lambda: floods[j].step(s)

    order = [(0, s) for s in range(1, length)] + [(j, s) for j in (1, 2) for s in range(length)]
    places = BIAS_PLACES if length == 4 else [k * 3 for k in range(len(order))]
    events = [(at, flood_event(*item)) for at, item in zip(places, order)]
    events += [(3 * s, functools.partial(lines.step, s)) for s in range(1, length)]
    late_floods = [event for at, event in events if at >= blocks]
    with_events(blocks, [(at, event) for at, event in events if at < blocks], bias_block)
    for copy in copies:
        copy.wait()
    lines.arrive()
    floods[0].arrive()
    for d in range(peers):
        r.vectors[:, d * depth : (d + 1) * depth] = r.all_lines[
            d * VECTORS : (d + 1) * VECTORS, :depth
        ]

    def vector(i):
        return r.vectors[i : i + 1, :]

    def moments(value):
        mean = jnp.mean(value, -1, keepdims=True)
        center = value - mean
        inverse = lax.rsqrt(jnp.mean(center * center, -1, keepdims=True) + EPS)
        return center * inverse, mean, inverse

    def both(ref, c):
        at, size = chunks[c]
        return jnp.concatenate((ref[at : at + size], ref[half + at : half + at + size]), 0)

    def put(ref, c, value):
        at, size = chunks[c]
        ref[at : at + size] = value[:size]
        ref[half + at : half + at + size] = value[size:]

    def add(i, value):
        r.running[i] += value.reshape(value.shape[0] // 8, 8, value.shape[1]).sum(0)

    r.running[...] = jnp.zeros_like(r.running)
    r.qkv_shift[...] = jnp.zeros_like(r.qkv_shift)
    r.qkv_shift[:, :inner] = r.query_bias[...].astype(f32).reshape(1, inner)
    r.qkv_shift[:, 2 * inner :] = r.value_bias[...].astype(f32).reshape(1, inner)
    r.hidden_shift[...] = r.fc1_bias[...].astype(f32).reshape(r.hidden_shift.shape)
    for c in range(count):
        normal, mean, inverse = moments(both(r.kept, c).astype(f32))
        put(r.mean[0], c, mean)
        put(r.inverse[0], c, inverse)
        normed = (normal * vector(0) + vector(1)).astype(bf16)
        put(r.normed[0], c, normed)
        projected = dot(normed, r.whole[0][:, : 3 * inner], 1, 0) + r.qkv_shift[...]
        put(r.qkv, c, projected.astype(bf16))

    def weights_of(h):
        part = slice(h * HEAD_DIM, (h + 1) * HEAD_DIM)
        keys = slice(inner + h * HEAD_DIM, inner + (h + 1) * HEAD_DIM)
        scores = dot(r.qkv[:, part], r.qkv[:, keys], 1, 1) * factor
        scores = scores + r.bias[h, :, :rows].astype(f32)
        weights = jnp.exp(scores - jnp.max(scores, -1, keepdims=True))
        return weights * (1.0 / jnp.sum(weights, -1, keepdims=True))

    for h in range(heads):
        for event in late_floods[h * len(late_floods) // heads : (h + 1) * len(late_floods) // heads]:
            event()
        part = slice(h * HEAD_DIM, (h + 1) * HEAD_DIM)
        values = slice(2 * inner + h * HEAD_DIM, 2 * inner + (h + 1) * HEAD_DIM)
        r.attended[:, part] = dot(weights_of(h).astype(bf16), r.qkv[:, values], 1, 0).astype(bf16)

    def out_turned():
        return r.whole[0][:, 3 * inner :]

    def live_rows(c):
        at, size = chunks[c]
        first = lax.broadcasted_iota(jnp.int32, (size, 1), 0) + at
        places = jnp.concatenate((first, first + half), 0).astype(f32)
        return jnp.where(places < r.slot[1:2, 0:1], 1.0, 0.0)

    def padded(ref, c):
        at, size = chunks[c]
        last = min(half + at + size, slot_rows)
        low = ref[half + at : last]
        missing = half + at + size - last
        if missing:
            low = jnp.concatenate(
                (low.astype(f32), jnp.zeros((missing, low.shape[1]), f32)), 0
            )
        return jnp.concatenate((ref[at : at + size].astype(f32), low.astype(f32)), 0)

    def keep(ref, c, value):
        at, size = chunks[c]
        last = min(half + at + size, slot_rows)
        ref[at : at + size] = value[:size]
        ref[half + at : last] = value[size : size + last - half - at]

    def project(c):
        put(r.part[0], c, dot(both(r.attended, c), out_turned(), 1, 1))
        sums[0].first(c).start()

    def forward(c):
        if c == 0:
            floods[1].arrive()
        sums[0].third(c).wait_recv()
        middle = both(r.kept, c).astype(f32) + vector(3) * (both(r.total[0], c) + vector(2))
        put(r.middle, c, middle)
        normal, mean, inverse = moments(middle)
        put(r.mean[1], c, mean)
        put(r.inverse[1], c, inverse)
        normed = (normal * vector(4) + vector(5)).astype(bf16)
        put(r.normed[1], c, normed)
        hidden = dot(normed, r.whole[1][...], 1, 0) + r.hidden_shift[...]
        cumulative = 0.5 * (1.0 + lax.erf(hidden * 0.7071067811865476))
        put(
            r.slope,
            c,
            cumulative + hidden * jnp.exp(-0.5 * hidden * hidden) * 0.3989422804014327,
        )
        active = (hidden * cumulative).astype(bf16)
        put(r.active, c, active)
        if c == 0:
            floods[2].arrive()
        put(r.part[1], c, dot(active, r.whole[2][...], 1, 1))
        sums[1].first(c).start()

    def turn(c):
        sums[1].third(c).wait_recv()
        result = both(r.total[1], c) + vector(6)
        live = live_rows(c)
        keep(r.out_here, c, (live * (both(r.middle, c) + vector(7) * result)).astype(bf16))
        grad = padded(r.grad_here, c) * live
        add(6, grad * result)
        grad_result = (grad * vector(7)).astype(bf16)
        put(r.grad_result, c, grad_result)
        add(5, grad_result.astype(f32))
        grad_hidden = (dot(grad_result, r.whole[2][...], 1, 0) * both(r.slope, c)).astype(bf16)
        put(r.grad_hidden, c, grad_hidden)
        add(0, grad_hidden.astype(f32))
        put(r.part[2], c, dot(grad_hidden, r.whole[1][...], 1, 1))
        sums[2].first(c).start()

    def back_norm(grad, normal, inverse, gain):
        scaled = grad * gain
        along = jnp.mean(scaled * normal, -1, keepdims=True)
        return inverse * (scaled - jnp.mean(scaled, -1, keepdims=True) - normal * along)

    def backward(c):
        sums[2].third(c).wait_recv()
        grad = both(r.total[2], c)
        inverse = both(r.inverse[1], c)
        normal = (both(r.middle, c) - both(r.mean[1], c)) * inverse
        add(3, grad * normal)
        add(4, grad)
        grad_middle = padded(r.grad_here, c) * live_rows(c)
        grad_middle = grad_middle + back_norm(grad, normal, inverse, vector(4))
        put(r.middle, c, grad_middle)
        add(2, grad_middle * (both(r.total[0], c) + vector(2)))
        grad_branch = (grad_middle * vector(3)).astype(bf16)
        put(r.grad_branch, c, grad_branch)
        add(1, grad_branch.astype(f32))
        put(r.grad_attended, c, dot(grad_branch, out_turned(), 1, 0).astype(bf16))

    def close(work):
        return lambda c: work.close_one(c)

    def cross(work):
        return lambda c: work.cross_one(c)

    stages = [project, cross(sums[0]), close(sums[0]), forward, cross(sums[1]), close(sums[1])]
    stages += [turn, cross(sums[2]), close(sums[2]), backward]

    def weight_grad(j, left, right, at=0):
        value = dot(left[...], right[...], 0, 0).astype(bf16)
        r.grad[j][:, at : at + value.shape[1]] = value

    def send_grads(j):
        for s in range(length - 1, -1, -1):
            scatters[j].start(s)

    slots = [0, 1, 2] + [k + LAG for k in range(3, 6)] + [k + 2 * LAG for k in range(6, 10)]
    for t in range(count + slots[-1]):
        for k in range(len(stages) - 1, -1, -1):
            if 0 <= t - slots[k] < count:
                stages[k](t - slots[k])
        if t == count + slots[6]:
            weight_grad(2, r.grad_result, r.active)
            send_grads(2)
        if t == count + slots[7]:
            weight_grad(1, r.normed[1], r.grad_hidden)
            send_grads(1)

    store = pltpu.make_async_copy(r.out_here, r.layer_out, r.load_sem.at[0])
    store.start()
    weight_grad(0, r.grad_branch, r.attended, 3 * inner)
    steps = list(range(length - 1, -1, -1))
    for h in range(heads):
        part = slice(h * HEAD_DIM, (h + 1) * HEAD_DIM)
        keys = slice(inner + h * HEAD_DIM, inner + (h + 1) * HEAD_DIM)
        values = slice(2 * inner + h * HEAD_DIM, 2 * inner + (h + 1) * HEAD_DIM)
        weights = weights_of(h)
        grad_part = r.grad_attended[:, part]
        r.grad_qkv[:, values] = dot(weights.astype(bf16), grad_part, 0, 0).astype(bf16)
        grad = dot(grad_part, r.qkv[:, values], 1, 1)
        mean = jnp.sum(weights * grad, -1, keepdims=True)
        grad = (weights * (grad - mean)).astype(bf16)
        r.bias[h, :, :rows] = grad
        r.grad_qkv[:, part] = (dot(grad, r.qkv[:, keys], 1, 0) * factor).astype(bf16)
        r.grad_qkv[:, keys] = (dot(grad, r.qkv[:, part], 0, 0) * factor).astype(bf16)
        if h + 1 < length:
            scatters[2].step(steps[h])

    sums[0].drain()
    last = sums[0]
    for c in range(count):
        put(r.part[0], c, dot(both(r.grad_qkv, c), r.whole[0][:, : 3 * inner], 1, 1))
        last.first(c).start()
    weight_grad(0, r.normed[0], r.grad_qkv)
    send_grads(0)

    wide = model // LANES
    at = 1
    r.own_early[...] = jnp.zeros_like(r.own_early)
    r.own_early[0:1] = r.slot[0:1, :]

    def line_to(at, line):
        for c in range(-(-line.shape[1] // LANES)):
            piece = line[:, c * LANES : (c + 1) * LANES]
            r.own_early[at + c : at + c + 1, : piece.shape[1]] = piece

    for line in (
        jnp.sum(r.running[0], 0, keepdims=True),
        jnp.sum(r.grad_qkv[:, :inner].astype(f32), 0, keepdims=True),
        jnp.sum(r.grad_qkv[:, 2 * inner :].astype(f32), 0, keepdims=True),
    ):
        line_to(at, line)
        at += up_to(line.shape[1], LANES) // LANES
    spreads[0].start(lambda peer: r.own_early)

    def to_owners(i, value):
        line = jnp.sum(value, 0, keepdims=True)
        for d in range(peers):
            r.own_late[d, i : i + 1, :depth] = line[:, d * depth : (d + 1) * depth]

    r.own_late[...] = jnp.zeros_like(r.own_late)
    for i in range(1, 7):
        to_owners(i - 1, r.running[i])
    r.table_sums[...] = jnp.zeros_like(r.table_sums)

    def norm_step(here, out_rows):
        grad = r.total[0][here]
        normal = (r.kept[here].astype(f32) - r.mean[0][here]) * r.inverse[0][here]
        back = back_norm(grad, normal, r.inverse[0][here], vector(0))
        value = (r.middle[here] + back).astype(bf16)
        if out_rows is None:
            r.input_grad[here] = value
        else:
            r.input_grad[out_rows] = value[:tail]
        product = (grad * normal).reshape(4, 8, model).sum(0)
        return product, grad.reshape(4, 8, model).sum(0)

    def norm_rows():
        last.arrive()

        def step(i, totals):
            gain, shift = norm_step(pl.ds(pl.multiple_of(i * 32, 32), 32), None)
            return totals[0] + gain, totals[1] + shift

        zero = jnp.zeros((8, model), f32)
        gain, shift = lax.fori_loop(0, body_rows // 32, step, (zero, zero))
        if tail:
            more = norm_step(slice(body_rows, rows), slice(body_rows, slot_rows))
            gain, shift = gain + more[0], shift + more[1]
        to_owners(6, gain)
        to_owners(7, shift)

    def scatter_event(j, s):
        return lambda: scatters[j].step(s)

    order = [(2, s) for s in steps[min(heads, length - 1) :]]
    order += [(j, s) for j in (1, 0) for s in steps]
    places = TABLE_PLACES if length == 4 else [4 * k for k in range(len(order))]
    events = [(at, scatter_event(*item)) for at, item in zip(places, order)]
    events += [(0, last.cross), (CLOSE_PLACE, last.close), (NORM_PLACE, norm_rows)]
    with_events(
        blocks,
        [(at, event) for at, event in events if at < blocks],
        lambda block: table_block(
            heads,
            groups,
            r.index,
            r.bias,
            r.table_sums,
            pl.ds(pl.multiple_of(block * ROW_STEP, ROW_STEP), ROW_STEP),
        ),
    )
    r.own_table[...] = r.table_sums[...].astype(bf16)
    spreads[2].start(lambda peer: r.own_table)
    spreads[1].start(lambda peer: r.own_late.at[peer])
    for at, event in events:
        if at >= blocks:
            event()
    r.all_early[grid.me] = r.own_early[...]
    r.all_late[grid.me] = r.own_late[grid.me]
    r.all_table[grid.me] = r.own_table[...]
    for spread in spreads:
        spread.arrive()
    early = jnp.zeros(r.early_sums.shape, f32)
    late = jnp.zeros(r.late_sums.shape, f32)
    small = jnp.zeros((height, LANES), f32)
    large = jnp.zeros((height, LANES), f32)
    for d in range(peers):
        kind = r.all_early[d, 0:1] > 0.5
        table = r.all_table[d].astype(f32)
        small += jnp.where(kind, 0.0, table)
        large += jnp.where(kind, table, 0.0)
        early += r.all_early[d]
        late += r.all_late[d]
    r.early_sums[...] = early
    r.late_sums[...] = late
    for out, value in ((r.small_sums, small), (r.large_sums, large)):
        entries = out.shape[1]
        for k in range(-(-entries // SPLIT)):
            first, size = k * SPLIT, min(SPLIT, entries - k * SPLIT)
            for h in range(heads):
                at = h * groups + k
                out[h : h + 1, first : first + size] = value[at : at + 1, :size]
    store.wait()
    for work in sums + floods + [lines] + scatters + spreads:
        work.drain()


def layer(arguments, peers, slot_rows):
    model = arguments["inputs"].shape[1]
    rows = up_to(slot_rows, 32)
    columns = up_to(rows, LANES)
    depth = model // peers
    hidden = arguments["fc1_bias"].shape[0]
    inner = arguments["query_bias"].shape[0]
    widths = [4 * inner, hidden, hidden]
    heads = inner // HEAD_DIM
    tables = [arguments["small_table"].shape, arguments["large_table"].shape]
    entries = up_to(max(shape[1] for shape in tables), LANES)
    groups = up_to(-(-entries // SPLIT), 16)
    height = heads * groups
    count = len(cuts_of(rows // 2, CHUNKS))
    length = peers // 2
    array = jax.ShapeDtypeStruct

    def sems(*shape):
        return pltpu.SemaphoreType.DMA(shape)

    def each(kind, shape, times):
        return [pltpu.VMEM(shape, kind) for _ in range(times)]

    outs = dict(
        layer_out=array((slot_rows, model), bf16),
        input_grad=array((slot_rows, model), bf16),
        small_sums=array(tables[0], f32),
        large_sums=array(tables[1], f32),
        early_sums=array((EARLY_LINES, LANES), f32),
        late_sums=array((VECTORS, LANES), f32),
        summed=[array((depth, w), f32) for w in widths],
    )
    blocks = [pltpu.VMEM((length, depth, w), bf16) for w in widths]
    scratch = dict(
        whole=[pltpu.VMEM((model, w), bf16) for w in widths],
        all_lines=pltpu.VMEM((peers * VECTORS, LANES), f32),
        grad=[pltpu.VMEM((model, w), bf16) for w in widths],
        side=blocks,
        up=blocks,
        down=blocks,
        scatter_sems=[[sems(length)] * 6] * 3,
        flood_sems=[[sems(length)] * 6] * 4,
        spread_sems=[[sems(peers)] * 2] * 3,
        part=each(f32, (rows, model), 3),
        total=each(f32, (rows, model), 3),
        near=each(f32, (rows // 2, model), 3),
        sent=each(bf16, (rows // 2, model), 3),
        far=each(bf16, (rows // 2, model), 3),
        sum_send=[sems(3, count)] * 3,
        sum_recv=[sems(3, count)] * 3,
        local_sem=sems(4),
        load_sem=sems(3),
        wide_from=pltpu.VMEM(arguments["large_index"].shape, jnp.int32),
        inputs_here=pltpu.VMEM((slot_rows, model), bf16),
        grad_here=pltpu.VMEM((slot_rows, model), bf16),
        out_here=pltpu.VMEM((slot_rows, model), bf16),
        own_first=pltpu.VMEM((depth, 4 * inner), bf16),
        own_lines=pltpu.VMEM((VECTORS, LANES), f32),
        slot=pltpu.VMEM((2, LANES), f32),
        hidden_shift=pltpu.VMEM((1, hidden), f32),
        index=pltpu.VMEM((rows, columns), jnp.int32),
        wide_index=pltpu.VMEM((rows, columns), jnp.int32),
        table=pltpu.VMEM((8, entries), f32),
        wide_table=pltpu.VMEM((8, entries), f32),
        bias=pltpu.VMEM((heads, rows, columns), bf16),
        vectors=pltpu.VMEM((VECTORS, model), f32),
        qkv_shift=pltpu.VMEM((1, 3 * inner), f32),
        running=pltpu.VMEM((7, 8, max(model, hidden)), f32),
        mean=each(f32, (rows, 1), 2),
        inverse=each(f32, (rows, 1), 2),
        normed=each(bf16, (rows, model), 2),
        kept=pltpu.VMEM((rows, model), bf16),
        grad_result=pltpu.VMEM((rows, model), bf16),
        grad_branch=pltpu.VMEM((rows, model), bf16),
        active=pltpu.VMEM((rows, hidden), bf16),
        grad_hidden=pltpu.VMEM((rows, hidden), bf16),
        qkv=pltpu.VMEM((rows, 3 * inner), bf16),
        grad_qkv=pltpu.VMEM((rows, 3 * inner), bf16),
        attended=pltpu.VMEM((rows, inner), bf16),
        grad_attended=pltpu.VMEM((rows, inner), bf16),
        middle=pltpu.VMEM((rows, model), f32),
        slope=pltpu.VMEM((rows, hidden), f32),
        table_sums=pltpu.VMEM((height, LANES), f32),
        own_table=pltpu.VMEM((height, LANES), bf16),
        all_table=pltpu.VMEM((peers, height, LANES), bf16),
        own_early=pltpu.VMEM((EARLY_LINES, LANES), f32),
        all_early=pltpu.VMEM((peers, EARLY_LINES, LANES), f32),
        own_late=pltpu.VMEM((peers, VECTORS, LANES), f32),
        all_late=pltpu.VMEM((peers, VECTORS, LANES), f32),
    )
    flat = jax.tree.leaves(arguments)
    near, apart = pl.BlockSpec(memory_space=pltpu.VMEM), pl.BlockSpec(memory_space=pl.ANY)
    specs = jax.tree.map(lambda _: near, arguments)
    specs.update(inputs=apart, out_grad=apart, large_index=apart)
    specs.update(slot_kind=pl.BlockSpec(memory_space=pltpu.SMEM))
    out_specs = jax.tree.map(lambda _: near, outs)
    out_specs.update(layer_out=apart)
    shapes, out_tree = jax.tree.flatten(outs)
    tree = jax.tree.structure((arguments, outs, scratch))
    results = pl.pallas_call(
        functools.partial(layer_body, (tree, heads, groups, slot_rows, peers)),
        out_shape=shapes,
        in_specs=jax.tree.leaves(specs),
        out_specs=jax.tree.leaves(out_specs),
        scratch_shapes=jax.tree.leaves(scratch),
        compiler_params=params(collective_id=0, has_side_effects=True),
        name="layer",
    )(*flat)
    return types.SimpleNamespace(**jax.tree.unflatten(out_tree, results))


def finish_body(tree, depth, *refs):
    found, out = (types.SimpleNamespace(**part) for part in jax.tree.unflatten(tree, refs))
    pairs = (
        (found.layer_out, out.layer_out),
        (found.input_grad, out.input_grad),
        (found.summed[1], out.fc1),
        (found.summed[2], out.fc2),
        (found.small_sums, out.small_table),
        (found.large_sums, out.large_table),
    )
    for src, dst in pairs:
        dst[...] = src[...]
    inner = out.query_bias.shape[0]
    for j in range(3):
        out.qkv[j] = found.summed[0][:, j * inner : (j + 1) * inner]
    out.out[...] = found.summed[0][:, 3 * inner :].T
    for i, vector in enumerate(out.vectors):
        vector[...] = found.late_sums[i, :depth]
    at = 1
    for line in (out.fc1_bias, out.query_bias, out.value_bias):
        size = line.shape[0]
        for first in range(0, size, LANES):
            count = min(LANES, size - first)
            line[pl.ds(first, count)] = found.early_sums[at, :count]
            at += 1


def finish(found, depth, inner, hidden):
    array = jax.ShapeDtypeStruct
    found = vars(found)
    outs = dict(
        layer_out=array(found["layer_out"].shape, bf16),
        input_grad=array(found["input_grad"].shape, bf16),
        fc1=array(found["summed"][1].shape, f32),
        fc2=array(found["summed"][2].shape, f32),
        small_table=array(found["small_sums"].shape, f32),
        large_table=array(found["large_sums"].shape, f32),
        qkv=array((3, depth, inner), f32),
        out=array((inner, depth), f32),
        vectors=[array((depth,), f32)] * VECTORS,
        fc1_bias=array((hidden,), f32),
        query_bias=array((inner,), f32),
        value_bias=array((inner,), f32),
    )
    shapes, out_tree = jax.tree.flatten(outs)
    results = pl.pallas_call(
        functools.partial(finish_body, jax.tree.structure((found, outs)), depth),
        out_shape=shapes,
        in_specs=in_vmem(len(jax.tree.leaves(found))),
        out_specs=in_vmem(len(shapes)),
        compiler_params=params(),
        name="finish",
    )(*jax.tree.leaves(found))
    return types.SimpleNamespace(**jax.tree.unflatten(out_tree, results))


def layer_norm(activations, norm_gain, norm_shift):
    center = activations - jnp.mean(activations, -1, keepdims=True)
    inverse = lax.rsqrt(jnp.mean(center * center, -1, keepdims=True) + EPS)
    normal = center * inverse
    return (normal * norm_gain + norm_shift, normal, inverse)


def norm_back(grad_normed, normal, inverse, norm_gain):
    scaled = grad_normed * norm_gain
    return inverse * (
        scaled
        - jnp.mean(scaled, -1, keepdims=True)
        - normal * jnp.mean(scaled * normal, -1, keepdims=True)
    )


def gelu_slope(hidden):
    cumulative = 0.5 * (1.0 + jax.scipy.special.erf(hidden * 0.7071067811865476))
    return cumulative + hidden * jnp.exp(-0.5 * hidden * hidden) * 0.3989422804014327


def pair_map(kind, small_index, large_index, rows, columns):
    def placed(index, at):
        side = index.shape[0]
        return jnp.pad(
            index, ((at, rows - at - side), (at, columns - at - side)), constant_values=-1
        )

    length = small_index.shape[0]
    small = placed(small_index, 0)
    for image in range(1, SLOT_ROWS // length):
        small = jnp.maximum(small, placed(small_index, image * length))
    return jnp.where(kind == 1, placed(large_index, 0), small)


def plain_device(
    images,
    out_grad,
    slot_kind,
    small_index,
    large_index,
    qkv_weight,
    out_weight,
    fc1_weight,
    fc2_weight,
    norm1_gain,
    norm1_shift,
    query_bias,
    value_bias,
    out_bias,
    gamma_attn,
    norm2_gain,
    norm2_shift,
    fc1_bias,
    fc2_bias,
    gamma_mlp,
    small_table,
    large_table,
):
    depth = qkv_weight.shape[0]
    width = query_bias.shape[0]
    hidden_width = fc1_bias.shape[0]
    heads = width // HEAD_DIM
    _, slot_rows, model_width = images.shape
    rows = up_to(slot_rows, 32)
    columns = up_to(rows, LANES)
    kind = slot_kind[0]

    block = jnp.concatenate(
        (
            qkv_weight.reshape(depth, 3 * width),
            fc1_weight,
            out_weight.T,
            fc2_weight.T,
        ),
        1,
    )
    whole = lax.all_gather(block, "dp", axis=0, tiled=True)
    cuts = (3 * width, 3 * width + hidden_width, 4 * width + hidden_width)
    qkv_matrix = whole[:, : cuts[0]]
    fc1_matrix = whole[:, cuts[0] : cuts[1]]
    out_turned = whole[:, cuts[1] : cuts[2]]
    fc2_turned = whole[:, cuts[2] :]
    small_vectors = jnp.stack(
        (norm1_gain, norm1_shift, out_bias, gamma_attn, norm2_gain, norm2_shift, fc2_bias, gamma_mlp)
    )
    vectors = lax.all_gather(small_vectors, "dp", axis=0)
    vectors = jnp.moveaxis(vectors, 0, 1).reshape(8, model_width).astype(f32)

    query_shift = query_bias.astype(f32)
    value_shift = value_bias.astype(f32)
    hidden_shift = fc1_bias.astype(f32)
    small_entries, large_entries = small_table.shape[0], large_table.shape[0]
    entries = up_to(max(small_entries, large_entries), LANES)
    table = jnp.where(
        kind == 1,
        jnp.pad(large_table, ((0, entries - large_entries), (0, 0))),
        jnp.pad(small_table, ((0, entries - small_entries), (0, 0))),
    )
    table = table.T.astype(f32)
    pair_index = pair_map(kind, small_index, large_index, rows, columns)
    bias = gather_bias(pair_index, table)

    positions = jnp.arange(rows)
    live_count = jnp.where(kind == 1, LARGE_LEN, slot_rows)
    live_rows = (positions < live_count).astype(f32).reshape(-1, 1)
    inputs = jnp.pad(images[0], ((0, rows - slot_rows), (0, 0))).astype(f32)
    normed_one, normal_one, inverse_one = layer_norm(inputs, vectors[0], vectors[1])
    normed_one = normed_one.astype(bf16)
    projected = dot(normed_one, qkv_matrix, 1, 0)
    queries = (projected[:, :width] + query_shift).astype(bf16)
    keys = projected[:, width : 2 * width].astype(bf16)
    values = (projected[:, 2 * width :] + value_shift).astype(bf16)
    pieces = attend_forward(queries, keys, values, bias)
    branch_part = dot(pieces, out_turned, 1, 1)
    branch = lax.psum(branch_part, "shard") + vectors[2]
    middle = inputs + vectors[3] * branch
    normed_two, normal_two, inverse_two = layer_norm(middle, vectors[4], vectors[5])
    normed_two = normed_two.astype(bf16)
    hidden = dot(normed_two, fc1_matrix, 1, 0) + hidden_shift
    active = jax.nn.gelu(hidden, approximate=False).astype(bf16)
    result_part = dot(active, fc2_turned, 1, 1)
    result = lax.psum(result_part.astype(bf16), "shard").astype(f32) + vectors[6]
    layer_out = ((middle + vectors[7] * result) * live_rows).astype(bf16)[:slot_rows][None]

    grad_out = jnp.pad(out_grad[0], ((0, rows - slot_rows), (0, 0))).astype(f32) * live_rows
    grad_gamma_mlp = jnp.sum(grad_out * result, 0)
    grad_result = (grad_out * vectors[7]).astype(bf16)
    grad_fc2_bias = jnp.sum(grad_result.astype(f32), 0)
    grad_fc2_turned = dot(grad_result, active, 0, 0)
    grad_active = dot(grad_result, fc2_turned, 1, 0)
    grad_hidden = (grad_active * gelu_slope(hidden)).astype(bf16)
    grad_fc1_bias = jnp.sum(grad_hidden.astype(f32), 0)
    grad_fc1 = dot(normed_two, grad_hidden, 0, 0)
    grad_normed_two = lax.psum(dot(grad_hidden, fc1_matrix, 1, 1), "shard")
    grad_norm2_gain = jnp.sum(grad_normed_two * normal_two, 0)
    grad_norm2_shift = jnp.sum(grad_normed_two, 0)
    grad_middle = grad_out + norm_back(grad_normed_two, normal_two, inverse_two, vectors[4])
    grad_gamma_attn = jnp.sum(grad_middle * branch, 0)
    grad_branch = (grad_middle * vectors[3]).astype(bf16)
    grad_out_bias = jnp.sum(grad_branch.astype(f32), 0)
    grad_out_turned = dot(grad_branch, pieces, 0, 0)
    grad_attended = dot(grad_branch, out_turned, 1, 0).astype(bf16)
    grad_queries, grad_keys, grad_values, grad_scores = attend_backward(
        queries, keys, values, bias, grad_attended
    )
    sums = table_sums(pair_index, grad_scores, entries)
    grad_projected = jnp.concatenate((grad_queries, grad_keys, grad_values), 1)
    grad_qkv = dot(normed_one, grad_projected, 0, 0)
    grad_query_bias = jnp.sum(grad_queries.astype(f32), 0)
    grad_value_bias = jnp.sum(grad_values.astype(f32), 0)
    grad_normed_one = lax.psum(dot(grad_projected, qkv_matrix, 1, 1), "shard")
    grad_norm1_gain = jnp.sum(grad_normed_one * normal_one, 0)
    grad_norm1_shift = jnp.sum(grad_normed_one, 0)
    input_grad = grad_middle + norm_back(grad_normed_one, normal_one, inverse_one, vectors[0])
    input_grad = input_grad.astype(bf16)[:slot_rows][None]

    small_sums = jnp.where(kind == 1, 0.0, sums[:, :small_entries])
    large_sums = jnp.where(kind == 1, sums[:, :large_entries], 0.0)
    local_sums = lax.psum(
        (small_sums, large_sums, grad_query_bias, grad_value_bias, grad_fc1_bias), "dp"
    )
    peers = lax.axis_size("dp")

    def sent_and_summed(value):
        parts = value.astype(bf16).reshape(peers, value.shape[0] // peers, -1)
        arrived = lax.all_to_all(parts, "dp", split_axis=0, concat_axis=0, tiled=True)
        return arrived.astype(f32).sum(axis=0)

    grad_block = sent_and_summed(
        jnp.concatenate((grad_qkv, grad_fc1, grad_out_turned, grad_fc2_turned), 1)
    )
    vector_grads = sent_and_summed(
        jnp.stack(
            (
                grad_norm1_gain,
                grad_norm1_shift,
                grad_out_bias,
                grad_gamma_attn,
                grad_norm2_gain,
                grad_norm2_shift,
                grad_fc2_bias,
                grad_gamma_mlp,
            ),
            1,
        )
    )
    return (
        layer_out,
        input_grad,
        grad_block[:, : cuts[0]].reshape(depth, 3, width),
        grad_block[:, cuts[1] : cuts[2]].T,
        grad_block[:, cuts[0] : cuts[1]],
        grad_block[:, cuts[2] :].T,
        vector_grads[:, 0],
        vector_grads[:, 1],
        local_sums[2],
        local_sums[3],
        vector_grads[:, 2],
        vector_grads[:, 3],
        vector_grads[:, 4],
        vector_grads[:, 5],
        local_sums[4],
        vector_grads[:, 6],
        vector_grads[:, 7],
        local_sums[0].T,
        local_sums[1].T,
    )


def on_device(*arguments):
    depth = arguments[5].shape[0]
    if depth % 16 or lax.axis_size("shard") != 4:
        return plain_device(*arguments)
    return whole_device(*arguments)


def whole_device(
    images,
    out_grad,
    slot_kind,
    small_index,
    large_index,
    qkv_weight,
    out_weight,
    fc1_weight,
    fc2_weight,
    norm1_gain,
    norm1_shift,
    query_bias,
    value_bias,
    out_bias,
    gamma_attn,
    norm2_gain,
    norm2_shift,
    fc1_bias,
    fc2_bias,
    gamma_mlp,
    small_table,
    large_table,
):
    depth = qkv_weight.shape[0]
    found = layer(
        dict(
            inputs=images[0],
            out_grad=out_grad[0],
            slot_kind=slot_kind,
            small_index=small_index,
            large_index=large_index,
            small_table=small_table.T,
            large_table=large_table.T,
            qkv_weight=qkv_weight.transpose(1, 0, 2),
            out_weight=out_weight,
            fc1_weight=fc1_weight,
            fc2_weight=fc2_weight.T,
            small_vectors=[
                norm1_gain,
                norm1_shift,
                out_bias,
                gamma_attn,
                norm2_gain,
                norm2_shift,
                fc2_bias,
                gamma_mlp,
            ],
            query_bias=query_bias,
            value_bias=value_bias,
            fc1_bias=fc1_bias,
        ),
        lax.axis_size("dp"),
        images.shape[1],
    )
    out = finish(found, depth, query_bias.shape[0], fc1_bias.shape[0])
    return (
        out.layer_out[None],
        out.input_grad[None],
        out.qkv.transpose(1, 0, 2),
        out.out,
        out.fc1,
        out.fc2.T,
        out.vectors[6],
        out.vectors[7],
        out.query_bias,
        out.value_bias,
        out.vectors[0],
        out.vectors[1],
        out.vectors[2],
        out.vectors[3],
        out.fc1_bias,
        out.vectors[4],
        out.vectors[5],
        out.small_table.T,
        out.large_table.T,
    )


def solution(mesh):
    return jax.shard_map(
        on_device,
        mesh=mesh,
        in_specs=(
            P("dp", None, None),
            P("dp", None, None),
            P("dp"),
            P(),
            P(),
            P("dp", None, "shard"),
            P("shard", "dp"),
            P("dp", "shard"),
            P("shard", "dp"),
            P("dp"),
            P("dp"),
            P("shard"),
            P("shard"),
            P("dp"),
            P("dp"),
            P("dp"),
            P("dp"),
            P("shard"),
            P("dp"),
            P("dp"),
            P(None, "shard"),
            P(None, "shard"),
        ),
        out_specs=(
            P("dp", None, None),
            P("dp", None, None),
            P("dp", None, "shard"),
            P("shard", "dp"),
            P("dp", "shard"),
            P("shard", "dp"),
            P("dp"),
            P("dp"),
            P("shard"),
            P("shard"),
            P("dp"),
            P("dp"),
            P("dp"),
            P("dp"),
            P("shard"),
            P("dp"),
            P("dp"),
            P(None, "shard"),
            P(None, "shard"),
        ),
        check_vma=False,
    )
```

```python
import functools
import types

import jax
import jax.numpy as jnp
from jax import lax
from jax.experimental import pallas as pl
from jax.experimental.pallas import tpu as pltpu
from jax.sharding import PartitionSpec as P

HEAD_DIM = 64
SMALL_LEN = 197
LARGE_LEN = 577
SLOT_ROWS = 591
EPS = 1e-06
NEG = -1e30
LANES = 128
SPLIT = 80
VMEM_LIMIT = 60 << 20

MESH = pl.DeviceIdType.MESH

f32 = jnp.float32
bf16 = jnp.bfloat16


def up_to(value, unit):
    return -(-value // unit) * unit


def in_vmem(count):
    return [pl.BlockSpec(memory_space=pltpu.VMEM)] * count


def params(**more):
    return pltpu.CompilerParams(vmem_limit_bytes=VMEM_LIMIT, **more)


def dot(a, b, da, db):
    return lax.dot_general(a, b, (((da,), (db,)), ((), ())), preferred_element_type=f32)


def bias_block_of(heads, index_ref, table_ref, out_ref, here):
    columns, entries = index_ref.shape[1], table_ref.shape[1]
    for c in range(columns // LANES):
        there = pl.ds(c * LANES, LANES)
        index = index_ref[here, there]
        high = lax.shift_right_arithmetic(index, 7)
        low = lax.bitwise_and(index, LANES - 1)
        found = [jnp.full(index.shape, NEG, f32) for _ in range(heads)]
        for k in range(entries // LANES):
            match = high == k
            for h in range(heads):
                line = table_ref[h : h + 1, k * LANES : (k + 1) * LANES]
                values = jnp.take_along_axis(jnp.broadcast_to(line, index.shape), low, axis=1)
                found[h] = jnp.where(match, values, found[h])
        for h in range(heads):
            out_ref[h, here, there] = found[h].astype(bf16)


def table_block(heads, groups, index_ref, grad_ref, out_ref, here):
    columns = index_ref.shape[1]
    inverse = -(-(1 << 22) // SPLIT)
    index = index_ref[here, :]
    high = lax.shift_right_arithmetic(index * inverse, 22)
    low = (index - high * SPLIT).astype(jnp.int16)
    high = high.astype(jnp.int16)
    grads = [grad_ref[h, here, :] for h in range(heads)]
    places_low = lax.broadcasted_iota(jnp.int16, (SPLIT, columns), 0)
    places_high = lax.broadcasted_iota(jnp.int16, (groups, columns), 0)
    one, zero = jnp.ones((), bf16), jnp.zeros((), bf16)
    total = jnp.zeros((heads * groups, SPLIT), f32)
    for pair in range(0, 16, 2):
        lows, highs = [], []
        for i in (pair, pair + 1):
            lows.append(
                jnp.where(
                    places_low == jnp.broadcast_to(low[i : i + 1], (SPLIT, columns)), one, zero
                )
            )
            match = places_high == jnp.broadcast_to(high[i : i + 1], (groups, columns))
            highs.append(
                jnp.concatenate(
                    [
                        jnp.where(
                            match,
                            jnp.broadcast_to(grads[h][i : i + 1], (groups, columns)),
                            zero,
                        )
                        for h in range(heads)
                    ],
                    0,
                )
            )
        total = total + dot(jnp.concatenate(highs, 1), jnp.concatenate(lows, 1), 1, 1)
    out_ref[: heads * groups, :SPLIT] += total


def forward_body(heads, q_ref, k_ref, v_ref, bias_ref, out_ref):
    rows = q_ref.shape[0]
    for h in range(heads):
        part = slice(h * HEAD_DIM, (h + 1) * HEAD_DIM)
        scores = dot(q_ref[:, part], k_ref[:, part], 1, 1) * HEAD_DIM ** (-0.5)
        scores = scores + bias_ref[h, :, :rows].astype(f32)
        weights = jnp.exp(scores - jnp.max(scores, -1, keepdims=True))
        weights = weights / jnp.sum(weights, -1, keepdims=True)
        out_ref[:, part] = dot(weights.astype(bf16), v_ref[:, part], 1, 0).astype(bf16)


def backward_body(
    heads, q_ref, k_ref, v_ref, bias_ref, grad_ref, dq_ref, dk_ref, dv_ref, ds_ref
):
    rows = q_ref.shape[0]
    factor = HEAD_DIM ** (-0.5)
    for h in range(heads):
        part = slice(h * HEAD_DIM, (h + 1) * HEAD_DIM)
        scores = dot(q_ref[:, part], k_ref[:, part], 1, 1) * factor
        scores = scores + bias_ref[h, :, :rows].astype(f32)
        weights = jnp.exp(scores - jnp.max(scores, -1, keepdims=True))
        weights = weights / jnp.sum(weights, -1, keepdims=True)
        dv_ref[:, part] = dot(weights.astype(bf16), grad_ref[:, part], 0, 0).astype(bf16)
        grad = dot(grad_ref[:, part], v_ref[:, part], 1, 1)
        mean = jnp.sum(weights * grad, -1, keepdims=True)
        grad = (weights * (grad - mean)).astype(bf16)
        ds_ref[h, :, :rows] = grad
        dq_ref[:, part] = (dot(grad, k_ref[:, part], 1, 0) * factor).astype(bf16)
        dk_ref[:, part] = (dot(grad, q_ref[:, part], 0, 0) * factor).astype(bf16)


def attend_forward(queries, keys, values, bias):
    heads = bias.shape[0]
    return pl.pallas_call(
        functools.partial(forward_body, heads),
        out_shape=jax.ShapeDtypeStruct(queries.shape, bf16),
        in_specs=in_vmem(4),
        out_specs=in_vmem(1)[0],
        compiler_params=params(),
        cost_estimate=pl.CostEstimate(flops=10**9, bytes_accessed=10**7, transcendentals=10**6),
        name="attend_forward",
    )(queries, keys, values, bias)


def attend_backward(queries, keys, values, bias, grad):
    heads = bias.shape[0]
    rows = jax.ShapeDtypeStruct(queries.shape, bf16)
    return pl.pallas_call(
        functools.partial(backward_body, heads),
        out_shape=(rows, rows, rows, jax.ShapeDtypeStruct(bias.shape, bf16)),
        in_specs=in_vmem(5),
        out_specs=tuple(in_vmem(4)),
        compiler_params=params(),
        cost_estimate=pl.CostEstimate(flops=2 * 10**9, bytes_accessed=2 * 10**7, transcendentals=10**6),
        name="attend_backward",
    )(queries, keys, values, bias, grad)


def bias_body(heads, index_ref, table_ref, out_ref):
    def work(block):
        here = pl.ds(pl.multiple_of(block * ROW_STEP, ROW_STEP), ROW_STEP)
        bias_block_of(heads, index_ref, table_ref, out_ref, here)

    with_events(index_ref.shape[0] // ROW_STEP, [], work)


def gather_bias(pair_index, table):
    heads, entries = table.shape
    return pl.pallas_call(
        functools.partial(bias_body, heads),
        out_shape=jax.ShapeDtypeStruct((heads,) + pair_index.shape, bf16),
        in_specs=in_vmem(2),
        out_specs=in_vmem(1)[0],
        compiler_params=params(),
        cost_estimate=pl.CostEstimate(flops=10**9, bytes_accessed=4 * 10**7, transcendentals=0),
        name="bias",
    )(pair_index, table)


def table_body(heads, groups, index_ref, grad_ref, out_ref):
    out_ref[...] = jnp.zeros_like(out_ref)

    def work(block):
        here = pl.ds(pl.multiple_of(block * ROW_STEP, ROW_STEP), ROW_STEP)
        table_block(heads, groups, index_ref, grad_ref, out_ref, here)

    with_events(index_ref.shape[0] // ROW_STEP, [], work)


def table_sums(pair_index, grad_scores, entries):
    heads = grad_scores.shape[0]
    groups = up_to(-(-entries // SPLIT), 16)
    sums = pl.pallas_call(
        functools.partial(table_body, heads, groups),
        out_shape=jax.ShapeDtypeStruct((heads * groups, SPLIT), f32),
        in_specs=in_vmem(2),
        out_specs=in_vmem(1)[0],
        compiler_params=params(),
        cost_estimate=pl.CostEstimate(flops=2 * 10**9, bytes_accessed=6 * 10**7, transcendentals=0),
        name="table_sums",
    )(pair_index, grad_scores)
    return sums.reshape(heads, groups * SPLIT)


def cuts_of(total, pieces, unit=16):
    count, extra = divmod(total // unit, pieces)
    cuts, at = [], 0
    for i in range(pieces):
        size = (count + (i < extra)) * unit
        if size:
            cuts.append((at, size))
        at += size
    return cuts


def remote(src, dst, send_sem, recv_sem, axis, peer):
    return pltpu.make_async_remote_copy(
        src_ref=src,
        dst_ref=dst,
        send_sem=send_sem,
        recv_sem=recv_sem,
        device_id={axis: peer},
        device_id_type=MESH,
    )


def greet(barrier, axis, peer):
    pl.semaphore_signal(barrier, inc=1, device_id={axis: peer}, device_id_type=MESH)


class ShardSum:
    def __init__(self, chunks, part_ref, out_ref, near, sent, far, send_sem, recv_sem):
        me = lax.axis_index("shard")
        outer, self.inner = me // 2, lax.rem(me, 2)
        self.near_peer = outer * 2 + (1 - self.inner)
        self.far_peer = (1 - outer) * 2 + self.inner
        self.chunks, self.part, self.out = chunks, part_ref, out_ref
        self.near, self.sent, self.far = near, sent, far
        self.sems = (send_sem, recv_sem)
        self.half = near.shape[0]

    def greet(self, barrier):
        greet(barrier, "shard", self.near_peer)
        greet(barrier, "shard", self.far_peer)
        return 2

    def rows(self, which, at, size):
        return pl.ds(pl.multiple_of(which * self.half + at, 16), size)

    def copy(self, stage, j, src, dst, peer):
        send_sem, recv_sem = self.sems
        return remote(src, dst, send_sem.at[stage, j], recv_sem.at[stage, j], "shard", peer)

    def first(self, j):
        at, size = self.chunks[j]
        return self.copy(
            0, j, self.part.at[self.rows(1 - self.inner, at, size)], self.near.at[pl.ds(at, size)], self.near_peer
        )

    def second(self, j):
        here = pl.ds(*self.chunks[j])
        return self.copy(1, j, self.sent.at[here], self.far.at[here], self.far_peer)

    def third(self, j):
        mine = self.out.at[self.rows(self.inner, *self.chunks[j])]
        return self.copy(2, j, mine, mine, self.near_peer)

    def start(self):
        for j in range(len(self.chunks)):
            self.first(j).start()

    def cross_one(self, j):
        at, size = self.chunks[j]
        self.first(j).wait_recv()
        here = pl.ds(at, size)
        mine = self.rows(self.inner, at, size)
        self.sent[here] = (self.part[mine] + self.near[here]).astype(bf16)
        self.second(j).start()

    def cross(self):
        for j in range(len(self.chunks)):
            self.cross_one(j)

    def close_one(self, j):
        at, size = self.chunks[j]
        self.second(j).wait_recv()
        here = pl.ds(at, size)
        mine = self.rows(self.inner, at, size)
        self.out[mine] = self.sent[here].astype(f32) + self.far[here].astype(f32)
        self.third(j).start()

    def close(self):
        for j in range(len(self.chunks)):
            self.close_one(j)

    def arrive(self):
        for j in range(len(self.chunks)):
            self.third(j).wait_recv()

    def drain(self):
        for j in range(len(self.chunks)):
            self.first(j).wait_send()
            self.second(j).wait_send()
            self.third(j).wait_send()


class Grid:
    def __init__(self, peers):
        self.length = peers // 2
        self.me = lax.axis_index("dp")
        self.at, self.side = self.me // 2, lax.rem(self.me, 2)
        self.up, self.down = self.me + 2, self.me - 2
        self.across = self.at * 2 + 1 - self.side
        self.has_up, self.has_down = self.at < self.length - 1, self.at > 0

    def greet(self, barrier):
        greet(barrier, "dp", self.across)

        @pl.when(self.has_up)
        def _():
            greet(barrier, "dp", self.up)

        @pl.when(self.has_down)
        def _():
            greet(barrier, "dp", self.down)

        return 1 + self.has_up.astype(jnp.int32) + self.has_down.astype(jnp.int32)

    def clip(self, place):
        return jnp.clip(place, 0, self.length - 1)


class Flood:
    def __init__(self, grid, own, out, up_send, up_recv, down_send, down_recv, side_send, side_recv):
        self.grid, self.own, self.out = grid, own, out
        self.up_sems, self.down_sems = (up_send, up_recv), (down_send, down_recv)
        self.side_sems = (side_send, side_recv)

    def at(self, device):
        depth = self.own.shape[0]
        return self.out.at[pl.ds(pl.multiple_of(device * depth, 8), depth)]

    def block(self, place):
        return self.at(self.grid.clip(place) * 2 + self.grid.side)

    def up(self, s):
        grid, (send, recv) = self.grid, self.up_sems
        block = self.block(grid.at - s)
        return remote(self.own if s == 0 else block, block, send.at[s], recv.at[s], "dp", grid.up)

    def down(self, s):
        grid, (send, recv) = self.grid, self.down_sems
        block = self.block(grid.at + s)
        return remote(self.own if s == 0 else block, block, send.at[s], recv.at[s], "dp", grid.down)

    def across(self, place, own=False):
        grid, (send, recv) = self.grid, self.side_sems
        place = grid.clip(place)
        block = self.block(place)
        return remote(
            self.own if own else block, block, send.at[place], recv.at[place], "dp", grid.across
        )

    def step(self, s):
        grid = self.grid
        if s == 0:

            @pl.when(grid.has_up)
            def _():
                self.up(0).start()

            @pl.when(grid.has_down)
            def _():
                self.down(0).start()

            self.across(grid.at, own=True).start()
            return

        @pl.when(grid.at - s >= 0)
        def _():
            block = self.block(grid.at - s)
            send, recv = self.up_sems
            remote(block, block, send.at[s - 1], recv.at[s - 1], "dp", grid.down).wait_recv()

            @pl.when(grid.has_up)
            def _():
                self.up(s).start()

            self.across(grid.at - s).start()

        @pl.when(grid.at + s < grid.length)
        def _():
            block = self.block(grid.at + s)
            send, recv = self.down_sems
            remote(block, block, send.at[s - 1], recv.at[s - 1], "dp", grid.up).wait_recv()

            @pl.when(grid.has_down)
            def _():
                self.down(s).start()

            self.across(grid.at + s).start()

    def arrive(self):
        grid, (send, recv) = self.grid, self.side_sems
        for place in range(grid.length):
            block = self.at(place * 2 + 1 - grid.side)
            remote(block, block, send.at[place], recv.at[place], "dp", grid.across).wait_recv()

    def drain(self):
        grid = self.grid
        for place in range(grid.length):
            self.across(place).wait_send()
        for s in range(grid.length - 1):

            @pl.when(jnp.logical_and(grid.at - s >= 0, grid.has_up))
            def _():
                self.up(s).wait_send()

            @pl.when(jnp.logical_and(grid.at + s < grid.length, grid.has_down))
            def _():
                self.down(s).wait_send()


SIDE, UP, DOWN = range(3)


class ReduceScatter:
    def __init__(self, grid, grads, out, side, up, down, sems):
        self.grid, self.grads, self.out = grid, grads, out
        self.buffers = (side, up, down)
        self.sems = (sems[:2], sems[2:4], sems[4:6])

    def at(self, device):
        depth = self.out.shape[0]
        return pl.ds(pl.multiple_of(device * depth, 16), depth)

    def prepare(self):
        grid = self.grid

        @pl.when(jnp.logical_not(grid.has_down))
        def _():
            self.buffers[UP][...] = jnp.zeros_like(self.buffers[UP])

        @pl.when(jnp.logical_not(grid.has_up))
        def _():
            self.buffers[DOWN][...] = jnp.zeros_like(self.buffers[DOWN])

    def copy(self, way, place, peer, src=None):
        send, recv = self.sems[way]
        place = self.grid.clip(place)
        dst = self.buffers[way].at[place]
        return remote(dst if src is None else src, dst, send.at[place], recv.at[place], "dp", peer)

    def cross(self, place):
        grid = self.grid
        src = self.grads.at[self.at(grid.clip(place) * 2 + 1 - grid.side)]
        return self.copy(SIDE, place, grid.across, src)

    def start(self, s):
        grid = self.grid

        @pl.when(grid.at + s < grid.length)
        def _():
            self.cross(grid.at + s).start()

        if s:

            @pl.when(grid.at - s >= 0)
            def _():
                self.cross(grid.at - s).start()

    def step(self, s):
        grid = self.grid
        side, up, down = self.buffers
        if s == 0:
            place = grid.at
            self.copy(SIDE, place, grid.across).wait_recv()

            @pl.when(grid.has_down)
            def _():
                self.copy(UP, place, grid.down).wait_recv()

            @pl.when(grid.has_up)
            def _():
                self.copy(DOWN, place, grid.up).wait_recv()

            total = self.grads[self.at(grid.me)].astype(f32) + side[place].astype(f32)
            self.out[...] = total + (up[place].astype(f32) + down[place].astype(f32))
            return

        @pl.when(grid.at + s < grid.length)
        def _():
            place = grid.clip(grid.at + s)
            self.copy(SIDE, place, grid.across).wait_recv()

            @pl.when(grid.has_down)
            def _():
                self.copy(UP, place, grid.down).wait_recv()

            total = self.grads[self.at(place * 2 + grid.side)].astype(f32) + side[place].astype(f32)
            side[place] = (total + up[place].astype(f32)).astype(bf16)
            self.copy(UP, place, grid.up, side.at[place]).start()

        @pl.when(grid.at - s >= 0)
        def _():
            place = grid.clip(grid.at - s)
            self.copy(SIDE, place, grid.across).wait_recv()

            @pl.when(grid.has_up)
            def _():
                self.copy(DOWN, place, grid.up).wait_recv()

            total = self.grads[self.at(place * 2 + grid.side)].astype(f32) + side[place].astype(f32)
            side[place] = (total + down[place].astype(f32)).astype(bf16)
            self.copy(DOWN, place, grid.down, side.at[place]).start()

    def drain(self):
        grid = self.grid
        for place in range(grid.length):
            self.cross(place).wait_send()
        for s in range(1, grid.length):

            @pl.when(grid.at + s < grid.length)
            def _():
                self.copy(UP, grid.at + s, grid.up).wait_send()

            @pl.when(grid.at - s >= 0)
            def _():
                self.copy(DOWN, grid.at - s, grid.down).wait_send()


ROW_STEP = 16
CHUNKS = 5
VECTORS = 8
EARLY_LINES = 16
BIAS_PLACES = [5, 11, 17, 11, 19, 25, 32, 20, 28, 36, 99]
TABLE_PLACES = [1, 3, 10, 15, 20, 24, 30, 36, 99]
FIRST_CLOSE = 2
RESULT_PLACE = 7
CLOSE_PLACE = 22
NORM_PLACE = 27


def with_events(blocks, events, work):
    def step(block, carry):
        for at, event in events:
            pl.when(block == at)(event)

        @pl.when(block < blocks)
        def _():
            work(block)

        return carry

    lax.fori_loop(0, max([blocks] + [at + 1 for at, _ in events]), step, 0)


class Spread:
    def __init__(self, peers, out, send_sem, recv_sem):
        self.peers, self.out, self.sems = peers, out, (send_sem, recv_sem)
        self.me = lax.axis_index("dp")

    def peer(self, i):
        return lax.rem(self.me + i, self.peers)

    def copy(self, src, slot, peer):
        send_sem, recv_sem = self.sems
        return remote(
            src, self.out.at[slot], send_sem.at[peer], recv_sem.at[slot], "dp", peer
        )

    def start(self, src_for):
        for i in range(1, self.peers):
            self.copy(src_for(self.peer(i)), self.me, self.peer(i)).start()

    def arrive(self):
        for i in range(1, self.peers):
            peer = self.peer(i)
            self.copy(self.out.at[peer], peer, peer).wait_recv()

    def drain(self):
        for i in range(1, self.peers):
            peer = self.peer(i)
            self.copy(self.out.at[peer], peer, peer).wait_send()


def layer_body(plan, *refs):
    tree, heads, groups, slot_rows, peers = plan
    named = {}
    for part in jax.tree.unflatten(tree, refs):
        named.update(part)
    r = types.SimpleNamespace(**named)
    rows, columns = r.index.shape
    model = r.inputs.shape[1]
    depth = model // peers
    inner = heads * HEAD_DIM
    half = rows // 2
    chunks = cuts_of(half, CHUNKS)
    count = len(chunks)
    factor = HEAD_DIM ** (-0.5)
    height = heads * groups

    grid = Grid(peers)
    sums = [
        ShardSum(chunks, *buffers)
        for buffers in zip(r.part, r.total, r.near, r.sent, r.far, r.sum_send, r.sum_recv)
    ]
    lines = Flood(grid, r.own_lines, r.all_lines, *r.flood_sems[3])
    floods = [
        Flood(grid, own, out, *sems) for own, out, sems in zip((r.own_first, r.fc1_weight, r.fc2_weight), r.whole, r.flood_sems)
    ]
    scatters = [
        ReduceScatter(grid, *buffers)
        for buffers in zip(r.grad, r.summed, r.side, r.up, r.down, r.scatter_sems)
    ]
    spreads = [
        Spread(peers, out, *sems)
        for out, sems in zip((r.all_early, r.all_late, r.all_table), r.spread_sems)
    ]

    loads = [
        pltpu.make_async_copy(src, dst, r.load_sem.at[j])
        for j, (src, dst) in enumerate(
            ((r.large_index, r.wide_from), (r.inputs, r.inputs_here), (r.out_grad, r.grad_here))
        )
    ]
    for load in loads:
        load.start()
    for i, member in enumerate(r.small_vectors):
        r.own_lines[i : i + 1, :depth] = member[...].astype(f32).reshape(1, depth)
    for j in range(3):
        r.own_first[:, j * inner : (j + 1) * inner] = r.qkv_weight[j]
    r.own_first[:, 3 * inner :] = r.out_weight[...].T
    barrier = pltpu.get_barrier_semaphore()
    met = sums[0].greet(barrier)
    for i in range(1, peers):
        greet(barrier, "dp", lax.rem(grid.me + i, peers))
    pl.semaphore_wait(barrier, met + peers - 1)
    lines.step(0)
    floods[0].step(0)
    copies = [
        pltpu.make_async_copy(flood.own, flood.at(grid.me), r.local_sem.at[j])
        for j, flood in enumerate(floods + [lines])
    ]
    for copy in copies:
        copy.start()
    for scatter in scatters:
        scatter.prepare()

    kind = r.slot_kind[0]
    r.slot[0:1] = jnp.full((1, LANES), kind.astype(f32))
    r.slot[1:2] = jnp.full((1, LANES), (slot_rows - kind * (slot_rows - LARGE_LEN)).astype(f32))
    is_large = jnp.broadcast_to(r.slot[0:1, :], (8, LANES)) > 0.5
    small_side, large_side = r.small_index.shape[0], r.large_index.shape[0]
    r.index[...] = jnp.full((rows, columns), -1, jnp.int32)
    for image in range(slot_rows // small_side):
        at = image * small_side
        r.index[at : at + small_side, at : at + small_side] = r.small_index[...]
    r.wide_index[...] = jnp.full((rows, columns), -1, jnp.int32)
    for load in loads:
        load.wait()
    r.wide_index[:large_side, :large_side] = r.wide_from[...]
    r.table[...] = jnp.zeros_like(r.table)
    entries_small, entries_large = r.small_table.shape[1], r.large_table.shape[1]
    r.table[:heads, :entries_small] = r.small_table[...].astype(f32)
    r.wide_table[...] = jnp.zeros_like(r.wide_table)
    r.wide_table[:heads, :entries_large] = r.large_table[...].astype(f32)
    tall = jnp.broadcast_to(is_large[:, 0:1], r.table.shape)
    r.table[...] = jnp.where(tall, r.wide_table[...], r.table[...])
    large_block = jnp.broadcast_to(r.slot[0:1, 0:1], (ROW_STEP, columns)) > 0.5

    body_rows = slot_rows // 32 * 32
    tail = slot_rows - body_rows
    r.kept[:body_rows] = r.inputs_here[:body_rows]
    r.kept[body_rows:] = jnp.concatenate(
        (
            r.inputs_here[body_rows:slot_rows].astype(f32),
            jnp.zeros((rows - slot_rows, model), f32),
        ),
        0,
    ).astype(bf16)
    blocks = up_to(slot_rows, ROW_STEP) // ROW_STEP

    def bias_block(block):
        here = pl.ds(pl.multiple_of(block * ROW_STEP, ROW_STEP), ROW_STEP)
        r.index[here] = jnp.where(large_block, r.wide_index[here], r.index[here])
        bias_block_of(heads, r.index, r.table, r.bias, here)

    r.index[blocks * ROW_STEP :] = jnp.full((rows - blocks * ROW_STEP, columns), -1, jnp.int32)
    r.bias[:, blocks * ROW_STEP :] = jnp.full(
        (heads, rows - blocks * ROW_STEP, columns), NEG, bf16
    )
    length = grid.length

    def flood_event(j, s):
        return lambda: floods[j].step(s)

    order = [(0, s) for s in range(1, length)] + [(j, s) for j in (1, 2) for s in range(length)]
    places = BIAS_PLACES if length == 4 else [k * 3 for k in range(len(order))]
    events = [(at, flood_event(*item)) for at, item in zip(places, order)]
    events += [(3 * s, functools.partial(lines.step, s)) for s in range(1, length)]
    late_floods = [event for at, event in events if at >= blocks]
    with_events(blocks, [(at, event) for at, event in events if at < blocks], bias_block)
    for copy in copies:
        copy.wait()
    lines.arrive()
    floods[0].arrive()
    for d in range(peers):
        r.vectors[:, d * depth : (d + 1) * depth] = r.all_lines[
            d * VECTORS : (d + 1) * VECTORS, :depth
        ]

    def vector(i):
        return r.vectors[i : i + 1, :]

    def moments(value):
        mean = jnp.mean(value, -1, keepdims=True)
        center = value - mean
        inverse = lax.rsqrt(jnp.mean(center * center, -1, keepdims=True) + EPS)
        return center * inverse, mean, inverse

    def both(ref, c):
        at, size = chunks[c]
        return jnp.concatenate((ref[at : at + size], ref[half + at : half + at + size]), 0)

    def put(ref, c, value):
        at, size = chunks[c]
        ref[at : at + size] = value[:size]
        ref[half + at : half + at + size] = value[size:]

    def add(i, value):
        r.running[i] += value.reshape(value.shape[0] // 8, 8, value.shape[1]).sum(0)

    r.running[...] = jnp.zeros_like(r.running)
    r.qkv_shift[...] = jnp.zeros_like(r.qkv_shift)
    r.qkv_shift[:, :inner] = r.query_bias[...].astype(f32).reshape(1, inner)
    r.qkv_shift[:, 2 * inner :] = r.value_bias[...].astype(f32).reshape(1, inner)
    r.hidden_shift[...] = r.fc1_bias[...].astype(f32).reshape(r.hidden_shift.shape)
    for c in range(count):
        normal, mean, inverse = moments(both(r.kept, c).astype(f32))
        put(r.mean[0], c, mean)
        put(r.inverse[0], c, inverse)
        normed = (normal * vector(0) + vector(1)).astype(bf16)
        put(r.normed[0], c, normed)
        projected = dot(normed, r.whole[0][:, : 3 * inner], 1, 0) + r.qkv_shift[...]
        put(r.qkv, c, projected.astype(bf16))

    def weights_of(h):
        part = slice(h * HEAD_DIM, (h + 1) * HEAD_DIM)
        keys = slice(inner + h * HEAD_DIM, inner + (h + 1) * HEAD_DIM)
        scores = dot(r.qkv[:, part], r.qkv[:, keys], 1, 1) * factor
        scores = scores + r.bias[h, :, :rows].astype(f32)
        weights = jnp.exp(scores - jnp.max(scores, -1, keepdims=True))
        return weights * (1.0 / jnp.sum(weights, -1, keepdims=True))

    for h in range(heads):
        for event in late_floods[h * len(late_floods) // heads : (h + 1) * len(late_floods) // heads]:
            event()
        part = slice(h * HEAD_DIM, (h + 1) * HEAD_DIM)
        values = slice(2 * inner + h * HEAD_DIM, 2 * inner + (h + 1) * HEAD_DIM)
        r.attended[:, part] = dot(weights_of(h).astype(bf16), r.qkv[:, values], 1, 0).astype(bf16)

    def out_turned():
        return r.whole[0][:, 3 * inner :]

    def live_rows(c):
        at, size = chunks[c]
        first = lax.broadcasted_iota(jnp.int32, (size, 1), 0) + at
        places = jnp.concatenate((first, first + half), 0).astype(f32)
        return jnp.where(places < r.slot[1:2, 0:1], 1.0, 0.0)

    def padded(ref, c):
        at, size = chunks[c]
        last = min(half + at + size, slot_rows)
        low = ref[half + at : last]
        missing = half + at + size - last
        if missing:
            low = jnp.concatenate(
                (low.astype(f32), jnp.zeros((missing, low.shape[1]), f32)), 0
            )
        return jnp.concatenate((ref[at : at + size].astype(f32), low.astype(f32)), 0)

    def keep(ref, c, value):
        at, size = chunks[c]
        last = min(half + at + size, slot_rows)
        ref[at : at + size] = value[:size]
        ref[half + at : last] = value[size : size + last - half - at]

    def project(c):
        put(r.part[0], c, dot(both(r.attended, c), out_turned(), 1, 1))
        sums[0].first(c).start()

    def forward(c):
        if c == 0:
            floods[1].arrive()
        sums[0].third(c).wait_recv()
        middle = both(r.kept, c).astype(f32) + vector(3) * (both(r.total[0], c) + vector(2))
        put(r.middle, c, middle)
        normal, mean, inverse = moments(middle)
        put(r.mean[1], c, mean)
        put(r.inverse[1], c, inverse)
        normed = (normal * vector(4) + vector(5)).astype(bf16)
        put(r.normed[1], c, normed)
        hidden = dot(normed, r.whole[1][...], 1, 0) + r.hidden_shift[...]
        cumulative = 0.5 * (1.0 + lax.erf(hidden * 0.7071067811865476))
        put(
            r.slope,
            c,
            cumulative + hidden * jnp.exp(-0.5 * hidden * hidden) * 0.3989422804014327,
        )
        active = (hidden * cumulative).astype(bf16)
        put(r.active, c, active)
        if c == 0:
            floods[2].arrive()
        put(r.part[1], c, dot(active, r.whole[2][...], 1, 1))
        sums[1].first(c).start()
        grad_result = (padded(r.grad_here, c) * live_rows(c) * vector(7)).astype(bf16)
        put(r.grad_result, c, grad_result)
        add(5, grad_result.astype(f32))
        grad_hidden = (dot(grad_result, r.whole[2][...], 1, 0) * both(r.slope, c)).astype(bf16)
        put(r.grad_hidden, c, grad_hidden)
        add(0, grad_hidden.astype(f32))
        put(r.part[2], c, dot(grad_hidden, r.whole[1][...], 1, 1))
        sums[2].first(c).start()

    def results():
        for c in range(count):
            sums[1].third(c).wait_recv()
            result = both(r.total[1], c) + vector(6)
            live = live_rows(c)
            keep(r.out_here, c, (live * (both(r.middle, c) + vector(7) * result)).astype(bf16))
            add(6, padded(r.grad_here, c) * live * result)
        to_owners(5, r.running[6])
        store.start()

    def back_norm(grad, normal, inverse, gain):
        scaled = grad * gain
        along = jnp.mean(scaled * normal, -1, keepdims=True)
        return inverse * (scaled - jnp.mean(scaled, -1, keepdims=True) - normal * along)

    def backward(c):
        sums[2].third(c).wait_recv()
        grad = both(r.total[2], c)
        inverse = both(r.inverse[1], c)
        normal = (both(r.middle, c) - both(r.mean[1], c)) * inverse
        add(3, grad * normal)
        add(4, grad)
        grad_middle = padded(r.grad_here, c) * live_rows(c)
        grad_middle = grad_middle + back_norm(grad, normal, inverse, vector(4))
        put(r.grad_middle, c, grad_middle)
        add(2, grad_middle * (both(r.total[0], c) + vector(2)))
        grad_branch = (grad_middle * vector(3)).astype(bf16)
        put(r.grad_branch, c, grad_branch)
        add(1, grad_branch.astype(f32))
        put(r.grad_attended, c, dot(grad_branch, out_turned(), 1, 0).astype(bf16))

    def close(work):
        return lambda c: work.close_one(c)

    def cross(work):
        return lambda c: work.cross_one(c)

    stages = [project, cross(sums[0]), close(sums[0]), forward]
    stages += [cross(sums[2]), close(sums[2]), backward]

    def weight_grad(j, left, right, at=0):
        value = dot(left[...], right[...], 0, 0).astype(bf16)
        r.grad[j][:, at : at + value.shape[1]] = value

    def send_grads(j):
        for s in range(length - 1, -1, -1):
            scatters[j].start(s)

    for t in range(count + len(stages) - 1):
        for k in range(len(stages) - 1, -1, -1):
            if 0 <= t - k < count:
                stages[k](t - k)
        if t == count + 2:
            weight_grad(2, r.grad_result, r.active)
            send_grads(2)
        if t == count + 3:
            sums[1].cross()
            weight_grad(1, r.normed[1], r.grad_hidden)
            send_grads(1)

    store = pltpu.make_async_copy(r.out_here, r.layer_out, r.load_sem.at[0])
    weight_grad(0, r.grad_branch, r.attended, 3 * inner)
    steps = list(range(length - 1, -1, -1))
    for h in range(heads):
        part = slice(h * HEAD_DIM, (h + 1) * HEAD_DIM)
        keys = slice(inner + h * HEAD_DIM, inner + (h + 1) * HEAD_DIM)
        values = slice(2 * inner + h * HEAD_DIM, 2 * inner + (h + 1) * HEAD_DIM)
        weights = weights_of(h)
        grad_part = r.grad_attended[:, part]
        r.grad_qkv[:, values] = dot(weights.astype(bf16), grad_part, 0, 0).astype(bf16)
        grad = dot(grad_part, r.qkv[:, values], 1, 1)
        mean = jnp.sum(weights * grad, -1, keepdims=True)
        grad = (weights * (grad - mean)).astype(bf16)
        r.bias[h, :, :rows] = grad
        r.grad_qkv[:, part] = (dot(grad, r.qkv[:, keys], 1, 0) * factor).astype(bf16)
        r.grad_qkv[:, keys] = (dot(grad, r.qkv[:, part], 0, 0) * factor).astype(bf16)
        if h + 1 < length:
            scatters[2].step(steps[h])

    sums[0].drain()
    last = sums[0]
    for c in range(count):
        put(r.part[0], c, dot(both(r.grad_qkv, c), r.whole[0][:, : 3 * inner], 1, 1))
        last.first(c).start()
    weight_grad(0, r.normed[0], r.grad_qkv)
    send_grads(0)

    wide = model // LANES
    at = 1
    r.own_early[...] = jnp.zeros_like(r.own_early)
    r.own_early[0:1] = r.slot[0:1, :]

    def line_to(at, line):
        for c in range(-(-line.shape[1] // LANES)):
            piece = line[:, c * LANES : (c + 1) * LANES]
            r.own_early[at + c : at + c + 1, : piece.shape[1]] = piece

    for line in (
        jnp.sum(r.running[0], 0, keepdims=True),
        jnp.sum(r.grad_qkv[:, :inner].astype(f32), 0, keepdims=True),
        jnp.sum(r.grad_qkv[:, 2 * inner :].astype(f32), 0, keepdims=True),
    ):
        line_to(at, line)
        at += up_to(line.shape[1], LANES) // LANES
    spreads[0].start(lambda peer: r.own_early)

    def to_owners(i, value):
        line = jnp.sum(value, 0, keepdims=True)
        for d in range(peers):
            r.own_late[d, i : i + 1, :depth] = line[:, d * depth : (d + 1) * depth]

    r.own_late[...] = jnp.zeros_like(r.own_late)
    for i in range(1, 6):
        to_owners(i - 1, r.running[i])
    r.table_sums[...] = jnp.zeros_like(r.table_sums)

    def norm_step(here, out_rows):
        grad = r.total[0][here]
        normal = (r.kept[here].astype(f32) - r.mean[0][here]) * r.inverse[0][here]
        back = back_norm(grad, normal, r.inverse[0][here], vector(0))
        value = (r.grad_middle[here] + back).astype(bf16)
        if out_rows is None:
            r.input_grad[here] = value
        else:
            r.input_grad[out_rows] = value[:tail]
        product = (grad * normal).reshape(4, 8, model).sum(0)
        return product, grad.reshape(4, 8, model).sum(0)

    def norm_rows():
        last.arrive()

        def step(i, totals):
            gain, shift = norm_step(pl.ds(pl.multiple_of(i * 32, 32), 32), None)
            return totals[0] + gain, totals[1] + shift

        zero = jnp.zeros((8, model), f32)
        gain, shift = lax.fori_loop(0, body_rows // 32, step, (zero, zero))
        if tail:
            more = norm_step(slice(body_rows, rows), slice(body_rows, slot_rows))
            gain, shift = gain + more[0], shift + more[1]
        to_owners(6, gain)
        to_owners(7, shift)

    def scatter_event(j, s):
        return lambda: scatters[j].step(s)

    order = [(2, s) for s in steps[min(heads, length - 1) :]]
    order += [(j, s) for j in (1, 0) for s in steps]
    places = TABLE_PLACES if length == 4 else [4 * k for k in range(len(order))]
    events = [(at, scatter_event(*item)) for at, item in zip(places, order)]
    events += [(0, last.cross), (FIRST_CLOSE, sums[1].close), (RESULT_PLACE, results)]
    events += [(CLOSE_PLACE, last.close), (NORM_PLACE, norm_rows)]
    events.sort(key=lambda item: item[0])
    with_events(
        blocks,
        [(at, event) for at, event in events if at < blocks],
        lambda block: table_block(
            heads,
            groups,
            r.index,
            r.bias,
            r.table_sums,
            pl.ds(pl.multiple_of(block * ROW_STEP, ROW_STEP), ROW_STEP),
        ),
    )
    r.own_table[...] = r.table_sums[...].astype(bf16)
    spreads[2].start(lambda peer: r.own_table)
    spreads[1].start(lambda peer: r.own_late.at[peer])
    for at, event in events:
        if at >= blocks:
            event()
    r.all_early[grid.me] = r.own_early[...]
    r.all_late[grid.me] = r.own_late[grid.me]
    r.all_table[grid.me] = r.own_table[...]
    for spread in spreads:
        spread.arrive()
    early = jnp.zeros(r.early_sums.shape, f32)
    late = jnp.zeros(r.late_sums.shape, f32)
    small = jnp.zeros((height, LANES), f32)
    large = jnp.zeros((height, LANES), f32)
    for d in range(peers):
        kind = r.all_early[d, 0:1] > 0.5
        table = r.all_table[d].astype(f32)
        small += jnp.where(kind, 0.0, table)
        large += jnp.where(kind, table, 0.0)
        early += r.all_early[d]
        late += r.all_late[d]
    r.early_sums[...] = early
    r.late_sums[...] = late
    for out, value in ((r.small_sums, small), (r.large_sums, large)):
        entries = out.shape[1]
        for k in range(-(-entries // SPLIT)):
            first, size = k * SPLIT, min(SPLIT, entries - k * SPLIT)
            for h in range(heads):
                at = h * groups + k
                out[h : h + 1, first : first + size] = value[at : at + 1, :size]
    store.wait()
    for work in sums + floods + [lines] + scatters + spreads:
        work.drain()


def layer(arguments, peers, slot_rows):
    model = arguments["inputs"].shape[1]
    rows = up_to(slot_rows, 32)
    columns = up_to(rows, LANES)
    depth = model // peers
    hidden = arguments["fc1_bias"].shape[0]
    inner = arguments["query_bias"].shape[0]
    widths = [4 * inner, hidden, hidden]
    heads = inner // HEAD_DIM
    tables = [arguments["small_table"].shape, arguments["large_table"].shape]
    entries = up_to(max(shape[1] for shape in tables), LANES)
    groups = up_to(-(-entries // SPLIT), 16)
    height = heads * groups
    count = len(cuts_of(rows // 2, CHUNKS))
    length = peers // 2
    array = jax.ShapeDtypeStruct

    def sems(*shape):
        return pltpu.SemaphoreType.DMA(shape)

    def each(kind, shape, times):
        return [pltpu.VMEM(shape, kind) for _ in range(times)]

    outs = dict(
        layer_out=array((slot_rows, model), bf16),
        input_grad=array((slot_rows, model), bf16),
        small_sums=array(tables[0], f32),
        large_sums=array(tables[1], f32),
        early_sums=array((EARLY_LINES, LANES), f32),
        late_sums=array((VECTORS, LANES), f32),
        summed=[array((depth, w), f32) for w in widths],
    )
    blocks = [pltpu.VMEM((length, depth, w), bf16) for w in widths]
    scratch = dict(
        whole=[pltpu.VMEM((model, w), bf16) for w in widths],
        all_lines=pltpu.VMEM((peers * VECTORS, LANES), f32),
        grad=[pltpu.VMEM((model, w), bf16) for w in widths],
        side=blocks,
        up=blocks,
        down=blocks,
        scatter_sems=[[sems(length)] * 6] * 3,
        flood_sems=[[sems(length)] * 6] * 4,
        spread_sems=[[sems(peers)] * 2] * 3,
        part=each(f32, (rows, model), 3),
        total=each(f32, (rows, model), 3),
        near=each(f32, (rows // 2, model), 3),
        sent=each(bf16, (rows // 2, model), 3),
        far=each(bf16, (rows // 2, model), 3),
        sum_send=[sems(3, count)] * 3,
        sum_recv=[sems(3, count)] * 3,
        local_sem=sems(4),
        load_sem=sems(3),
        wide_from=pltpu.VMEM(arguments["large_index"].shape, jnp.int32),
        inputs_here=pltpu.VMEM((slot_rows, model), bf16),
        grad_here=pltpu.VMEM((slot_rows, model), bf16),
        out_here=pltpu.VMEM((slot_rows, model), bf16),
        own_first=pltpu.VMEM((depth, 4 * inner), bf16),
        own_lines=pltpu.VMEM((VECTORS, LANES), f32),
        slot=pltpu.VMEM((2, LANES), f32),
        hidden_shift=pltpu.VMEM((1, hidden), f32),
        index=pltpu.VMEM((rows, columns), jnp.int32),
        wide_index=pltpu.VMEM((rows, columns), jnp.int32),
        table=pltpu.VMEM((8, entries), f32),
        wide_table=pltpu.VMEM((8, entries), f32),
        bias=pltpu.VMEM((heads, rows, columns), bf16),
        vectors=pltpu.VMEM((VECTORS, model), f32),
        qkv_shift=pltpu.VMEM((1, 3 * inner), f32),
        running=pltpu.VMEM((7, 8, max(model, hidden)), f32),
        mean=each(f32, (rows, 1), 2),
        inverse=each(f32, (rows, 1), 2),
        normed=each(bf16, (rows, model), 2),
        kept=pltpu.VMEM((rows, model), bf16),
        grad_result=pltpu.VMEM((rows, model), bf16),
        grad_branch=pltpu.VMEM((rows, model), bf16),
        active=pltpu.VMEM((rows, hidden), bf16),
        grad_hidden=pltpu.VMEM((rows, hidden), bf16),
        qkv=pltpu.VMEM((rows, 3 * inner), bf16),
        grad_qkv=pltpu.VMEM((rows, 3 * inner), bf16),
        attended=pltpu.VMEM((rows, inner), bf16),
        grad_attended=pltpu.VMEM((rows, inner), bf16),
        middle=pltpu.VMEM((rows, model), f32),
        grad_middle=pltpu.VMEM((rows, model), f32),
        slope=pltpu.VMEM((rows, hidden), f32),
        table_sums=pltpu.VMEM((height, LANES), f32),
        own_table=pltpu.VMEM((height, LANES), bf16),
        all_table=pltpu.VMEM((peers, height, LANES), bf16),
        own_early=pltpu.VMEM((EARLY_LINES, LANES), f32),
        all_early=pltpu.VMEM((peers, EARLY_LINES, LANES), f32),
        own_late=pltpu.VMEM((peers, VECTORS, LANES), f32),
        all_late=pltpu.VMEM((peers, VECTORS, LANES), f32),
    )
    flat = jax.tree.leaves(arguments)
    near, apart = pl.BlockSpec(memory_space=pltpu.VMEM), pl.BlockSpec(memory_space=pl.ANY)
    specs = jax.tree.map(lambda _: near, arguments)
    specs.update(inputs=apart, out_grad=apart, large_index=apart)
    specs.update(slot_kind=pl.BlockSpec(memory_space=pltpu.SMEM))
    out_specs = jax.tree.map(lambda _: near, outs)
    out_specs.update(layer_out=apart)
    shapes, out_tree = jax.tree.flatten(outs)
    tree = jax.tree.structure((arguments, outs, scratch))
    results = pl.pallas_call(
        functools.partial(layer_body, (tree, heads, groups, slot_rows, peers)),
        out_shape=shapes,
        in_specs=jax.tree.leaves(specs),
        out_specs=jax.tree.leaves(out_specs),
        scratch_shapes=jax.tree.leaves(scratch),
        compiler_params=params(collective_id=0, has_side_effects=True),
        name="layer",
    )(*flat)
    return types.SimpleNamespace(**jax.tree.unflatten(out_tree, results))


def finish_body(tree, depth, *refs):
    found, out = (types.SimpleNamespace(**part) for part in jax.tree.unflatten(tree, refs))
    pairs = (
        (found.layer_out, out.layer_out),
        (found.input_grad, out.input_grad),
        (found.summed[1], out.fc1),
        (found.summed[2], out.fc2),
        (found.small_sums, out.small_table),
        (found.large_sums, out.large_table),
    )
    for src, dst in pairs:
        dst[...] = src[...]
    inner = out.query_bias.shape[0]
    for j in range(3):
        out.qkv[j] = found.summed[0][:, j * inner : (j + 1) * inner]
    out.out[...] = found.summed[0][:, 3 * inner :].T
    for i, vector in enumerate(out.vectors):
        vector[...] = found.late_sums[i, :depth]
    at = 1
    for line in (out.fc1_bias, out.query_bias, out.value_bias):
        size = line.shape[0]
        for first in range(0, size, LANES):
            count = min(LANES, size - first)
            line[pl.ds(first, count)] = found.early_sums[at, :count]
            at += 1


def finish(found, depth, inner, hidden):
    array = jax.ShapeDtypeStruct
    found = vars(found)
    outs = dict(
        layer_out=array(found["layer_out"].shape, bf16),
        input_grad=array(found["input_grad"].shape, bf16),
        fc1=array(found["summed"][1].shape, f32),
        fc2=array(found["summed"][2].shape, f32),
        small_table=array(found["small_sums"].shape, f32),
        large_table=array(found["large_sums"].shape, f32),
        qkv=array((3, depth, inner), f32),
        out=array((inner, depth), f32),
        vectors=[array((depth,), f32)] * VECTORS,
        fc1_bias=array((hidden,), f32),
        query_bias=array((inner,), f32),
        value_bias=array((inner,), f32),
    )
    shapes, out_tree = jax.tree.flatten(outs)
    results = pl.pallas_call(
        functools.partial(finish_body, jax.tree.structure((found, outs)), depth),
        out_shape=shapes,
        in_specs=in_vmem(len(jax.tree.leaves(found))),
        out_specs=in_vmem(len(shapes)),
        compiler_params=params(),
        name="finish",
    )(*jax.tree.leaves(found))
    return types.SimpleNamespace(**jax.tree.unflatten(out_tree, results))


def layer_norm(activations, norm_gain, norm_shift):
    center = activations - jnp.mean(activations, -1, keepdims=True)
    inverse = lax.rsqrt(jnp.mean(center * center, -1, keepdims=True) + EPS)
    normal = center * inverse
    return (normal * norm_gain + norm_shift, normal, inverse)


def norm_back(grad_normed, normal, inverse, norm_gain):
    scaled = grad_normed * norm_gain
    return inverse * (
        scaled
        - jnp.mean(scaled, -1, keepdims=True)
        - normal * jnp.mean(scaled * normal, -1, keepdims=True)
    )


def gelu_slope(hidden):
    cumulative = 0.5 * (1.0 + jax.scipy.special.erf(hidden * 0.7071067811865476))
    return cumulative + hidden * jnp.exp(-0.5 * hidden * hidden) * 0.3989422804014327


def pair_map(kind, small_index, large_index, rows, columns):
    def placed(index, at):
        side = index.shape[0]
        return jnp.pad(
            index, ((at, rows - at - side), (at, columns - at - side)), constant_values=-1
        )

    length = small_index.shape[0]
    small = placed(small_index, 0)
    for image in range(1, SLOT_ROWS // length):
        small = jnp.maximum(small, placed(small_index, image * length))
    return jnp.where(kind == 1, placed(large_index, 0), small)


def plain_device(
    images,
    out_grad,
    slot_kind,
    small_index,
    large_index,
    qkv_weight,
    out_weight,
    fc1_weight,
    fc2_weight,
    norm1_gain,
    norm1_shift,
    query_bias,
    value_bias,
    out_bias,
    gamma_attn,
    norm2_gain,
    norm2_shift,
    fc1_bias,
    fc2_bias,
    gamma_mlp,
    small_table,
    large_table,
):
    depth = qkv_weight.shape[0]
    width = query_bias.shape[0]
    hidden_width = fc1_bias.shape[0]
    heads = width // HEAD_DIM
    _, slot_rows, model_width = images.shape
    rows = up_to(slot_rows, 32)
    columns = up_to(rows, LANES)
    kind = slot_kind[0]

    block = jnp.concatenate(
        (
            qkv_weight.reshape(depth, 3 * width),
            fc1_weight,
            out_weight.T,
            fc2_weight.T,
        ),
        1,
    )
    whole = lax.all_gather(block, "dp", axis=0, tiled=True)
    cuts = (3 * width, 3 * width + hidden_width, 4 * width + hidden_width)
    qkv_matrix = whole[:, : cuts[0]]
    fc1_matrix = whole[:, cuts[0] : cuts[1]]
    out_turned = whole[:, cuts[1] : cuts[2]]
    fc2_turned = whole[:, cuts[2] :]
    small_vectors = jnp.stack(
        (norm1_gain, norm1_shift, out_bias, gamma_attn, norm2_gain, norm2_shift, fc2_bias, gamma_mlp)
    )
    vectors = lax.all_gather(small_vectors, "dp", axis=0)
    vectors = jnp.moveaxis(vectors, 0, 1).reshape(8, model_width).astype(f32)

    query_shift = query_bias.astype(f32)
    value_shift = value_bias.astype(f32)
    hidden_shift = fc1_bias.astype(f32)
    small_entries, large_entries = small_table.shape[0], large_table.shape[0]
    entries = up_to(max(small_entries, large_entries), LANES)
    table = jnp.where(
        kind == 1,
        jnp.pad(large_table, ((0, entries - large_entries), (0, 0))),
        jnp.pad(small_table, ((0, entries - small_entries), (0, 0))),
    )
    table = table.T.astype(f32)
    pair_index = pair_map(kind, small_index, large_index, rows, columns)
    bias = gather_bias(pair_index, table)

    positions = jnp.arange(rows)
    live_count = jnp.where(kind == 1, LARGE_LEN, slot_rows)
    live_rows = (positions < live_count).astype(f32).reshape(-1, 1)
    inputs = jnp.pad(images[0], ((0, rows - slot_rows), (0, 0))).astype(f32)
    normed_one, normal_one, inverse_one = layer_norm(inputs, vectors[0], vectors[1])
    normed_one = normed_one.astype(bf16)
    projected = dot(normed_one, qkv_matrix, 1, 0)
    queries = (projected[:, :width] + query_shift).astype(bf16)
    keys = projected[:, width : 2 * width].astype(bf16)
    values = (projected[:, 2 * width :] + value_shift).astype(bf16)
    pieces = attend_forward(queries, keys, values, bias)
    branch_part = dot(pieces, out_turned, 1, 1)
    branch = lax.psum(branch_part, "shard") + vectors[2]
    middle = inputs + vectors[3] * branch
    normed_two, normal_two, inverse_two = layer_norm(middle, vectors[4], vectors[5])
    normed_two = normed_two.astype(bf16)
    hidden = dot(normed_two, fc1_matrix, 1, 0) + hidden_shift
    active = jax.nn.gelu(hidden, approximate=False).astype(bf16)
    result_part = dot(active, fc2_turned, 1, 1)
    result = lax.psum(result_part.astype(bf16), "shard").astype(f32) + vectors[6]
    layer_out = ((middle + vectors[7] * result) * live_rows).astype(bf16)[:slot_rows][None]

    grad_out = jnp.pad(out_grad[0], ((0, rows - slot_rows), (0, 0))).astype(f32) * live_rows
    grad_gamma_mlp = jnp.sum(grad_out * result, 0)
    grad_result = (grad_out * vectors[7]).astype(bf16)
    grad_fc2_bias = jnp.sum(grad_result.astype(f32), 0)
    grad_fc2_turned = dot(grad_result, active, 0, 0)
    grad_active = dot(grad_result, fc2_turned, 1, 0)
    grad_hidden = (grad_active * gelu_slope(hidden)).astype(bf16)
    grad_fc1_bias = jnp.sum(grad_hidden.astype(f32), 0)
    grad_fc1 = dot(normed_two, grad_hidden, 0, 0)
    grad_normed_two = lax.psum(dot(grad_hidden, fc1_matrix, 1, 1), "shard")
    grad_norm2_gain = jnp.sum(grad_normed_two * normal_two, 0)
    grad_norm2_shift = jnp.sum(grad_normed_two, 0)
    grad_middle = grad_out + norm_back(grad_normed_two, normal_two, inverse_two, vectors[4])
    grad_gamma_attn = jnp.sum(grad_middle * branch, 0)
    grad_branch = (grad_middle * vectors[3]).astype(bf16)
    grad_out_bias = jnp.sum(grad_branch.astype(f32), 0)
    grad_out_turned = dot(grad_branch, pieces, 0, 0)
    grad_attended = dot(grad_branch, out_turned, 1, 0).astype(bf16)
    grad_queries, grad_keys, grad_values, grad_scores = attend_backward(
        queries, keys, values, bias, grad_attended
    )
    sums = table_sums(pair_index, grad_scores, entries)
    grad_projected = jnp.concatenate((grad_queries, grad_keys, grad_values), 1)
    grad_qkv = dot(normed_one, grad_projected, 0, 0)
    grad_query_bias = jnp.sum(grad_queries.astype(f32), 0)
    grad_value_bias = jnp.sum(grad_values.astype(f32), 0)
    grad_normed_one = lax.psum(dot(grad_projected, qkv_matrix, 1, 1), "shard")
    grad_norm1_gain = jnp.sum(grad_normed_one * normal_one, 0)
    grad_norm1_shift = jnp.sum(grad_normed_one, 0)
    input_grad = grad_middle + norm_back(grad_normed_one, normal_one, inverse_one, vectors[0])
    input_grad = input_grad.astype(bf16)[:slot_rows][None]

    small_sums = jnp.where(kind == 1, 0.0, sums[:, :small_entries])
    large_sums = jnp.where(kind == 1, sums[:, :large_entries], 0.0)
    local_sums = lax.psum(
        (small_sums, large_sums, grad_query_bias, grad_value_bias, grad_fc1_bias), "dp"
    )
    peers = lax.axis_size("dp")

    def sent_and_summed(value):
        parts = value.astype(bf16).reshape(peers, value.shape[0] // peers, -1)
        arrived = lax.all_to_all(parts, "dp", split_axis=0, concat_axis=0, tiled=True)
        return arrived.astype(f32).sum(axis=0)

    grad_block = sent_and_summed(
        jnp.concatenate((grad_qkv, grad_fc1, grad_out_turned, grad_fc2_turned), 1)
    )
    vector_grads = sent_and_summed(
        jnp.stack(
            (
                grad_norm1_gain,
                grad_norm1_shift,
                grad_out_bias,
                grad_gamma_attn,
                grad_norm2_gain,
                grad_norm2_shift,
                grad_fc2_bias,
                grad_gamma_mlp,
            ),
            1,
        )
    )
    return (
        layer_out,
        input_grad,
        grad_block[:, : cuts[0]].reshape(depth, 3, width),
        grad_block[:, cuts[1] : cuts[2]].T,
        grad_block[:, cuts[0] : cuts[1]],
        grad_block[:, cuts[2] :].T,
        vector_grads[:, 0],
        vector_grads[:, 1],
        local_sums[2],
        local_sums[3],
        vector_grads[:, 2],
        vector_grads[:, 3],
        vector_grads[:, 4],
        vector_grads[:, 5],
        local_sums[4],
        vector_grads[:, 6],
        vector_grads[:, 7],
        local_sums[0].T,
        local_sums[1].T,
    )


def on_device(*arguments):
    depth = arguments[5].shape[0]
    if depth % 16 or lax.axis_size("shard") != 4:
        return plain_device(*arguments)
    return whole_device(*arguments)


def whole_device(
    images,
    out_grad,
    slot_kind,
    small_index,
    large_index,
    qkv_weight,
    out_weight,
    fc1_weight,
    fc2_weight,
    norm1_gain,
    norm1_shift,
    query_bias,
    value_bias,
    out_bias,
    gamma_attn,
    norm2_gain,
    norm2_shift,
    fc1_bias,
    fc2_bias,
    gamma_mlp,
    small_table,
    large_table,
):
    depth = qkv_weight.shape[0]
    found = layer(
        dict(
            inputs=images[0],
            out_grad=out_grad[0],
            slot_kind=slot_kind,
            small_index=small_index,
            large_index=large_index,
            small_table=small_table.T,
            large_table=large_table.T,
            qkv_weight=qkv_weight.transpose(1, 0, 2),
            out_weight=out_weight,
            fc1_weight=fc1_weight,
            fc2_weight=fc2_weight.T,
            small_vectors=[
                norm1_gain,
                norm1_shift,
                out_bias,
                gamma_attn,
                norm2_gain,
                norm2_shift,
                fc2_bias,
                gamma_mlp,
            ],
            query_bias=query_bias,
            value_bias=value_bias,
            fc1_bias=fc1_bias,
        ),
        lax.axis_size("dp"),
        images.shape[1],
    )
    out = finish(found, depth, query_bias.shape[0], fc1_bias.shape[0])
    return (
        out.layer_out[None],
        out.input_grad[None],
        out.qkv.transpose(1, 0, 2),
        out.out,
        out.fc1,
        out.fc2.T,
        out.vectors[6],
        out.vectors[7],
        out.query_bias,
        out.value_bias,
        out.vectors[0],
        out.vectors[1],
        out.vectors[2],
        out.vectors[3],
        out.fc1_bias,
        out.vectors[4],
        out.vectors[5],
        out.small_table.T,
        out.large_table.T,
    )


def solution(mesh):
    return jax.shard_map(
        on_device,
        mesh=mesh,
        in_specs=(
            P("dp", None, None),
            P("dp", None, None),
            P("dp"),
            P(),
            P(),
            P("dp", None, "shard"),
            P("shard", "dp"),
            P("dp", "shard"),
            P("shard", "dp"),
            P("dp"),
            P("dp"),
            P("shard"),
            P("shard"),
            P("dp"),
            P("dp"),
            P("dp"),
            P("dp"),
            P("shard"),
            P("dp"),
            P("dp"),
            P(None, "shard"),
            P(None, "shard"),
        ),
        out_specs=(
            P("dp", None, None),
            P("dp", None, None),
            P("dp", None, "shard"),
            P("shard", "dp"),
            P("dp", "shard"),
            P("shard", "dp"),
            P("dp"),
            P("dp"),
            P("shard"),
            P("shard"),
            P("dp"),
            P("dp"),
            P("dp"),
            P("dp"),
            P("shard"),
            P("dp"),
            P("dp"),
            P(None, "shard"),
            P(None, "shard"),
        ),
        check_vma=False,
    )
```

```python
import functools
import types

import jax
import jax.numpy as jnp
from jax import lax
from jax.experimental import pallas as pl
from jax.experimental.pallas import tpu as pltpu
from jax.sharding import PartitionSpec as P

HEAD_DIM = 64
SMALL_LEN = 197
LARGE_LEN = 577
SLOT_ROWS = 591
EPS = 1e-06
NEG = -1e30
LANES = 128
SPLIT = 80
VMEM_LIMIT = 60 << 20

MESH = pl.DeviceIdType.MESH

f32 = jnp.float32
bf16 = jnp.bfloat16


def up_to(value, unit):
    return -(-value // unit) * unit


def in_vmem(count):
    return [pl.BlockSpec(memory_space=pltpu.VMEM)] * count


def params(**more):
    return pltpu.CompilerParams(vmem_limit_bytes=VMEM_LIMIT, **more)


def dot(a, b, da, db):
    return lax.dot_general(a, b, (((da,), (db,)), ((), ())), preferred_element_type=f32)


def bias_block_of(heads, index_ref, table_ref, out_ref, here):
    columns, entries = index_ref.shape[1], table_ref.shape[1]
    for c in range(columns // LANES):
        there = pl.ds(c * LANES, LANES)
        index = index_ref[here, there]
        high = lax.shift_right_arithmetic(index, 7)
        low = lax.bitwise_and(index, LANES - 1)
        found = [jnp.full(index.shape, NEG, f32) for _ in range(heads)]
        for k in range(entries // LANES):
            match = high == k
            for h in range(heads):
                line = table_ref[h : h + 1, k * LANES : (k + 1) * LANES]
                values = jnp.take_along_axis(jnp.broadcast_to(line, index.shape), low, axis=1)
                found[h] = jnp.where(match, values, found[h])
        for h in range(heads):
            out_ref[h, here, there] = found[h].astype(bf16)


def table_block(heads, groups, index_ref, grad_ref, out_ref, here):
    columns = index_ref.shape[1]
    inverse = -(-(1 << 22) // SPLIT)
    index = index_ref[here, :]
    high = lax.shift_right_arithmetic(index * inverse, 22)
    low = (index - high * SPLIT).astype(jnp.int16)
    high = high.astype(jnp.int16)
    grads = [grad_ref[h, here, :] for h in range(heads)]
    places_low = lax.broadcasted_iota(jnp.int16, (SPLIT, columns), 0)
    places_high = lax.broadcasted_iota(jnp.int16, (groups, columns), 0)
    one, zero = jnp.ones((), bf16), jnp.zeros((), bf16)
    total = jnp.zeros((heads * groups, SPLIT), f32)
    for pair in range(0, 16, 2):
        lows, highs = [], []
        for i in (pair, pair + 1):
            lows.append(
                jnp.where(
                    places_low == jnp.broadcast_to(low[i : i + 1], (SPLIT, columns)), one, zero
                )
            )
            match = places_high == jnp.broadcast_to(high[i : i + 1], (groups, columns))
            highs.append(
                jnp.concatenate(
                    [
                        jnp.where(
                            match,
                            jnp.broadcast_to(grads[h][i : i + 1], (groups, columns)),
                            zero,
                        )
                        for h in range(heads)
                    ],
                    0,
                )
            )
        total = total + dot(jnp.concatenate(highs, 1), jnp.concatenate(lows, 1), 1, 1)
    out_ref[: heads * groups, :SPLIT] += total


def forward_body(heads, q_ref, k_ref, v_ref, bias_ref, out_ref):
    rows = q_ref.shape[0]
    for h in range(heads):
        part = slice(h * HEAD_DIM, (h + 1) * HEAD_DIM)
        scores = dot(q_ref[:, part], k_ref[:, part], 1, 1) * HEAD_DIM ** (-0.5)
        scores = scores + bias_ref[h, :, :rows].astype(f32)
        weights = jnp.exp(scores - jnp.max(scores, -1, keepdims=True))
        weights = weights / jnp.sum(weights, -1, keepdims=True)
        out_ref[:, part] = dot(weights.astype(bf16), v_ref[:, part], 1, 0).astype(bf16)


def backward_body(
    heads, q_ref, k_ref, v_ref, bias_ref, grad_ref, dq_ref, dk_ref, dv_ref, ds_ref
):
    rows = q_ref.shape[0]
    factor = HEAD_DIM ** (-0.5)
    for h in range(heads):
        part = slice(h * HEAD_DIM, (h + 1) * HEAD_DIM)
        scores = dot(q_ref[:, part], k_ref[:, part], 1, 1) * factor
        scores = scores + bias_ref[h, :, :rows].astype(f32)
        weights = jnp.exp(scores - jnp.max(scores, -1, keepdims=True))
        weights = weights / jnp.sum(weights, -1, keepdims=True)
        dv_ref[:, part] = dot(weights.astype(bf16), grad_ref[:, part], 0, 0).astype(bf16)
        grad = dot(grad_ref[:, part], v_ref[:, part], 1, 1)
        mean = jnp.sum(weights * grad, -1, keepdims=True)
        grad = (weights * (grad - mean)).astype(bf16)
        ds_ref[h, :, :rows] = grad
        dq_ref[:, part] = (dot(grad, k_ref[:, part], 1, 0) * factor).astype(bf16)
        dk_ref[:, part] = (dot(grad, q_ref[:, part], 0, 0) * factor).astype(bf16)


def attend_forward(queries, keys, values, bias):
    heads = bias.shape[0]
    return pl.pallas_call(
        functools.partial(forward_body, heads),
        out_shape=jax.ShapeDtypeStruct(queries.shape, bf16),
        in_specs=in_vmem(4),
        out_specs=in_vmem(1)[0],
        compiler_params=params(),
        cost_estimate=pl.CostEstimate(flops=10**9, bytes_accessed=10**7, transcendentals=10**6),
        name="attend_forward",
    )(queries, keys, values, bias)


def attend_backward(queries, keys, values, bias, grad):
    heads = bias.shape[0]
    rows = jax.ShapeDtypeStruct(queries.shape, bf16)
    return pl.pallas_call(
        functools.partial(backward_body, heads),
        out_shape=(rows, rows, rows, jax.ShapeDtypeStruct(bias.shape, bf16)),
        in_specs=in_vmem(5),
        out_specs=tuple(in_vmem(4)),
        compiler_params=params(),
        cost_estimate=pl.CostEstimate(flops=2 * 10**9, bytes_accessed=2 * 10**7, transcendentals=10**6),
        name="attend_backward",
    )(queries, keys, values, bias, grad)


def bias_body(heads, index_ref, table_ref, out_ref):
    def work(block):
        here = pl.ds(pl.multiple_of(block * ROW_STEP, ROW_STEP), ROW_STEP)
        bias_block_of(heads, index_ref, table_ref, out_ref, here)

    with_events(index_ref.shape[0] // ROW_STEP, [], work)


def gather_bias(pair_index, table):
    heads, entries = table.shape
    return pl.pallas_call(
        functools.partial(bias_body, heads),
        out_shape=jax.ShapeDtypeStruct((heads,) + pair_index.shape, bf16),
        in_specs=in_vmem(2),
        out_specs=in_vmem(1)[0],
        compiler_params=params(),
        cost_estimate=pl.CostEstimate(flops=10**9, bytes_accessed=4 * 10**7, transcendentals=0),
        name="bias",
    )(pair_index, table)


def table_body(heads, groups, index_ref, grad_ref, out_ref):
    out_ref[...] = jnp.zeros_like(out_ref)

    def work(block):
        here = pl.ds(pl.multiple_of(block * ROW_STEP, ROW_STEP), ROW_STEP)
        table_block(heads, groups, index_ref, grad_ref, out_ref, here)

    with_events(index_ref.shape[0] // ROW_STEP, [], work)


def table_sums(pair_index, grad_scores, entries):
    heads = grad_scores.shape[0]
    groups = up_to(-(-entries // SPLIT), 16)
    sums = pl.pallas_call(
        functools.partial(table_body, heads, groups),
        out_shape=jax.ShapeDtypeStruct((heads * groups, SPLIT), f32),
        in_specs=in_vmem(2),
        out_specs=in_vmem(1)[0],
        compiler_params=params(),
        cost_estimate=pl.CostEstimate(flops=2 * 10**9, bytes_accessed=6 * 10**7, transcendentals=0),
        name="table_sums",
    )(pair_index, grad_scores)
    return sums.reshape(heads, groups * SPLIT)


def cuts_of(total, pieces, unit=16):
    count, extra = divmod(total // unit, pieces)
    cuts, at = [], 0
    for i in range(pieces):
        size = (count + (i < extra)) * unit
        if size:
            cuts.append((at, size))
        at += size
    return cuts


def remote(src, dst, send_sem, recv_sem, axis, peer):
    return pltpu.make_async_remote_copy(
        src_ref=src,
        dst_ref=dst,
        send_sem=send_sem,
        recv_sem=recv_sem,
        device_id={axis: peer},
        device_id_type=MESH,
    )


def greet(barrier, axis, peer):
    pl.semaphore_signal(barrier, inc=1, device_id={axis: peer}, device_id_type=MESH)


class ShardSum:
    def __init__(self, chunks, part_ref, out_ref, near, sent, far, send_sem, recv_sem):
        me = lax.axis_index("shard")
        outer, self.inner = me // 2, lax.rem(me, 2)
        self.near_peer = outer * 2 + (1 - self.inner)
        self.far_peer = (1 - outer) * 2 + self.inner
        self.chunks, self.part, self.out = chunks, part_ref, out_ref
        self.near, self.sent, self.far = near, sent, far
        self.sems = (send_sem, recv_sem)
        self.half = near.shape[0]

    def greet(self, barrier):
        greet(barrier, "shard", self.near_peer)
        greet(barrier, "shard", self.far_peer)
        return 2

    def rows(self, which, at, size):
        return pl.ds(pl.multiple_of(which * self.half + at, 16), size)

    def copy(self, stage, j, src, dst, peer):
        send_sem, recv_sem = self.sems
        return remote(src, dst, send_sem.at[stage, j], recv_sem.at[stage, j], "shard", peer)

    def first(self, j):
        at, size = self.chunks[j]
        return self.copy(
            0, j, self.part.at[self.rows(1 - self.inner, at, size)], self.near.at[pl.ds(at, size)], self.near_peer
        )

    def second(self, j):
        here = pl.ds(*self.chunks[j])
        return self.copy(1, j, self.sent.at[here], self.far.at[here], self.far_peer)

    def third(self, j):
        mine = self.out.at[self.rows(self.inner, *self.chunks[j])]
        return self.copy(2, j, mine, mine, self.near_peer)

    def start(self):
        for j in range(len(self.chunks)):
            self.first(j).start()

    def cross_one(self, j):
        at, size = self.chunks[j]
        self.first(j).wait_recv()
        here = pl.ds(at, size)
        mine = self.rows(self.inner, at, size)
        self.sent[here] = (self.part[mine] + self.near[here]).astype(bf16)
        self.second(j).start()

    def cross(self):
        for j in range(len(self.chunks)):
            self.cross_one(j)

    def close_one(self, j):
        at, size = self.chunks[j]
        self.second(j).wait_recv()
        here = pl.ds(at, size)
        mine = self.rows(self.inner, at, size)
        self.out[mine] = self.sent[here].astype(f32) + self.far[here].astype(f32)
        self.third(j).start()

    def close(self):
        for j in range(len(self.chunks)):
            self.close_one(j)

    def arrive(self):
        for j in range(len(self.chunks)):
            self.third(j).wait_recv()

    def drain(self):
        for j in range(len(self.chunks)):
            self.first(j).wait_send()
            self.second(j).wait_send()
            self.third(j).wait_send()


class Grid:
    def __init__(self, peers):
        self.length = peers // 2
        self.me = lax.axis_index("dp")
        self.at, self.side = self.me // 2, lax.rem(self.me, 2)
        self.up, self.down = self.me + 2, self.me - 2
        self.across = self.at * 2 + 1 - self.side
        self.has_up, self.has_down = self.at < self.length - 1, self.at > 0

    def greet(self, barrier):
        greet(barrier, "dp", self.across)

        @pl.when(self.has_up)
        def _():
            greet(barrier, "dp", self.up)

        @pl.when(self.has_down)
        def _():
            greet(barrier, "dp", self.down)

        return 1 + self.has_up.astype(jnp.int32) + self.has_down.astype(jnp.int32)

    def clip(self, place):
        return jnp.clip(place, 0, self.length - 1)


class Flood:
    def __init__(self, grid, own, out, up_send, up_recv, down_send, down_recv, side_send, side_recv):
        self.grid, self.own, self.out = grid, own, out
        self.up_sems, self.down_sems = (up_send, up_recv), (down_send, down_recv)
        self.side_sems = (side_send, side_recv)

    def at(self, device):
        depth = self.own.shape[0]
        return self.out.at[pl.ds(pl.multiple_of(device * depth, 8), depth)]

    def block(self, place):
        return self.at(self.grid.clip(place) * 2 + self.grid.side)

    def up(self, s):
        grid, (send, recv) = self.grid, self.up_sems
        block = self.block(grid.at - s)
        return remote(self.own if s == 0 else block, block, send.at[s], recv.at[s], "dp", grid.up)

    def down(self, s):
        grid, (send, recv) = self.grid, self.down_sems
        block = self.block(grid.at + s)
        return remote(self.own if s == 0 else block, block, send.at[s], recv.at[s], "dp", grid.down)

    def across(self, place, own=False):
        grid, (send, recv) = self.grid, self.side_sems
        place = grid.clip(place)
        block = self.block(place)
        return remote(
            self.own if own else block, block, send.at[place], recv.at[place], "dp", grid.across
        )

    def step(self, s):
        grid = self.grid
        if s == 0:

            @pl.when(grid.has_up)
            def _():
                self.up(0).start()

            @pl.when(grid.has_down)
            def _():
                self.down(0).start()

            self.across(grid.at, own=True).start()
            return

        @pl.when(grid.at - s >= 0)
        def _():
            block = self.block(grid.at - s)
            send, recv = self.up_sems
            remote(block, block, send.at[s - 1], recv.at[s - 1], "dp", grid.down).wait_recv()

            @pl.when(grid.has_up)
            def _():
                self.up(s).start()

            self.across(grid.at - s).start()

        @pl.when(grid.at + s < grid.length)
        def _():
            block = self.block(grid.at + s)
            send, recv = self.down_sems
            remote(block, block, send.at[s - 1], recv.at[s - 1], "dp", grid.up).wait_recv()

            @pl.when(grid.has_down)
            def _():
                self.down(s).start()

            self.across(grid.at + s).start()

    def arrive(self):
        grid, (send, recv) = self.grid, self.side_sems
        for place in range(grid.length):
            block = self.at(place * 2 + 1 - grid.side)
            remote(block, block, send.at[place], recv.at[place], "dp", grid.across).wait_recv()

    def drain(self):
        grid = self.grid
        for place in range(grid.length):
            self.across(place).wait_send()
        for s in range(grid.length - 1):

            @pl.when(jnp.logical_and(grid.at - s >= 0, grid.has_up))
            def _():
                self.up(s).wait_send()

            @pl.when(jnp.logical_and(grid.at + s < grid.length, grid.has_down))
            def _():
                self.down(s).wait_send()


SIDE, UP, DOWN = range(3)


class ReduceScatter:
    def __init__(self, grid, grads, out, side, up, down, sems):
        self.grid, self.grads, self.out = grid, grads, out
        self.buffers = (side, up, down)
        self.sems = (sems[:2], sems[2:4], sems[4:6])

    def at(self, device):
        depth = self.out.shape[0]
        return pl.ds(pl.multiple_of(device * depth, 16), depth)

    def prepare(self):
        grid = self.grid

        @pl.when(jnp.logical_not(grid.has_down))
        def _():
            self.buffers[UP][...] = jnp.zeros_like(self.buffers[UP])

        @pl.when(jnp.logical_not(grid.has_up))
        def _():
            self.buffers[DOWN][...] = jnp.zeros_like(self.buffers[DOWN])

    def copy(self, way, place, peer, src=None):
        send, recv = self.sems[way]
        place = self.grid.clip(place)
        dst = self.buffers[way].at[place]
        return remote(dst if src is None else src, dst, send.at[place], recv.at[place], "dp", peer)

    def cross(self, place):
        grid = self.grid
        src = self.grads.at[self.at(grid.clip(place) * 2 + 1 - grid.side)]
        return self.copy(SIDE, place, grid.across, src)

    def start(self, s):
        grid = self.grid

        @pl.when(grid.at + s < grid.length)
        def _():
            self.cross(grid.at + s).start()

        if s:

            @pl.when(grid.at - s >= 0)
            def _():
                self.cross(grid.at - s).start()

    def step(self, s):
        grid = self.grid
        side, up, down = self.buffers
        if s == 0:
            place = grid.at
            self.copy(SIDE, place, grid.across).wait_recv()

            @pl.when(grid.has_down)
            def _():
                self.copy(UP, place, grid.down).wait_recv()

            @pl.when(grid.has_up)
            def _():
                self.copy(DOWN, place, grid.up).wait_recv()

            total = self.grads[self.at(grid.me)].astype(f32) + side[place].astype(f32)
            self.out[...] = total + (up[place].astype(f32) + down[place].astype(f32))
            return

        @pl.when(grid.at + s < grid.length)
        def _():
            place = grid.clip(grid.at + s)
            self.copy(SIDE, place, grid.across).wait_recv()

            @pl.when(grid.has_down)
            def _():
                self.copy(UP, place, grid.down).wait_recv()

            total = self.grads[self.at(place * 2 + grid.side)].astype(f32) + side[place].astype(f32)
            side[place] = (total + up[place].astype(f32)).astype(bf16)
            self.copy(UP, place, grid.up, side.at[place]).start()

        @pl.when(grid.at - s >= 0)
        def _():
            place = grid.clip(grid.at - s)
            self.copy(SIDE, place, grid.across).wait_recv()

            @pl.when(grid.has_up)
            def _():
                self.copy(DOWN, place, grid.up).wait_recv()

            total = self.grads[self.at(place * 2 + grid.side)].astype(f32) + side[place].astype(f32)
            side[place] = (total + down[place].astype(f32)).astype(bf16)
            self.copy(DOWN, place, grid.down, side.at[place]).start()

    def drain(self):
        grid = self.grid
        for place in range(grid.length):
            self.cross(place).wait_send()
        for s in range(1, grid.length):

            @pl.when(grid.at + s < grid.length)
            def _():
                self.copy(UP, grid.at + s, grid.up).wait_send()

            @pl.when(grid.at - s >= 0)
            def _():
                self.copy(DOWN, grid.at - s, grid.down).wait_send()


ROW_STEP = 16
CHUNKS = 4
VECTORS = 8
EARLY_LINES = 16
BIAS_PLACES = [4, 14, 24, 18, 32, 99, 7, 25, 36, 99]
TABLE_PLACES = [-1, 6, 31, 2, 10, 21, 44, 16, 26, 29, 39]
FIRST_CLOSE = 2
RESULT_PLACE = 7
CLOSE_PLACE = 22
NORM_PLACE = 27


def with_events(blocks, events, work):
    def step(block, carry):
        for at, event in events:
            pl.when(block == at)(event)

        @pl.when(block < blocks)
        def _():
            work(block)

        return carry

    lax.fori_loop(0, max([blocks] + [at + 1 for at, _ in events]), step, 0)


class Spread:
    def __init__(self, peers, out, send_sem, recv_sem):
        self.peers, self.out, self.sems = peers, out, (send_sem, recv_sem)
        self.me = lax.axis_index("dp")

    def peer(self, i):
        return lax.rem(self.me + i, self.peers)

    def copy(self, src, slot, peer):
        send_sem, recv_sem = self.sems
        return remote(
            src, self.out.at[slot], send_sem.at[peer], recv_sem.at[slot], "dp", peer
        )

    def start(self, src_for):
        for i in range(1, self.peers):
            self.copy(src_for(self.peer(i)), self.me, self.peer(i)).start()

    def arrive(self):
        for i in range(1, self.peers):
            peer = self.peer(i)
            self.copy(self.out.at[peer], peer, peer).wait_recv()

    def drain(self):
        for i in range(1, self.peers):
            peer = self.peer(i)
            self.copy(self.out.at[peer], peer, peer).wait_send()


def layer_body(plan, *refs):
    tree, heads, groups, slot_rows, peers = plan
    named = {}
    for part in jax.tree.unflatten(tree, refs):
        named.update(part)
    r = types.SimpleNamespace(**named)
    rows, columns = r.index.shape
    model = r.inputs.shape[1]
    depth = model // peers
    inner = heads * HEAD_DIM
    half = rows // 2
    chunks = cuts_of(half, CHUNKS)
    count = len(chunks)
    factor = HEAD_DIM ** (-0.5)
    height = heads * groups

    grid = Grid(peers)
    sums = [
        ShardSum(chunks, *buffers)
        for buffers in zip(r.part, r.total, r.near, r.sent, r.far, r.sum_send, r.sum_recv)
    ]
    lines = Flood(grid, r.own_lines, r.all_lines, *r.flood_sems[3])
    floods = [
        Flood(grid, own, out, *sems) for own, out, sems in zip((r.own_first, r.fc1_weight, r.fc2_weight), r.whole, r.flood_sems)
    ]
    scatters = [
        ReduceScatter(grid, *buffers)
        for buffers in zip(r.grad, r.summed, r.side, r.up, r.down, r.scatter_sems)
    ]
    spreads = [
        Spread(peers, out, *sems)
        for out, sems in zip((r.all_early, r.all_late, r.all_table), r.spread_sems)
    ]

    loads = [
        pltpu.make_async_copy(src, dst, r.load_sem.at[j])
        for j, (src, dst) in enumerate(
            ((r.large_index, r.wide_from), (r.inputs, r.inputs_here), (r.out_grad, r.grad_here))
        )
    ]
    for load in loads:
        load.start()
    for i, member in enumerate(r.small_vectors):
        r.own_lines[i : i + 1, :depth] = member[...].astype(f32).reshape(1, depth)
    for j in range(3):
        r.own_first[:, j * inner : (j + 1) * inner] = r.qkv_weight[j]
    r.own_first[:, 3 * inner :] = r.out_weight[...].T
    barrier = pltpu.get_barrier_semaphore()
    met = sums[0].greet(barrier)
    for i in range(1, peers):
        greet(barrier, "dp", lax.rem(grid.me + i, peers))
    pl.semaphore_wait(barrier, met + peers - 1)
    lines.step(0)
    floods[0].step(0)
    floods[1].step(0)
    copies = [
        pltpu.make_async_copy(flood.own, flood.at(grid.me), r.local_sem.at[j])
        for j, flood in enumerate(floods + [lines])
    ]
    for copy in copies:
        copy.start()
    for scatter in scatters:
        scatter.prepare()

    kind = r.slot_kind[0]
    r.slot[0:1] = jnp.full((1, LANES), kind.astype(f32))
    r.slot[1:2] = jnp.full((1, LANES), (slot_rows - kind * (slot_rows - LARGE_LEN)).astype(f32))
    is_large = jnp.broadcast_to(r.slot[0:1, :], (8, LANES)) > 0.5
    small_side, large_side = r.small_index.shape[0], r.large_index.shape[0]
    r.index[...] = jnp.full((rows, columns), -1, jnp.int32)
    for image in range(slot_rows // small_side):
        at = image * small_side
        r.index[at : at + small_side, at : at + small_side] = r.small_index[...]
    r.wide_index[...] = jnp.full((rows, columns), -1, jnp.int32)
    for load in loads:
        load.wait()
    r.wide_index[:large_side, :large_side] = r.wide_from[...]
    r.table[...] = jnp.zeros_like(r.table)
    entries_small, entries_large = r.small_table.shape[1], r.large_table.shape[1]
    r.table[:heads, :entries_small] = r.small_table[...].astype(f32)
    r.wide_table[...] = jnp.zeros_like(r.wide_table)
    r.wide_table[:heads, :entries_large] = r.large_table[...].astype(f32)
    tall = jnp.broadcast_to(is_large[:, 0:1], r.table.shape)
    r.table[...] = jnp.where(tall, r.wide_table[...], r.table[...])
    large_block = jnp.broadcast_to(r.slot[0:1, 0:1], (ROW_STEP, columns)) > 0.5

    body_rows = slot_rows // 32 * 32
    tail = slot_rows - body_rows
    r.kept[:body_rows] = r.inputs_here[:body_rows]
    r.kept[body_rows:] = jnp.concatenate(
        (
            r.inputs_here[body_rows:slot_rows].astype(f32),
            jnp.zeros((rows - slot_rows, model), f32),
        ),
        0,
    ).astype(bf16)
    blocks = up_to(slot_rows, ROW_STEP) // ROW_STEP

    def bias_block(block):
        here = pl.ds(pl.multiple_of(block * ROW_STEP, ROW_STEP), ROW_STEP)
        r.index[here] = jnp.where(large_block, r.wide_index[here], r.index[here])
        bias_block_of(heads, r.index, r.table, r.bias, here)

    r.index[blocks * ROW_STEP :] = jnp.full((rows - blocks * ROW_STEP, columns), -1, jnp.int32)
    r.bias[:, blocks * ROW_STEP :] = jnp.full(
        (heads, rows - blocks * ROW_STEP, columns), NEG, bf16
    )
    length = grid.length

    def flood_event(j, s):
        return lambda: floods[j].step(s)

    order = [(j, s) for j in range(2) for s in range(1, length)]
    order += [(2, s) for s in range(length)]
    places = BIAS_PLACES if length == 4 else [k * 3 for k in range(len(order))]
    events = [(at, flood_event(*item)) for at, item in zip(places, order)]
    events += [(3 * s, functools.partial(lines.step, s)) for s in range(1, length)]
    late_floods = [event for at, event in events if at >= blocks]
    with_events(blocks, [(at, event) for at, event in events if at < blocks], bias_block)
    for copy in copies:
        copy.wait()
    lines.arrive()
    floods[0].arrive()
    for d in range(peers):
        r.vectors[:, d * depth : (d + 1) * depth] = r.all_lines[
            d * VECTORS : (d + 1) * VECTORS, :depth
        ]

    def vector(i):
        return r.vectors[i : i + 1, :]

    def moments(value):
        mean = jnp.mean(value, -1, keepdims=True)
        center = value - mean
        inverse = lax.rsqrt(jnp.mean(center * center, -1, keepdims=True) + EPS)
        return center * inverse, mean, inverse

    def both(ref, c):
        at, size = chunks[c]
        return jnp.concatenate((ref[at : at + size], ref[half + at : half + at + size]), 0)

    def put(ref, c, value):
        at, size = chunks[c]
        ref[at : at + size] = value[:size]
        ref[half + at : half + at + size] = value[size:]

    def add(i, value):
        r.running[i] += value.reshape(value.shape[0] // 8, 8, value.shape[1]).sum(0)

    r.running[...] = jnp.zeros_like(r.running)
    r.qkv_shift[...] = jnp.zeros_like(r.qkv_shift)
    r.qkv_shift[:, :inner] = r.query_bias[...].astype(f32).reshape(1, inner)
    r.qkv_shift[:, 2 * inner :] = r.value_bias[...].astype(f32).reshape(1, inner)
    r.hidden_shift[...] = r.fc1_bias[...].astype(f32).reshape(r.hidden_shift.shape)
    for c in range(count):
        normal, mean, inverse = moments(both(r.kept, c).astype(f32))
        put(r.mean[0], c, mean)
        put(r.inverse[0], c, inverse)
        normed = (normal * vector(0) + vector(1)).astype(bf16)
        put(r.normed[0], c, normed)
        projected = dot(normed, r.whole[0][:, : 3 * inner], 1, 0) + r.qkv_shift[...]
        put(r.qkv, c, projected.astype(bf16))

    def weights_of(h):
        part = slice(h * HEAD_DIM, (h + 1) * HEAD_DIM)
        keys = slice(inner + h * HEAD_DIM, inner + (h + 1) * HEAD_DIM)
        scores = dot(r.qkv[:, part], r.qkv[:, keys], 1, 1) * factor
        scores = scores + r.bias[h, :, :rows].astype(f32)
        weights = jnp.exp(scores - jnp.max(scores, -1, keepdims=True))
        return weights * (1.0 / jnp.sum(weights, -1, keepdims=True))

    for h in range(heads):
        for event in late_floods if h == heads - 1 else ():
            event()
        part = slice(h * HEAD_DIM, (h + 1) * HEAD_DIM)
        values = slice(2 * inner + h * HEAD_DIM, 2 * inner + (h + 1) * HEAD_DIM)
        r.attended[:, part] = dot(weights_of(h).astype(bf16), r.qkv[:, values], 1, 0).astype(bf16)

    def out_turned():
        return r.whole[0][:, 3 * inner :]

    def live_rows(c):
        at, size = chunks[c]
        first = lax.broadcasted_iota(jnp.int32, (size, 1), 0) + at
        places = jnp.concatenate((first, first + half), 0).astype(f32)
        return jnp.where(places < r.slot[1:2, 0:1], 1.0, 0.0)

    def padded(ref, c):
        at, size = chunks[c]
        last = min(half + at + size, slot_rows)
        low = ref[half + at : last]
        missing = half + at + size - last
        if missing:
            low = jnp.concatenate(
                (low.astype(f32), jnp.zeros((missing, low.shape[1]), f32)), 0
            )
        return jnp.concatenate((ref[at : at + size].astype(f32), low.astype(f32)), 0)

    def keep(ref, c, value):
        at, size = chunks[c]
        last = min(half + at + size, slot_rows)
        ref[at : at + size] = value[:size]
        ref[half + at : last] = value[size : size + last - half - at]

    def project(c):
        put(r.part[0], c, dot(both(r.attended, c), out_turned(), 1, 1))
        sums[0].first(c).start()

    def forward(c):
        if c == 0:
            floods[1].arrive()
        sums[0].third(c).wait_recv()
        middle = both(r.kept, c).astype(f32) + vector(3) * (both(r.total[0], c) + vector(2))
        put(r.middle, c, middle)
        normal, mean, inverse = moments(middle)
        put(r.mean[1], c, mean)
        put(r.inverse[1], c, inverse)
        normed = (normal * vector(4) + vector(5)).astype(bf16)
        put(r.normed[1], c, normed)
        hidden = dot(normed, r.whole[1][...], 1, 0) + r.hidden_shift[...]
        cumulative = 0.5 * (1.0 + lax.erf(hidden * 0.7071067811865476))
        put(
            r.slope,
            c,
            cumulative + hidden * jnp.exp(-0.5 * hidden * hidden) * 0.3989422804014327,
        )
        active = (hidden * cumulative).astype(bf16)
        put(r.active, c, active)
        if c == 0:
            floods[2].arrive()
        put(r.part[1], c, dot(active, r.whole[2][...], 1, 1))
        sums[1].first(c).start()
        grad_result = (padded(r.grad_here, c) * live_rows(c) * vector(7)).astype(bf16)
        put(r.grad_result, c, grad_result)
        add(5, grad_result.astype(f32))
        grad_hidden = (dot(grad_result, r.whole[2][...], 1, 0) * both(r.slope, c)).astype(bf16)
        put(r.grad_hidden, c, grad_hidden)
        add(0, grad_hidden.astype(f32))
        put(r.part[2], c, dot(grad_hidden, r.whole[1][...], 1, 1))
        sums[2].first(c).start()

    def results():
        for c in range(count):
            sums[1].third(c).wait_recv()
            result = both(r.total[1], c) + vector(6)
            live = live_rows(c)
            keep(r.out_here, c, (live * (both(r.middle, c) + vector(7) * result)).astype(bf16))
            add(6, padded(r.grad_here, c) * live * result)
        to_owners(5, r.running[6])
        store.start()

    def back_norm(grad, normal, inverse, gain):
        scaled = grad * gain
        along = jnp.mean(scaled * normal, -1, keepdims=True)
        return inverse * (scaled - jnp.mean(scaled, -1, keepdims=True) - normal * along)

    def backward(c):
        sums[2].third(c).wait_recv()
        grad = both(r.total[2], c)
        inverse = both(r.inverse[1], c)
        normal = (both(r.middle, c) - both(r.mean[1], c)) * inverse
        add(3, grad * normal)
        add(4, grad)
        grad_middle = padded(r.grad_here, c) * live_rows(c)
        grad_middle = grad_middle + back_norm(grad, normal, inverse, vector(4))
        put(r.grad_middle, c, grad_middle)
        add(2, grad_middle * (both(r.total[0], c) + vector(2)))
        grad_branch = (grad_middle * vector(3)).astype(bf16)
        put(r.grad_branch, c, grad_branch)
        add(1, grad_branch.astype(f32))
        put(r.grad_attended, c, dot(grad_branch, out_turned(), 1, 0).astype(bf16))

    def close(work):
        return lambda c: work.close_one(c)

    def cross(work):
        return lambda c: work.cross_one(c)

    stages = [project, cross(sums[0]), close(sums[0]), forward]
    stages += [cross(sums[2]), close(sums[2]), backward]

    def weight_grad(j, left, right, at=0):
        value = dot(left[...], right[...], 0, 0).astype(bf16)
        r.grad[j][:, at : at + value.shape[1]] = value

    def send_grads(j):
        for s in range(length - 1, -1, -1):
            scatters[j].start(s)

    for t in range(count + len(stages) - 1):
        for k in range(len(stages) - 1, -1, -1):
            if 0 <= t - k < count:
                stages[k](t - k)
        if t == count + 2:
            weight_grad(2, r.grad_result, r.active)
            send_grads(2)
        if t == count + 3:
            sums[1].cross()
            weight_grad(1, r.normed[1], r.grad_hidden)
            send_grads(1)

    store = pltpu.make_async_copy(r.out_here, r.layer_out, r.load_sem.at[0])
    weight_grad(0, r.grad_branch, r.attended, 3 * inner)
    steps = list(range(length - 1, -1, -1))
    for h in range(heads):
        part = slice(h * HEAD_DIM, (h + 1) * HEAD_DIM)
        keys = slice(inner + h * HEAD_DIM, inner + (h + 1) * HEAD_DIM)
        values = slice(2 * inner + h * HEAD_DIM, 2 * inner + (h + 1) * HEAD_DIM)
        weights = weights_of(h)
        grad_part = r.grad_attended[:, part]
        r.grad_qkv[:, values] = dot(weights.astype(bf16), grad_part, 0, 0).astype(bf16)
        grad = dot(grad_part, r.qkv[:, values], 1, 1)
        mean = jnp.sum(weights * grad, -1, keepdims=True)
        grad = (weights * (grad - mean)).astype(bf16)
        r.bias[h, :, :rows] = grad
        r.grad_qkv[:, part] = (dot(grad, r.qkv[:, keys], 1, 0) * factor).astype(bf16)
        r.grad_qkv[:, keys] = (dot(grad, r.qkv[:, part], 0, 0) * factor).astype(bf16)
        if h == 0:
            scatters[2].step(steps[0])

    def scatter_event(j, s):
        return lambda: scatters[j].step(s)

    order = [(2, s) for s in steps[1:]] + [(j, s) for j in (1, 0) for s in steps]
    places = TABLE_PLACES if length == 4 else [4 * k for k in range(len(order))]
    events = [(at, scatter_event(*item)) for at, item in zip(places, order)]
    for at, event in events:
        if at < 0:
            event()
    events = [(at, event) for at, event in events if at >= 0]

    sums[0].drain()
    last = sums[0]
    for c in range(count):
        put(r.part[0], c, dot(both(r.grad_qkv, c), r.whole[0][:, : 3 * inner], 1, 1))
        last.first(c).start()
    weight_grad(0, r.normed[0], r.grad_qkv)
    send_grads(0)

    wide = model // LANES
    at = 1
    r.own_early[...] = jnp.zeros_like(r.own_early)
    r.own_early[0:1] = r.slot[0:1, :]

    def line_to(at, line):
        for c in range(-(-line.shape[1] // LANES)):
            piece = line[:, c * LANES : (c + 1) * LANES]
            r.own_early[at + c : at + c + 1, : piece.shape[1]] = piece

    for line in (
        jnp.sum(r.running[0], 0, keepdims=True),
        jnp.sum(r.grad_qkv[:, :inner].astype(f32), 0, keepdims=True),
        jnp.sum(r.grad_qkv[:, 2 * inner :].astype(f32), 0, keepdims=True),
    ):
        line_to(at, line)
        at += up_to(line.shape[1], LANES) // LANES
    spreads[0].start(lambda peer: r.own_early)

    def to_owners(i, value):
        line = jnp.sum(value, 0, keepdims=True)
        for d in range(peers):
            r.own_late[d, i : i + 1, :depth] = line[:, d * depth : (d + 1) * depth]

    r.own_late[...] = jnp.zeros_like(r.own_late)
    for i in range(1, 6):
        to_owners(i - 1, r.running[i])
    r.table_sums[...] = jnp.zeros_like(r.table_sums)

    def norm_step(here, out_rows):
        grad = r.total[0][here]
        normal = (r.kept[here].astype(f32) - r.mean[0][here]) * r.inverse[0][here]
        back = back_norm(grad, normal, r.inverse[0][here], vector(0))
        value = (r.grad_middle[here] + back).astype(bf16)
        if out_rows is None:
            r.input_grad[here] = value
        else:
            r.input_grad[out_rows] = value[:tail]
        product = (grad * normal).reshape(4, 8, model).sum(0)
        return product, grad.reshape(4, 8, model).sum(0)

    def norm_rows():
        last.arrive()

        def step(i, totals):
            gain, shift = norm_step(pl.ds(pl.multiple_of(i * 32, 32), 32), None)
            return totals[0] + gain, totals[1] + shift

        zero = jnp.zeros((8, model), f32)
        gain, shift = lax.fori_loop(0, body_rows // 32, step, (zero, zero))
        if tail:
            more = norm_step(slice(body_rows, rows), slice(body_rows, slot_rows))
            gain, shift = gain + more[0], shift + more[1]
        to_owners(6, gain)
        to_owners(7, shift)

    events += [(0, last.cross), (FIRST_CLOSE, sums[1].close), (RESULT_PLACE, results)]
    events += [(CLOSE_PLACE, last.close), (NORM_PLACE, norm_rows)]
    events.sort(key=lambda item: item[0])
    with_events(
        blocks,
        [(at, event) for at, event in events if at < blocks],
        lambda block: table_block(
            heads,
            groups,
            r.index,
            r.bias,
            r.table_sums,
            pl.ds(pl.multiple_of(block * ROW_STEP, ROW_STEP), ROW_STEP),
        ),
    )
    r.own_table[...] = r.table_sums[...].astype(bf16)
    spreads[2].start(lambda peer: r.own_table)
    spreads[1].start(lambda peer: r.own_late.at[peer])
    for at, event in events:
        if at >= blocks:
            event()
    r.all_early[grid.me] = r.own_early[...]
    r.all_late[grid.me] = r.own_late[grid.me]
    r.all_table[grid.me] = r.own_table[...]
    for spread in spreads:
        spread.arrive()
    early = jnp.zeros(r.early_sums.shape, f32)
    late = jnp.zeros(r.late_sums.shape, f32)
    small = jnp.zeros((height, LANES), f32)
    large = jnp.zeros((height, LANES), f32)
    for d in range(peers):
        kind = r.all_early[d, 0:1] > 0.5
        table = r.all_table[d].astype(f32)
        small += jnp.where(kind, 0.0, table)
        large += jnp.where(kind, table, 0.0)
        early += r.all_early[d]
        late += r.all_late[d]
    r.early_sums[...] = early
    r.late_sums[...] = late
    for out, value in ((r.small_sums, small), (r.large_sums, large)):
        entries = out.shape[1]
        for k in range(-(-entries // SPLIT)):
            first, size = k * SPLIT, min(SPLIT, entries - k * SPLIT)
            for h in range(heads):
                at = h * groups + k
                out[h : h + 1, first : first + size] = value[at : at + 1, :size]
    store.wait()
    for work in sums + floods + [lines] + scatters + spreads:
        work.drain()


def layer(arguments, peers, slot_rows):
    model = arguments["inputs"].shape[1]
    rows = up_to(slot_rows, 32)
    columns = up_to(rows, LANES)
    depth = model // peers
    hidden = arguments["fc1_bias"].shape[0]
    inner = arguments["query_bias"].shape[0]
    widths = [4 * inner, hidden, hidden]
    heads = inner // HEAD_DIM
    tables = [arguments["small_table"].shape, arguments["large_table"].shape]
    entries = up_to(max(shape[1] for shape in tables), LANES)
    groups = up_to(-(-entries // SPLIT), 16)
    height = heads * groups
    count = len(cuts_of(rows // 2, CHUNKS))
    length = peers // 2
    array = jax.ShapeDtypeStruct

    def sems(*shape):
        return pltpu.SemaphoreType.DMA(shape)

    def each(kind, shape, times):
        return [pltpu.VMEM(shape, kind) for _ in range(times)]

    outs = dict(
        layer_out=array((slot_rows, model), bf16),
        input_grad=array((slot_rows, model), bf16),
        small_sums=array(tables[0], f32),
        large_sums=array(tables[1], f32),
        early_sums=array((EARLY_LINES, LANES), f32),
        late_sums=array((VECTORS, LANES), f32),
        summed=[array((depth, w), f32) for w in widths],
    )
    blocks = [pltpu.VMEM((length, depth, w), bf16) for w in widths]
    scratch = dict(
        whole=[pltpu.VMEM((model, w), bf16) for w in widths],
        all_lines=pltpu.VMEM((peers * VECTORS, LANES), f32),
        grad=[pltpu.VMEM((model, w), bf16) for w in widths],
        side=blocks,
        up=blocks,
        down=blocks,
        scatter_sems=[[sems(length)] * 6] * 3,
        flood_sems=[[sems(length)] * 6] * 4,
        spread_sems=[[sems(peers)] * 2] * 3,
        part=each(f32, (rows, model), 3),
        total=each(f32, (rows, model), 3),
        near=each(f32, (rows // 2, model), 3),
        sent=each(bf16, (rows // 2, model), 3),
        far=each(bf16, (rows // 2, model), 3),
        sum_send=[sems(3, count)] * 3,
        sum_recv=[sems(3, count)] * 3,
        local_sem=sems(4),
        load_sem=sems(3),
        wide_from=pltpu.VMEM(arguments["large_index"].shape, jnp.int32),
        inputs_here=pltpu.VMEM((slot_rows, model), bf16),
        grad_here=pltpu.VMEM((slot_rows, model), bf16),
        out_here=pltpu.VMEM((slot_rows, model), bf16),
        own_first=pltpu.VMEM((depth, 4 * inner), bf16),
        own_lines=pltpu.VMEM((VECTORS, LANES), f32),
        slot=pltpu.VMEM((2, LANES), f32),
        hidden_shift=pltpu.VMEM((1, hidden), f32),
        index=pltpu.VMEM((rows, columns), jnp.int32),
        wide_index=pltpu.VMEM((rows, columns), jnp.int32),
        table=pltpu.VMEM((8, entries), f32),
        wide_table=pltpu.VMEM((8, entries), f32),
        bias=pltpu.VMEM((heads, rows, columns), bf16),
        vectors=pltpu.VMEM((VECTORS, model), f32),
        qkv_shift=pltpu.VMEM((1, 3 * inner), f32),
        running=pltpu.VMEM((7, 8, max(model, hidden)), f32),
        mean=each(f32, (rows, 1), 2),
        inverse=each(f32, (rows, 1), 2),
        normed=each(bf16, (rows, model), 2),
        kept=pltpu.VMEM((rows, model), bf16),
        grad_result=pltpu.VMEM((rows, model), bf16),
        grad_branch=pltpu.VMEM((rows, model), bf16),
        active=pltpu.VMEM((rows, hidden), bf16),
        grad_hidden=pltpu.VMEM((rows, hidden), bf16),
        qkv=pltpu.VMEM((rows, 3 * inner), bf16),
        grad_qkv=pltpu.VMEM((rows, 3 * inner), bf16),
        attended=pltpu.VMEM((rows, inner), bf16),
        grad_attended=pltpu.VMEM((rows, inner), bf16),
        middle=pltpu.VMEM((rows, model), f32),
        grad_middle=pltpu.VMEM((rows, model), f32),
        slope=pltpu.VMEM((rows, hidden), f32),
        table_sums=pltpu.VMEM((height, LANES), f32),
        own_table=pltpu.VMEM((height, LANES), bf16),
        all_table=pltpu.VMEM((peers, height, LANES), bf16),
        own_early=pltpu.VMEM((EARLY_LINES, LANES), f32),
        all_early=pltpu.VMEM((peers, EARLY_LINES, LANES), f32),
        own_late=pltpu.VMEM((peers, VECTORS, LANES), f32),
        all_late=pltpu.VMEM((peers, VECTORS, LANES), f32),
    )
    flat = jax.tree.leaves(arguments)
    near, apart = pl.BlockSpec(memory_space=pltpu.VMEM), pl.BlockSpec(memory_space=pl.ANY)
    specs = jax.tree.map(lambda _: near, arguments)
    specs.update(inputs=apart, out_grad=apart, large_index=apart)
    specs.update(slot_kind=pl.BlockSpec(memory_space=pltpu.SMEM))
    out_specs = jax.tree.map(lambda _: near, outs)
    out_specs.update(layer_out=apart)
    shapes, out_tree = jax.tree.flatten(outs)
    tree = jax.tree.structure((arguments, outs, scratch))
    results = pl.pallas_call(
        functools.partial(layer_body, (tree, heads, groups, slot_rows, peers)),
        out_shape=shapes,
        in_specs=jax.tree.leaves(specs),
        out_specs=jax.tree.leaves(out_specs),
        scratch_shapes=jax.tree.leaves(scratch),
        compiler_params=params(collective_id=0, has_side_effects=True),
        name="layer",
    )(*flat)
    return types.SimpleNamespace(**jax.tree.unflatten(out_tree, results))


def finish_body(tree, depth, *refs):
    found, out = (types.SimpleNamespace(**part) for part in jax.tree.unflatten(tree, refs))
    pairs = (
        (found.layer_out, out.layer_out),
        (found.input_grad, out.input_grad),
        (found.summed[1], out.fc1),
        (found.summed[2], out.fc2),
        (found.small_sums, out.small_table),
        (found.large_sums, out.large_table),
    )
    for src, dst in pairs:
        dst[...] = src[...]
    inner = out.query_bias.shape[0]
    for j in range(3):
        out.qkv[j] = found.summed[0][:, j * inner : (j + 1) * inner]
    out.out[...] = found.summed[0][:, 3 * inner :].T
    for i, vector in enumerate(out.vectors):
        vector[...] = found.late_sums[i, :depth]
    at = 1
    for line in (out.fc1_bias, out.query_bias, out.value_bias):
        size = line.shape[0]
        for first in range(0, size, LANES):
            count = min(LANES, size - first)
            line[pl.ds(first, count)] = found.early_sums[at, :count]
            at += 1


def finish(found, depth, inner, hidden):
    array = jax.ShapeDtypeStruct
    found = vars(found)
    outs = dict(
        layer_out=array(found["layer_out"].shape, bf16),
        input_grad=array(found["input_grad"].shape, bf16),
        fc1=array(found["summed"][1].shape, f32),
        fc2=array(found["summed"][2].shape, f32),
        small_table=array(found["small_sums"].shape, f32),
        large_table=array(found["large_sums"].shape, f32),
        qkv=array((3, depth, inner), f32),
        out=array((inner, depth), f32),
        vectors=[array((depth,), f32)] * VECTORS,
        fc1_bias=array((hidden,), f32),
        query_bias=array((inner,), f32),
        value_bias=array((inner,), f32),
    )
    shapes, out_tree = jax.tree.flatten(outs)
    results = pl.pallas_call(
        functools.partial(finish_body, jax.tree.structure((found, outs)), depth),
        out_shape=shapes,
        in_specs=in_vmem(len(jax.tree.leaves(found))),
        out_specs=in_vmem(len(shapes)),
        compiler_params=params(),
        name="finish",
    )(*jax.tree.leaves(found))
    return types.SimpleNamespace(**jax.tree.unflatten(out_tree, results))


def layer_norm(activations, norm_gain, norm_shift):
    center = activations - jnp.mean(activations, -1, keepdims=True)
    inverse = lax.rsqrt(jnp.mean(center * center, -1, keepdims=True) + EPS)
    normal = center * inverse
    return (normal * norm_gain + norm_shift, normal, inverse)


def norm_back(grad_normed, normal, inverse, norm_gain):
    scaled = grad_normed * norm_gain
    return inverse * (
        scaled
        - jnp.mean(scaled, -1, keepdims=True)
        - normal * jnp.mean(scaled * normal, -1, keepdims=True)
    )


def gelu_slope(hidden):
    cumulative = 0.5 * (1.0 + jax.scipy.special.erf(hidden * 0.7071067811865476))
    return cumulative + hidden * jnp.exp(-0.5 * hidden * hidden) * 0.3989422804014327


def pair_map(kind, small_index, large_index, rows, columns):
    def placed(index, at):
        side = index.shape[0]
        return jnp.pad(
            index, ((at, rows - at - side), (at, columns - at - side)), constant_values=-1
        )

    length = small_index.shape[0]
    small = placed(small_index, 0)
    for image in range(1, SLOT_ROWS // length):
        small = jnp.maximum(small, placed(small_index, image * length))
    return jnp.where(kind == 1, placed(large_index, 0), small)


def plain_device(
    images,
    out_grad,
    slot_kind,
    small_index,
    large_index,
    qkv_weight,
    out_weight,
    fc1_weight,
    fc2_weight,
    norm1_gain,
    norm1_shift,
    query_bias,
    value_bias,
    out_bias,
    gamma_attn,
    norm2_gain,
    norm2_shift,
    fc1_bias,
    fc2_bias,
    gamma_mlp,
    small_table,
    large_table,
):
    depth = qkv_weight.shape[0]
    width = query_bias.shape[0]
    hidden_width = fc1_bias.shape[0]
    heads = width // HEAD_DIM
    _, slot_rows, model_width = images.shape
    rows = up_to(slot_rows, 32)
    columns = up_to(rows, LANES)
    kind = slot_kind[0]

    block = jnp.concatenate(
        (
            qkv_weight.reshape(depth, 3 * width),
            fc1_weight,
            out_weight.T,
            fc2_weight.T,
        ),
        1,
    )
    whole = lax.all_gather(block, "dp", axis=0, tiled=True)
    cuts = (3 * width, 3 * width + hidden_width, 4 * width + hidden_width)
    qkv_matrix = whole[:, : cuts[0]]
    fc1_matrix = whole[:, cuts[0] : cuts[1]]
    out_turned = whole[:, cuts[1] : cuts[2]]
    fc2_turned = whole[:, cuts[2] :]
    small_vectors = jnp.stack(
        (norm1_gain, norm1_shift, out_bias, gamma_attn, norm2_gain, norm2_shift, fc2_bias, gamma_mlp)
    )
    vectors = lax.all_gather(small_vectors, "dp", axis=0)
    vectors = jnp.moveaxis(vectors, 0, 1).reshape(8, model_width).astype(f32)

    query_shift = query_bias.astype(f32)
    value_shift = value_bias.astype(f32)
    hidden_shift = fc1_bias.astype(f32)
    small_entries, large_entries = small_table.shape[0], large_table.shape[0]
    entries = up_to(max(small_entries, large_entries), LANES)
    table = jnp.where(
        kind == 1,
        jnp.pad(large_table, ((0, entries - large_entries), (0, 0))),
        jnp.pad(small_table, ((0, entries - small_entries), (0, 0))),
    )
    table = table.T.astype(f32)
    pair_index = pair_map(kind, small_index, large_index, rows, columns)
    bias = gather_bias(pair_index, table)

    positions = jnp.arange(rows)
    live_count = jnp.where(kind == 1, LARGE_LEN, slot_rows)
    live_rows = (positions < live_count).astype(f32).reshape(-1, 1)
    inputs = jnp.pad(images[0], ((0, rows - slot_rows), (0, 0))).astype(f32)
    normed_one, normal_one, inverse_one = layer_norm(inputs, vectors[0], vectors[1])
    normed_one = normed_one.astype(bf16)
    projected = dot(normed_one, qkv_matrix, 1, 0)
    queries = (projected[:, :width] + query_shift).astype(bf16)
    keys = projected[:, width : 2 * width].astype(bf16)
    values = (projected[:, 2 * width :] + value_shift).astype(bf16)
    pieces = attend_forward(queries, keys, values, bias)
    branch_part = dot(pieces, out_turned, 1, 1)
    branch = lax.psum(branch_part, "shard") + vectors[2]
    middle = inputs + vectors[3] * branch
    normed_two, normal_two, inverse_two = layer_norm(middle, vectors[4], vectors[5])
    normed_two = normed_two.astype(bf16)
    hidden = dot(normed_two, fc1_matrix, 1, 0) + hidden_shift
    active = jax.nn.gelu(hidden, approximate=False).astype(bf16)
    result_part = dot(active, fc2_turned, 1, 1)
    result = lax.psum(result_part.astype(bf16), "shard").astype(f32) + vectors[6]
    layer_out = ((middle + vectors[7] * result) * live_rows).astype(bf16)[:slot_rows][None]

    grad_out = jnp.pad(out_grad[0], ((0, rows - slot_rows), (0, 0))).astype(f32) * live_rows
    grad_gamma_mlp = jnp.sum(grad_out * result, 0)
    grad_result = (grad_out * vectors[7]).astype(bf16)
    grad_fc2_bias = jnp.sum(grad_result.astype(f32), 0)
    grad_fc2_turned = dot(grad_result, active, 0, 0)
    grad_active = dot(grad_result, fc2_turned, 1, 0)
    grad_hidden = (grad_active * gelu_slope(hidden)).astype(bf16)
    grad_fc1_bias = jnp.sum(grad_hidden.astype(f32), 0)
    grad_fc1 = dot(normed_two, grad_hidden, 0, 0)
    grad_normed_two = lax.psum(dot(grad_hidden, fc1_matrix, 1, 1), "shard")
    grad_norm2_gain = jnp.sum(grad_normed_two * normal_two, 0)
    grad_norm2_shift = jnp.sum(grad_normed_two, 0)
    grad_middle = grad_out + norm_back(grad_normed_two, normal_two, inverse_two, vectors[4])
    grad_gamma_attn = jnp.sum(grad_middle * branch, 0)
    grad_branch = (grad_middle * vectors[3]).astype(bf16)
    grad_out_bias = jnp.sum(grad_branch.astype(f32), 0)
    grad_out_turned = dot(grad_branch, pieces, 0, 0)
    grad_attended = dot(grad_branch, out_turned, 1, 0).astype(bf16)
    grad_queries, grad_keys, grad_values, grad_scores = attend_backward(
        queries, keys, values, bias, grad_attended
    )
    sums = table_sums(pair_index, grad_scores, entries)
    grad_projected = jnp.concatenate((grad_queries, grad_keys, grad_values), 1)
    grad_qkv = dot(normed_one, grad_projected, 0, 0)
    grad_query_bias = jnp.sum(grad_queries.astype(f32), 0)
    grad_value_bias = jnp.sum(grad_values.astype(f32), 0)
    grad_normed_one = lax.psum(dot(grad_projected, qkv_matrix, 1, 1), "shard")
    grad_norm1_gain = jnp.sum(grad_normed_one * normal_one, 0)
    grad_norm1_shift = jnp.sum(grad_normed_one, 0)
    input_grad = grad_middle + norm_back(grad_normed_one, normal_one, inverse_one, vectors[0])
    input_grad = input_grad.astype(bf16)[:slot_rows][None]

    small_sums = jnp.where(kind == 1, 0.0, sums[:, :small_entries])
    large_sums = jnp.where(kind == 1, sums[:, :large_entries], 0.0)
    local_sums = lax.psum(
        (small_sums, large_sums, grad_query_bias, grad_value_bias, grad_fc1_bias), "dp"
    )
    peers = lax.axis_size("dp")

    def sent_and_summed(value):
        parts = value.astype(bf16).reshape(peers, value.shape[0] // peers, -1)
        arrived = lax.all_to_all(parts, "dp", split_axis=0, concat_axis=0, tiled=True)
        return arrived.astype(f32).sum(axis=0)

    grad_block = sent_and_summed(
        jnp.concatenate((grad_qkv, grad_fc1, grad_out_turned, grad_fc2_turned), 1)
    )
    vector_grads = sent_and_summed(
        jnp.stack(
            (
                grad_norm1_gain,
                grad_norm1_shift,
                grad_out_bias,
                grad_gamma_attn,
                grad_norm2_gain,
                grad_norm2_shift,
                grad_fc2_bias,
                grad_gamma_mlp,
            ),
            1,
        )
    )
    return (
        layer_out,
        input_grad,
        grad_block[:, : cuts[0]].reshape(depth, 3, width),
        grad_block[:, cuts[1] : cuts[2]].T,
        grad_block[:, cuts[0] : cuts[1]],
        grad_block[:, cuts[2] :].T,
        vector_grads[:, 0],
        vector_grads[:, 1],
        local_sums[2],
        local_sums[3],
        vector_grads[:, 2],
        vector_grads[:, 3],
        vector_grads[:, 4],
        vector_grads[:, 5],
        local_sums[4],
        vector_grads[:, 6],
        vector_grads[:, 7],
        local_sums[0].T,
        local_sums[1].T,
    )


def on_device(*arguments):
    depth = arguments[5].shape[0]
    if depth % 16 or lax.axis_size("shard") != 4:
        return plain_device(*arguments)
    return whole_device(*arguments)


def whole_device(
    images,
    out_grad,
    slot_kind,
    small_index,
    large_index,
    qkv_weight,
    out_weight,
    fc1_weight,
    fc2_weight,
    norm1_gain,
    norm1_shift,
    query_bias,
    value_bias,
    out_bias,
    gamma_attn,
    norm2_gain,
    norm2_shift,
    fc1_bias,
    fc2_bias,
    gamma_mlp,
    small_table,
    large_table,
):
    depth = qkv_weight.shape[0]
    found = layer(
        dict(
            inputs=images[0],
            out_grad=out_grad[0],
            slot_kind=slot_kind,
            small_index=small_index,
            large_index=large_index,
            small_table=small_table.T,
            large_table=large_table.T,
            qkv_weight=qkv_weight.transpose(1, 0, 2),
            out_weight=out_weight,
            fc1_weight=fc1_weight,
            fc2_weight=fc2_weight.T,
            small_vectors=[
                norm1_gain,
                norm1_shift,
                out_bias,
                gamma_attn,
                norm2_gain,
                norm2_shift,
                fc2_bias,
                gamma_mlp,
            ],
            query_bias=query_bias,
            value_bias=value_bias,
            fc1_bias=fc1_bias,
        ),
        lax.axis_size("dp"),
        images.shape[1],
    )
    out = finish(found, depth, query_bias.shape[0], fc1_bias.shape[0])
    return (
        out.layer_out[None],
        out.input_grad[None],
        out.qkv.transpose(1, 0, 2),
        out.out,
        out.fc1,
        out.fc2.T,
        out.vectors[6],
        out.vectors[7],
        out.query_bias,
        out.value_bias,
        out.vectors[0],
        out.vectors[1],
        out.vectors[2],
        out.vectors[3],
        out.fc1_bias,
        out.vectors[4],
        out.vectors[5],
        out.small_table.T,
        out.large_table.T,
    )


def solution(mesh):
    return jax.shard_map(
        on_device,
        mesh=mesh,
        in_specs=(
            P("dp", None, None),
            P("dp", None, None),
            P("dp"),
            P(),
            P(),
            P("dp", None, "shard"),
            P("shard", "dp"),
            P("dp", "shard"),
            P("shard", "dp"),
            P("dp"),
            P("dp"),
            P("shard"),
            P("shard"),
            P("dp"),
            P("dp"),
            P("dp"),
            P("dp"),
            P("shard"),
            P("dp"),
            P("dp"),
            P(None, "shard"),
            P(None, "shard"),
        ),
        out_specs=(
            P("dp", None, None),
            P("dp", None, None),
            P("dp", None, "shard"),
            P("shard", "dp"),
            P("dp", "shard"),
            P("shard", "dp"),
            P("dp"),
            P("dp"),
            P("shard"),
            P("shard"),
            P("dp"),
            P("dp"),
            P("dp"),
            P("dp"),
            P("shard"),
            P("dp"),
            P("dp"),
            P(None, "shard"),
            P(None, "shard"),
        ),
        check_vma=False,
    )
```

```python
import functools
import types

import jax
import jax.numpy as jnp
from jax import lax
from jax.experimental import pallas as pl
from jax.experimental.pallas import tpu as pltpu
from jax.sharding import PartitionSpec as P

HEAD_DIM = 64
SMALL_LEN = 197
LARGE_LEN = 577
SLOT_ROWS = 591
EPS = 1e-06
NEG = -1e30
LANES = 128
SPLIT = 80
VMEM_LIMIT = 60 << 20

MESH = pl.DeviceIdType.MESH

f32 = jnp.float32
bf16 = jnp.bfloat16


def up_to(value, unit):
    return -(-value // unit) * unit


def in_vmem(count):
    return [pl.BlockSpec(memory_space=pltpu.VMEM)] * count


def params(**more):
    return pltpu.CompilerParams(vmem_limit_bytes=VMEM_LIMIT, **more)


def dot(a, b, da, db):
    return lax.dot_general(a, b, (((da,), (db,)), ((), ())), preferred_element_type=f32)


def bias_block_of(heads, index_ref, table_ref, out_ref, here):
    columns, entries = index_ref.shape[1], table_ref.shape[1]
    for c in range(columns // LANES):
        there = pl.ds(c * LANES, LANES)
        index = index_ref[here, there]
        high = lax.shift_right_arithmetic(index, 7)
        low = lax.bitwise_and(index, LANES - 1)
        found = [jnp.full(index.shape, NEG, f32) for _ in range(heads)]
        for k in range(entries // LANES):
            match = high == k
            for h in range(heads):
                line = table_ref[h : h + 1, k * LANES : (k + 1) * LANES]
                values = jnp.take_along_axis(jnp.broadcast_to(line, index.shape), low, axis=1)
                found[h] = jnp.where(match, values, found[h])
        for h in range(heads):
            out_ref[h, here, there] = found[h].astype(bf16)


def table_block(heads, groups, index_ref, grad_ref, out_ref, here):
    columns = index_ref.shape[1]
    inverse = -(-(1 << 22) // SPLIT)
    index = index_ref[here, :]
    high = lax.shift_right_arithmetic(index * inverse, 22)
    low = (index - high * SPLIT).astype(jnp.int16)
    high = high.astype(jnp.int16)
    grads = [grad_ref[h, here, :] for h in range(heads)]
    places_low = lax.broadcasted_iota(jnp.int16, (SPLIT, columns), 0)
    places_high = lax.broadcasted_iota(jnp.int16, (groups, columns), 0)
    one, zero = jnp.ones((), bf16), jnp.zeros((), bf16)
    total = jnp.zeros((heads * groups, SPLIT), f32)
    for pair in range(0, 16, 2):
        lows, highs = [], []
        for i in (pair, pair + 1):
            lows.append(
                jnp.where(
                    places_low == jnp.broadcast_to(low[i : i + 1], (SPLIT, columns)), one, zero
                )
            )
            match = places_high == jnp.broadcast_to(high[i : i + 1], (groups, columns))
            highs.append(
                jnp.concatenate(
                    [
                        jnp.where(
                            match,
                            jnp.broadcast_to(grads[h][i : i + 1], (groups, columns)),
                            zero,
                        )
                        for h in range(heads)
                    ],
                    0,
                )
            )
        total = total + dot(jnp.concatenate(highs, 1), jnp.concatenate(lows, 1), 1, 1)
    out_ref[: heads * groups, :SPLIT] += total


def forward_body(heads, q_ref, k_ref, v_ref, bias_ref, out_ref):
    rows = q_ref.shape[0]
    for h in range(heads):
        part = slice(h * HEAD_DIM, (h + 1) * HEAD_DIM)
        scores = dot(q_ref[:, part], k_ref[:, part], 1, 1) * HEAD_DIM ** (-0.5)
        scores = scores + bias_ref[h, :, :rows].astype(f32)
        weights = jnp.exp(scores - jnp.max(scores, -1, keepdims=True))
        weights = weights / jnp.sum(weights, -1, keepdims=True)
        out_ref[:, part] = dot(weights.astype(bf16), v_ref[:, part], 1, 0).astype(bf16)


def backward_body(
    heads, q_ref, k_ref, v_ref, bias_ref, grad_ref, dq_ref, dk_ref, dv_ref, ds_ref
):
    rows = q_ref.shape[0]
    factor = HEAD_DIM ** (-0.5)
    for h in range(heads):
        part = slice(h * HEAD_DIM, (h + 1) * HEAD_DIM)
        scores = dot(q_ref[:, part], k_ref[:, part], 1, 1) * factor
        scores = scores + bias_ref[h, :, :rows].astype(f32)
        weights = jnp.exp(scores - jnp.max(scores, -1, keepdims=True))
        weights = weights / jnp.sum(weights, -1, keepdims=True)
        dv_ref[:, part] = dot(weights.astype(bf16), grad_ref[:, part], 0, 0).astype(bf16)
        grad = dot(grad_ref[:, part], v_ref[:, part], 1, 1)
        mean = jnp.sum(weights * grad, -1, keepdims=True)
        grad = (weights * (grad - mean)).astype(bf16)
        ds_ref[h, :, :rows] = grad
        dq_ref[:, part] = (dot(grad, k_ref[:, part], 1, 0) * factor).astype(bf16)
        dk_ref[:, part] = (dot(grad, q_ref[:, part], 0, 0) * factor).astype(bf16)


def attend_forward(queries, keys, values, bias):
    heads = bias.shape[0]
    return pl.pallas_call(
        functools.partial(forward_body, heads),
        out_shape=jax.ShapeDtypeStruct(queries.shape, bf16),
        in_specs=in_vmem(4),
        out_specs=in_vmem(1)[0],
        compiler_params=params(),
        cost_estimate=pl.CostEstimate(flops=10**9, bytes_accessed=10**7, transcendentals=10**6),
        name="attend_forward",
    )(queries, keys, values, bias)


def attend_backward(queries, keys, values, bias, grad):
    heads = bias.shape[0]
    rows = jax.ShapeDtypeStruct(queries.shape, bf16)
    return pl.pallas_call(
        functools.partial(backward_body, heads),
        out_shape=(rows, rows, rows, jax.ShapeDtypeStruct(bias.shape, bf16)),
        in_specs=in_vmem(5),
        out_specs=tuple(in_vmem(4)),
        compiler_params=params(),
        cost_estimate=pl.CostEstimate(flops=2 * 10**9, bytes_accessed=2 * 10**7, transcendentals=10**6),
        name="attend_backward",
    )(queries, keys, values, bias, grad)


def bias_body(heads, index_ref, table_ref, out_ref):
    def work(block):
        here = pl.ds(pl.multiple_of(block * ROW_STEP, ROW_STEP), ROW_STEP)
        bias_block_of(heads, index_ref, table_ref, out_ref, here)

    with_events(index_ref.shape[0] // ROW_STEP, [], work)


def gather_bias(pair_index, table):
    heads, entries = table.shape
    return pl.pallas_call(
        functools.partial(bias_body, heads),
        out_shape=jax.ShapeDtypeStruct((heads,) + pair_index.shape, bf16),
        in_specs=in_vmem(2),
        out_specs=in_vmem(1)[0],
        compiler_params=params(),
        cost_estimate=pl.CostEstimate(flops=10**9, bytes_accessed=4 * 10**7, transcendentals=0),
        name="bias",
    )(pair_index, table)


def table_body(heads, groups, index_ref, grad_ref, out_ref):
    out_ref[...] = jnp.zeros_like(out_ref)

    def work(block):
        here = pl.ds(pl.multiple_of(block * ROW_STEP, ROW_STEP), ROW_STEP)
        table_block(heads, groups, index_ref, grad_ref, out_ref, here)

    with_events(index_ref.shape[0] // ROW_STEP, [], work)


def table_sums(pair_index, grad_scores, entries):
    heads = grad_scores.shape[0]
    groups = up_to(-(-entries // SPLIT), 16)
    sums = pl.pallas_call(
        functools.partial(table_body, heads, groups),
        out_shape=jax.ShapeDtypeStruct((heads * groups, SPLIT), f32),
        in_specs=in_vmem(2),
        out_specs=in_vmem(1)[0],
        compiler_params=params(),
        cost_estimate=pl.CostEstimate(flops=2 * 10**9, bytes_accessed=6 * 10**7, transcendentals=0),
        name="table_sums",
    )(pair_index, grad_scores)
    return sums.reshape(heads, groups * SPLIT)


def cuts_of(total, pieces, unit=16):
    count, extra = divmod(total // unit, pieces)
    cuts, at = [], 0
    for i in range(pieces):
        size = (count + (i < extra)) * unit
        if size:
            cuts.append((at, size))
        at += size
    return cuts


def remote(src, dst, send_sem, recv_sem, axis, peer):
    return pltpu.make_async_remote_copy(
        src_ref=src,
        dst_ref=dst,
        send_sem=send_sem,
        recv_sem=recv_sem,
        device_id={axis: peer},
        device_id_type=MESH,
    )


def greet(barrier, axis, peer):
    pl.semaphore_signal(barrier, inc=1, device_id={axis: peer}, device_id_type=MESH)


class ShardSum:
    def __init__(self, chunks, part_ref, out_ref, near, sent, far, send_sem, recv_sem):
        me = lax.axis_index("shard")
        outer, self.inner = me // 2, lax.rem(me, 2)
        self.near_peer = outer * 2 + (1 - self.inner)
        self.far_peer = (1 - outer) * 2 + self.inner
        self.chunks, self.part, self.out = chunks, part_ref, out_ref
        self.near, self.sent, self.far = near, sent, far
        self.sems = (send_sem, recv_sem)
        self.half = near.shape[0]

    def greet(self, barrier):
        greet(barrier, "shard", self.near_peer)
        greet(barrier, "shard", self.far_peer)
        return 2

    def rows(self, which, at, size):
        return pl.ds(pl.multiple_of(which * self.half + at, 16), size)

    def copy(self, stage, j, src, dst, peer):
        send_sem, recv_sem = self.sems
        return remote(src, dst, send_sem.at[stage, j], recv_sem.at[stage, j], "shard", peer)

    def first(self, j):
        at, size = self.chunks[j]
        return self.copy(
            0, j, self.part.at[self.rows(1 - self.inner, at, size)], self.near.at[pl.ds(at, size)], self.near_peer
        )

    def second(self, j):
        here = pl.ds(*self.chunks[j])
        return self.copy(1, j, self.sent.at[here], self.far.at[here], self.far_peer)

    def third(self, j):
        mine = self.out.at[self.rows(self.inner, *self.chunks[j])]
        return self.copy(2, j, mine, mine, self.near_peer)

    def start(self):
        for j in range(len(self.chunks)):
            self.first(j).start()

    def cross_one(self, j):
        at, size = self.chunks[j]
        self.first(j).wait_recv()
        here = pl.ds(at, size)
        mine = self.rows(self.inner, at, size)
        self.sent[here] = (self.part[mine] + self.near[here]).astype(bf16)
        self.second(j).start()

    def cross(self):
        for j in range(len(self.chunks)):
            self.cross_one(j)

    def close_one(self, j):
        at, size = self.chunks[j]
        self.second(j).wait_recv()
        here = pl.ds(at, size)
        mine = self.rows(self.inner, at, size)
        self.out[mine] = self.sent[here].astype(f32) + self.far[here].astype(f32)
        self.third(j).start()

    def close(self):
        for j in range(len(self.chunks)):
            self.close_one(j)

    def arrive(self):
        for j in range(len(self.chunks)):
            self.third(j).wait_recv()

    def drain(self):
        for j in range(len(self.chunks)):
            self.first(j).wait_send()
            self.second(j).wait_send()
            self.third(j).wait_send()


class Grid:
    def __init__(self, peers):
        self.length = peers // 2
        self.me = lax.axis_index("dp")
        self.at, self.side = self.me // 2, lax.rem(self.me, 2)
        self.up, self.down = self.me + 2, self.me - 2
        self.across = self.at * 2 + 1 - self.side
        self.has_up, self.has_down = self.at < self.length - 1, self.at > 0

    def greet(self, barrier):
        greet(barrier, "dp", self.across)

        @pl.when(self.has_up)
        def _():
            greet(barrier, "dp", self.up)

        @pl.when(self.has_down)
        def _():
            greet(barrier, "dp", self.down)

        return 1 + self.has_up.astype(jnp.int32) + self.has_down.astype(jnp.int32)

    def clip(self, place):
        return jnp.clip(place, 0, self.length - 1)


class Flood:
    def __init__(self, grid, own, out, up_send, up_recv, down_send, down_recv, side_send, side_recv):
        self.grid, self.own, self.out = grid, own, out
        self.up_sems, self.down_sems = (up_send, up_recv), (down_send, down_recv)
        self.side_sems = (side_send, side_recv)

    def at(self, device):
        depth = self.own.shape[0]
        return self.out.at[pl.ds(pl.multiple_of(device * depth, 8), depth)]

    def block(self, place):
        return self.at(self.grid.clip(place) * 2 + self.grid.side)

    def up(self, s):
        grid, (send, recv) = self.grid, self.up_sems
        block = self.block(grid.at - s)
        return remote(self.own if s == 0 else block, block, send.at[s], recv.at[s], "dp", grid.up)

    def down(self, s):
        grid, (send, recv) = self.grid, self.down_sems
        block = self.block(grid.at + s)
        return remote(self.own if s == 0 else block, block, send.at[s], recv.at[s], "dp", grid.down)

    def across(self, place, own=False):
        grid, (send, recv) = self.grid, self.side_sems
        place = grid.clip(place)
        block = self.block(place)
        return remote(
            self.own if own else block, block, send.at[place], recv.at[place], "dp", grid.across
        )

    def step(self, s):
        grid = self.grid
        if s == 0:

            @pl.when(grid.has_up)
            def _():
                self.up(0).start()

            @pl.when(grid.has_down)
            def _():
                self.down(0).start()

            self.across(grid.at, own=True).start()
            return

        @pl.when(grid.at - s >= 0)
        def _():
            block = self.block(grid.at - s)
            send, recv = self.up_sems
            remote(block, block, send.at[s - 1], recv.at[s - 1], "dp", grid.down).wait_recv()

            @pl.when(grid.has_up)
            def _():
                self.up(s).start()

            self.across(grid.at - s).start()

        @pl.when(grid.at + s < grid.length)
        def _():
            block = self.block(grid.at + s)
            send, recv = self.down_sems
            remote(block, block, send.at[s - 1], recv.at[s - 1], "dp", grid.up).wait_recv()

            @pl.when(grid.has_down)
            def _():
                self.down(s).start()

            self.across(grid.at + s).start()

    def arrive(self):
        grid, (send, recv) = self.grid, self.side_sems
        for place in range(grid.length):
            block = self.at(place * 2 + 1 - grid.side)
            remote(block, block, send.at[place], recv.at[place], "dp", grid.across).wait_recv()

    def drain(self):
        grid = self.grid
        for place in range(grid.length):
            self.across(place).wait_send()
        for s in range(grid.length - 1):

            @pl.when(jnp.logical_and(grid.at - s >= 0, grid.has_up))
            def _():
                self.up(s).wait_send()

            @pl.when(jnp.logical_and(grid.at + s < grid.length, grid.has_down))
            def _():
                self.down(s).wait_send()


SIDE, UP, DOWN = range(3)


class ReduceScatter:
    def __init__(self, grid, grads, out, side, up, down, sems):
        self.grid, self.grads, self.out = grid, grads, out
        self.buffers = (side, up, down)
        self.sems = (sems[:2], sems[2:4], sems[4:6])

    def at(self, device):
        depth = self.out.shape[0]
        return pl.ds(pl.multiple_of(device * depth, 16), depth)

    def prepare(self):
        grid = self.grid

        @pl.when(jnp.logical_not(grid.has_down))
        def _():
            self.buffers[UP][...] = jnp.zeros_like(self.buffers[UP])

        @pl.when(jnp.logical_not(grid.has_up))
        def _():
            self.buffers[DOWN][...] = jnp.zeros_like(self.buffers[DOWN])

    def copy(self, way, place, peer, src=None):
        send, recv = self.sems[way]
        place = self.grid.clip(place)
        dst = self.buffers[way].at[place]
        return remote(dst if src is None else src, dst, send.at[place], recv.at[place], "dp", peer)

    def cross(self, place):
        grid = self.grid
        src = self.grads.at[self.at(grid.clip(place) * 2 + 1 - grid.side)]
        return self.copy(SIDE, place, grid.across, src)

    def start(self, s):
        grid = self.grid

        @pl.when(grid.at + s < grid.length)
        def _():
            self.cross(grid.at + s).start()

        if s:

            @pl.when(grid.at - s >= 0)
            def _():
                self.cross(grid.at - s).start()

    def step(self, s):
        grid = self.grid
        side, up, down = self.buffers
        if s == 0:
            place = grid.at
            self.copy(SIDE, place, grid.across).wait_recv()

            @pl.when(grid.has_down)
            def _():
                self.copy(UP, place, grid.down).wait_recv()

            @pl.when(grid.has_up)
            def _():
                self.copy(DOWN, place, grid.up).wait_recv()

            total = self.grads[self.at(grid.me)].astype(f32) + side[place].astype(f32)
            self.out[...] = total + (up[place].astype(f32) + down[place].astype(f32))
            return

        @pl.when(grid.at + s < grid.length)
        def _():
            place = grid.clip(grid.at + s)
            self.copy(SIDE, place, grid.across).wait_recv()

            @pl.when(grid.has_down)
            def _():
                self.copy(UP, place, grid.down).wait_recv()

            total = self.grads[self.at(place * 2 + grid.side)].astype(f32) + side[place].astype(f32)
            side[place] = (total + up[place].astype(f32)).astype(bf16)
            self.copy(UP, place, grid.up, side.at[place]).start()

        @pl.when(grid.at - s >= 0)
        def _():
            place = grid.clip(grid.at - s)
            self.copy(SIDE, place, grid.across).wait_recv()

            @pl.when(grid.has_up)
            def _():
                self.copy(DOWN, place, grid.up).wait_recv()

            total = self.grads[self.at(place * 2 + grid.side)].astype(f32) + side[place].astype(f32)
            side[place] = (total + down[place].astype(f32)).astype(bf16)
            self.copy(DOWN, place, grid.down, side.at[place]).start()

    def drain(self):
        grid = self.grid
        for place in range(grid.length):
            self.cross(place).wait_send()
        for s in range(1, grid.length):

            @pl.when(grid.at + s < grid.length)
            def _():
                self.copy(UP, grid.at + s, grid.up).wait_send()

            @pl.when(grid.at - s >= 0)
            def _():
                self.copy(DOWN, grid.at - s, grid.down).wait_send()


ROW_STEP = 16
CHUNKS = 4
VECTORS = 8
EARLY_LINES = 16
BIAS_PLACES = [4, 14, 24, 18, 32, 99, 7, 25, 36, 99]
TABLE_PLACES = [-1, 6, 31, 2, 10, 21, 44, 16, 26, 29, 39]
FIRST_CLOSE = 2
RESULT_PLACE = 7
CLOSE_PLACE = 22
NORM_PLACE = 27


def with_events(blocks, events, work):
    def step(block, carry):
        for at, event in events:
            pl.when(block == at)(event)

        @pl.when(block < blocks)
        def _():
            work(block)

        return carry

    lax.fori_loop(0, max([blocks] + [at + 1 for at, _ in events]), step, 0)


class Spread:
    def __init__(self, peers, out, send_sem, recv_sem):
        self.peers, self.out, self.sems = peers, out, (send_sem, recv_sem)
        self.me = lax.axis_index("dp")

    def peer(self, i):
        return lax.rem(self.me + i, self.peers)

    def copy(self, src, slot, peer):
        send_sem, recv_sem = self.sems
        return remote(
            src, self.out.at[slot], send_sem.at[peer], recv_sem.at[slot], "dp", peer
        )

    def start(self, src_for):
        for i in range(1, self.peers):
            self.copy(src_for(self.peer(i)), self.me, self.peer(i)).start()

    def arrive(self):
        for i in range(1, self.peers):
            peer = self.peer(i)
            self.copy(self.out.at[peer], peer, peer).wait_recv()

    def drain(self):
        for i in range(1, self.peers):
            peer = self.peer(i)
            self.copy(self.out.at[peer], peer, peer).wait_send()


def layer_body(plan, *refs):
    tree, heads, groups, slot_rows, peers = plan
    named = {}
    for part in jax.tree.unflatten(tree, refs):
        named.update(part)
    r = types.SimpleNamespace(**named)
    rows, columns = r.index.shape
    model = r.inputs.shape[1]
    depth = model // peers
    inner = heads * HEAD_DIM
    half = rows // 2
    chunks = cuts_of(half, CHUNKS)
    count = len(chunks)
    factor = HEAD_DIM ** (-0.5)
    height = heads * groups

    grid = Grid(peers)
    sums = [
        ShardSum(chunks, *buffers)
        for buffers in zip(r.part, r.total, r.near, r.sent, r.far, r.sum_send, r.sum_recv)
    ]
    lines = Flood(grid, r.own_lines, r.all_lines, *r.flood_sems[3])
    floods = [
        Flood(grid, own, out, *sems) for own, out, sems in zip((r.own_first, r.fc1_weight, r.fc2_weight), r.whole, r.flood_sems)
    ]
    scatters = [
        ReduceScatter(grid, *buffers)
        for buffers in zip(r.grad, r.summed, r.side, r.up, r.down, r.scatter_sems)
    ]
    spreads = [
        Spread(peers, out, *sems)
        for out, sems in zip((r.all_early, r.all_late, r.all_table), r.spread_sems)
    ]

    loads = [
        pltpu.make_async_copy(src, dst, r.load_sem.at[j])
        for j, (src, dst) in enumerate(
            ((r.large_index, r.wide_from), (r.inputs, r.inputs_here), (r.out_grad, r.grad_here))
        )
    ]
    for load in loads:
        load.start()
    for i, member in enumerate(r.small_vectors):
        r.own_lines[i : i + 1, :depth] = member[...].astype(f32).reshape(1, depth)
    for j in range(3):
        r.own_first[:, j * inner : (j + 1) * inner] = r.qkv_weight[j]
    r.own_first[:, 3 * inner :] = r.out_weight[...].T
    barrier = pltpu.get_barrier_semaphore()
    met = sums[0].greet(barrier)
    for i in range(1, peers):
        greet(barrier, "dp", lax.rem(grid.me + i, peers))
    pl.semaphore_wait(barrier, met + peers - 1)
    lines.step(0)
    floods[0].step(0)
    floods[1].step(0)
    copies = [
        pltpu.make_async_copy(flood.own, flood.at(grid.me), r.local_sem.at[j])
        for j, flood in enumerate(floods + [lines])
    ]
    for copy in copies:
        copy.start()
    for scatter in scatters:
        scatter.prepare()

    kind = r.slot_kind[0]
    r.slot[0:1] = jnp.full((1, LANES), kind.astype(f32))
    r.slot[1:2] = jnp.full((1, LANES), (slot_rows - kind * (slot_rows - LARGE_LEN)).astype(f32))
    is_large = jnp.broadcast_to(r.slot[0:1, :], (8, LANES)) > 0.5
    small_side, large_side = r.small_index.shape[0], r.large_index.shape[0]
    r.index[...] = jnp.full((rows, columns), -1, jnp.int32)
    for image in range(slot_rows // small_side):
        at = image * small_side
        r.index[at : at + small_side, at : at + small_side] = r.small_index[...]
    r.wide_index[...] = jnp.full((rows, columns), -1, jnp.int32)
    for load in loads:
        load.wait()
    r.wide_index[:large_side, :large_side] = r.wide_from[...]
    r.table[...] = jnp.zeros_like(r.table)
    entries_small, entries_large = r.small_table.shape[1], r.large_table.shape[1]
    r.table[:heads, :entries_small] = r.small_table[...].astype(f32)
    r.wide_table[...] = jnp.zeros_like(r.wide_table)
    r.wide_table[:heads, :entries_large] = r.large_table[...].astype(f32)
    tall = jnp.broadcast_to(is_large[:, 0:1], r.table.shape)
    r.table[...] = jnp.where(tall, r.wide_table[...], r.table[...])
    large_block = jnp.broadcast_to(r.slot[0:1, 0:1], (ROW_STEP, columns)) > 0.5

    body_rows = slot_rows // 32 * 32
    tail = slot_rows - body_rows
    r.kept[:body_rows] = r.inputs_here[:body_rows]
    r.kept[body_rows:] = jnp.concatenate(
        (
            r.inputs_here[body_rows:slot_rows].astype(f32),
            jnp.zeros((rows - slot_rows, model), f32),
        ),
        0,
    ).astype(bf16)
    blocks = up_to(slot_rows, ROW_STEP) // ROW_STEP

    def bias_block(block):
        here = pl.ds(pl.multiple_of(block * ROW_STEP, ROW_STEP), ROW_STEP)
        r.index[here] = jnp.where(large_block, r.wide_index[here], r.index[here])
        bias_block_of(heads, r.index, r.table, r.bias, here)

    r.index[blocks * ROW_STEP :] = jnp.full((rows - blocks * ROW_STEP, columns), -1, jnp.int32)
    r.bias[:, blocks * ROW_STEP :] = jnp.full(
        (heads, rows - blocks * ROW_STEP, columns), NEG, bf16
    )
    length = grid.length

    def flood_event(j, s):
        return lambda: floods[j].step(s)

    order = [(j, s) for j in range(2) for s in range(1, length)]
    order += [(2, s) for s in range(length)]
    places = BIAS_PLACES if length == 4 else [k * 3 for k in range(len(order))]
    events = [(at, flood_event(*item)) for at, item in zip(places, order)]
    events += [(3 * s, functools.partial(lines.step, s)) for s in range(1, length)]
    late_floods = [event for at, event in events if at >= blocks]
    with_events(blocks, [(at, event) for at, event in events if at < blocks], bias_block)
    for copy in copies:
        copy.wait()
    lines.arrive()
    floods[0].arrive()
    for d in range(peers):
        r.vectors[:, d * depth : (d + 1) * depth] = r.all_lines[
            d * VECTORS : (d + 1) * VECTORS, :depth
        ]

    def vector(i):
        return r.vectors[i : i + 1, :]

    def moments(value):
        mean = jnp.mean(value, -1, keepdims=True)
        center = value - mean
        inverse = lax.rsqrt(jnp.mean(center * center, -1, keepdims=True) + EPS)
        return center * inverse, mean, inverse

    def both(ref, c):
        at, size = chunks[c]
        return jnp.concatenate((ref[at : at + size], ref[half + at : half + at + size]), 0)

    def put(ref, c, value):
        at, size = chunks[c]
        ref[at : at + size] = value[:size]
        ref[half + at : half + at + size] = value[size:]

    def add(i, value):
        r.running[i] += value.reshape(value.shape[0] // 8, 8, value.shape[1]).sum(0)

    r.running[...] = jnp.zeros_like(r.running)
    r.qkv_shift[...] = jnp.zeros_like(r.qkv_shift)
    r.qkv_shift[:, :inner] = r.query_bias[...].astype(f32).reshape(1, inner)
    r.qkv_shift[:, 2 * inner :] = r.value_bias[...].astype(f32).reshape(1, inner)
    r.hidden_shift[...] = r.fc1_bias[...].astype(f32).reshape(r.hidden_shift.shape)
    for c in range(count):
        normal, mean, inverse = moments(both(r.kept, c).astype(f32))
        put(r.mean[0], c, mean)
        put(r.inverse[0], c, inverse)
        normed = (normal * vector(0) + vector(1)).astype(bf16)
        put(r.normed[0], c, normed)
        projected = dot(normed, r.whole[0][:, : 3 * inner], 1, 0) + r.qkv_shift[...]
        put(r.qkv, c, projected.astype(bf16))

    def weights_of(h):
        part = slice(h * HEAD_DIM, (h + 1) * HEAD_DIM)
        keys = slice(inner + h * HEAD_DIM, inner + (h + 1) * HEAD_DIM)
        scores = dot(r.qkv[:, part], r.qkv[:, keys], 1, 1) * factor
        scores = scores + r.bias[h, :, :rows].astype(f32)
        weights = jnp.exp(scores - jnp.max(scores, -1, keepdims=True))
        return weights * (1.0 / jnp.sum(weights, -1, keepdims=True))

    for h in range(heads):
        for event in late_floods if h == heads - 1 else ():
            event()
        part = slice(h * HEAD_DIM, (h + 1) * HEAD_DIM)
        values = slice(2 * inner + h * HEAD_DIM, 2 * inner + (h + 1) * HEAD_DIM)
        r.bias[h, :, :rows] = weights_of(h).astype(bf16)
        r.attended[:, part] = dot(r.bias[h, :, :rows], r.qkv[:, values], 1, 0).astype(bf16)

    def out_turned():
        return r.whole[0][:, 3 * inner :]

    def live_rows(c):
        at, size = chunks[c]
        first = lax.broadcasted_iota(jnp.int32, (size, 1), 0) + at
        places = jnp.concatenate((first, first + half), 0).astype(f32)
        return jnp.where(places < r.slot[1:2, 0:1], 1.0, 0.0)

    def padded(ref, c):
        at, size = chunks[c]
        last = min(half + at + size, slot_rows)
        low = ref[half + at : last]
        missing = half + at + size - last
        if missing:
            low = jnp.concatenate(
                (low.astype(f32), jnp.zeros((missing, low.shape[1]), f32)), 0
            )
        return jnp.concatenate((ref[at : at + size].astype(f32), low.astype(f32)), 0)

    def keep(ref, c, value):
        at, size = chunks[c]
        last = min(half + at + size, slot_rows)
        ref[at : at + size] = value[:size]
        ref[half + at : last] = value[size : size + last - half - at]

    def project(c):
        put(r.part[0], c, dot(both(r.attended, c), out_turned(), 1, 1))
        sums[0].first(c).start()

    def forward(c):
        if c == 0:
            floods[1].arrive()
        sums[0].third(c).wait_recv()
        middle = both(r.kept, c).astype(f32) + vector(3) * (both(r.total[0], c) + vector(2))
        put(r.middle, c, middle)
        normal, mean, inverse = moments(middle)
        put(r.mean[1], c, mean)
        put(r.inverse[1], c, inverse)
        normed = (normal * vector(4) + vector(5)).astype(bf16)
        put(r.normed[1], c, normed)
        hidden = dot(normed, r.whole[1][...], 1, 0) + r.hidden_shift[...]
        cumulative = 0.5 * (1.0 + lax.erf(hidden * 0.7071067811865476))
        put(
            r.slope,
            c,
            cumulative + hidden * jnp.exp(-0.5 * hidden * hidden) * 0.3989422804014327,
        )
        active = (hidden * cumulative).astype(bf16)
        put(r.active, c, active)
        if c == 0:
            floods[2].arrive()
        put(r.part[1], c, dot(active, r.whole[2][...], 1, 1))
        sums[1].first(c).start()
        grad_result = (padded(r.grad_here, c) * live_rows(c) * vector(7)).astype(bf16)
        put(r.grad_result, c, grad_result)
        add(5, grad_result.astype(f32))
        grad_hidden = (dot(grad_result, r.whole[2][...], 1, 0) * both(r.slope, c)).astype(bf16)
        put(r.grad_hidden, c, grad_hidden)
        add(0, grad_hidden.astype(f32))
        put(r.part[2], c, dot(grad_hidden, r.whole[1][...], 1, 1))
        sums[2].first(c).start()

    def results():
        for c in range(count):
            sums[1].third(c).wait_recv()
            result = both(r.total[1], c) + vector(6)
            live = live_rows(c)
            keep(r.out_here, c, (live * (both(r.middle, c) + vector(7) * result)).astype(bf16))
            add(6, padded(r.grad_here, c) * live * result)
        to_owners(5, r.running[6])
        store.start()

    def back_norm(grad, normal, inverse, gain):
        scaled = grad * gain
        along = jnp.mean(scaled * normal, -1, keepdims=True)
        return inverse * (scaled - jnp.mean(scaled, -1, keepdims=True) - normal * along)

    def backward(c):
        sums[2].third(c).wait_recv()
        grad = both(r.total[2], c)
        inverse = both(r.inverse[1], c)
        normal = (both(r.middle, c) - both(r.mean[1], c)) * inverse
        add(3, grad * normal)
        add(4, grad)
        grad_middle = padded(r.grad_here, c) * live_rows(c)
        grad_middle = grad_middle + back_norm(grad, normal, inverse, vector(4))
        put(r.grad_middle, c, grad_middle)
        add(2, grad_middle * (both(r.total[0], c) + vector(2)))
        grad_branch = (grad_middle * vector(3)).astype(bf16)
        put(r.grad_branch, c, grad_branch)
        add(1, grad_branch.astype(f32))
        put(r.grad_attended, c, dot(grad_branch, out_turned(), 1, 0).astype(bf16))

    def close(work):
        return lambda c: work.close_one(c)

    def cross(work):
        return lambda c: work.cross_one(c)

    stages = [project, cross(sums[0]), close(sums[0]), forward]
    stages += [cross(sums[2]), close(sums[2]), backward]

    def weight_grad(j, left, right, at=0):
        value = dot(left[...], right[...], 0, 0).astype(bf16)
        r.grad[j][:, at : at + value.shape[1]] = value

    def send_grads(j):
        for s in range(length - 1, -1, -1):
            scatters[j].start(s)

    for t in range(count + len(stages) - 1):
        for k in range(len(stages) - 1, -1, -1):
            if 0 <= t - k < count:
                stages[k](t - k)
        if t == count + 2:
            weight_grad(2, r.grad_result, r.active)
            send_grads(2)
        if t == count + 3:
            sums[1].cross()
            weight_grad(1, r.normed[1], r.grad_hidden)
            send_grads(1)

    store = pltpu.make_async_copy(r.out_here, r.layer_out, r.load_sem.at[0])
    weight_grad(0, r.grad_branch, r.attended, 3 * inner)
    steps = list(range(length - 1, -1, -1))
    for h in range(heads):
        part = slice(h * HEAD_DIM, (h + 1) * HEAD_DIM)
        keys = slice(inner + h * HEAD_DIM, inner + (h + 1) * HEAD_DIM)
        values = slice(2 * inner + h * HEAD_DIM, 2 * inner + (h + 1) * HEAD_DIM)
        grad_part = r.grad_attended[:, part]
        r.grad_qkv[:, values] = dot(r.bias[h, :, :rows], grad_part, 0, 0).astype(bf16)
        weights = r.bias[h, :, :rows].astype(f32)
        grad = dot(grad_part, r.qkv[:, values], 1, 1)
        mean = jnp.sum(weights * grad, -1, keepdims=True)
        grad = (weights * (grad - mean)).astype(bf16)
        r.bias[h, :, :rows] = grad
        r.grad_qkv[:, part] = (dot(grad, r.qkv[:, keys], 1, 0) * factor).astype(bf16)
        r.grad_qkv[:, keys] = (dot(grad, r.qkv[:, part], 0, 0) * factor).astype(bf16)
        if h == 0:
            scatters[2].step(steps[0])

    def scatter_event(j, s):
        return lambda: scatters[j].step(s)

    order = [(2, s) for s in steps[1:]] + [(j, s) for j in (1, 0) for s in steps]
    places = TABLE_PLACES if length == 4 else [4 * k for k in range(len(order))]
    events = [(at, scatter_event(*item)) for at, item in zip(places, order)]
    for at, event in events:
        if at < 0:
            event()
    events = [(at, event) for at, event in events if at >= 0]

    sums[0].drain()
    last = sums[0]
    for c in range(count):
        put(r.part[0], c, dot(both(r.grad_qkv, c), r.whole[0][:, : 3 * inner], 1, 1))
        last.first(c).start()
    weight_grad(0, r.normed[0], r.grad_qkv)
    send_grads(0)

    wide = model // LANES
    at = 1
    r.own_early[...] = jnp.zeros_like(r.own_early)
    r.own_early[0:1] = r.slot[0:1, :]

    def line_to(at, line):
        for c in range(-(-line.shape[1] // LANES)):
            piece = line[:, c * LANES : (c + 1) * LANES]
            r.own_early[at + c : at + c + 1, : piece.shape[1]] = piece

    for line in (
        jnp.sum(r.running[0], 0, keepdims=True),
        jnp.sum(r.grad_qkv[:, :inner].astype(f32), 0, keepdims=True),
        jnp.sum(r.grad_qkv[:, 2 * inner :].astype(f32), 0, keepdims=True),
    ):
        line_to(at, line)
        at += up_to(line.shape[1], LANES) // LANES
    spreads[0].start(lambda peer: r.own_early)

    def to_owners(i, value):
        line = jnp.sum(value, 0, keepdims=True)
        for d in range(peers):
            r.own_late[d, i : i + 1, :depth] = line[:, d * depth : (d + 1) * depth]

    r.own_late[...] = jnp.zeros_like(r.own_late)
    for i in range(1, 6):
        to_owners(i - 1, r.running[i])
    r.table_sums[...] = jnp.zeros_like(r.table_sums)

    def norm_step(here, out_rows):
        grad = r.total[0][here]
        normal = (r.kept[here].astype(f32) - r.mean[0][here]) * r.inverse[0][here]
        back = back_norm(grad, normal, r.inverse[0][here], vector(0))
        value = (r.grad_middle[here] + back).astype(bf16)
        if out_rows is None:
            r.input_grad[here] = value
        else:
            r.input_grad[out_rows] = value[:tail]
        product = (grad * normal).reshape(4, 8, model).sum(0)
        return product, grad.reshape(4, 8, model).sum(0)

    def norm_rows():
        last.arrive()

        def step(i, totals):
            gain, shift = norm_step(pl.ds(pl.multiple_of(i * 32, 32), 32), None)
            return totals[0] + gain, totals[1] + shift

        zero = jnp.zeros((8, model), f32)
        gain, shift = lax.fori_loop(0, body_rows // 32, step, (zero, zero))
        if tail:
            more = norm_step(slice(body_rows, rows), slice(body_rows, slot_rows))
            gain, shift = gain + more[0], shift + more[1]
        to_owners(6, gain)
        to_owners(7, shift)

    events += [(0, last.cross), (FIRST_CLOSE, sums[1].close), (RESULT_PLACE, results)]
    events += [(CLOSE_PLACE, last.close), (NORM_PLACE, norm_rows)]
    events.sort(key=lambda item: item[0])
    with_events(
        blocks,
        [(at, event) for at, event in events if at < blocks],
        lambda block: table_block(
            heads,
            groups,
            r.index,
            r.bias,
            r.table_sums,
            pl.ds(pl.multiple_of(block * ROW_STEP, ROW_STEP), ROW_STEP),
        ),
    )
    r.own_table[...] = r.table_sums[...].astype(bf16)
    spreads[2].start(lambda peer: r.own_table)
    spreads[1].start(lambda peer: r.own_late.at[peer])
    for at, event in events:
        if at >= blocks:
            event()
    r.all_early[grid.me] = r.own_early[...]
    r.all_late[grid.me] = r.own_late[grid.me]
    r.all_table[grid.me] = r.own_table[...]
    for spread in spreads:
        spread.arrive()
    early = jnp.zeros(r.early_sums.shape, f32)
    late = jnp.zeros(r.late_sums.shape, f32)
    small = jnp.zeros((height, LANES), f32)
    large = jnp.zeros((height, LANES), f32)
    for d in range(peers):
        kind = r.all_early[d, 0:1] > 0.5
        table = r.all_table[d].astype(f32)
        small += jnp.where(kind, 0.0, table)
        large += jnp.where(kind, table, 0.0)
        early += r.all_early[d]
        late += r.all_late[d]
    r.early_sums[...] = early
    r.late_sums[...] = late
    for out, value in ((r.small_sums, small), (r.large_sums, large)):
        entries = out.shape[1]
        for k in range(-(-entries // SPLIT)):
            first, size = k * SPLIT, min(SPLIT, entries - k * SPLIT)
            for h in range(heads):
                at = h * groups + k
                out[h : h + 1, first : first + size] = value[at : at + 1, :size]
    store.wait()
    for work in sums + floods + [lines] + scatters + spreads:
        work.drain()


def layer(arguments, peers, slot_rows):
    model = arguments["inputs"].shape[1]
    rows = up_to(slot_rows, 32)
    columns = up_to(rows, LANES)
    depth = model // peers
    hidden = arguments["fc1_bias"].shape[0]
    inner = arguments["query_bias"].shape[0]
    widths = [4 * inner, hidden, hidden]
    heads = inner // HEAD_DIM
    tables = [arguments["small_table"].shape, arguments["large_table"].shape]
    entries = up_to(max(shape[1] for shape in tables), LANES)
    groups = up_to(-(-entries // SPLIT), 16)
    height = heads * groups
    count = len(cuts_of(rows // 2, CHUNKS))
    length = peers // 2
    array = jax.ShapeDtypeStruct

    def sems(*shape):
        return pltpu.SemaphoreType.DMA(shape)

    def each(kind, shape, times):
        return [pltpu.VMEM(shape, kind) for _ in range(times)]

    outs = dict(
        layer_out=array((slot_rows, model), bf16),
        input_grad=array((slot_rows, model), bf16),
        small_sums=array(tables[0], f32),
        large_sums=array(tables[1], f32),
        early_sums=array((EARLY_LINES, LANES), f32),
        late_sums=array((VECTORS, LANES), f32),
        summed=[array((depth, w), f32) for w in widths],
    )
    blocks = [pltpu.VMEM((length, depth, w), bf16) for w in widths]
    scratch = dict(
        whole=[pltpu.VMEM((model, w), bf16) for w in widths],
        all_lines=pltpu.VMEM((peers * VECTORS, LANES), f32),
        grad=[pltpu.VMEM((model, w), bf16) for w in widths],
        side=blocks,
        up=blocks,
        down=blocks,
        scatter_sems=[[sems(length)] * 6] * 3,
        flood_sems=[[sems(length)] * 6] * 4,
        spread_sems=[[sems(peers)] * 2] * 3,
        part=each(f32, (rows, model), 3),
        total=each(f32, (rows, model), 3),
        near=each(f32, (rows // 2, model), 3),
        sent=each(bf16, (rows // 2, model), 3),
        far=each(bf16, (rows // 2, model), 3),
        sum_send=[sems(3, count)] * 3,
        sum_recv=[sems(3, count)] * 3,
        local_sem=sems(4),
        load_sem=sems(3),
        wide_from=pltpu.VMEM(arguments["large_index"].shape, jnp.int32),
        inputs_here=pltpu.VMEM((slot_rows, model), bf16),
        grad_here=pltpu.VMEM((slot_rows, model), bf16),
        out_here=pltpu.VMEM((slot_rows, model), bf16),
        own_first=pltpu.VMEM((depth, 4 * inner), bf16),
        own_lines=pltpu.VMEM((VECTORS, LANES), f32),
        slot=pltpu.VMEM((2, LANES), f32),
        hidden_shift=pltpu.VMEM((1, hidden), f32),
        index=pltpu.VMEM((rows, columns), jnp.int32),
        wide_index=pltpu.VMEM((rows, columns), jnp.int32),
        table=pltpu.VMEM((8, entries), f32),
        wide_table=pltpu.VMEM((8, entries), f32),
        bias=pltpu.VMEM((heads, rows, columns), bf16),
        vectors=pltpu.VMEM((VECTORS, model), f32),
        qkv_shift=pltpu.VMEM((1, 3 * inner), f32),
        running=pltpu.VMEM((7, 8, max(model, hidden)), f32),
        mean=each(f32, (rows, 1), 2),
        inverse=each(f32, (rows, 1), 2),
        normed=each(bf16, (rows, model), 2),
        kept=pltpu.VMEM((rows, model), bf16),
        grad_result=pltpu.VMEM((rows, model), bf16),
        grad_branch=pltpu.VMEM((rows, model), bf16),
        active=pltpu.VMEM((rows, hidden), bf16),
        grad_hidden=pltpu.VMEM((rows, hidden), bf16),
        qkv=pltpu.VMEM((rows, 3 * inner), bf16),
        grad_qkv=pltpu.VMEM((rows, 3 * inner), bf16),
        attended=pltpu.VMEM((rows, inner), bf16),
        grad_attended=pltpu.VMEM((rows, inner), bf16),
        middle=pltpu.VMEM((rows, model), f32),
        grad_middle=pltpu.VMEM((rows, model), f32),
        slope=pltpu.VMEM((rows, hidden), f32),
        table_sums=pltpu.VMEM((height, LANES), f32),
        own_table=pltpu.VMEM((height, LANES), bf16),
        all_table=pltpu.VMEM((peers, height, LANES), bf16),
        own_early=pltpu.VMEM((EARLY_LINES, LANES), f32),
        all_early=pltpu.VMEM((peers, EARLY_LINES, LANES), f32),
        own_late=pltpu.VMEM((peers, VECTORS, LANES), f32),
        all_late=pltpu.VMEM((peers, VECTORS, LANES), f32),
    )
    flat = jax.tree.leaves(arguments)
    near, apart = pl.BlockSpec(memory_space=pltpu.VMEM), pl.BlockSpec(memory_space=pl.ANY)
    specs = jax.tree.map(lambda _: near, arguments)
    specs.update(inputs=apart, out_grad=apart, large_index=apart)
    specs.update(slot_kind=pl.BlockSpec(memory_space=pltpu.SMEM))
    out_specs = jax.tree.map(lambda _: near, outs)
    out_specs.update(layer_out=apart)
    shapes, out_tree = jax.tree.flatten(outs)
    tree = jax.tree.structure((arguments, outs, scratch))
    results = pl.pallas_call(
        functools.partial(layer_body, (tree, heads, groups, slot_rows, peers)),
        out_shape=shapes,
        in_specs=jax.tree.leaves(specs),
        out_specs=jax.tree.leaves(out_specs),
        scratch_shapes=jax.tree.leaves(scratch),
        compiler_params=params(collective_id=0, has_side_effects=True),
        name="layer",
    )(*flat)
    return types.SimpleNamespace(**jax.tree.unflatten(out_tree, results))


def finish_body(tree, depth, *refs):
    found, out = (types.SimpleNamespace(**part) for part in jax.tree.unflatten(tree, refs))
    pairs = (
        (found.layer_out, out.layer_out),
        (found.input_grad, out.input_grad),
        (found.summed[1], out.fc1),
        (found.summed[2], out.fc2),
        (found.small_sums, out.small_table),
        (found.large_sums, out.large_table),
    )
    for src, dst in pairs:
        dst[...] = src[...]
    inner = out.query_bias.shape[0]
    for j in range(3):
        out.qkv[j] = found.summed[0][:, j * inner : (j + 1) * inner]
    out.out[...] = found.summed[0][:, 3 * inner :].T
    for i, vector in enumerate(out.vectors):
        vector[...] = found.late_sums[i, :depth]
    at = 1
    for line in (out.fc1_bias, out.query_bias, out.value_bias):
        size = line.shape[0]
        for first in range(0, size, LANES):
            count = min(LANES, size - first)
            line[pl.ds(first, count)] = found.early_sums[at, :count]
            at += 1


def finish(found, depth, inner, hidden):
    array = jax.ShapeDtypeStruct
    found = vars(found)
    outs = dict(
        layer_out=array(found["layer_out"].shape, bf16),
        input_grad=array(found["input_grad"].shape, bf16),
        fc1=array(found["summed"][1].shape, f32),
        fc2=array(found["summed"][2].shape, f32),
        small_table=array(found["small_sums"].shape, f32),
        large_table=array(found["large_sums"].shape, f32),
        qkv=array((3, depth, inner), f32),
        out=array((inner, depth), f32),
        vectors=[array((depth,), f32)] * VECTORS,
        fc1_bias=array((hidden,), f32),
        query_bias=array((inner,), f32),
        value_bias=array((inner,), f32),
    )
    shapes, out_tree = jax.tree.flatten(outs)
    results = pl.pallas_call(
        functools.partial(finish_body, jax.tree.structure((found, outs)), depth),
        out_shape=shapes,
        in_specs=in_vmem(len(jax.tree.leaves(found))),
        out_specs=in_vmem(len(shapes)),
        compiler_params=params(),
        name="finish",
    )(*jax.tree.leaves(found))
    return types.SimpleNamespace(**jax.tree.unflatten(out_tree, results))


def layer_norm(activations, norm_gain, norm_shift):
    center = activations - jnp.mean(activations, -1, keepdims=True)
    inverse = lax.rsqrt(jnp.mean(center * center, -1, keepdims=True) + EPS)
    normal = center * inverse
    return (normal * norm_gain + norm_shift, normal, inverse)


def norm_back(grad_normed, normal, inverse, norm_gain):
    scaled = grad_normed * norm_gain
    return inverse * (
        scaled
        - jnp.mean(scaled, -1, keepdims=True)
        - normal * jnp.mean(scaled * normal, -1, keepdims=True)
    )


def gelu_slope(hidden):
    cumulative = 0.5 * (1.0 + jax.scipy.special.erf(hidden * 0.7071067811865476))
    return cumulative + hidden * jnp.exp(-0.5 * hidden * hidden) * 0.3989422804014327


def pair_map(kind, small_index, large_index, rows, columns):
    def placed(index, at):
        side = index.shape[0]
        return jnp.pad(
            index, ((at, rows - at - side), (at, columns - at - side)), constant_values=-1
        )

    length = small_index.shape[0]
    small = placed(small_index, 0)
    for image in range(1, SLOT_ROWS // length):
        small = jnp.maximum(small, placed(small_index, image * length))
    return jnp.where(kind == 1, placed(large_index, 0), small)


def plain_device(
    images,
    out_grad,
    slot_kind,
    small_index,
    large_index,
    qkv_weight,
    out_weight,
    fc1_weight,
    fc2_weight,
    norm1_gain,
    norm1_shift,
    query_bias,
    value_bias,
    out_bias,
    gamma_attn,
    norm2_gain,
    norm2_shift,
    fc1_bias,
    fc2_bias,
    gamma_mlp,
    small_table,
    large_table,
):
    depth = qkv_weight.shape[0]
    width = query_bias.shape[0]
    hidden_width = fc1_bias.shape[0]
    heads = width // HEAD_DIM
    _, slot_rows, model_width = images.shape
    rows = up_to(slot_rows, 32)
    columns = up_to(rows, LANES)
    kind = slot_kind[0]

    block = jnp.concatenate(
        (
            qkv_weight.reshape(depth, 3 * width),
            fc1_weight,
            out_weight.T,
            fc2_weight.T,
        ),
        1,
    )
    whole = lax.all_gather(block, "dp", axis=0, tiled=True)
    cuts = (3 * width, 3 * width + hidden_width, 4 * width + hidden_width)
    qkv_matrix = whole[:, : cuts[0]]
    fc1_matrix = whole[:, cuts[0] : cuts[1]]
    out_turned = whole[:, cuts[1] : cuts[2]]
    fc2_turned = whole[:, cuts[2] :]
    small_vectors = jnp.stack(
        (norm1_gain, norm1_shift, out_bias, gamma_attn, norm2_gain, norm2_shift, fc2_bias, gamma_mlp)
    )
    vectors = lax.all_gather(small_vectors, "dp", axis=0)
    vectors = jnp.moveaxis(vectors, 0, 1).reshape(8, model_width).astype(f32)

    query_shift = query_bias.astype(f32)
    value_shift = value_bias.astype(f32)
    hidden_shift = fc1_bias.astype(f32)
    small_entries, large_entries = small_table.shape[0], large_table.shape[0]
    entries = up_to(max(small_entries, large_entries), LANES)
    table = jnp.where(
        kind == 1,
        jnp.pad(large_table, ((0, entries - large_entries), (0, 0))),
        jnp.pad(small_table, ((0, entries - small_entries), (0, 0))),
    )
    table = table.T.astype(f32)
    pair_index = pair_map(kind, small_index, large_index, rows, columns)
    bias = gather_bias(pair_index, table)

    positions = jnp.arange(rows)
    live_count = jnp.where(kind == 1, LARGE_LEN, slot_rows)
    live_rows = (positions < live_count).astype(f32).reshape(-1, 1)
    inputs = jnp.pad(images[0], ((0, rows - slot_rows), (0, 0))).astype(f32)
    normed_one, normal_one, inverse_one = layer_norm(inputs, vectors[0], vectors[1])
    normed_one = normed_one.astype(bf16)
    projected = dot(normed_one, qkv_matrix, 1, 0)
    queries = (projected[:, :width] + query_shift).astype(bf16)
    keys = projected[:, width : 2 * width].astype(bf16)
    values = (projected[:, 2 * width :] + value_shift).astype(bf16)
    pieces = attend_forward(queries, keys, values, bias)
    branch_part = dot(pieces, out_turned, 1, 1)
    branch = lax.psum(branch_part, "shard") + vectors[2]
    middle = inputs + vectors[3] * branch
    normed_two, normal_two, inverse_two = layer_norm(middle, vectors[4], vectors[5])
    normed_two = normed_two.astype(bf16)
    hidden = dot(normed_two, fc1_matrix, 1, 0) + hidden_shift
    active = jax.nn.gelu(hidden, approximate=False).astype(bf16)
    result_part = dot(active, fc2_turned, 1, 1)
    result = lax.psum(result_part.astype(bf16), "shard").astype(f32) + vectors[6]
    layer_out = ((middle + vectors[7] * result) * live_rows).astype(bf16)[:slot_rows][None]

    grad_out = jnp.pad(out_grad[0], ((0, rows - slot_rows), (0, 0))).astype(f32) * live_rows
    grad_gamma_mlp = jnp.sum(grad_out * result, 0)
    grad_result = (grad_out * vectors[7]).astype(bf16)
    grad_fc2_bias = jnp.sum(grad_result.astype(f32), 0)
    grad_fc2_turned = dot(grad_result, active, 0, 0)
    grad_active = dot(grad_result, fc2_turned, 1, 0)
    grad_hidden = (grad_active * gelu_slope(hidden)).astype(bf16)
    grad_fc1_bias = jnp.sum(grad_hidden.astype(f32), 0)
    grad_fc1 = dot(normed_two, grad_hidden, 0, 0)
    grad_normed_two = lax.psum(dot(grad_hidden, fc1_matrix, 1, 1), "shard")
    grad_norm2_gain = jnp.sum(grad_normed_two * normal_two, 0)
    grad_norm2_shift = jnp.sum(grad_normed_two, 0)
    grad_middle = grad_out + norm_back(grad_normed_two, normal_two, inverse_two, vectors[4])
    grad_gamma_attn = jnp.sum(grad_middle * branch, 0)
    grad_branch = (grad_middle * vectors[3]).astype(bf16)
    grad_out_bias = jnp.sum(grad_branch.astype(f32), 0)
    grad_out_turned = dot(grad_branch, pieces, 0, 0)
    grad_attended = dot(grad_branch, out_turned, 1, 0).astype(bf16)
    grad_queries, grad_keys, grad_values, grad_scores = attend_backward(
        queries, keys, values, bias, grad_attended
    )
    sums = table_sums(pair_index, grad_scores, entries)
    grad_projected = jnp.concatenate((grad_queries, grad_keys, grad_values), 1)
    grad_qkv = dot(normed_one, grad_projected, 0, 0)
    grad_query_bias = jnp.sum(grad_queries.astype(f32), 0)
    grad_value_bias = jnp.sum(grad_values.astype(f32), 0)
    grad_normed_one = lax.psum(dot(grad_projected, qkv_matrix, 1, 1), "shard")
    grad_norm1_gain = jnp.sum(grad_normed_one * normal_one, 0)
    grad_norm1_shift = jnp.sum(grad_normed_one, 0)
    input_grad = grad_middle + norm_back(grad_normed_one, normal_one, inverse_one, vectors[0])
    input_grad = input_grad.astype(bf16)[:slot_rows][None]

    small_sums = jnp.where(kind == 1, 0.0, sums[:, :small_entries])
    large_sums = jnp.where(kind == 1, sums[:, :large_entries], 0.0)
    local_sums = lax.psum(
        (small_sums, large_sums, grad_query_bias, grad_value_bias, grad_fc1_bias), "dp"
    )
    peers = lax.axis_size("dp")

    def sent_and_summed(value):
        parts = value.astype(bf16).reshape(peers, value.shape[0] // peers, -1)
        arrived = lax.all_to_all(parts, "dp", split_axis=0, concat_axis=0, tiled=True)
        return arrived.astype(f32).sum(axis=0)

    grad_block = sent_and_summed(
        jnp.concatenate((grad_qkv, grad_fc1, grad_out_turned, grad_fc2_turned), 1)
    )
    vector_grads = sent_and_summed(
        jnp.stack(
            (
                grad_norm1_gain,
                grad_norm1_shift,
                grad_out_bias,
                grad_gamma_attn,
                grad_norm2_gain,
                grad_norm2_shift,
                grad_fc2_bias,
                grad_gamma_mlp,
            ),
            1,
        )
    )
    return (
        layer_out,
        input_grad,
        grad_block[:, : cuts[0]].reshape(depth, 3, width),
        grad_block[:, cuts[1] : cuts[2]].T,
        grad_block[:, cuts[0] : cuts[1]],
        grad_block[:, cuts[2] :].T,
        vector_grads[:, 0],
        vector_grads[:, 1],
        local_sums[2],
        local_sums[3],
        vector_grads[:, 2],
        vector_grads[:, 3],
        vector_grads[:, 4],
        vector_grads[:, 5],
        local_sums[4],
        vector_grads[:, 6],
        vector_grads[:, 7],
        local_sums[0].T,
        local_sums[1].T,
    )


def on_device(*arguments):
    depth = arguments[5].shape[0]
    if depth % 16 or lax.axis_size("shard") != 4:
        return plain_device(*arguments)
    return whole_device(*arguments)


def whole_device(
    images,
    out_grad,
    slot_kind,
    small_index,
    large_index,
    qkv_weight,
    out_weight,
    fc1_weight,
    fc2_weight,
    norm1_gain,
    norm1_shift,
    query_bias,
    value_bias,
    out_bias,
    gamma_attn,
    norm2_gain,
    norm2_shift,
    fc1_bias,
    fc2_bias,
    gamma_mlp,
    small_table,
    large_table,
):
    depth = qkv_weight.shape[0]
    found = layer(
        dict(
            inputs=images[0],
            out_grad=out_grad[0],
            slot_kind=slot_kind,
            small_index=small_index,
            large_index=large_index,
            small_table=small_table.T,
            large_table=large_table.T,
            qkv_weight=qkv_weight.transpose(1, 0, 2),
            out_weight=out_weight,
            fc1_weight=fc1_weight,
            fc2_weight=fc2_weight.T,
            small_vectors=[
                norm1_gain,
                norm1_shift,
                out_bias,
                gamma_attn,
                norm2_gain,
                norm2_shift,
                fc2_bias,
                gamma_mlp,
            ],
            query_bias=query_bias,
            value_bias=value_bias,
            fc1_bias=fc1_bias,
        ),
        lax.axis_size("dp"),
        images.shape[1],
    )
    out = finish(found, depth, query_bias.shape[0], fc1_bias.shape[0])
    return (
        out.layer_out[None],
        out.input_grad[None],
        out.qkv.transpose(1, 0, 2),
        out.out,
        out.fc1,
        out.fc2.T,
        out.vectors[6],
        out.vectors[7],
        out.query_bias,
        out.value_bias,
        out.vectors[0],
        out.vectors[1],
        out.vectors[2],
        out.vectors[3],
        out.fc1_bias,
        out.vectors[4],
        out.vectors[5],
        out.small_table.T,
        out.large_table.T,
    )


def solution(mesh):
    return jax.shard_map(
        on_device,
        mesh=mesh,
        in_specs=(
            P("dp", None, None),
            P("dp", None, None),
            P("dp"),
            P(),
            P(),
            P("dp", None, "shard"),
            P("shard", "dp"),
            P("dp", "shard"),
            P("shard", "dp"),
            P("dp"),
            P("dp"),
            P("shard"),
            P("shard"),
            P("dp"),
            P("dp"),
            P("dp"),
            P("dp"),
            P("shard"),
            P("dp"),
            P("dp"),
            P(None, "shard"),
            P(None, "shard"),
        ),
        out_specs=(
            P("dp", None, None),
            P("dp", None, None),
            P("dp", None, "shard"),
            P("shard", "dp"),
            P("dp", "shard"),
            P("shard", "dp"),
            P("dp"),
            P("dp"),
            P("shard"),
            P("shard"),
            P("dp"),
            P("dp"),
            P("dp"),
            P("dp"),
            P("shard"),
            P("dp"),
            P("dp"),
            P(None, "shard"),
            P(None, "shard"),
        ),
        check_vma=False,
    )
```

```python
import functools
import types

import jax
import jax.numpy as jnp
from jax import lax
from jax.experimental import pallas as pl
from jax.experimental.pallas import tpu as pltpu
from jax.sharding import PartitionSpec as P

HEAD_DIM = 64
SMALL_LEN = 197
LARGE_LEN = 577
SLOT_ROWS = 591
EPS = 1e-06
NEG = -1e30
LANES = 128
SPLIT = 80
VMEM_LIMIT = 60 << 20

MESH = pl.DeviceIdType.MESH

f32 = jnp.float32
bf16 = jnp.bfloat16


def up_to(value, unit):
    return -(-value // unit) * unit


def in_vmem(count):
    return [pl.BlockSpec(memory_space=pltpu.VMEM)] * count


def params(**more):
    return pltpu.CompilerParams(vmem_limit_bytes=VMEM_LIMIT, **more)


def dot(a, b, da, db):
    return lax.dot_general(a, b, (((da,), (db,)), ((), ())), preferred_element_type=f32)


def bias_block_of(heads, index_ref, table_ref, out_ref, here):
    columns, entries = index_ref.shape[1], table_ref.shape[1]
    for c in range(columns // LANES):
        there = pl.ds(c * LANES, LANES)
        index = index_ref[here, there]
        high = lax.shift_right_arithmetic(index, 7)
        low = lax.bitwise_and(index, LANES - 1)
        found = [jnp.full(index.shape, NEG, f32) for _ in range(heads)]
        for k in range(entries // LANES):
            match = high == k
            for h in range(heads):
                line = table_ref[h : h + 1, k * LANES : (k + 1) * LANES]
                values = jnp.take_along_axis(jnp.broadcast_to(line, index.shape), low, axis=1)
                found[h] = jnp.where(match, values, found[h])
        for h in range(heads):
            out_ref[h, here, there] = found[h].astype(bf16)


def table_block(heads, groups, index_ref, grad_ref, out_ref, here):
    columns = index_ref.shape[1]
    inverse = -(-(1 << 22) // SPLIT)
    index = index_ref[here, :]
    high = lax.shift_right_arithmetic(index * inverse, 22)
    low = (index - high * SPLIT).astype(jnp.int16)
    high = high.astype(jnp.int16)
    grads = [grad_ref[h, here, :] for h in range(heads)]
    places_low = lax.broadcasted_iota(jnp.int16, (SPLIT, columns), 0)
    places_high = lax.broadcasted_iota(jnp.int16, (groups, columns), 0)
    one, zero = jnp.ones((), bf16), jnp.zeros((), bf16)
    total = jnp.zeros((heads * groups, SPLIT), f32)
    for pair in range(0, 16, 2):
        lows, highs = [], []
        for i in (pair, pair + 1):
            lows.append(
                jnp.where(
                    places_low == jnp.broadcast_to(low[i : i + 1], (SPLIT, columns)), one, zero
                )
            )
            match = places_high == jnp.broadcast_to(high[i : i + 1], (groups, columns))
            highs.append(
                jnp.concatenate(
                    [
                        jnp.where(
                            match,
                            jnp.broadcast_to(grads[h][i : i + 1], (groups, columns)),
                            zero,
                        )
                        for h in range(heads)
                    ],
                    0,
                )
            )
        total = total + dot(jnp.concatenate(highs, 1), jnp.concatenate(lows, 1), 1, 1)
    out_ref[: heads * groups, :SPLIT] += total


def forward_body(heads, q_ref, k_ref, v_ref, bias_ref, out_ref):
    rows = q_ref.shape[0]
    for h in range(heads):
        part = slice(h * HEAD_DIM, (h + 1) * HEAD_DIM)
        scores = dot(q_ref[:, part], k_ref[:, part], 1, 1) * HEAD_DIM ** (-0.5)
        scores = scores + bias_ref[h, :, :rows].astype(f32)
        weights = jnp.exp(scores - jnp.max(scores, -1, keepdims=True))
        weights = weights / jnp.sum(weights, -1, keepdims=True)
        out_ref[:, part] = dot(weights.astype(bf16), v_ref[:, part], 1, 0).astype(bf16)


def backward_body(
    heads, q_ref, k_ref, v_ref, bias_ref, grad_ref, dq_ref, dk_ref, dv_ref, ds_ref
):
    rows = q_ref.shape[0]
    factor = HEAD_DIM ** (-0.5)
    for h in range(heads):
        part = slice(h * HEAD_DIM, (h + 1) * HEAD_DIM)
        scores = dot(q_ref[:, part], k_ref[:, part], 1, 1) * factor
        scores = scores + bias_ref[h, :, :rows].astype(f32)
        weights = jnp.exp(scores - jnp.max(scores, -1, keepdims=True))
        weights = weights / jnp.sum(weights, -1, keepdims=True)
        dv_ref[:, part] = dot(weights.astype(bf16), grad_ref[:, part], 0, 0).astype(bf16)
        grad = dot(grad_ref[:, part], v_ref[:, part], 1, 1)
        mean = jnp.sum(weights * grad, -1, keepdims=True)
        grad = (weights * (grad - mean)).astype(bf16)
        ds_ref[h, :, :rows] = grad
        dq_ref[:, part] = (dot(grad, k_ref[:, part], 1, 0) * factor).astype(bf16)
        dk_ref[:, part] = (dot(grad, q_ref[:, part], 0, 0) * factor).astype(bf16)


def attend_forward(queries, keys, values, bias):
    heads = bias.shape[0]
    return pl.pallas_call(
        functools.partial(forward_body, heads),
        out_shape=jax.ShapeDtypeStruct(queries.shape, bf16),
        in_specs=in_vmem(4),
        out_specs=in_vmem(1)[0],
        compiler_params=params(),
        cost_estimate=pl.CostEstimate(flops=10**9, bytes_accessed=10**7, transcendentals=10**6),
        name="attend_forward",
    )(queries, keys, values, bias)


def attend_backward(queries, keys, values, bias, grad):
    heads = bias.shape[0]
    rows = jax.ShapeDtypeStruct(queries.shape, bf16)
    return pl.pallas_call(
        functools.partial(backward_body, heads),
        out_shape=(rows, rows, rows, jax.ShapeDtypeStruct(bias.shape, bf16)),
        in_specs=in_vmem(5),
        out_specs=tuple(in_vmem(4)),
        compiler_params=params(),
        cost_estimate=pl.CostEstimate(flops=2 * 10**9, bytes_accessed=2 * 10**7, transcendentals=10**6),
        name="attend_backward",
    )(queries, keys, values, bias, grad)


def bias_body(heads, index_ref, table_ref, out_ref):
    def work(block):
        here = pl.ds(pl.multiple_of(block * ROW_STEP, ROW_STEP), ROW_STEP)
        bias_block_of(heads, index_ref, table_ref, out_ref, here)

    with_events(index_ref.shape[0] // ROW_STEP, [], work)


def gather_bias(pair_index, table):
    heads, entries = table.shape
    return pl.pallas_call(
        functools.partial(bias_body, heads),
        out_shape=jax.ShapeDtypeStruct((heads,) + pair_index.shape, bf16),
        in_specs=in_vmem(2),
        out_specs=in_vmem(1)[0],
        compiler_params=params(),
        cost_estimate=pl.CostEstimate(flops=10**9, bytes_accessed=4 * 10**7, transcendentals=0),
        name="bias",
    )(pair_index, table)


def table_body(heads, groups, index_ref, grad_ref, out_ref):
    out_ref[...] = jnp.zeros_like(out_ref)

    def work(block):
        here = pl.ds(pl.multiple_of(block * ROW_STEP, ROW_STEP), ROW_STEP)
        table_block(heads, groups, index_ref, grad_ref, out_ref, here)

    with_events(index_ref.shape[0] // ROW_STEP, [], work)


def table_sums(pair_index, grad_scores, entries):
    heads = grad_scores.shape[0]
    groups = up_to(-(-entries // SPLIT), 16)
    sums = pl.pallas_call(
        functools.partial(table_body, heads, groups),
        out_shape=jax.ShapeDtypeStruct((heads * groups, SPLIT), f32),
        in_specs=in_vmem(2),
        out_specs=in_vmem(1)[0],
        compiler_params=params(),
        cost_estimate=pl.CostEstimate(flops=2 * 10**9, bytes_accessed=6 * 10**7, transcendentals=0),
        name="table_sums",
    )(pair_index, grad_scores)
    return sums.reshape(heads, groups * SPLIT)


def cuts_of(total, pieces, unit=16):
    count, extra = divmod(total // unit, pieces)
    cuts, at = [], 0
    for i in range(pieces):
        size = (count + (i < extra)) * unit
        if size:
            cuts.append((at, size))
        at += size
    return cuts


def remote(src, dst, send_sem, recv_sem, axis, peer):
    return pltpu.make_async_remote_copy(
        src_ref=src,
        dst_ref=dst,
        send_sem=send_sem,
        recv_sem=recv_sem,
        device_id={axis: peer},
        device_id_type=MESH,
    )


def greet(barrier, axis, peer):
    pl.semaphore_signal(barrier, inc=1, device_id={axis: peer}, device_id_type=MESH)


class ShardSum:
    def __init__(self, chunks, part_ref, out_ref, near, sent, far, send_sem, recv_sem):
        me = lax.axis_index("shard")
        outer, self.inner = me // 2, lax.rem(me, 2)
        self.near_peer = outer * 2 + (1 - self.inner)
        self.far_peer = (1 - outer) * 2 + self.inner
        self.chunks, self.part, self.out = chunks, part_ref, out_ref
        self.near, self.sent, self.far = near, sent, far
        self.sems = (send_sem, recv_sem)
        self.half = near.shape[0]

    def greet(self, barrier):
        greet(barrier, "shard", self.near_peer)
        greet(barrier, "shard", self.far_peer)
        return 2

    def rows(self, which, at, size):
        return pl.ds(pl.multiple_of(which * self.half + at, 16), size)

    def copy(self, stage, j, src, dst, peer):
        send_sem, recv_sem = self.sems
        return remote(src, dst, send_sem.at[stage, j], recv_sem.at[stage, j], "shard", peer)

    def first(self, j):
        at, size = self.chunks[j]
        return self.copy(
            0, j, self.part.at[self.rows(1 - self.inner, at, size)], self.near.at[pl.ds(at, size)], self.near_peer
        )

    def second(self, j):
        here = pl.ds(*self.chunks[j])
        return self.copy(1, j, self.sent.at[here], self.far.at[here], self.far_peer)

    def third(self, j):
        mine = self.out.at[self.rows(self.inner, *self.chunks[j])]
        return self.copy(2, j, mine, mine, self.near_peer)

    def start(self):
        for j in range(len(self.chunks)):
            self.first(j).start()

    def cross_one(self, j):
        at, size = self.chunks[j]
        self.first(j).wait_recv()
        here = pl.ds(at, size)
        mine = self.rows(self.inner, at, size)
        self.sent[here] = (self.part[mine] + self.near[here]).astype(bf16)
        self.second(j).start()

    def cross(self):
        for j in range(len(self.chunks)):
            self.cross_one(j)

    def close_one(self, j):
        at, size = self.chunks[j]
        self.second(j).wait_recv()
        here = pl.ds(at, size)
        mine = self.rows(self.inner, at, size)
        self.out[mine] = self.sent[here].astype(f32) + self.far[here].astype(f32)
        self.third(j).start()

    def close(self):
        for j in range(len(self.chunks)):
            self.close_one(j)

    def arrive(self):
        for j in range(len(self.chunks)):
            self.third(j).wait_recv()

    def drain(self):
        for j in range(len(self.chunks)):
            self.first(j).wait_send()
            self.second(j).wait_send()
            self.third(j).wait_send()


class Grid:
    def __init__(self, peers):
        self.length = peers // 2
        self.me = lax.axis_index("dp")
        self.at, self.side = self.me // 2, lax.rem(self.me, 2)
        self.up, self.down = self.me + 2, self.me - 2
        self.across = self.at * 2 + 1 - self.side
        self.has_up, self.has_down = self.at < self.length - 1, self.at > 0

    def greet(self, barrier):
        greet(barrier, "dp", self.across)

        @pl.when(self.has_up)
        def _():
            greet(barrier, "dp", self.up)

        @pl.when(self.has_down)
        def _():
            greet(barrier, "dp", self.down)

        return 1 + self.has_up.astype(jnp.int32) + self.has_down.astype(jnp.int32)

    def clip(self, place):
        return jnp.clip(place, 0, self.length - 1)


class Flood:
    def __init__(self, grid, own, out, up_send, up_recv, down_send, down_recv, side_send, side_recv):
        self.grid, self.own, self.out = grid, own, out
        self.up_sems, self.down_sems = (up_send, up_recv), (down_send, down_recv)
        self.side_sems = (side_send, side_recv)

    def at(self, device):
        depth = self.own.shape[0]
        return self.out.at[pl.ds(pl.multiple_of(device * depth, 8), depth)]

    def block(self, place):
        return self.at(self.grid.clip(place) * 2 + self.grid.side)

    def up(self, s):
        grid, (send, recv) = self.grid, self.up_sems
        block = self.block(grid.at - s)
        return remote(self.own if s == 0 else block, block, send.at[s], recv.at[s], "dp", grid.up)

    def down(self, s):
        grid, (send, recv) = self.grid, self.down_sems
        block = self.block(grid.at + s)
        return remote(self.own if s == 0 else block, block, send.at[s], recv.at[s], "dp", grid.down)

    def across(self, place, own=False):
        grid, (send, recv) = self.grid, self.side_sems
        place = grid.clip(place)
        block = self.block(place)
        return remote(
            self.own if own else block, block, send.at[place], recv.at[place], "dp", grid.across
        )

    def step(self, s):
        grid = self.grid
        if s == 0:

            @pl.when(grid.has_up)
            def _():
                self.up(0).start()

            @pl.when(grid.has_down)
            def _():
                self.down(0).start()

            self.across(grid.at, own=True).start()
            return

        @pl.when(grid.at - s >= 0)
        def _():
            block = self.block(grid.at - s)
            send, recv = self.up_sems
            remote(block, block, send.at[s - 1], recv.at[s - 1], "dp", grid.down).wait_recv()

            @pl.when(grid.has_up)
            def _():
                self.up(s).start()

            self.across(grid.at - s).start()

        @pl.when(grid.at + s < grid.length)
        def _():
            block = self.block(grid.at + s)
            send, recv = self.down_sems
            remote(block, block, send.at[s - 1], recv.at[s - 1], "dp", grid.up).wait_recv()

            @pl.when(grid.has_down)
            def _():
                self.down(s).start()

            self.across(grid.at + s).start()

    def arrive(self):
        grid, (send, recv) = self.grid, self.side_sems
        for place in range(grid.length):
            block = self.at(place * 2 + 1 - grid.side)
            remote(block, block, send.at[place], recv.at[place], "dp", grid.across).wait_recv()

    def drain(self):
        grid = self.grid
        for place in range(grid.length):
            self.across(place).wait_send()
        for s in range(grid.length - 1):

            @pl.when(jnp.logical_and(grid.at - s >= 0, grid.has_up))
            def _():
                self.up(s).wait_send()

            @pl.when(jnp.logical_and(grid.at + s < grid.length, grid.has_down))
            def _():
                self.down(s).wait_send()


SIDE, UP, DOWN = range(3)


class ReduceScatter:
    def __init__(self, grid, grads, out, side, up, down, sems):
        self.grid, self.grads, self.out = grid, grads, out
        self.buffers = (side, up, down)
        self.sems = (sems[:2], sems[2:4], sems[4:6])

    def at(self, device):
        depth = self.out.shape[0]
        return pl.ds(pl.multiple_of(device * depth, 16), depth)

    def prepare(self):
        grid = self.grid

        @pl.when(jnp.logical_not(grid.has_down))
        def _():
            self.buffers[UP][...] = jnp.zeros_like(self.buffers[UP])

        @pl.when(jnp.logical_not(grid.has_up))
        def _():
            self.buffers[DOWN][...] = jnp.zeros_like(self.buffers[DOWN])

    def copy(self, way, place, peer, src=None):
        send, recv = self.sems[way]
        place = self.grid.clip(place)
        dst = self.buffers[way].at[place]
        return remote(dst if src is None else src, dst, send.at[place], recv.at[place], "dp", peer)

    def cross(self, place):
        grid = self.grid
        src = self.grads.at[self.at(grid.clip(place) * 2 + 1 - grid.side)]
        return self.copy(SIDE, place, grid.across, src)

    def start(self, s):
        grid = self.grid

        @pl.when(grid.at + s < grid.length)
        def _():
            self.cross(grid.at + s).start()

        if s:

            @pl.when(grid.at - s >= 0)
            def _():
                self.cross(grid.at - s).start()

    def step(self, s):
        grid = self.grid
        side, up, down = self.buffers
        if s == 0:
            place = grid.at
            self.copy(SIDE, place, grid.across).wait_recv()

            @pl.when(grid.has_down)
            def _():
                self.copy(UP, place, grid.down).wait_recv()

            @pl.when(grid.has_up)
            def _():
                self.copy(DOWN, place, grid.up).wait_recv()

            total = self.grads[self.at(grid.me)].astype(f32) + side[place].astype(f32)
            self.out[...] = total + (up[place].astype(f32) + down[place].astype(f32))
            return

        @pl.when(grid.at + s < grid.length)
        def _():
            place = grid.clip(grid.at + s)
            self.copy(SIDE, place, grid.across).wait_recv()

            @pl.when(grid.has_down)
            def _():
                self.copy(UP, place, grid.down).wait_recv()

            total = self.grads[self.at(place * 2 + grid.side)].astype(f32) + side[place].astype(f32)
            side[place] = (total + up[place].astype(f32)).astype(bf16)
            self.copy(UP, place, grid.up, side.at[place]).start()

        @pl.when(grid.at - s >= 0)
        def _():
            place = grid.clip(grid.at - s)
            self.copy(SIDE, place, grid.across).wait_recv()

            @pl.when(grid.has_up)
            def _():
                self.copy(DOWN, place, grid.up).wait_recv()

            total = self.grads[self.at(place * 2 + grid.side)].astype(f32) + side[place].astype(f32)
            side[place] = (total + down[place].astype(f32)).astype(bf16)
            self.copy(DOWN, place, grid.down, side.at[place]).start()

    def drain(self):
        grid = self.grid
        for place in range(grid.length):
            self.cross(place).wait_send()
        for s in range(1, grid.length):

            @pl.when(grid.at + s < grid.length)
            def _():
                self.copy(UP, grid.at + s, grid.up).wait_send()

            @pl.when(grid.at - s >= 0)
            def _():
                self.copy(DOWN, grid.at - s, grid.down).wait_send()


ROW_STEP = 16
CHUNKS = 4
VECTORS = 8
EARLY_LINES = 16
BIAS_PLACES = [4, 14, 24, 18, 32, 99, 7, 25, 36, 99]
TABLE_PLACES = [-1, 6, 31, 2, 10, 21, 44, 16, 26, 29, 39]
FIRST_CLOSE = 2
RESULT_PLACE = 7
CLOSE_PLACE = 22
NORM_PLACE = 27


def with_events(blocks, events, work):
    def step(block, carry):
        for at, event in events:
            pl.when(block == at)(event)

        @pl.when(block < blocks)
        def _():
            work(block)

        return carry

    lax.fori_loop(0, max([blocks] + [at + 1 for at, _ in events]), step, 0)


class Spread:
    def __init__(self, peers, out, send_sem, recv_sem):
        self.peers, self.out, self.sems = peers, out, (send_sem, recv_sem)
        self.me = lax.axis_index("dp")

    def peer(self, i):
        return lax.rem(self.me + i, self.peers)

    def copy(self, src, slot, peer):
        send_sem, recv_sem = self.sems
        return remote(
            src, self.out.at[slot], send_sem.at[peer], recv_sem.at[slot], "dp", peer
        )

    def start(self, src_for):
        for i in range(1, self.peers):
            self.copy(src_for(self.peer(i)), self.me, self.peer(i)).start()

    def arrive(self):
        for i in range(1, self.peers):
            peer = self.peer(i)
            self.copy(self.out.at[peer], peer, peer).wait_recv()

    def drain(self):
        for i in range(1, self.peers):
            peer = self.peer(i)
            self.copy(self.out.at[peer], peer, peer).wait_send()


def layer_body(plan, *refs):
    tree, heads, groups, slot_rows, peers = plan
    named = {}
    for part in jax.tree.unflatten(tree, refs):
        named.update(part)
    r = types.SimpleNamespace(**named)
    rows, columns = r.index.shape
    model = r.inputs.shape[1]
    depth = model // peers
    inner = heads * HEAD_DIM
    half = rows // 2
    chunks = cuts_of(half, CHUNKS)
    count = len(chunks)
    factor = HEAD_DIM ** (-0.5)
    height = heads * groups

    grid = Grid(peers)
    sums = [
        ShardSum(chunks, *buffers)
        for buffers in zip(r.part, r.total, r.near, r.sent, r.far, r.sum_send, r.sum_recv)
    ]
    lines = Flood(grid, r.own_lines, r.all_lines, *r.flood_sems[3])
    floods = [
        Flood(grid, own, out, *sems) for own, out, sems in zip((r.own_first, r.fc1_weight, r.fc2_weight), r.whole, r.flood_sems)
    ]
    scatters = [
        ReduceScatter(grid, *buffers)
        for buffers in zip(r.grad, r.summed, r.side, r.up, r.down, r.scatter_sems)
    ]
    spreads = [
        Spread(peers, out, *sems)
        for out, sems in zip((r.all_early, r.all_late, r.all_table), r.spread_sems)
    ]

    loads = [
        pltpu.make_async_copy(src, dst, r.load_sem.at[j])
        for j, (src, dst) in enumerate(
            ((r.large_index, r.wide_from), (r.inputs, r.inputs_here), (r.out_grad, r.grad_here))
        )
    ]
    for load in loads:
        load.start()
    for i, member in enumerate(r.small_vectors):
        r.own_lines[i : i + 1, :depth] = member[...].astype(f32).reshape(1, depth)
    for j in range(3):
        r.own_first[:, j * inner : (j + 1) * inner] = r.qkv_weight[j]
    r.own_first[:, 3 * inner :] = r.out_weight[...].T
    barrier = pltpu.get_barrier_semaphore()
    met = sums[0].greet(barrier)
    for i in range(1, peers):
        greet(barrier, "dp", lax.rem(grid.me + i, peers))
    pl.semaphore_wait(barrier, met + peers - 1)
    lines.step(0)
    floods[0].step(0)
    floods[1].step(0)
    copies = [
        pltpu.make_async_copy(flood.own, flood.at(grid.me), r.local_sem.at[j])
        for j, flood in enumerate(floods + [lines])
    ]
    for copy in copies:
        copy.start()
    for scatter in scatters:
        scatter.prepare()

    kind = r.slot_kind[0]
    r.slot[0:1] = jnp.full((1, LANES), kind.astype(f32))
    r.slot[1:2] = jnp.full((1, LANES), (slot_rows - kind * (slot_rows - LARGE_LEN)).astype(f32))
    is_large = jnp.broadcast_to(r.slot[0:1, :], (8, LANES)) > 0.5
    small_side, large_side = r.small_index.shape[0], r.large_index.shape[0]
    r.index[...] = jnp.full((rows, columns), -1, jnp.int32)
    for image in range(slot_rows // small_side):
        at = image * small_side
        r.index[at : at + small_side, at : at + small_side] = r.small_index[...]
    r.wide_index[...] = jnp.full((rows, columns), -1, jnp.int32)
    for load in loads:
        load.wait()
    r.wide_index[:large_side, :large_side] = r.wide_from[...]
    r.table[...] = jnp.zeros_like(r.table)
    entries_small, entries_large = r.small_table.shape[1], r.large_table.shape[1]
    r.table[:heads, :entries_small] = r.small_table[...].astype(f32)
    r.wide_table[...] = jnp.zeros_like(r.wide_table)
    r.wide_table[:heads, :entries_large] = r.large_table[...].astype(f32)
    tall = jnp.broadcast_to(is_large[:, 0:1], r.table.shape)
    r.table[...] = jnp.where(tall, r.wide_table[...], r.table[...])
    large_block = jnp.broadcast_to(r.slot[0:1, 0:1], (ROW_STEP, columns)) > 0.5

    body_rows = slot_rows // 32 * 32
    tail = slot_rows - body_rows
    r.kept[:body_rows] = r.inputs_here[:body_rows]
    r.kept[body_rows:] = jnp.concatenate(
        (
            r.inputs_here[body_rows:slot_rows].astype(f32),
            jnp.zeros((rows - slot_rows, model), f32),
        ),
        0,
    ).astype(bf16)
    blocks = up_to(slot_rows, ROW_STEP) // ROW_STEP

    def bias_block(block):
        here = pl.ds(pl.multiple_of(block * ROW_STEP, ROW_STEP), ROW_STEP)
        r.index[here] = jnp.where(large_block, r.wide_index[here], r.index[here])
        bias_block_of(heads, r.index, r.table, r.bias, here)

    r.index[blocks * ROW_STEP :] = jnp.full((rows - blocks * ROW_STEP, columns), -1, jnp.int32)
    r.bias[:, blocks * ROW_STEP :] = jnp.full(
        (heads, rows - blocks * ROW_STEP, columns), NEG, bf16
    )
    length = grid.length

    def flood_event(j, s):
        return lambda: floods[j].step(s)

    order = [(j, s) for j in range(2) for s in range(1, length)]
    order += [(2, s) for s in range(length)]
    places = BIAS_PLACES if length == 4 else [k * 3 for k in range(len(order))]
    events = [(at, flood_event(*item)) for at, item in zip(places, order)]
    events += [(3 * s, functools.partial(lines.step, s)) for s in range(1, length)]
    late_floods = [event for at, event in events if at >= blocks]
    with_events(blocks, [(at, event) for at, event in events if at < blocks], bias_block)
    for copy in copies:
        copy.wait()
    lines.arrive()
    floods[0].arrive()
    for d in range(peers):
        r.vectors[:, d * depth : (d + 1) * depth] = r.all_lines[
            d * VECTORS : (d + 1) * VECTORS, :depth
        ]

    def vector(i):
        return r.vectors[i : i + 1, :]

    def moments(value):
        mean = jnp.mean(value, -1, keepdims=True)
        center = value - mean
        inverse = lax.rsqrt(jnp.mean(center * center, -1, keepdims=True) + EPS)
        return center * inverse, mean, inverse

    def both(ref, c):
        at, size = chunks[c]
        return jnp.concatenate((ref[at : at + size], ref[half + at : half + at + size]), 0)

    def put(ref, c, value):
        at, size = chunks[c]
        ref[at : at + size] = value[:size]
        ref[half + at : half + at + size] = value[size:]

    def add(i, value):
        r.running[i] += value.reshape(value.shape[0] // 8, 8, value.shape[1]).sum(0)

    r.running[...] = jnp.zeros_like(r.running)
    r.qkv_shift[...] = jnp.zeros_like(r.qkv_shift)
    r.qkv_shift[:, :inner] = r.query_bias[...].astype(f32).reshape(1, inner)
    r.qkv_shift[:, 2 * inner :] = r.value_bias[...].astype(f32).reshape(1, inner)
    r.hidden_shift[...] = r.fc1_bias[...].astype(f32).reshape(r.hidden_shift.shape)
    for c in range(count):
        normal, mean, inverse = moments(both(r.kept, c).astype(f32))
        put(r.mean[0], c, mean)
        put(r.inverse[0], c, inverse)
        normed = (normal * vector(0) + vector(1)).astype(bf16)
        put(r.normed[0], c, normed)
        projected = dot(normed, r.whole[0][:, : 3 * inner], 1, 0) + r.qkv_shift[...]
        put(r.qkv, c, projected.astype(bf16))

    def weights_of(h):
        part = slice(h * HEAD_DIM, (h + 1) * HEAD_DIM)
        keys = slice(inner + h * HEAD_DIM, inner + (h + 1) * HEAD_DIM)
        scores = dot(r.qkv[:, part], r.qkv[:, keys], 1, 1) * factor
        scores = scores + r.bias[h, :, :rows].astype(f32)
        weights = jnp.exp(scores - jnp.max(scores, -1, keepdims=True))
        return weights * (1.0 / jnp.sum(weights, -1, keepdims=True))

    for h in range(heads):
        part = slice(h * HEAD_DIM, (h + 1) * HEAD_DIM)
        values = slice(2 * inner + h * HEAD_DIM, 2 * inner + (h + 1) * HEAD_DIM)
        r.bias[h, :, :rows] = weights_of(h).astype(bf16)
        r.attended[:, part] = dot(r.bias[h, :, :rows], r.qkv[:, values], 1, 0).astype(bf16)

    for event in late_floods:
        event()

    def out_turned():
        return r.whole[0][:, 3 * inner :]

    def live_rows(c):
        at, size = chunks[c]
        first = lax.broadcasted_iota(jnp.int32, (size, 1), 0) + at
        places = jnp.concatenate((first, first + half), 0).astype(f32)
        return jnp.where(places < r.slot[1:2, 0:1], 1.0, 0.0)

    def padded(ref, c):
        at, size = chunks[c]
        last = min(half + at + size, slot_rows)
        low = ref[half + at : last]
        missing = half + at + size - last
        if missing:
            low = jnp.concatenate(
                (low.astype(f32), jnp.zeros((missing, low.shape[1]), f32)), 0
            )
        return jnp.concatenate((ref[at : at + size].astype(f32), low.astype(f32)), 0)

    def keep(ref, c, value):
        at, size = chunks[c]
        last = min(half + at + size, slot_rows)
        ref[at : at + size] = value[:size]
        ref[half + at : last] = value[size : size + last - half - at]

    def project(c):
        put(r.part[0], c, dot(both(r.attended, c), out_turned(), 1, 1))
        sums[0].first(c).start()

    def forward(c):
        if c == 0:
            floods[1].arrive()
        sums[0].third(c).wait_recv()
        middle = both(r.kept, c).astype(f32) + vector(3) * (both(r.total[0], c) + vector(2))
        put(r.middle, c, middle)
        normal, mean, inverse = moments(middle)
        put(r.mean[1], c, mean)
        put(r.inverse[1], c, inverse)
        normed = (normal * vector(4) + vector(5)).astype(bf16)
        put(r.normed[1], c, normed)
        hidden = dot(normed, r.whole[1][...], 1, 0) + r.hidden_shift[...]
        cumulative = 0.5 * (1.0 + lax.erf(hidden * 0.7071067811865476))
        put(
            r.slope,
            c,
            cumulative + hidden * jnp.exp(-0.5 * hidden * hidden) * 0.3989422804014327,
        )
        active = (hidden * cumulative).astype(bf16)
        put(r.active, c, active)
        if c == 0:
            floods[2].arrive()
        put(r.part[1], c, dot(active, r.whole[2][...], 1, 1))
        sums[1].first(c).start()
        grad_result = (padded(r.grad_here, c) * live_rows(c) * vector(7)).astype(bf16)
        put(r.grad_result, c, grad_result)
        add(5, grad_result.astype(f32))
        grad_hidden = (dot(grad_result, r.whole[2][...], 1, 0) * both(r.slope, c)).astype(bf16)
        put(r.grad_hidden, c, grad_hidden)
        add(0, grad_hidden.astype(f32))
        put(r.part[2], c, dot(grad_hidden, r.whole[1][...], 1, 1))
        sums[2].first(c).start()

    def results():
        for c in range(count):
            sums[1].third(c).wait_recv()
            result = both(r.total[1], c) + vector(6)
            live = live_rows(c)
            keep(r.out_here, c, (live * (both(r.middle, c) + vector(7) * result)).astype(bf16))
            add(6, padded(r.grad_here, c) * live * result)
        to_owners(5, r.running[6])
        store.start()

    def back_norm(grad, normal, inverse, gain):
        scaled = grad * gain
        along = jnp.mean(scaled * normal, -1, keepdims=True)
        return inverse * (scaled - jnp.mean(scaled, -1, keepdims=True) - normal * along)

    def backward(c):
        sums[2].third(c).wait_recv()
        grad = both(r.total[2], c)
        inverse = both(r.inverse[1], c)
        normal = (both(r.middle, c) - both(r.mean[1], c)) * inverse
        add(3, grad * normal)
        add(4, grad)
        grad_middle = padded(r.grad_here, c) * live_rows(c)
        grad_middle = grad_middle + back_norm(grad, normal, inverse, vector(4))
        put(r.grad_middle, c, grad_middle)
        add(2, grad_middle * (both(r.total[0], c) + vector(2)))
        grad_branch = (grad_middle * vector(3)).astype(bf16)
        put(r.grad_branch, c, grad_branch)
        add(1, grad_branch.astype(f32))
        put(r.grad_attended, c, dot(grad_branch, out_turned(), 1, 0).astype(bf16))

    def close(work):
        return lambda c: work.close_one(c)

    def cross(work):
        return lambda c: work.cross_one(c)

    stages = [project, cross(sums[0]), close(sums[0]), forward]
    stages += [cross(sums[2]), close(sums[2]), backward]

    def weight_grad(j, left, right, at=0):
        value = dot(left[...], right[...], 0, 0).astype(bf16)
        r.grad[j][:, at : at + value.shape[1]] = value

    def send_grads(j):
        for s in range(length - 1, -1, -1):
            scatters[j].start(s)

    for t in range(count + len(stages) - 1):
        for k in range(len(stages) - 1, -1, -1):
            if 0 <= t - k < count:
                stages[k](t - k)
        if t == count + 2:
            weight_grad(2, r.grad_result, r.active)
            send_grads(2)
        if t == count + 3:
            sums[1].cross()
            weight_grad(1, r.normed[1], r.grad_hidden)
            send_grads(1)

    store = pltpu.make_async_copy(r.out_here, r.layer_out, r.load_sem.at[0])
    weight_grad(0, r.grad_branch, r.attended, 3 * inner)
    steps = list(range(length - 1, -1, -1))
    for h in range(heads):
        part = slice(h * HEAD_DIM, (h + 1) * HEAD_DIM)
        keys = slice(inner + h * HEAD_DIM, inner + (h + 1) * HEAD_DIM)
        values = slice(2 * inner + h * HEAD_DIM, 2 * inner + (h + 1) * HEAD_DIM)
        grad_part = r.grad_attended[:, part]
        r.grad_qkv[:, values] = dot(r.bias[h, :, :rows], grad_part, 0, 0).astype(bf16)
        weights = r.bias[h, :, :rows].astype(f32)
        grad = dot(grad_part, r.qkv[:, values], 1, 1)
        mean = jnp.sum(weights * grad, -1, keepdims=True)
        grad = (weights * (grad - mean)).astype(bf16)
        r.bias[h, :, :rows] = grad
        r.grad_qkv[:, part] = (dot(grad, r.qkv[:, keys], 1, 0) * factor).astype(bf16)
        r.grad_qkv[:, keys] = (dot(grad, r.qkv[:, part], 0, 0) * factor).astype(bf16)
        if h == 0:
            scatters[2].step(steps[0])

    def scatter_event(j, s):
        return lambda: scatters[j].step(s)

    order = [(2, s) for s in steps[1:]] + [(j, s) for j in (1, 0) for s in steps]
    places = TABLE_PLACES if length == 4 else [4 * k for k in range(len(order))]
    events = [(at, scatter_event(*item)) for at, item in zip(places, order)]
    for at, event in events:
        if at < 0:
            event()
    events = [(at, event) for at, event in events if at >= 0]

    sums[0].drain()
    last = sums[0]
    for c in range(count):
        put(r.part[0], c, dot(both(r.grad_qkv, c), r.whole[0][:, : 3 * inner], 1, 1))
        last.first(c).start()
    weight_grad(0, r.normed[0], r.grad_qkv)
    send_grads(0)

    wide = model // LANES
    at = 1
    r.own_early[...] = jnp.zeros_like(r.own_early)
    r.own_early[0:1] = r.slot[0:1, :]

    def line_to(at, line):
        for c in range(-(-line.shape[1] // LANES)):
            piece = line[:, c * LANES : (c + 1) * LANES]
            r.own_early[at + c : at + c + 1, : piece.shape[1]] = piece

    for line in (
        jnp.sum(r.running[0], 0, keepdims=True),
        jnp.sum(r.grad_qkv[:, :inner].astype(f32), 0, keepdims=True),
        jnp.sum(r.grad_qkv[:, 2 * inner :].astype(f32), 0, keepdims=True),
    ):
        line_to(at, line)
        at += up_to(line.shape[1], LANES) // LANES
    spreads[0].start(lambda peer: r.own_early)

    def to_owners(i, value):
        line = jnp.sum(value, 0, keepdims=True)
        for d in range(peers):
            r.own_late[d, i : i + 1, :depth] = line[:, d * depth : (d + 1) * depth]

    r.own_late[...] = jnp.zeros_like(r.own_late)
    for i in range(1, 6):
        to_owners(i - 1, r.running[i])
    r.table_sums[...] = jnp.zeros_like(r.table_sums)

    def norm_step(here, out_rows):
        grad = r.total[0][here]
        normal = (r.kept[here].astype(f32) - r.mean[0][here]) * r.inverse[0][here]
        back = back_norm(grad, normal, r.inverse[0][here], vector(0))
        value = (r.grad_middle[here] + back).astype(bf16)
        if out_rows is None:
            r.input_grad[here] = value
        else:
            r.input_grad[out_rows] = value[:tail]
        product = (grad * normal).reshape(4, 8, model).sum(0)
        return product, grad.reshape(4, 8, model).sum(0)

    def norm_rows():
        last.arrive()

        def step(i, totals):
            gain, shift = norm_step(pl.ds(pl.multiple_of(i * 32, 32), 32), None)
            return totals[0] + gain, totals[1] + shift

        zero = jnp.zeros((8, model), f32)
        gain, shift = lax.fori_loop(0, body_rows // 32, step, (zero, zero))
        if tail:
            more = norm_step(slice(body_rows, rows), slice(body_rows, slot_rows))
            gain, shift = gain + more[0], shift + more[1]
        to_owners(6, gain)
        to_owners(7, shift)
        spreads[1].start(lambda peer: r.own_late.at[peer])

    events += [(0, last.cross), (FIRST_CLOSE, sums[1].close), (RESULT_PLACE, results)]
    events += [(CLOSE_PLACE, last.close), (NORM_PLACE, norm_rows)]
    events.sort(key=lambda item: item[0])
    with_events(
        blocks,
        [(at, event) for at, event in events if at < blocks],
        lambda block: table_block(
            heads,
            groups,
            r.index,
            r.bias,
            r.table_sums,
            pl.ds(pl.multiple_of(block * ROW_STEP, ROW_STEP), ROW_STEP),
        ),
    )
    r.own_table[...] = r.table_sums[...].astype(bf16)
    spreads[2].start(lambda peer: r.own_table)
    for at, event in events:
        if at >= blocks:
            event()
    r.all_early[grid.me] = r.own_early[...]
    r.all_late[grid.me] = r.own_late[grid.me]
    r.all_table[grid.me] = r.own_table[...]
    for spread in spreads:
        spread.arrive()
    early = jnp.zeros(r.early_sums.shape, f32)
    late = jnp.zeros(r.late_sums.shape, f32)
    small = jnp.zeros((height, LANES), f32)
    large = jnp.zeros((height, LANES), f32)
    for d in range(peers):
        kind = r.all_early[d, 0:1] > 0.5
        table = r.all_table[d].astype(f32)
        small += jnp.where(kind, 0.0, table)
        large += jnp.where(kind, table, 0.0)
        early += r.all_early[d]
        late += r.all_late[d]
    r.early_sums[...] = early
    r.late_sums[...] = late
    for out, value in ((r.small_sums, small), (r.large_sums, large)):
        entries = out.shape[1]
        for k in range(-(-entries // SPLIT)):
            first, size = k * SPLIT, min(SPLIT, entries - k * SPLIT)
            for h in range(heads):
                at = h * groups + k
                out[h : h + 1, first : first + size] = value[at : at + 1, :size]
    store.wait()
    for work in sums + floods + [lines] + scatters + spreads:
        work.drain()


def layer(arguments, peers, slot_rows):
    model = arguments["inputs"].shape[1]
    rows = up_to(slot_rows, 32)
    columns = up_to(rows, LANES)
    depth = model // peers
    hidden = arguments["fc1_bias"].shape[0]
    inner = arguments["query_bias"].shape[0]
    widths = [4 * inner, hidden, hidden]
    heads = inner // HEAD_DIM
    tables = [arguments["small_table"].shape, arguments["large_table"].shape]
    entries = up_to(max(shape[1] for shape in tables), LANES)
    groups = up_to(-(-entries // SPLIT), 16)
    height = heads * groups
    count = len(cuts_of(rows // 2, CHUNKS))
    length = peers // 2
    array = jax.ShapeDtypeStruct

    def sems(*shape):
        return pltpu.SemaphoreType.DMA(shape)

    def each(kind, shape, times):
        return [pltpu.VMEM(shape, kind) for _ in range(times)]

    outs = dict(
        layer_out=array((slot_rows, model), bf16),
        input_grad=array((slot_rows, model), bf16),
        small_sums=array(tables[0], f32),
        large_sums=array(tables[1], f32),
        early_sums=array((EARLY_LINES, LANES), f32),
        late_sums=array((VECTORS, LANES), f32),
        summed=[array((depth, w), f32) for w in widths],
    )
    blocks = [pltpu.VMEM((length, depth, w), bf16) for w in widths]
    scratch = dict(
        whole=[pltpu.VMEM((model, w), bf16) for w in widths],
        all_lines=pltpu.VMEM((peers * VECTORS, LANES), f32),
        grad=[pltpu.VMEM((model, w), bf16) for w in widths],
        side=blocks,
        up=blocks,
        down=blocks,
        scatter_sems=[[sems(length)] * 6] * 3,
        flood_sems=[[sems(length)] * 6] * 4,
        spread_sems=[[sems(peers)] * 2] * 3,
        part=each(f32, (rows, model), 3),
        total=each(f32, (rows, model), 3),
        near=each(f32, (rows // 2, model), 3),
        sent=each(bf16, (rows // 2, model), 3),
        far=each(bf16, (rows // 2, model), 3),
        sum_send=[sems(3, count)] * 3,
        sum_recv=[sems(3, count)] * 3,
        local_sem=sems(4),
        load_sem=sems(3),
        wide_from=pltpu.VMEM(arguments["large_index"].shape, jnp.int32),
        inputs_here=pltpu.VMEM((slot_rows, model), bf16),
        grad_here=pltpu.VMEM((slot_rows, model), bf16),
        out_here=pltpu.VMEM((slot_rows, model), bf16),
        own_first=pltpu.VMEM((depth, 4 * inner), bf16),
        own_lines=pltpu.VMEM((VECTORS, LANES), f32),
        slot=pltpu.VMEM((2, LANES), f32),
        hidden_shift=pltpu.VMEM((1, hidden), f32),
        index=pltpu.VMEM((rows, columns), jnp.int32),
        wide_index=pltpu.VMEM((rows, columns), jnp.int32),
        table=pltpu.VMEM((8, entries), f32),
        wide_table=pltpu.VMEM((8, entries), f32),
        bias=pltpu.VMEM((heads, rows, columns), bf16),
        vectors=pltpu.VMEM((VECTORS, model), f32),
        qkv_shift=pltpu.VMEM((1, 3 * inner), f32),
        running=pltpu.VMEM((7, 8, max(model, hidden)), f32),
        mean=each(f32, (rows, 1), 2),
        inverse=each(f32, (rows, 1), 2),
        normed=each(bf16, (rows, model), 2),
        kept=pltpu.VMEM((rows, model), bf16),
        grad_result=pltpu.VMEM((rows, model), bf16),
        grad_branch=pltpu.VMEM((rows, model), bf16),
        active=pltpu.VMEM((rows, hidden), bf16),
        grad_hidden=pltpu.VMEM((rows, hidden), bf16),
        qkv=pltpu.VMEM((rows, 3 * inner), bf16),
        grad_qkv=pltpu.VMEM((rows, 3 * inner), bf16),
        attended=pltpu.VMEM((rows, inner), bf16),
        grad_attended=pltpu.VMEM((rows, inner), bf16),
        middle=pltpu.VMEM((rows, model), f32),
        grad_middle=pltpu.VMEM((rows, model), f32),
        slope=pltpu.VMEM((rows, hidden), f32),
        table_sums=pltpu.VMEM((height, LANES), f32),
        own_table=pltpu.VMEM((height, LANES), bf16),
        all_table=pltpu.VMEM((peers, height, LANES), bf16),
        own_early=pltpu.VMEM((EARLY_LINES, LANES), f32),
        all_early=pltpu.VMEM((peers, EARLY_LINES, LANES), f32),
        own_late=pltpu.VMEM((peers, VECTORS, LANES), f32),
        all_late=pltpu.VMEM((peers, VECTORS, LANES), f32),
    )
    flat = jax.tree.leaves(arguments)
    near, apart = pl.BlockSpec(memory_space=pltpu.VMEM), pl.BlockSpec(memory_space=pl.ANY)
    specs = jax.tree.map(lambda _: near, arguments)
    specs.update(inputs=apart, out_grad=apart, large_index=apart)
    specs.update(slot_kind=pl.BlockSpec(memory_space=pltpu.SMEM))
    out_specs = jax.tree.map(lambda _: near, outs)
    out_specs.update(layer_out=apart)
    shapes, out_tree = jax.tree.flatten(outs)
    tree = jax.tree.structure((arguments, outs, scratch))
    results = pl.pallas_call(
        functools.partial(layer_body, (tree, heads, groups, slot_rows, peers)),
        out_shape=shapes,
        in_specs=jax.tree.leaves(specs),
        out_specs=jax.tree.leaves(out_specs),
        scratch_shapes=jax.tree.leaves(scratch),
        compiler_params=params(collective_id=0, has_side_effects=True),
        name="layer",
    )(*flat)
    return types.SimpleNamespace(**jax.tree.unflatten(out_tree, results))


def finish_body(tree, depth, *refs):
    found, out = (types.SimpleNamespace(**part) for part in jax.tree.unflatten(tree, refs))
    pairs = (
        (found.layer_out, out.layer_out),
        (found.input_grad, out.input_grad),
        (found.summed[1], out.fc1),
        (found.summed[2], out.fc2),
        (found.small_sums, out.small_table),
        (found.large_sums, out.large_table),
    )
    for src, dst in pairs:
        dst[...] = src[...]
    inner = out.query_bias.shape[0]
    for j in range(3):
        out.qkv[j] = found.summed[0][:, j * inner : (j + 1) * inner]
    out.out[...] = found.summed[0][:, 3 * inner :].T
    for i, vector in enumerate(out.vectors):
        vector[...] = found.late_sums[i, :depth]
    at = 1
    for line in (out.fc1_bias, out.query_bias, out.value_bias):
        size = line.shape[0]
        for first in range(0, size, LANES):
            count = min(LANES, size - first)
            line[pl.ds(first, count)] = found.early_sums[at, :count]
            at += 1


def finish(found, depth, inner, hidden):
    array = jax.ShapeDtypeStruct
    found = vars(found)
    outs = dict(
        layer_out=array(found["layer_out"].shape, bf16),
        input_grad=array(found["input_grad"].shape, bf16),
        fc1=array(found["summed"][1].shape, f32),
        fc2=array(found["summed"][2].shape, f32),
        small_table=array(found["small_sums"].shape, f32),
        large_table=array(found["large_sums"].shape, f32),
        qkv=array((3, depth, inner), f32),
        out=array((inner, depth), f32),
        vectors=[array((depth,), f32)] * VECTORS,
        fc1_bias=array((hidden,), f32),
        query_bias=array((inner,), f32),
        value_bias=array((inner,), f32),
    )
    shapes, out_tree = jax.tree.flatten(outs)
    results = pl.pallas_call(
        functools.partial(finish_body, jax.tree.structure((found, outs)), depth),
        out_shape=shapes,
        in_specs=in_vmem(len(jax.tree.leaves(found))),
        out_specs=in_vmem(len(shapes)),
        compiler_params=params(),
        name="finish",
    )(*jax.tree.leaves(found))
    return types.SimpleNamespace(**jax.tree.unflatten(out_tree, results))


def layer_norm(activations, norm_gain, norm_shift):
    center = activations - jnp.mean(activations, -1, keepdims=True)
    inverse = lax.rsqrt(jnp.mean(center * center, -1, keepdims=True) + EPS)
    normal = center * inverse
    return (normal * norm_gain + norm_shift, normal, inverse)


def norm_back(grad_normed, normal, inverse, norm_gain):
    scaled = grad_normed * norm_gain
    return inverse * (
        scaled
        - jnp.mean(scaled, -1, keepdims=True)
        - normal * jnp.mean(scaled * normal, -1, keepdims=True)
    )


def gelu_slope(hidden):
    cumulative = 0.5 * (1.0 + jax.scipy.special.erf(hidden * 0.7071067811865476))
    return cumulative + hidden * jnp.exp(-0.5 * hidden * hidden) * 0.3989422804014327


def pair_map(kind, small_index, large_index, rows, columns):
    def placed(index, at):
        side = index.shape[0]
        return jnp.pad(
            index, ((at, rows - at - side), (at, columns - at - side)), constant_values=-1
        )

    length = small_index.shape[0]
    small = placed(small_index, 0)
    for image in range(1, SLOT_ROWS // length):
        small = jnp.maximum(small, placed(small_index, image * length))
    return jnp.where(kind == 1, placed(large_index, 0), small)


def plain_device(
    images,
    out_grad,
    slot_kind,
    small_index,
    large_index,
    qkv_weight,
    out_weight,
    fc1_weight,
    fc2_weight,
    norm1_gain,
    norm1_shift,
    query_bias,
    value_bias,
    out_bias,
    gamma_attn,
    norm2_gain,
    norm2_shift,
    fc1_bias,
    fc2_bias,
    gamma_mlp,
    small_table,
    large_table,
):
    depth = qkv_weight.shape[0]
    width = query_bias.shape[0]
    hidden_width = fc1_bias.shape[0]
    heads = width // HEAD_DIM
    _, slot_rows, model_width = images.shape
    rows = up_to(slot_rows, 32)
    columns = up_to(rows, LANES)
    kind = slot_kind[0]

    block = jnp.concatenate(
        (
            qkv_weight.reshape(depth, 3 * width),
            fc1_weight,
            out_weight.T,
            fc2_weight.T,
        ),
        1,
    )
    whole = lax.all_gather(block, "dp", axis=0, tiled=True)
    cuts = (3 * width, 3 * width + hidden_width, 4 * width + hidden_width)
    qkv_matrix = whole[:, : cuts[0]]
    fc1_matrix = whole[:, cuts[0] : cuts[1]]
    out_turned = whole[:, cuts[1] : cuts[2]]
    fc2_turned = whole[:, cuts[2] :]
    small_vectors = jnp.stack(
        (norm1_gain, norm1_shift, out_bias, gamma_attn, norm2_gain, norm2_shift, fc2_bias, gamma_mlp)
    )
    vectors = lax.all_gather(small_vectors, "dp", axis=0)
    vectors = jnp.moveaxis(vectors, 0, 1).reshape(8, model_width).astype(f32)

    query_shift = query_bias.astype(f32)
    value_shift = value_bias.astype(f32)
    hidden_shift = fc1_bias.astype(f32)
    small_entries, large_entries = small_table.shape[0], large_table.shape[0]
    entries = up_to(max(small_entries, large_entries), LANES)
    table = jnp.where(
        kind == 1,
        jnp.pad(large_table, ((0, entries - large_entries), (0, 0))),
        jnp.pad(small_table, ((0, entries - small_entries), (0, 0))),
    )
    table = table.T.astype(f32)
    pair_index = pair_map(kind, small_index, large_index, rows, columns)
    bias = gather_bias(pair_index, table)

    positions = jnp.arange(rows)
    live_count = jnp.where(kind == 1, LARGE_LEN, slot_rows)
    live_rows = (positions < live_count).astype(f32).reshape(-1, 1)
    inputs = jnp.pad(images[0], ((0, rows - slot_rows), (0, 0))).astype(f32)
    normed_one, normal_one, inverse_one = layer_norm(inputs, vectors[0], vectors[1])
    normed_one = normed_one.astype(bf16)
    projected = dot(normed_one, qkv_matrix, 1, 0)
    queries = (projected[:, :width] + query_shift).astype(bf16)
    keys = projected[:, width : 2 * width].astype(bf16)
    values = (projected[:, 2 * width :] + value_shift).astype(bf16)
    pieces = attend_forward(queries, keys, values, bias)
    branch_part = dot(pieces, out_turned, 1, 1)
    branch = lax.psum(branch_part, "shard") + vectors[2]
    middle = inputs + vectors[3] * branch
    normed_two, normal_two, inverse_two = layer_norm(middle, vectors[4], vectors[5])
    normed_two = normed_two.astype(bf16)
    hidden = dot(normed_two, fc1_matrix, 1, 0) + hidden_shift
    active = jax.nn.gelu(hidden, approximate=False).astype(bf16)
    result_part = dot(active, fc2_turned, 1, 1)
    result = lax.psum(result_part.astype(bf16), "shard").astype(f32) + vectors[6]
    layer_out = ((middle + vectors[7] * result) * live_rows).astype(bf16)[:slot_rows][None]

    grad_out = jnp.pad(out_grad[0], ((0, rows - slot_rows), (0, 0))).astype(f32) * live_rows
    grad_gamma_mlp = jnp.sum(grad_out * result, 0)
    grad_result = (grad_out * vectors[7]).astype(bf16)
    grad_fc2_bias = jnp.sum(grad_result.astype(f32), 0)
    grad_fc2_turned = dot(grad_result, active, 0, 0)
    grad_active = dot(grad_result, fc2_turned, 1, 0)
    grad_hidden = (grad_active * gelu_slope(hidden)).astype(bf16)
    grad_fc1_bias = jnp.sum(grad_hidden.astype(f32), 0)
    grad_fc1 = dot(normed_two, grad_hidden, 0, 0)
    grad_normed_two = lax.psum(dot(grad_hidden, fc1_matrix, 1, 1), "shard")
    grad_norm2_gain = jnp.sum(grad_normed_two * normal_two, 0)
    grad_norm2_shift = jnp.sum(grad_normed_two, 0)
    grad_middle = grad_out + norm_back(grad_normed_two, normal_two, inverse_two, vectors[4])
    grad_gamma_attn = jnp.sum(grad_middle * branch, 0)
    grad_branch = (grad_middle * vectors[3]).astype(bf16)
    grad_out_bias = jnp.sum(grad_branch.astype(f32), 0)
    grad_out_turned = dot(grad_branch, pieces, 0, 0)
    grad_attended = dot(grad_branch, out_turned, 1, 0).astype(bf16)
    grad_queries, grad_keys, grad_values, grad_scores = attend_backward(
        queries, keys, values, bias, grad_attended
    )
    sums = table_sums(pair_index, grad_scores, entries)
    grad_projected = jnp.concatenate((grad_queries, grad_keys, grad_values), 1)
    grad_qkv = dot(normed_one, grad_projected, 0, 0)
    grad_query_bias = jnp.sum(grad_queries.astype(f32), 0)
    grad_value_bias = jnp.sum(grad_values.astype(f32), 0)
    grad_normed_one = lax.psum(dot(grad_projected, qkv_matrix, 1, 1), "shard")
    grad_norm1_gain = jnp.sum(grad_normed_one * normal_one, 0)
    grad_norm1_shift = jnp.sum(grad_normed_one, 0)
    input_grad = grad_middle + norm_back(grad_normed_one, normal_one, inverse_one, vectors[0])
    input_grad = input_grad.astype(bf16)[:slot_rows][None]

    small_sums = jnp.where(kind == 1, 0.0, sums[:, :small_entries])
    large_sums = jnp.where(kind == 1, sums[:, :large_entries], 0.0)
    local_sums = lax.psum(
        (small_sums, large_sums, grad_query_bias, grad_value_bias, grad_fc1_bias), "dp"
    )
    peers = lax.axis_size("dp")

    def sent_and_summed(value):
        parts = value.astype(bf16).reshape(peers, value.shape[0] // peers, -1)
        arrived = lax.all_to_all(parts, "dp", split_axis=0, concat_axis=0, tiled=True)
        return arrived.astype(f32).sum(axis=0)

    grad_block = sent_and_summed(
        jnp.concatenate((grad_qkv, grad_fc1, grad_out_turned, grad_fc2_turned), 1)
    )
    vector_grads = sent_and_summed(
        jnp.stack(
            (
                grad_norm1_gain,
                grad_norm1_shift,
                grad_out_bias,
                grad_gamma_attn,
                grad_norm2_gain,
                grad_norm2_shift,
                grad_fc2_bias,
                grad_gamma_mlp,
            ),
            1,
        )
    )
    return (
        layer_out,
        input_grad,
        grad_block[:, : cuts[0]].reshape(depth, 3, width),
        grad_block[:, cuts[1] : cuts[2]].T,
        grad_block[:, cuts[0] : cuts[1]],
        grad_block[:, cuts[2] :].T,
        vector_grads[:, 0],
        vector_grads[:, 1],
        local_sums[2],
        local_sums[3],
        vector_grads[:, 2],
        vector_grads[:, 3],
        vector_grads[:, 4],
        vector_grads[:, 5],
        local_sums[4],
        vector_grads[:, 6],
        vector_grads[:, 7],
        local_sums[0].T,
        local_sums[1].T,
    )


def on_device(*arguments):
    depth = arguments[5].shape[0]
    if depth % 16 or lax.axis_size("shard") != 4:
        return plain_device(*arguments)
    return whole_device(*arguments)


def whole_device(
    images,
    out_grad,
    slot_kind,
    small_index,
    large_index,
    qkv_weight,
    out_weight,
    fc1_weight,
    fc2_weight,
    norm1_gain,
    norm1_shift,
    query_bias,
    value_bias,
    out_bias,
    gamma_attn,
    norm2_gain,
    norm2_shift,
    fc1_bias,
    fc2_bias,
    gamma_mlp,
    small_table,
    large_table,
):
    depth = qkv_weight.shape[0]
    found = layer(
        dict(
            inputs=images[0],
            out_grad=out_grad[0],
            slot_kind=slot_kind,
            small_index=small_index,
            large_index=large_index,
            small_table=small_table.T,
            large_table=large_table.T,
            qkv_weight=qkv_weight.transpose(1, 0, 2),
            out_weight=out_weight,
            fc1_weight=fc1_weight,
            fc2_weight=fc2_weight.T,
            small_vectors=[
                norm1_gain,
                norm1_shift,
                out_bias,
                gamma_attn,
                norm2_gain,
                norm2_shift,
                fc2_bias,
                gamma_mlp,
            ],
            query_bias=query_bias,
            value_bias=value_bias,
            fc1_bias=fc1_bias,
        ),
        lax.axis_size("dp"),
        images.shape[1],
    )
    out = finish(found, depth, query_bias.shape[0], fc1_bias.shape[0])
    return (
        out.layer_out[None],
        out.input_grad[None],
        out.qkv.transpose(1, 0, 2),
        out.out,
        out.fc1,
        out.fc2.T,
        out.vectors[6],
        out.vectors[7],
        out.query_bias,
        out.value_bias,
        out.vectors[0],
        out.vectors[1],
        out.vectors[2],
        out.vectors[3],
        out.fc1_bias,
        out.vectors[4],
        out.vectors[5],
        out.small_table.T,
        out.large_table.T,
    )


def solution(mesh):
    return jax.shard_map(
        on_device,
        mesh=mesh,
        in_specs=(
            P("dp", None, None),
            P("dp", None, None),
            P("dp"),
            P(),
            P(),
            P("dp", None, "shard"),
            P("shard", "dp"),
            P("dp", "shard"),
            P("shard", "dp"),
            P("dp"),
            P("dp"),
            P("shard"),
            P("shard"),
            P("dp"),
            P("dp"),
            P("dp"),
            P("dp"),
            P("shard"),
            P("dp"),
            P("dp"),
            P(None, "shard"),
            P(None, "shard"),
        ),
        out_specs=(
            P("dp", None, None),
            P("dp", None, None),
            P("dp", None, "shard"),
            P("shard", "dp"),
            P("dp", "shard"),
            P("shard", "dp"),
            P("dp"),
            P("dp"),
            P("shard"),
            P("shard"),
            P("dp"),
            P("dp"),
            P("dp"),
            P("dp"),
            P("shard"),
            P("dp"),
            P("dp"),
            P(None, "shard"),
            P(None, "shard"),
        ),
        check_vma=False,
    )
```
